32 devices in a mesh: batch: 16 (over z, y, core), seq: 2 (over x).
Axes of the slice: x: 2, y: 2, z: 4, core: 2. Of those that a mesh axis runs over, the one named last changes fastest.
Arguments:
- frames: bfloat16 [4096, 1024], P(('batch', 'seq')), may hold values from -6 to 6
- lengths: int32 [16, 4], P('batch'), may hold values from 1 to 128, as said below
- cotangent: bfloat16 [4096, 1024], P(('batch', 'seq')), may hold values from -6 to 6
- ffn1_in: bfloat16 [1024, 4096], P(('batch', 'seq')), may hold values from -0.1875 to 0.1875
- ffn1_out: bfloat16 [4096, 1024], P(('batch', 'seq')), may hold values from -0.1875 to 0.1875
- query_w: bfloat16 [1024, 1024], P(('batch', 'seq')), may hold values from -0.1875 to 0.1875
- key_w: bfloat16 [1024, 1024], P(('batch', 'seq')), may hold values from -0.1875 to 0.1875
- value_w: bfloat16 [1024, 1024], P(('batch', 'seq')), may hold values from -0.1875 to 0.1875
- out_w: bfloat16 [1024, 1024], P(('batch', 'seq')), may hold values from -0.75 to 0.75
- point_in: bfloat16 [1024, 2048], P(('batch', 'seq')), may hold values from -0.1875 to 0.1875
- point_out: bfloat16 [1024, 1024], P(('batch', 'seq')), may hold values from -0.375 to 0.375
- ffn2_in: bfloat16 [1024, 4096], P(('batch', 'seq')), may hold values from -0.1875 to 0.1875
- ffn2_out: bfloat16 [4096, 1024], P(('batch', 'seq')), may hold values from -0.1875 to 0.1875
- depth_w: bfloat16 [5, 1024], replicated, may hold values from -2.5 to 2.5
- rel_table: bfloat16 [73, 128], replicated, may hold values from -4 to 4
- norm_gains: float32 [5, 1024], replicated, may hold values from 0.25 to 1.75
- norm_biases: float32 [5, 1024], replicated, may hold values from -2 to 2
- bn_gain: float32 [1024], replicated, may hold values from 0.25 to 1.75
- bn_shift: float32 [1024], replicated, may hold values from -2 to 2
Outputs:
- out_frames: bfloat16 [4096, 1024], P(('batch', 'seq'))
- grad_frames: bfloat16 [4096, 1024], P(('batch', 'seq'))
- grad_ffn1_in: float32 [1024, 4096], P(('batch', 'seq'))
- grad_ffn1_out: float32 [4096, 1024], P(('batch', 'seq'))
- grad_query_w: float32 [1024, 1024], P(('batch', 'seq'))
- grad_key_w: float32 [1024, 1024], P(('batch', 'seq'))
- grad_value_w: float32 [1024, 1024], P(('batch', 'seq'))
- grad_out_w: float32 [1024, 1024], P(('batch', 'seq'))
- grad_point_in: float32 [1024, 2048], P(('batch', 'seq'))
- grad_point_out: float32 [1024, 1024], P(('batch', 'seq'))
- grad_ffn2_in: float32 [1024, 4096], P(('batch', 'seq'))
- grad_ffn2_out: float32 [4096, 1024], P(('batch', 'seq'))
- grad_depth: float32 [5, 1024], replicated
- grad_rel: float32 [73, 128], replicated
- grad_gains: float32 [5, 1024], replicated
- grad_biases: float32 [5, 1024], replicated
- grad_bn_gain: float32 [1024], replicated
- grad_bn_shift: float32 [1024], replicated
- sample_variance: float32 [1024], replicated
The draws below stay inside these ranges and needn't reach their ends.
Inputs may be any that keep to these rules, and one draw needn't show every extreme that they name: In each row the first 3 entries are the lengths of the utterances packed in order into the group, the last entry the frames of the padded tail; each row sums to 256. Some group holds an utterance of 128 frames.
All inputs are finite; a program needn't handle non-finite values.
Results may differ from the reference program's by a relative error of at most 0.023.
Values may be sent and summed in bfloat16 or wider, within the bound.
A program may use at most 256 MiB of HBM per device.

```python
import math
import jax
import jax.numpy as jnp
from jax import lax

D = 1024
HEADS = 8
HEAD_DIM = 128
FF = 4096
KERNEL = 5
REL_LEFT = 64
REL_RIGHT = 8
UTT = 4
REL = 73
GROUP = 256
GROUPS = 16
TOKENS = 4096
MAXLEN = 128
QB = 256


def draw_lengths(key, part):
    keys = jax.random.split(jax.random.fold_in(key, 71), 5)
    group_index = jnp.arange(GROUPS, dtype=jnp.int32)
    picked = jax.random.randint(keys[0], (GROUPS,), 0, 4) == 0
    forced = jax.random.randint(keys[1], (), 0, GROUPS)
    with_longest = picked | (group_index == forced)
    shorter = jax.random.randint(keys[2], (GROUPS, 3), GROUP * 5 // 32, GROUP * 15 // 64 + 1)
    drawn = jax.random.randint(keys[3], (GROUPS, 3), GROUP * 7 // 32, GROUP * 5 // 16 + 1)
    where_long = jax.random.randint(keys[4], (GROUPS,), 0, 3)
    slot = jnp.arange(3, dtype=jnp.int32)
    mixed_row = jnp.where(slot[None, :] == where_long[:, None], MAXLEN, shorter)
    utterances = jnp.where(with_longest[:, None], mixed_row, drawn).astype(jnp.int32)
    tail = (GROUP - jnp.sum(utterances, axis=1)).astype(jnp.int32)
    return jnp.concatenate([utterances, tail[:, None]], axis=1).astype(jnp.int32)


def with_spikes(result, stream_key, source, target, shards_of, factor):
    owner, partner = [(jnp.arange(result.shape[dim]) // (result.shape[dim] // shards_of)).reshape([-1 if axis == dim else 1 for axis in range(result.ndim)]) for dim in (source, target)]
    chosen = jax.random.permutation(stream_key, shards_of)[partner]
    strong = (owner == chosen) | (owner == (partner + shards_of // 2) % shards_of)
    return jnp.where(strong, factor * result, result)


def steps_of(rng, shape, cuts, smallest, high):
    def one(position, parts):
        heights = jax.random.uniform(jax.random.fold_in(jax.random.fold_in(rng, 6), position), (parts,), jnp.float32, smallest / len(cuts), high / len(cuts))
        return jnp.repeat(jnp.exp(heights), shape[position] // parts).reshape((-1,) + (1,) * (len(shape) - position - 1))

    level = one(*cuts[0])
    for cut in cuts[1:]:
        level = level * one(*cut)
    return level


def normal_values(own_key, dims, scale, bound, cuts=(), held_as=jnp.bfloat16):
    result = scale * jax.random.normal(own_key, dims, jnp.float32)
    if cuts:
        result = result * steps_of(own_key, dims, cuts, -0.22, 0.18)
    return jnp.clip(result, -bound, bound).astype(held_as)


def bell_draw_with(key, shape, width, most, shards, heavy, kind=jnp.bfloat16):
    array = width * jax.random.normal(key, shape, jnp.float32)
    if shards:
        array = array * steps_of(key, shape, shards, -0.22, 0.18)
    return jnp.clip(with_spikes(array, jax.random.fold_in(key, 3), *heavy), -most, most).astype(kind)


def setup_inputs(seed: int = 0) -> dict:
    seeds = jax.random.split(jax.random.key(seed), 20)
    return {
        "frames": normal_values(seeds[0], (TOKENS, D), 1.0, 6.0, ((0, 32),)),
        "lengths": draw_lengths(jax.random.fold_in(seeds[19], 71), 0),
        "cotangent": bell_draw_with(seeds[2], (TOKENS, D), 1.0, 6.0, ((0, 32),), (0, 1, 32, 2.75)),
        "ffn1_in": normal_values(seeds[3], (D, FF), D ** -0.5, 0.1875, ((0, 32),)),
        "ffn1_out": normal_values(seeds[4], (FF, D), (FF // 4) ** -0.5, 0.1875, ((0, 32),)),
        "query_w": normal_values(seeds[5], (D, D), D ** -0.5, 0.1875, ((0, 32),)),
        "key_w": normal_values(seeds[6], (D, D), D ** -0.5, 0.1875, ((0, 32),)),
        "value_w": normal_values(seeds[7], (D, D), D ** -0.5, 0.1875, ((0, 32),)),
        "out_w": normal_values(seeds[8], (D, D), (D // 16) ** -0.5, 0.75, ((0, 32),)),
        "point_in": normal_values(seeds[9], (D, 2 * D), D ** -0.5, 0.1875, ((0, 32),)),
        "point_out": normal_values(seeds[10], (D, D), (D // 4) ** -0.5, 0.375, ((0, 32),)),
        "ffn2_in": normal_values(seeds[11], (D, FF), D ** -0.5, 0.1875, ((0, 32),)),
        "ffn2_out": normal_values(seeds[12], (FF, D), (FF // 4) ** -0.5, 0.1875, ((0, 32),)),
        "depth_w": normal_values(seeds[13], (KERNEL, D), KERNEL ** -0.5, 2.5),
        "rel_table": normal_values(seeds[14], (REL, HEAD_DIM), 1.0, 4.0),
        "norm_gains": jnp.clip(1.0 + 0.15 * jax.random.normal(seeds[15], (5, D), jnp.float32), 0.25, 1.75),
        "norm_biases": normal_values(seeds[16], (5, D), 0.3, 2.0, (), jnp.float32),
        "bn_gain": jnp.clip(1.0 + 0.15 * jax.random.normal(seeds[17], (D,), jnp.float32), 0.25, 1.75),
        "bn_shift": normal_values(seeds[18], (D,), 0.3, 2.0, (), jnp.float32),
    }


epsilon = 1e-05
masked_score = -1000000000.0
highest = lax.Precision.HIGHEST

@jax.custom_vjp
def low(v):
    return lax.optimization_barrier(v.astype(jnp.bfloat16)).astype(jnp.float32)

@jax.custom_vjp
def low_back(v):
    return v

def low_keep(v):
    return (low(v), None)

def low_pass(kept, grad):
    return (grad,)

def back_keep(v):
    return (v, None)

def back_low(kept, grad):
    return (low(grad),)
low.defvjp(low_keep, low_pass)
low_back.defvjp(back_keep, back_low)

def matmul(left, right):
    return jnp.dot(left, right, precision=highest)

def layer_norm(values, gain, shift):
    mean = lax.optimization_barrier(jnp.mean(values, axis=-1, keepdims=True))
    centred = values - mean
    spread = lax.optimization_barrier(jnp.mean(centred * centred, axis=-1, keepdims=True))
    return centred * lax.rsqrt(spread + epsilon) * gain + shift

def feed_forward(values, gain, shift, weight_in, weight_out):
    hidden = low(layer_norm(values, gain, shift))
    act = low_back(matmul(hidden, weight_in))
    swish = low(jax.nn.silu(act))
    branch = low_back(matmul(swish, weight_out))
    return values + 0.5 * branch

def attend_group(query, keys, values, table, segment):
    scale = 1.0 / math.sqrt(HEAD_DIM)
    key_place = jnp.arange(GROUP, dtype=jnp.int32)

    def block(operands):
        rows_query, start = operands
        row_place = start + jnp.arange(QB, dtype=jnp.int32)
        project = low_back(jnp.einsum('qhd,rd->hqr', rows_query, table, precision=highest))
        index = jnp.clip(key_place[None, :] - row_place[:, None], -REL_LEFT, REL_RIGHT) + REL_LEFT
        index = jnp.broadcast_to(index[None], (HEADS, QB, GROUP)).astype(jnp.int32)
        relative = jnp.take_along_axis(project, index, axis=2)
        content = jnp.einsum('qhd,khd->hqk', rows_query, keys, precision=highest)
        row_segment = lax.dynamic_slice_in_dim(segment, start, QB)
        same = row_segment[:, None] == segment[None, :]
        scores = low_back(jnp.where(same[None], scale * (content + relative), masked_score))
        probs = jax.nn.softmax(scores, axis=-1)
        return jnp.einsum('hqk,khd->qhd', low(probs), values, precision=highest)
    starts = jnp.arange(GROUP // QB, dtype=jnp.int32) * QB
    pieces = lax.map(jax.checkpoint(block), (query.reshape(GROUP // QB, QB, HEADS, HEAD_DIM), starts))
    return pieces.reshape(GROUP, HEADS * HEAD_DIM)

def depthwise(gated, kernel, segment):
    reach = KERNEL // 2
    rows = gated.shape[0]
    padded = jnp.pad(gated, ((reach, reach), (0, 0)))
    padded_segment = jnp.pad(segment, (reach, reach), constant_values=-1)
    mixed = jnp.zeros_like(gated)
    for offset in range(KERNEL):
        same = (padded_segment[offset:offset + rows] == segment).astype(jnp.float32)
        mixed = mixed + kernel[offset] * padded[offset:offset + rows] * same[:, None]
    return mixed

def conv_module(values, gain, shift, weight_in, weight_out, kernel, bn_gain, bn_shift, segment_flat, weight, count):
    hidden = low(layer_norm(values, gain, shift))
    pointwise = low_back(matmul(hidden, weight_in))
    gated = low(pointwise[:, :D] * jax.nn.sigmoid(pointwise[:, D:]))
    mixed = low_back(depthwise(gated, kernel, segment_flat))
    column = weight[:, None]
    mean = lax.optimization_barrier(jnp.sum(mixed * column, axis=0)) / count
    var = lax.optimization_barrier(jnp.sum(mixed * mixed * column, axis=0)) / count - mean * mean
    normed = (mixed - mean) * lax.rsqrt(var + epsilon) * bn_gain + bn_shift
    swish = low(jax.nn.silu(normed))
    return (values + low_back(matmul(swish, weight_out)), mean, var)

def split_heads(array_in):
    return array_in.reshape(GROUPS, GROUP, HEADS, HEAD_DIM)

def forward(params, segment, segment_flat, weight, count):
    frames, ffn1_in, ffn1_out, query_w, key_w, value_w, out_w, point_in, point_out, ffn2_in, ffn2_out, depth_w, rel_table, norm_gains, norm_biases, bn_gain, bn_shift = params
    after_first = feed_forward(frames, norm_gains[0], norm_biases[0], ffn1_in, ffn1_out)
    hidden = low(layer_norm(after_first, norm_gains[1], norm_biases[1]))
    query = low(low_back(matmul(hidden, query_w)))
    keys = low(low_back(matmul(hidden, key_w)))
    values = low(low_back(matmul(hidden, value_w)))

    def per_group(operands):
        return attend_group(operands[0], operands[1], operands[2], rel_table, operands[3])
    context = lax.map(per_group, (split_heads(query), split_heads(keys), split_heads(values), segment))
    context = low(low_back(context.reshape(TOKENS, D)))
    after_attn = after_first + low_back(matmul(context, out_w))
    after_conv, mean, var = conv_module(after_attn, norm_gains[2], norm_biases[2], point_in, point_out, depth_w, bn_gain, bn_shift, segment_flat, weight, count)
    after_second = feed_forward(after_conv, norm_gains[3], norm_biases[3], ffn2_in, ffn2_out)
    return (layer_norm(after_second, norm_gains[4], norm_biases[4]), (mean, var))

def reference(frames, lengths, cotangent, ffn1_in, ffn1_out, query_w, key_w, value_w, out_w, point_in, point_out, ffn2_in, ffn2_out, depth_w, rel_table, norm_gains, norm_biases, bn_gain, bn_shift):
    ends = jnp.cumsum(lengths, axis=1).astype(jnp.int32)
    place = jnp.arange(GROUP, dtype=jnp.int32)
    segment = lax.optimization_barrier(jnp.sum((place[None, :, None] >= ends[:, None, :]).astype(jnp.int32), axis=2)).astype(jnp.int32)
    weight = (segment < UTT - 1).astype(jnp.float32).reshape(TOKENS)
    count = jnp.sum(weight)
    offsets = (UTT * jnp.arange(GROUPS, dtype=jnp.int32))[:, None]
    segment_flat = (segment + offsets).astype(jnp.int32).reshape(TOKENS)
    params = tuple((array_in.astype(jnp.float32) for array_in in (frames, ffn1_in, ffn1_out, query_w, key_w, value_w, out_w, point_in, point_out, ffn2_in, ffn2_out, depth_w, rel_table, norm_gains, norm_biases, bn_gain, bn_shift)))

    def run(operands):
        return forward(operands, segment, segment_flat, weight, count)
    output, pull, stats = jax.vjp(run, params, has_aux=True)
    grads, = pull(cotangent.astype(jnp.float32) * weight[:, None])
    mean, var = stats
    sample_variance = var * count / (count - 1.0)
    return (output.astype(jnp.bfloat16), grads[0].astype(jnp.bfloat16), grads[1], grads[2], grads[3], grads[4], grads[5], grads[6], grads[7], grads[8], grads[9], grads[10], grads[11], grads[12], grads[13], grads[14], grads[15], grads[16], sample_variance)
```

```python
import functools
import math

import jax
import jax.numpy as jnp
from jax import lax
from jax.experimental import pallas as pl
from jax.experimental.pallas import tpu as pltpu
from jax.sharding import PartitionSpec as P

MESH = pl.DeviceIdType.MESH
AXES = ("batch", "seq")

HEADS = 8
REL_LEFT = 64
REL_RIGHT = 8


epsilon = 1e-05
masked_score = -1000000000.0


def padded_2(shard, sides, width):
    for axis, dim in sides:
        peers, length = (lax.axis_size(axis), shard.shape[dim])
        up = [(i, (i + 1) % peers) for i in range(peers - 1)]
        down = [(j, i) for i, j in up]
        last = lax.slice_in_dim(shard, length - width, length, axis=dim)
        first = lax.slice_in_dim(shard, 0, width, axis=dim)
        before = lax.ppermute(last, axis, up)
        after = lax.ppermute(first, axis, down)
        shard = jnp.concatenate([before, shard, after], axis=dim)
    return shard


def matmul(left, right):
    return jnp.dot(left, right, preferred_element_type=jnp.float32)


def transposed_left(left, right):
    return lax.dot_general(
        left, right, (((0,), (0,)), ((), ())), preferred_element_type=jnp.float32
    )


def transposed_right(left, right):
    return lax.dot_general(
        left, right, (((1,), (1,)), ((), ())), preferred_element_type=jnp.float32
    )


class Cube:
    def __init__(self, batch, seq):
        self.seq_bits, self.batch_bits = (seq.bit_length() - 1, batch.bit_length() - 1)
        self.count = self.seq_bits + self.batch_bits
        self.core = self.seq_bits
        wide = (self.batch_bits - 1) // 2
        self.x = list(range(self.seq_bits))[::-1]
        self.y = list(range(self.core + 1, self.core + 1 + wide))[::-1]
        self.z = list(range(self.core + 1 + wide, self.count))[::-1]

    def bit(self, k):
        if k < self.seq_bits:
            return lax.rem(lax.axis_index("seq") // (1 << k), 2)
        return lax.rem(lax.axis_index("batch") // (1 << (k - self.seq_bits)), 2)

    def partner(self, k):
        batch, seq = (lax.axis_index("batch"), lax.axis_index("seq"))
        step = 1 - 2 * self.bit(k)
        if k < self.seq_bits:
            return (batch, seq + step * (1 << k))
        return (batch + step * (1 << (k - self.seq_bits)), seq)

    def swap(self, values, k):
        if k < self.seq_bits:
            axis, step = ("seq", 1 << k)
        else:
            axis, step = ("batch", 1 << (k - self.seq_bits))
        pairs = [(i, i ^ step) for i in range(lax.axis_size(axis))]
        return lax.ppermute(values, axis, pairs)


def greet(cube, bits):
    barrier = pltpu.get_barrier_semaphore()
    for k in bits:
        pl.semaphore_signal(barrier, inc=1, device_id=cube.partner(k), device_id_type=MESH)
    pl.semaphore_wait(barrier, len(bits))


def gather_kernel(cube, orders, count, which, cuts, *refs):
    shards, outs = (refs[:count], refs[count : 2 * count])
    send, recv, local = refs[2 * count :]
    bits = range(cube.count)
    own = [cube.bit(k) for k in bits]
    kept = []
    for m in range(count):
        kept.append(
            pltpu.make_async_copy(shards[m], outs[m].at[tuple(own[::-1])], local.at[m])
        )
        kept[m].start()
    greet(cube, bits)
    lanes = len(orders)

    def copy(chunk, lane, stage):
        m, order = (which[chunk], orders[lane])
        row, rows, column, columns = cuts[chunk][lane]
        block = (pl.ds(row, rows), pl.ds(column, columns))
        lead = tuple(slice(None) if k in order[:stage] else own[k] for k in reversed(bits))
        place = outs[m].at[lead + block]
        return pltpu.make_async_remote_copy(
            src_ref=shards[m].at[block] if stage == 0 else place,
            dst_ref=place,
            send_sem=send.at[chunk * lanes + lane, stage],
            recv_sem=recv.at[chunk * lanes + lane, stage],
            device_id=cube.partner(order[stage]),
            device_id_type=MESH,
        )

    for chunk in range(len(cuts)):
        for lane in range(lanes):
            copy(chunk, lane, 0).start()
    for one in kept:
        one.wait()
    stages = cube.count
    for turn in range(len(cuts) + stages):
        for stage in range(stages):
            chunk = turn - stage - (stage == stages - 1)
            if 0 <= chunk < len(cuts):
                for lane in range(lanes):
                    copy(chunk, lane, stage).wait_recv()
                    if stage + 1 < stages:
                        copy(chunk, lane, stage + 1).start()
    for chunk in range(len(cuts)):
        for lane in range(lanes):
            for stage in range(stages):
                copy(chunk, lane, stage).wait_send()


def column_parts(width, shares):
    units, total, at, parts = (width // 128, sum(shares), 0, [])
    for share in shares:
        size = units * share // total
        parts.append((at * 128, size * 128))
        at += size
    return parts


def gather_fast(shards, cube):
    core = [cube.core]
    orders = [
        cube.z + cube.y + cube.x + core,
        cube.z + cube.x + cube.y + core,
        cube.x + cube.y + cube.z + core,
    ]
    which, cuts = ([], [])
    for m, shard in enumerate(shards):
        rows, columns = (min(64, shard.shape[0]), min(2048, shard.shape[1]))
        for row in range(0, shard.shape[0], rows):
            for column in range(0, shard.shape[1], columns):
                which.append(m)
                cuts.append(
                    [(row, rows, column + a, w) for a, w in column_parts(columns, (3, 3, 2))]
                )
    count, items = (len(shards), len(cuts) * len(orders))
    outs = pl.pallas_call(
        functools.partial(gather_kernel, cube, orders, count, which, cuts),
        out_shape=[
            jax.ShapeDtypeStruct((2,) * cube.count + shard.shape, shard.dtype) for shard in shards
        ],
        in_specs=[pl.BlockSpec(memory_space=pl.ANY)] * count,
        out_specs=[pl.BlockSpec(memory_space=pl.ANY)] * count,
        scratch_shapes=[
            pltpu.SemaphoreType.DMA((items, cube.count)),
            pltpu.SemaphoreType.DMA((items, cube.count)),
            pltpu.SemaphoreType.DMA((count,)),
        ],
        compiler_params=pltpu.CompilerParams(collective_id=0, has_side_effects=True),
        name="gather_weights",
    )(*shards)
    return tuple(out.reshape(-1, shard.shape[1]) for out, shard in zip(outs, shards))


def sum_kernel(cube, value, out, held, sent, send, recv):
    bits = range(cube.count)
    greet(cube, bits)
    sent[0] = value[...]
    for k in bits:
        copy = pltpu.make_async_remote_copy(
            src_ref=sent.at[k],
            dst_ref=held.at[k],
            send_sem=send.at[k],
            recv_sem=recv.at[k],
            device_id=cube.partner(k),
            device_id_type=MESH,
        )
        copy.start()
        copy.wait()
        if k + 1 < cube.count:
            sent[k + 1] = sent[k] + held[k]
        else:
            out[...] = sent[k] + held[k]


def sum_fast(value, cube, number):
    return pl.pallas_call(
        functools.partial(sum_kernel, cube),
        out_shape=jax.ShapeDtypeStruct(value.shape, value.dtype),
        in_specs=[pl.BlockSpec(memory_space=pltpu.VMEM)],
        out_specs=pl.BlockSpec(memory_space=pltpu.VMEM),
        scratch_shapes=[
            pltpu.VMEM((cube.count,) + value.shape, value.dtype),
            pltpu.VMEM((cube.count,) + value.shape, value.dtype),
            pltpu.SemaphoreType.DMA((cube.count,)),
            pltpu.SemaphoreType.DMA((cube.count,)),
        ],
        compiler_params=pltpu.CompilerParams(collective_id=number, has_side_effects=True),
        name="sum_over_devices",
    )(value)


def sum_everywhere(values, cube, number):
    if cube is None:
        return lax.psum(values, AXES)
    flat = jnp.concatenate([value.reshape(-1) for value in values])
    size = -(-flat.shape[0] // 8192) * 8192
    flat = jnp.pad(flat, (0, size - flat.shape[0])).reshape(-1, 1024)
    flat = sum_fast(flat, cube, number).reshape(-1)
    out, at = ([], 0)
    for value in values:
        out.append(flat[at : at + value.size].reshape(value.shape))
        at += value.size
    return tuple(out)


def reduce_kernel(cube, order, rows, columns, count, places, *refs):
    parts, out, refs = (refs[:count], refs[count], refs[count + 1 :])
    stages, number = (len(order), len(places))
    own, refs = (refs[0], refs[1:])
    recv_at, refs = (refs[:stages], refs[stages:])
    send_at, refs = ((None,) + refs[: stages - 1], refs[stages - 1 :])
    keep_at, refs = ((None,) + refs[: stages - 1], refs[stages - 1 :])
    send, recv, local = refs
    bits = [cube.bit(k) for k in order]
    dims = sorted(order, reverse=True)

    def spot(stage, flip):
        left = [k for k in dims if k not in order[:stage]]
        side = bits[stage]
        side = 1 - side if flip else side
        return tuple(side if k == order[stage] else slice(None) for k in left)

    def remote(stage, chunk, source):
        return pltpu.make_async_remote_copy(
            src_ref=source,
            dst_ref=recv_at[stage].at[chunk],
            send_sem=send.at[stage, chunk],
            recv_sem=recv.at[stage, chunk],
            device_id=cube.partner(order[stage]),
            device_id_type=MESH,
        )

    greet(cube, order)
    for chunk, (m, row, column) in enumerate(places):
        block = (pl.ds(row, rows), pl.ds(column, columns))
        remote(0, chunk, parts[m].at[spot(0, True) + block]).start()
        pltpu.make_async_copy(
            parts[m].at[spot(0, False) + block], own.at[chunk], local.at[chunk]
        ).start()

    def turn(step, carry):
        for stage in range(stages):
            chunk = step - stage

            @pl.when((chunk >= 0) & (chunk < number))
            def _():
                source = own if stage == 0 else keep_at[stage]
                if stage == 0:
                    pltpu.make_async_copy(own.at[chunk], own.at[chunk], local.at[chunk]).wait()
                remote(stage, chunk, recv_at[stage].at[chunk]).wait_recv()
                arrived = recv_at[stage]
                if stage + 1 == stages:
                    out[chunk] = source[chunk] + arrived[chunk].astype(jnp.float32)
                else:
                    away, home = (spot(stage + 1, True), spot(stage + 1, False))
                    send_at[stage + 1][chunk] = (
                        source[(chunk,) + away].astype(jnp.float32)
                        + arrived[(chunk,) + away].astype(jnp.float32)
                    ).astype(jnp.bfloat16)
                    remote(stage + 1, chunk, send_at[stage + 1].at[chunk]).start()
                    keep_at[stage + 1][chunk] = source[(chunk,) + home].astype(
                        jnp.float32
                    ) + arrived[(chunk,) + home].astype(jnp.float32)

        return carry

    lax.fori_loop(0, number + stages, turn, 0)

    def finish(chunk, carry):
        for stage in range(stages):
            remote(stage, chunk, recv_at[stage].at[chunk]).wait_send()
        return carry

    lax.fori_loop(0, number, finish, 0)


def reduce_fast(parts, cube, rows, columns):
    order = cube.y + cube.z[::-1]
    stages, count = (len(order), len(parts))
    places = []
    for m, part in enumerate(parts):
        for row in range(0, part.shape[-2], rows):
            for column in range(0, part.shape[-1], columns):
                places.append((m, row, column))
    number, tile = (len(places), (rows, columns))

    def held(stage, dtype):
        return pltpu.VMEM((number,) + (2,) * (stages - 1 - stage) + tile, dtype)

    out = pl.pallas_call(
        functools.partial(reduce_kernel, cube, order, rows, columns, count, places),
        out_shape=jax.ShapeDtypeStruct((number,) + tile, jnp.float32),
        in_specs=[pl.BlockSpec(memory_space=pl.ANY)] * count,
        out_specs=pl.BlockSpec(memory_space=pltpu.VMEM),
        scratch_shapes=[held(0, jnp.bfloat16)]
        + [held(stage, jnp.bfloat16) for stage in range(stages)]
        + [held(stage, jnp.bfloat16) for stage in range(1, stages)]
        + [held(stage, jnp.float32) for stage in range(1, stages)]
        + [
            pltpu.SemaphoreType.DMA((stages, number)),
            pltpu.SemaphoreType.DMA((stages, number)),
            pltpu.SemaphoreType.DMA((number,)),
        ],
        compiler_params=pltpu.CompilerParams(
            collective_id=4, has_side_effects=True, vmem_limit_bytes=56 * 1024 * 1024
        ),
        name="reduce_gradients",
    )(*parts)
    results, at = ([], 0)
    for part in parts:
        down, across = (part.shape[-2] // rows, part.shape[-1] // columns)
        piece = out[at : at + down * across].reshape(down, across, rows, columns)
        results.append(piece.transpose(0, 2, 1, 3).reshape(part.shape[-2], part.shape[-1]))
        at += down * across
    return results


def near_sum(left, right, cube):
    near = cube.seq_bits + 1
    flipped = left.T
    rows = flipped.shape[0] >> cube.count
    flipped = flipped.reshape((-1,) + (2,) * near + (rows, left.shape[0]))
    for k in range(near):
        axis = flipped.ndim - 3
        away = lax.dynamic_index_in_dim(flipped, 1 - cube.bit(k), axis, keepdims=False)
        home = lax.dynamic_index_in_dim(flipped, cube.bit(k), axis, keepdims=False)
        flipped = jnp.concatenate([home, cube.swap(away, k)], axis=-1)
        right = jnp.concatenate([right, cube.swap(right, k)], axis=0)
    sums = matmul(flipped.reshape(-1, flipped.shape[-1]), right).astype(jnp.bfloat16)
    return sums.reshape((2,) * (cube.count - near) + (rows, right.shape[1]))


def gradient_shards(pairs, cube):
    if cube is None:
        results = []
        for left, right in pairs:
            whole = transposed_left(left, right)
            flat = whole.reshape(-1, 128)
            shard = lax.psum_scatter(flat, AXES, scatter_dimension=0, tiled=True)
            results.append(shard.reshape(-1, whole.shape[1]))
        return results
    return reduce_fast([near_sum(left, right, cube) for left, right in pairs], cube, 32, 1024)


def gather_all(shards, cube):
    if cube is None:
        return tuple(lax.all_gather(shard, AXES, axis=0, tiled=True) for shard in shards)
    return gather_fast(shards, cube)


def cube_of(shards):
    batch, seq = (lax.axis_size("batch"), lax.axis_size("seq"))
    if seq != 2 or batch < 8 or batch & (batch - 1):
        return None
    if any(shard.shape[0] % 32 or shard.shape[1] % 1024 for shard in shards):
        return None
    return Cube(batch, seq)


def swish_slope(values):
    sigma = jax.nn.sigmoid(values)
    return sigma * (1.0 + values * (1.0 - sigma))


def norm_forward(values, gain, shift):
    mean = jnp.mean(values, axis=-1, keepdims=True)
    centred = values - mean
    inverse = lax.rsqrt(jnp.mean(centred * centred, axis=-1, keepdims=True) + epsilon)
    unit = centred * inverse
    return (unit * gain + shift, unit, inverse)


def norm_backward(d_out, unit, inverse, gain):
    d_unit = d_out * gain
    d_values = inverse * (
        d_unit
        - jnp.mean(d_unit, axis=-1, keepdims=True)
        - unit * jnp.mean(d_unit * unit, axis=-1, keepdims=True)
    )
    return (d_values, jnp.sum(d_out * unit, axis=0), jnp.sum(d_out, axis=0))


def ffn_forward(values, gain, shift, weight_in, weight_out):
    normed, unit, inverse = norm_forward(values, gain, shift)
    hidden = normed.astype(jnp.bfloat16)
    act = matmul(hidden, weight_in)
    swish = jax.nn.silu(act).astype(jnp.bfloat16)
    return (values + 0.5 * matmul(swish, weight_out), (hidden, act, swish, unit, inverse))


def ffn_backward(d_out, kept, gain, weight_in, weight_out):
    hidden, act, swish, unit, inverse = kept
    d_branch = (0.5 * d_out).astype(jnp.bfloat16)
    d_act = (transposed_right(d_branch, weight_out) * swish_slope(act)).astype(jnp.bfloat16)
    d_norm, d_gain, d_shift = norm_backward(transposed_right(d_act, weight_in), unit, inverse, gain)
    return (d_out + d_norm, (hidden, d_act), (swish, d_branch), d_gain, d_shift)


def segment_ids(place, ends, group):
    inside = jnp.sum((place[:, None] >= ends[None, :]).astype(jnp.int32), axis=1)
    return jnp.where((place >= 0) & (place < group), inside, -1)


def to_heads(hidden, weight, heads):
    return matmul(hidden, weight).astype(jnp.bfloat16).reshape(hidden.shape[0], heads, -1)


def spread_band(project, start, group, left, right):
    heads, rows, width = project.shape
    band = rows + width - 1
    blank = jnp.zeros_like(project[:, :, :1])
    middle = jnp.concatenate([blank, project[:, :, 1 : width - 1], blank], axis=2)
    padded = jnp.pad(middle, ((0, 0), (0, 0), (0, band + 1 - width)))
    skewed = padded.reshape(heads, rows * (band + 1))[:, : rows * band].reshape(heads, rows, band)
    canvas = jnp.zeros((heads, rows, group + left + right), jnp.float32)
    anchor = jnp.zeros((), jnp.int32)
    canvas = lax.dynamic_update_slice(canvas, skewed, (anchor, anchor, start))
    return canvas[:, :, left : left + group]


def relative_bins(grad, difference, start, width, left, right):
    heads, rows, group = grad.shape
    band = rows + width - 1
    canvas = jnp.pad(grad, ((0, 0), (0, 0), (left, right)))
    anchor = jnp.zeros((), jnp.int32)
    strip = lax.dynamic_slice(canvas, (anchor, anchor, start), (heads, rows, band))
    flat = jnp.pad(strip.reshape(heads, rows * band), ((0, 0), (0, rows)))
    inner = flat.reshape(heads, rows, band + 1)[:, :, 1 : width - 1]
    below = jnp.sum(jnp.where(difference[None] <= -left, grad, 0.0), axis=2, keepdims=True)
    above = jnp.sum(jnp.where(difference[None] >= right, grad, 0.0), axis=2, keepdims=True)
    return jnp.concatenate([below, inner, above], axis=2)


def block_scores(rows_query, keys, table, segment, start, left, right):
    rows, heads, depth = rows_query.shape
    group = keys.shape[0]
    width = table.shape[0]
    scale = 1.0 / math.sqrt(depth)
    project = jnp.einsum("qhd,rd->hqr", rows_query, table, preferred_element_type=jnp.float32)
    content = jnp.einsum("qhd,khd->hqk", rows_query, keys, preferred_element_type=jnp.float32)
    key_place = jnp.arange(group, dtype=jnp.int32)
    row_place = start + jnp.arange(rows, dtype=jnp.int32)
    difference = key_place[None, :] - row_place[:, None]
    relative = spread_band(project, start, group, left, right)
    relative = relative + jnp.where(difference[None] <= -left, project[:, :, :1], 0.0)
    relative = relative + jnp.where(difference[None] >= right, project[:, :, width - 1 :], 0.0)
    row_segment = lax.dynamic_slice_in_dim(segment, start, rows)
    same = row_segment[:, None] == segment[None, :]
    return (jnp.where(same[None], scale * (content + relative), masked_score), difference)


def attention_forward(query, keys, values, table, segment, block_rows, left, right):
    group = query.shape[0]
    starts = jnp.arange(group // block_rows, dtype=jnp.int32) * block_rows

    def one_block(carry, start):
        rows_query = lax.dynamic_slice_in_dim(query, start, block_rows, 0)
        scores, difference = block_scores(rows_query, keys, table, segment, start, left, right)
        top = jnp.max(scores, axis=2, keepdims=True)
        weights = jnp.exp(scores - top)
        total = jnp.sum(weights, axis=2, keepdims=True)
        probs = (weights / total).astype(jnp.bfloat16)
        rows_out = jnp.einsum("hqk,khd->qhd", probs, values, preferred_element_type=jnp.float32)
        return (carry, (rows_out.astype(jnp.bfloat16), (top + jnp.log(total))[:, :, 0]))

    unused, (pieces, log_total) = lax.scan(one_block, 0, starts)
    return (pieces.reshape(query.shape), log_total)


def attention_backward(
    query, keys, values, table, segment, log_total, d_context, block_rows, left, right
):
    group, heads, depth = query.shape
    width = table.shape[0]
    scale = 1.0 / math.sqrt(depth)
    starts = jnp.arange(group // block_rows, dtype=jnp.int32) * block_rows

    def one_block(carry, operands):
        d_keys, d_values, d_table = carry
        start, block_total = operands
        rows_query = lax.dynamic_slice_in_dim(query, start, block_rows, 0)
        rows_grad = lax.dynamic_slice_in_dim(d_context, start, block_rows, 0)
        scores, difference = block_scores(rows_query, keys, table, segment, start, left, right)
        probs = jnp.exp(scores - block_total[:, :, None])
        d_values = d_values + jnp.einsum(
            "hqk,qhd->khd",
            probs.astype(jnp.bfloat16),
            rows_grad,
            preferred_element_type=jnp.float32,
        )
        d_probs = jnp.einsum("qhd,khd->hqk", rows_grad, values, preferred_element_type=jnp.float32)
        weighted = jnp.sum(probs * d_probs, axis=2, keepdims=True)
        d_scores = (probs * (d_probs - weighted)).astype(jnp.bfloat16)
        bins = relative_bins(
            scale * d_scores.astype(jnp.float32), difference, start, width, left, right
        )
        bins = bins.astype(jnp.bfloat16)
        d_rows = scale * jnp.einsum(
            "hqk,khd->qhd", d_scores, keys, preferred_element_type=jnp.float32
        )
        d_rows = d_rows + jnp.einsum("hqr,rd->qhd", bins, table, preferred_element_type=jnp.float32)
        d_keys = d_keys + scale * jnp.einsum(
            "hqk,qhd->khd", d_scores, rows_query, preferred_element_type=jnp.float32
        )
        d_table = d_table + jnp.einsum(
            "hqr,qhd->rd", bins, rows_query, preferred_element_type=jnp.float32
        )
        return ((d_keys, d_values, d_table), d_rows.astype(jnp.bfloat16))

    zeros_heads = jnp.zeros(query.shape, jnp.float32)
    zeros_table = jnp.zeros(table.shape, jnp.float32)
    (d_keys, d_values, d_table), d_rows = lax.scan(
        one_block, (zeros_heads, zeros_heads, zeros_table), (starts, log_total)
    )
    return (
        d_rows.reshape(query.shape),
        d_keys.astype(jnp.bfloat16),
        d_values.astype(jnp.bfloat16),
        d_table,
    )


def on_device(
    frames,
    lengths,
    cotangent,
    ffn1_in,
    ffn1_out,
    query_w,
    key_w,
    value_w,
    out_w,
    point_in,
    point_out,
    ffn2_in,
    ffn2_out,
    depth_w,
    rel_table,
    norm_gains,
    norm_biases,
    bn_gain,
    bn_shift,
):
    seq_count = lax.axis_size("seq")
    seq_rank = lax.axis_index("seq")
    frames_here, width = frames.shape
    group = frames_here * seq_count
    block_rows = min(512, group)
    kernel_size = depth_w.shape[0]
    reach = kernel_size // 2
    ends = jnp.cumsum(lengths[0])
    last_entry = lengths.shape[1] - 1
    first = seq_rank * frames_here
    wide_place = first - reach + jnp.arange(frames_here + 2 * reach, dtype=jnp.int32)
    wide_segment = segment_ids(wide_place, ends, group)
    own_segment = wide_segment[reach : reach + frames_here]
    mask = (own_segment < last_entry).astype(jnp.float32)[:, None]
    group_segment = segment_ids(jnp.arange(group, dtype=jnp.int32), ends, group)
    shards = (
        ffn1_in,
        ffn1_out,
        query_w,
        key_w,
        value_w,
        out_w,
        point_in,
        point_out,
        ffn2_in,
        ffn2_out,
    )
    cube = cube_of(shards)
    gathered = gather_all(shards, cube)
    start_values = frames.astype(jnp.float32)
    after_first, kept_first = ffn_forward(
        start_values, norm_gains[0], norm_biases[0], gathered[0], gathered[1]
    )
    attn_norm, attn_unit, attn_inverse = norm_forward(after_first, norm_gains[1], norm_biases[1])
    attn_hidden = attn_norm.astype(jnp.bfloat16)
    query_heads, key_heads, value_heads = (
        lax.all_to_all(
            to_heads(attn_hidden, gathered[2], HEADS),
            "seq",
            split_axis=1,
            concat_axis=0,
            tiled=True,
        ),
        lax.all_to_all(
            to_heads(attn_hidden, gathered[3], HEADS),
            "seq",
            split_axis=1,
            concat_axis=0,
            tiled=True,
        ),
        lax.all_to_all(
            to_heads(attn_hidden, gathered[4], HEADS),
            "seq",
            split_axis=1,
            concat_axis=0,
            tiled=True,
        ),
    )
    context_heads, log_total = attention_forward(
        query_heads,
        key_heads,
        value_heads,
        rel_table,
        group_segment,
        block_rows,
        REL_LEFT,
        REL_RIGHT,
    )
    context = lax.all_to_all(context_heads, "seq", split_axis=0, concat_axis=1, tiled=True).reshape(
        frames_here, width
    )
    after_attn = after_first + matmul(context, gathered[5])
    conv_norm, conv_unit, conv_inverse = norm_forward(after_attn, norm_gains[2], norm_biases[2])
    conv_hidden = conv_norm.astype(jnp.bfloat16)
    pointwise = matmul(conv_hidden, gathered[6])
    gate_half = pointwise[:, :width]
    sigma_half = jax.nn.sigmoid(pointwise[:, width:])
    gated = (gate_half * sigma_half).astype(jnp.bfloat16)
    gated_wide = padded_2(gated, (("seq", 0),), reach)
    kernel = depth_w.astype(jnp.float32)
    mixed = jnp.zeros((frames_here, width), jnp.float32)
    for offset in range(kernel_size):
        same = (wide_segment[offset : offset + frames_here] == own_segment).astype(jnp.float32)[
            :, None
        ]
        mixed = (
            mixed
            + kernel[offset] * gated_wide[offset : offset + frames_here].astype(jnp.float32) * same
        )
    total, squares, count = sum_everywhere(
        (jnp.sum(mixed * mask, axis=0), jnp.sum(mixed * mixed * mask, axis=0), jnp.sum(mask)),
        cube,
        1,
    )
    mean = total / count
    var = squares / count - mean * mean
    bn_inverse = lax.rsqrt(var + epsilon)
    centred = (mixed - mean) * bn_inverse
    bn_out = centred * bn_gain + bn_shift
    conv_swish = jax.nn.silu(bn_out).astype(jnp.bfloat16)
    after_conv = after_attn + matmul(conv_swish, gathered[7])
    after_second, kept_second = ffn_forward(
        after_conv, norm_gains[3], norm_biases[3], gathered[8], gathered[9]
    )
    final_norm, final_unit, final_inverse = norm_forward(
        after_second, norm_gains[4], norm_biases[4]
    )
    sample_variance = var * count / (count - 1.0)
    d_final = cotangent.astype(jnp.float32) * mask
    d_second, gain_four, shift_four = norm_backward(
        d_final, final_unit, final_inverse, norm_gains[4]
    )
    d_conv_res, grad_two_in, grad_two_out, gain_three, shift_three = ffn_backward(
        d_second, kept_second, norm_gains[3], gathered[8], gathered[9]
    )
    conv_branch = d_conv_res.astype(jnp.bfloat16)
    d_bn_out = transposed_right(conv_branch, gathered[7]) * swish_slope(bn_out)
    grad_bn_gain, grad_bn_shift = sum_everywhere(
        (jnp.sum(d_bn_out * centred * mask, axis=0), jnp.sum(d_bn_out * mask, axis=0)), cube, 2
    )
    d_mixed = (
        bn_gain * bn_inverse * (d_bn_out - mask * (grad_bn_shift + centred * grad_bn_gain) / count)
    )
    d_mixed = d_mixed.astype(jnp.bfloat16)
    d_mixed_wide = padded_2(d_mixed, (("seq", 0),), reach)
    d_mixed_value = d_mixed.astype(jnp.float32)
    d_gated = jnp.zeros((frames_here, width), jnp.float32)
    kernel_rows = []
    for offset in range(kernel_size):
        same = (wide_segment[offset : offset + frames_here] == own_segment).astype(jnp.float32)[
            :, None
        ]
        shifted_in = gated_wide[offset : offset + frames_here].astype(jnp.float32)
        kernel_rows.append(jnp.sum(d_mixed_value * shifted_in * same, axis=0))
        back = 2 * reach - offset
        same_back = (wide_segment[back : back + frames_here] == own_segment).astype(jnp.float32)[
            :, None
        ]
        d_gated = (
            d_gated
            + kernel[offset]
            * d_mixed_wide[back : back + frames_here].astype(jnp.float32)
            * same_back
        )
    d_pointwise = jnp.concatenate(
        [d_gated * sigma_half, d_gated * gate_half * sigma_half * (1.0 - sigma_half)], axis=1
    ).astype(jnp.bfloat16)
    d_conv_norm, gain_two, shift_two = norm_backward(
        transposed_right(d_pointwise, gathered[6]), conv_unit, conv_inverse, norm_gains[2]
    )
    d_attn_res = d_conv_res + d_conv_norm
    attn_branch = d_attn_res.astype(jnp.bfloat16)
    d_context = (
        transposed_right(attn_branch, gathered[5])
        .astype(jnp.bfloat16)
        .reshape(frames_here, HEADS, -1)
    )
    d_context_heads = lax.all_to_all(d_context, "seq", split_axis=1, concat_axis=0, tiled=True)
    d_query_heads, d_key_heads, d_value_heads, d_table = attention_backward(
        query_heads,
        key_heads,
        value_heads,
        rel_table,
        group_segment,
        log_total,
        d_context_heads,
        block_rows,
        REL_LEFT,
        REL_RIGHT,
    )
    d_query, d_keys, d_values = (
        lax.all_to_all(d_query_heads, "seq", split_axis=0, concat_axis=1, tiled=True),
        lax.all_to_all(d_key_heads, "seq", split_axis=0, concat_axis=1, tiled=True),
        lax.all_to_all(d_value_heads, "seq", split_axis=0, concat_axis=1, tiled=True),
    )
    d_query = d_query.reshape(frames_here, width)
    d_keys = d_keys.reshape(frames_here, width)
    d_values = d_values.reshape(frames_here, width)
    d_attn_hidden = (
        transposed_right(d_query, gathered[2])
        + transposed_right(d_keys, gathered[3])
        + transposed_right(d_values, gathered[4])
    )
    d_attn_norm, gain_one, shift_one = norm_backward(
        d_attn_hidden, attn_unit, attn_inverse, norm_gains[1]
    )
    d_first_res = d_attn_res + d_attn_norm
    d_input, grad_one_in, grad_one_out, gain_zero, shift_zero = ffn_backward(
        d_first_res, kept_first, norm_gains[0], gathered[0], gathered[1]
    )
    heads_in = jnp.concatenate([d_query, d_keys, d_values], axis=1)
    two_out, two_in, conv_out, conv_in, attn_out, attn_in, one_out, one_in = gradient_shards(
        (
            grad_two_out,
            grad_two_in,
            (conv_swish, conv_branch),
            (conv_hidden, d_pointwise),
            (context, attn_branch),
            (attn_hidden, heads_in),
            grad_one_out,
            grad_one_in,
        ),
        cube,
    )
    gains_local = jnp.stack([gain_zero, gain_one, gain_two, gain_three, gain_four])
    shifts_local = jnp.stack([shift_zero, shift_one, shift_two, shift_three, shift_four])
    kernel_local = jnp.stack(kernel_rows)
    grad_gains, grad_biases, grad_depth, grad_rel = sum_everywhere(
        (gains_local, shifts_local, kernel_local, d_table), cube, 3
    )
    return (
        final_norm.astype(jnp.bfloat16),
        d_input.astype(jnp.bfloat16),
        one_in,
        one_out,
        attn_in[:, :width],
        attn_in[:, width : 2 * width],
        attn_in[:, 2 * width :],
        attn_out,
        conv_in,
        conv_out,
        two_in,
        two_out,
        grad_depth,
        grad_rel,
        grad_gains,
        grad_biases,
        grad_bn_gain,
        grad_bn_shift,
        sample_variance,
    )


def solution(mesh):
    placed = (
        P(("batch", "seq"), None),
        P("batch", None),
        P(("batch", "seq"), None),
        P(("batch", "seq"), None),
        P(("batch", "seq"), None),
        P(("batch", "seq"), None),
        P(("batch", "seq"), None),
        P(("batch", "seq"), None),
        P(("batch", "seq"), None),
        P(("batch", "seq"), None),
        P(("batch", "seq"), None),
        P(("batch", "seq"), None),
        P(("batch", "seq"), None),
        P(),
        P(),
        P(),
        P(),
        P(),
        P(),
    )
    return jax.shard_map(
        on_device,
        mesh=mesh,
        in_specs=placed,
        out_specs=(
            P(("batch", "seq"), None),
            P(("batch", "seq"), None),
            P(("batch", "seq"), None),
            P(("batch", "seq"), None),
            P(("batch", "seq"), None),
            P(("batch", "seq"), None),
            P(("batch", "seq"), None),
            P(("batch", "seq"), None),
            P(("batch", "seq"), None),
            P(("batch", "seq"), None),
            P(("batch", "seq"), None),
            P(("batch", "seq"), None),
            P(),
            P(),
            P(),
            P(),
            P(),
            P(),
            P(),
        ),
        check_vma=False,
    )
```

```python
import functools
import math

import jax
import jax.numpy as jnp
from jax import lax
from jax.experimental import pallas as pl
from jax.experimental.pallas import tpu as pltpu
from jax.sharding import PartitionSpec as P

MESH = pl.DeviceIdType.MESH
AXES = ("batch", "seq")

HEADS = 8
REL_LEFT = 64
REL_RIGHT = 8


epsilon = 1e-05
masked_score = -1000000000.0


def padded_2(shard, sides, width):
    for axis, dim in sides:
        peers, length = (lax.axis_size(axis), shard.shape[dim])
        up = [(i, (i + 1) % peers) for i in range(peers - 1)]
        down = [(j, i) for i, j in up]
        last = lax.slice_in_dim(shard, length - width, length, axis=dim)
        first = lax.slice_in_dim(shard, 0, width, axis=dim)
        before = lax.ppermute(last, axis, up)
        after = lax.ppermute(first, axis, down)
        shard = jnp.concatenate([before, shard, after], axis=dim)
    return shard


def matmul(left, right):
    return jnp.dot(left, right, preferred_element_type=jnp.float32)


def transposed_left(left, right):
    return lax.dot_general(
        left, right, (((0,), (0,)), ((), ())), preferred_element_type=jnp.float32
    )


def transposed_right(left, right):
    return lax.dot_general(
        left, right, (((1,), (1,)), ((), ())), preferred_element_type=jnp.float32
    )


class Cube:
    def __init__(self, batch, seq):
        self.seq_bits, self.batch_bits = (seq.bit_length() - 1, batch.bit_length() - 1)
        self.count = self.seq_bits + self.batch_bits
        self.core = self.seq_bits
        wide = (self.batch_bits - 1) // 2
        self.x = list(range(self.seq_bits))[::-1]
        self.y = list(range(self.core + 1, self.core + 1 + wide))[::-1]
        self.z = list(range(self.core + 1 + wide, self.count))[::-1]

    def bit(self, k):
        if k < self.seq_bits:
            return lax.rem(lax.axis_index("seq") // (1 << k), 2)
        return lax.rem(lax.axis_index("batch") // (1 << (k - self.seq_bits)), 2)

    def partner(self, k):
        batch, seq = (lax.axis_index("batch"), lax.axis_index("seq"))
        step = 1 - 2 * self.bit(k)
        if k < self.seq_bits:
            return (batch, seq + step * (1 << k))
        return (batch + step * (1 << (k - self.seq_bits)), seq)

    def swap(self, values, k):
        if k < self.seq_bits:
            axis, step = ("seq", 1 << k)
        else:
            axis, step = ("batch", 1 << (k - self.seq_bits))
        pairs = [(i, i ^ step) for i in range(lax.axis_size(axis))]
        return lax.ppermute(values, axis, pairs)


def greet(cube, bits):
    barrier = pltpu.get_barrier_semaphore()
    for k in bits:
        pl.semaphore_signal(barrier, inc=1, device_id=cube.partner(k), device_id_type=MESH)
    pl.semaphore_wait(barrier, len(bits))


def gather_kernel(cube, orders, count, which, cuts, *refs):
    shards, outs = (refs[:count], refs[count : 2 * count])
    send, recv, local = refs[2 * count :]
    bits = range(cube.count)
    own = [cube.bit(k) for k in bits]
    kept = []
    for m in range(count):
        kept.append(
            pltpu.make_async_copy(shards[m], outs[m].at[tuple(own[::-1])], local.at[m])
        )
        kept[m].start()
    greet(cube, bits)
    lanes = len(orders)

    def copy(chunk, lane, stage):
        m, order = (which[chunk], orders[lane])
        row, rows, column, columns = cuts[chunk][lane]
        block = (pl.ds(row, rows), pl.ds(column, columns))
        lead = tuple(slice(None) if k in order[:stage] else own[k] for k in reversed(bits))
        place = outs[m].at[lead + block]
        return pltpu.make_async_remote_copy(
            src_ref=shards[m].at[block] if stage == 0 else place,
            dst_ref=place,
            send_sem=send.at[chunk * lanes + lane, stage],
            recv_sem=recv.at[chunk * lanes + lane, stage],
            device_id=cube.partner(order[stage]),
            device_id_type=MESH,
        )

    for chunk in range(len(cuts)):
        for lane in range(lanes):
            copy(chunk, lane, 0).start()
    for one in kept:
        one.wait()
    stages = cube.count
    for turn in range(len(cuts) + stages):
        for stage in range(stages):
            chunk = turn - stage - (stage == stages - 1)
            if 0 <= chunk < len(cuts):
                for lane in range(lanes):
                    copy(chunk, lane, stage).wait_recv()
                    if stage + 1 < stages:
                        copy(chunk, lane, stage + 1).start()
    for chunk in range(len(cuts)):
        for lane in range(lanes):
            for stage in range(stages):
                copy(chunk, lane, stage).wait_send()


def column_parts(width, shares):
    units, total, at, parts = (width // 128, sum(shares), 0, [])
    for share in shares:
        size = units * share // total
        parts.append((at * 128, size * 128))
        at += size
    return parts


def gather_fast(shards, cube):
    core = [cube.core]
    orders = [
        cube.z + cube.y + cube.x + core,
        cube.z + cube.x + cube.y + core,
        cube.x + cube.y + cube.z + core,
    ]
    which, cuts = ([], [])
    for m, shard in enumerate(shards):
        rows, columns = (min(64, shard.shape[0]), min(2048, shard.shape[1]))
        for row in range(0, shard.shape[0], rows):
            for column in range(0, shard.shape[1], columns):
                which.append(m)
                cuts.append(
                    [(row, rows, column + a, w) for a, w in column_parts(columns, (3, 3, 2))]
                )
    count, items = (len(shards), len(cuts) * len(orders))
    outs = pl.pallas_call(
        functools.partial(gather_kernel, cube, orders, count, which, cuts),
        out_shape=[
            jax.ShapeDtypeStruct((2,) * cube.count + shard.shape, shard.dtype) for shard in shards
        ],
        in_specs=[pl.BlockSpec(memory_space=pl.ANY)] * count,
        out_specs=[pl.BlockSpec(memory_space=pl.ANY)] * count,
        scratch_shapes=[
            pltpu.SemaphoreType.DMA((items, cube.count)),
            pltpu.SemaphoreType.DMA((items, cube.count)),
            pltpu.SemaphoreType.DMA((count,)),
        ],
        compiler_params=pltpu.CompilerParams(collective_id=0, has_side_effects=True),
        name="gather_weights",
    )(*shards)
    return tuple(out.reshape(-1, shard.shape[1]) for out, shard in zip(outs, shards))


def sum_kernel(cube, value, out, held, sent, send, recv):
    bits = range(cube.count)
    greet(cube, bits)
    sent[0] = value[...]
    for k in bits:
        copy = pltpu.make_async_remote_copy(
            src_ref=sent.at[k],
            dst_ref=held.at[k],
            send_sem=send.at[k],
            recv_sem=recv.at[k],
            device_id=cube.partner(k),
            device_id_type=MESH,
        )
        copy.start()
        copy.wait()
        if k + 1 < cube.count:
            sent[k + 1] = sent[k] + held[k]
        else:
            out[...] = sent[k] + held[k]


def sum_fast(value, cube, number):
    return pl.pallas_call(
        functools.partial(sum_kernel, cube),
        out_shape=jax.ShapeDtypeStruct(value.shape, value.dtype),
        in_specs=[pl.BlockSpec(memory_space=pltpu.VMEM)],
        out_specs=pl.BlockSpec(memory_space=pltpu.VMEM),
        scratch_shapes=[
            pltpu.VMEM((cube.count,) + value.shape, value.dtype),
            pltpu.VMEM((cube.count,) + value.shape, value.dtype),
            pltpu.SemaphoreType.DMA((cube.count,)),
            pltpu.SemaphoreType.DMA((cube.count,)),
        ],
        compiler_params=pltpu.CompilerParams(collective_id=number, has_side_effects=True),
        name="sum_over_devices",
    )(value)


def sum_everywhere(values, cube, number):
    if cube is None:
        return lax.psum(values, AXES)
    flat = jnp.concatenate([value.reshape(-1) for value in values])
    size = -(-flat.shape[0] // 8192) * 8192
    flat = jnp.pad(flat, (0, size - flat.shape[0])).reshape(-1, 1024)
    flat = sum_fast(flat, cube, number).reshape(-1)
    out, at = ([], 0)
    for value in values:
        out.append(flat[at : at + value.size].reshape(value.shape))
        at += value.size
    return tuple(out)


def reduce_kernel(cube, order, rows, columns, count, places, *refs):
    parts, out, refs = (refs[:count], refs[count], refs[count + 1 :])
    stages, number = (len(order), len(places))
    own, refs = (refs[0], refs[1:])
    recv_at, refs = (refs[:stages], refs[stages:])
    send_at, refs = ((None,) + refs[: stages - 1], refs[stages - 1 :])
    keep_at, refs = ((None,) + refs[: stages - 1], refs[stages - 1 :])
    send, recv, local = refs
    bits = [cube.bit(k) for k in order]
    dims = sorted(order, reverse=True)

    def spot(stage, flip):
        left = [k for k in dims if k not in order[:stage]]
        side = bits[stage]
        side = 1 - side if flip else side
        return tuple(side if k == order[stage] else slice(None) for k in left)

    def remote(stage, chunk, source):
        return pltpu.make_async_remote_copy(
            src_ref=source,
            dst_ref=recv_at[stage].at[chunk],
            send_sem=send.at[stage, chunk],
            recv_sem=recv.at[stage, chunk],
            device_id=cube.partner(order[stage]),
            device_id_type=MESH,
        )

    greet(cube, order)
    for chunk, (m, row, column) in enumerate(places):
        block = (pl.ds(row, rows), pl.ds(column, columns))
        remote(0, chunk, parts[m].at[spot(0, True) + block]).start()
        pltpu.make_async_copy(
            parts[m].at[spot(0, False) + block], own.at[chunk], local.at[chunk]
        ).start()

    def turn(step, carry):
        for stage in range(stages):
            chunk = step - stage

            @pl.when((chunk >= 0) & (chunk < number))
            def _():
                source = own if stage == 0 else keep_at[stage]
                if stage == 0:
                    pltpu.make_async_copy(own.at[chunk], own.at[chunk], local.at[chunk]).wait()
                remote(stage, chunk, recv_at[stage].at[chunk]).wait_recv()
                arrived = recv_at[stage]
                if stage + 1 == stages:
                    out[chunk] = source[chunk] + arrived[chunk].astype(jnp.float32)
                else:
                    away, home = (spot(stage + 1, True), spot(stage + 1, False))
                    send_at[stage + 1][chunk] = (
                        source[(chunk,) + away].astype(jnp.float32)
                        + arrived[(chunk,) + away].astype(jnp.float32)
                    ).astype(jnp.bfloat16)
                    remote(stage + 1, chunk, send_at[stage + 1].at[chunk]).start()
                    keep_at[stage + 1][chunk] = source[(chunk,) + home].astype(
                        jnp.float32
                    ) + arrived[(chunk,) + home].astype(jnp.float32)

        return carry

    lax.fori_loop(0, number + stages, turn, 0)

    def finish(chunk, carry):
        for stage in range(stages):
            remote(stage, chunk, recv_at[stage].at[chunk]).wait_send()
        return carry

    lax.fori_loop(0, number, finish, 0)


def reduce_fast(parts, cube, rows, columns):
    order = cube.y + cube.z[::-1]
    stages, count = (len(order), len(parts))
    places = []
    for m, part in enumerate(parts):
        for row in range(0, part.shape[-2], rows):
            for column in range(0, part.shape[-1], columns):
                places.append((m, row, column))
    number, tile = (len(places), (rows, columns))

    def held(stage, dtype):
        return pltpu.VMEM((number,) + (2,) * (stages - 1 - stage) + tile, dtype)

    out = pl.pallas_call(
        functools.partial(reduce_kernel, cube, order, rows, columns, count, places),
        out_shape=jax.ShapeDtypeStruct((number,) + tile, jnp.float32),
        in_specs=[pl.BlockSpec(memory_space=pl.ANY)] * count,
        out_specs=pl.BlockSpec(memory_space=pltpu.VMEM),
        scratch_shapes=[held(0, jnp.bfloat16)]
        + [held(stage, jnp.bfloat16) for stage in range(stages)]
        + [held(stage, jnp.bfloat16) for stage in range(1, stages)]
        + [held(stage, jnp.float32) for stage in range(1, stages)]
        + [
            pltpu.SemaphoreType.DMA((stages, number)),
            pltpu.SemaphoreType.DMA((stages, number)),
            pltpu.SemaphoreType.DMA((number,)),
        ],
        compiler_params=pltpu.CompilerParams(
            collective_id=4, has_side_effects=True, vmem_limit_bytes=56 * 1024 * 1024
        ),
        name="reduce_gradients",
    )(*parts)
    results, at = ([], 0)
    for part in parts:
        down, across = (part.shape[-2] // rows, part.shape[-1] // columns)
        piece = out[at : at + down * across].reshape(down, across, rows, columns)
        results.append(piece.transpose(0, 2, 1, 3).reshape(part.shape[-2], part.shape[-1]))
        at += down * across
    return results


def near_sum(left, right, cube):
    near = cube.seq_bits + 1
    flipped = left.T
    rows = flipped.shape[0] >> cube.count
    flipped = flipped.reshape((-1,) + (2,) * near + (rows, left.shape[0]))
    for k in range(near):
        axis = flipped.ndim - 3
        away = lax.dynamic_index_in_dim(flipped, 1 - cube.bit(k), axis, keepdims=False)
        home = lax.dynamic_index_in_dim(flipped, cube.bit(k), axis, keepdims=False)
        flipped = jnp.concatenate([home, cube.swap(away, k)], axis=-1)
        right = jnp.concatenate([right, cube.swap(right, k)], axis=0)
    sums = matmul(flipped.reshape(-1, flipped.shape[-1]), right).astype(jnp.bfloat16)
    return sums.reshape((2,) * (cube.count - near) + (rows, right.shape[1]))


def gradient_shards(pairs, cube):
    if cube is None:
        results = []
        for left, right in pairs:
            whole = transposed_left(left, right)
            flat = whole.reshape(-1, 128)
            shard = lax.psum_scatter(flat, AXES, scatter_dimension=0, tiled=True)
            results.append(shard.reshape(-1, whole.shape[1]))
        return results
    return reduce_fast([near_sum(left, right, cube) for left, right in pairs], cube, 32, 1024)


def gather_all(shards, cube):
    if cube is None:
        return tuple(lax.all_gather(shard, AXES, axis=0, tiled=True) for shard in shards)
    return gather_fast(shards, cube)


def distance_rows(group, left, right, backwards):
    row = lax.broadcasted_iota(jnp.int32, (group, 128), 0)
    row = group - 1 - row if backwards else row
    distance = jnp.where(row >= group // 2, row - group, row)
    index = jnp.clip(distance, -left, right) + left
    hit = index == lax.broadcasted_iota(jnp.int32, (group, 128), 1)
    return jnp.where(hit, 1.0, 0.0).astype(jnp.bfloat16)


def halves(cube, rows, half):
    mine = cube.bit(0)
    return (
        pl.ds(pl.multiple_of(mine * half, half), half),
        pl.ds(pl.multiple_of((1 - mine) * half, half), half),
        pl.ds(pl.multiple_of(mine * rows, rows), rows),
        pl.ds(pl.multiple_of((1 - mine) * rows, rows), rows),
    )


def to_partner(cube, k, source, target, send, recv):
    return pltpu.make_async_remote_copy(
        src_ref=source,
        dst_ref=target,
        send_sem=send,
        recv_sem=recv,
        device_id=cube.partner(k),
        device_id_type=MESH,
    )


def attend_kernel(cube, left, right, *refs):
    hidden, before, same, table, query_w, key_w, value_w, out_w = refs[:8]
    after, context, heads_out, probs_out = refs[8:12]
    weights, heads_in, away, wide, context_away, load, send, recv, head_send, head_recv = refs[12:]
    rows, width = hidden.shape
    group, half = (2 * rows, width // 2)
    heads = half // 128
    scale = 1.0 / math.sqrt(128)
    mine = cube.bit(0)
    own_columns, away_columns, own_rows, away_rows = halves(cube, rows, half)
    loads = []
    for i, matrix in enumerate((query_w, key_w, value_w, out_w)):
        loads.append(pltpu.make_async_copy(matrix, weights.at[i], load.at[i]))
        loads[i].start()
    greet(cube, [0])

    def exchange(i):
        return to_partner(
            cube, 0, away.at[i], heads_in.at[i, own_rows], send.at[i], recv.at[i]
        )

    def context_copy(head):
        column = pl.ds(pl.multiple_of(mine * half + head * 128, 128), 128)
        return to_partner(
            cube, 0, context_away.at[head], wide.at[:, column], head_send.at[head], head_recv.at[head]
        )

    for i in range(3):
        loads[i].wait()
        away[i] = matmul(hidden[...], weights[i, :, away_columns]).astype(jnp.bfloat16)
        exchange(i).start()
    for i in range(3):
        heads_in[i, own_rows, :] = matmul(hidden[...], weights[i, :, own_columns]).astype(
            jnp.bfloat16
        )
    spread = matmul(distance_rows(group, left, right, False), table[...]).astype(jnp.bfloat16)
    loads[3].wait()
    for i in range(3):
        exchange(i).wait_recv()

    def one_head(head, carry):
        column = pl.ds(pl.multiple_of(head * 128, 128), 128)
        place = pl.ds(pl.multiple_of(mine * half + head * 128, 128), 128)
        query, keys, values = (heads_in[i, :, column] for i in range(3))
        relative = pltpu.roll(transposed_right(query, spread), 0, 1, stride=1, stride_axis=0)
        scores = scale * (transposed_right(query, keys) + relative)
        scores = jnp.where(same[...] > 0, scores, masked_score)
        weight = jnp.exp(scores - jnp.max(scores, axis=1, keepdims=True))
        probs_out[head] = weight / jnp.sum(weight, axis=1, keepdims=True)
        there = probs_out[head, away_rows, :].astype(jnp.bfloat16)
        context_away[head] = matmul(there, values).astype(jnp.bfloat16)
        context_copy(head).start()
        here = probs_out[head, own_rows, :].astype(jnp.bfloat16)
        wide[:, place] = matmul(here, values).astype(jnp.bfloat16)
        return carry

    lax.fori_loop(0, heads, one_head, 0)
    heads_out[...] = heads_in[...]
    after[...] = before[...] + matmul(wide[:, own_columns], weights[3, own_columns, :])
    for head in range(heads):
        context_copy(head).wait_recv()
    after[...] += matmul(wide[:, away_columns], weights[3, away_columns, :])
    context[...] = wide[...]
    for i in range(3):
        exchange(i).wait_send()
    for head in range(heads):
        context_copy(head).wait_send()


def attend_fast(cube, hidden, before, same, table, matrices):
    rows, width = hidden.shape
    group, half = (2 * rows, width // 2)
    heads = half // 128
    vmem = pl.BlockSpec(memory_space=pltpu.VMEM)
    return pl.pallas_call(
        functools.partial(attend_kernel, cube, REL_LEFT, REL_RIGHT),
        out_shape=[
            jax.ShapeDtypeStruct((rows, width), jnp.float32),
            jax.ShapeDtypeStruct((rows, width), jnp.bfloat16),
            jax.ShapeDtypeStruct((3, group, half), jnp.bfloat16),
            jax.ShapeDtypeStruct((heads, group, group), jnp.float32),
        ],
        in_specs=[vmem] * 4 + [pl.BlockSpec(memory_space=pl.ANY)] * 4,
        out_specs=[vmem] * 4,
        scratch_shapes=[
            pltpu.VMEM((4, width, width), jnp.bfloat16),
            pltpu.VMEM((3, group, half), jnp.bfloat16),
            pltpu.VMEM((3, rows, half), jnp.bfloat16),
            pltpu.VMEM((rows, width), jnp.bfloat16),
            pltpu.VMEM((heads, rows, 128), jnp.bfloat16),
            pltpu.SemaphoreType.DMA((4,)),
            pltpu.SemaphoreType.DMA((3,)),
            pltpu.SemaphoreType.DMA((3,)),
            pltpu.SemaphoreType.DMA((heads,)),
            pltpu.SemaphoreType.DMA((heads,)),
        ],
        compiler_params=pltpu.CompilerParams(
            collective_id=5, has_side_effects=True, vmem_limit_bytes=48 * 1024 * 1024
        ),
        name="attend",
    )(hidden, before, same, table, *matrices)


def attend_back_kernel(cube, left, right, *refs):
    branch, heads_in, probs_in, table, query_w, key_w, value_w, out_w = refs[:8]
    d_hidden, d_heads, d_table = refs[8:11]
    weights, d_context, d_context_away, wide, away, load, send, recv, head_send, head_recv = refs[
        11:
    ]
    rows, width = branch.shape
    group, half = (2 * rows, width // 2)
    heads = half // 128
    scale = 1.0 / math.sqrt(128)
    mine = cube.bit(0)
    own_columns, away_columns, own_rows, away_rows = halves(cube, rows, half)
    loads = []
    for i, matrix in enumerate((out_w, query_w, key_w, value_w)):
        loads.append(pltpu.make_async_copy(matrix, weights.at[i], load.at[i]))
        loads[i].start()
    greet(cube, [0])
    loads[0].wait()
    exchange = to_partner(
        cube, 0, d_context_away, d_context.at[own_rows], send.at[0], recv.at[0]
    )
    d_context_away[...] = transposed_right(branch[...], weights[0, away_columns, :]).astype(
        jnp.bfloat16
    )
    exchange.start()
    d_context[own_rows, :] = transposed_right(branch[...], weights[0, own_columns, :]).astype(
        jnp.bfloat16
    )
    spread = distance_rows(group, left, right, True)
    down = lax.broadcasted_iota(jnp.int32, (group, group), 0)
    across = lax.broadcasted_iota(jnp.int32, (group, group), 1)
    mirror = jnp.where(down + across == group - 1, 1.0, 0.0).astype(jnp.bfloat16)
    d_table[...] = jnp.zeros_like(d_table)
    exchange.wait_recv()

    def head_copy(head, i):
        column = pl.ds(pl.multiple_of(i * width + mine * half + head * 128, 128), 128)
        return to_partner(
            cube,
            0,
            away.at[head, i, away_rows],
            wide.at[:, column],
            head_send.at[head, i],
            head_recv.at[head, i],
        )

    def one_head(head, carry):
        column = pl.ds(pl.multiple_of(head * 128, 128), 128)
        query, keys, values = (heads_in[i, :, column] for i in range(3))
        d_rows = d_context[:, column]
        probs = probs_in[head]
        d_probs = transposed_right(d_rows, values)
        weighted = jnp.sum(probs * d_probs, axis=1, keepdims=True)
        d_scores = (probs * (d_probs - weighted)).astype(jnp.bfloat16)
        away[head, 2] = transposed_left(probs.astype(jnp.bfloat16), d_rows).astype(jnp.bfloat16)
        head_copy(head, 2).start()
        away[head, 1] = (scale * transposed_left(d_scores, query)).astype(jnp.bfloat16)
        head_copy(head, 1).start()
        turned = pltpu.roll(matmul(d_scores, mirror), 0, 1, stride=1, stride_axis=0)
        bins = (scale * matmul(turned.astype(jnp.bfloat16), spread)).astype(jnp.bfloat16)
        away[head, 0] = (scale * matmul(d_scores, keys) + matmul(bins, table[...])).astype(
            jnp.bfloat16
        )
        head_copy(head, 0).start()
        d_table[...] += transposed_left(bins, query)
        for i in range(3):
            place = pl.ds(pl.multiple_of(i * width + mine * half + head * 128, 128), 128)
            wide[:, place] = away[head, i, own_rows, :]
        return carry

    lax.fori_loop(0, heads, one_head, 0)
    for i in range(3):
        loads[1 + i].wait()

    def part(i, offset, columns):
        place = pl.ds(pl.multiple_of(i * width + offset * half, half), half)
        return transposed_right(wide[:, place], weights[1 + i, :, columns])

    total = part(0, mine, own_columns)
    for i in range(1, 3):
        total += part(i, mine, own_columns)
    d_hidden[...] = total
    for head in range(heads):
        for i in range(3):
            head_copy(head, i).wait_recv()
    total = part(0, 1 - mine, away_columns)
    for i in range(1, 3):
        total += part(i, 1 - mine, away_columns)
    d_hidden[...] += total
    d_heads[...] = wide[...]
    exchange.wait_send()
    for head in range(heads):
        for i in range(3):
            head_copy(head, i).wait_send()


def attend_back_fast(cube, branch, heads_in, probs, table, matrices):
    rows, width = branch.shape
    group, half = (2 * rows, width // 2)
    heads = half // 128
    vmem = pl.BlockSpec(memory_space=pltpu.VMEM)
    return pl.pallas_call(
        functools.partial(attend_back_kernel, cube, REL_LEFT, REL_RIGHT),
        out_shape=[
            jax.ShapeDtypeStruct((rows, width), jnp.float32),
            jax.ShapeDtypeStruct((rows, 3 * width), jnp.bfloat16),
            jax.ShapeDtypeStruct((128, 128), jnp.float32),
        ],
        in_specs=[vmem] * 4 + [pl.BlockSpec(memory_space=pl.ANY)] * 4,
        out_specs=[vmem] * 3,
        scratch_shapes=[
            pltpu.VMEM((4, width, width), jnp.bfloat16),
            pltpu.VMEM((group, half), jnp.bfloat16),
            pltpu.VMEM((rows, half), jnp.bfloat16),
            pltpu.VMEM((rows, 3 * width), jnp.bfloat16),
            pltpu.VMEM((heads, 3, group, 128), jnp.bfloat16),
            pltpu.SemaphoreType.DMA((4,)),
            pltpu.SemaphoreType.DMA((1,)),
            pltpu.SemaphoreType.DMA((1,)),
            pltpu.SemaphoreType.DMA((heads, 3)),
            pltpu.SemaphoreType.DMA((heads, 3)),
        ],
        compiler_params=pltpu.CompilerParams(
            collective_id=6, has_side_effects=True, vmem_limit_bytes=48 * 1024 * 1024
        ),
        name="attend_back",
    )(branch, heads_in, probs, table, *matrices)


def cube_of(shards, rel_table):
    batch, seq = (lax.axis_size("batch"), lax.axis_size("seq"))
    if seq != 2 or batch < 8 or batch & (batch - 1):
        return None
    if rel_table.shape[0] > 128 or rel_table.shape[1] != 128:
        return None
    if any(shard.shape[0] % 32 or shard.shape[1] % 1024 for shard in shards):
        return None
    return Cube(batch, seq)


def swish_slope(values):
    sigma = jax.nn.sigmoid(values)
    return sigma * (1.0 + values * (1.0 - sigma))


def norm_forward(values, gain, shift):
    mean = jnp.mean(values, axis=-1, keepdims=True)
    centred = values - mean
    inverse = lax.rsqrt(jnp.mean(centred * centred, axis=-1, keepdims=True) + epsilon)
    unit = centred * inverse
    return (unit * gain + shift, unit, inverse)


def norm_backward(d_out, unit, inverse, gain):
    d_unit = d_out * gain
    d_values = inverse * (
        d_unit
        - jnp.mean(d_unit, axis=-1, keepdims=True)
        - unit * jnp.mean(d_unit * unit, axis=-1, keepdims=True)
    )
    return (d_values, jnp.sum(d_out * unit, axis=0), jnp.sum(d_out, axis=0))


def ffn_forward(values, gain, shift, weight_in, weight_out):
    normed, unit, inverse = norm_forward(values, gain, shift)
    hidden = normed.astype(jnp.bfloat16)
    act = matmul(hidden, weight_in)
    swish = jax.nn.silu(act).astype(jnp.bfloat16)
    return (values + 0.5 * matmul(swish, weight_out), (hidden, act, swish, unit, inverse))


def ffn_backward(d_out, kept, gain, weight_in, weight_out):
    hidden, act, swish, unit, inverse = kept
    d_branch = (0.5 * d_out).astype(jnp.bfloat16)
    d_act = (transposed_right(d_branch, weight_out) * swish_slope(act)).astype(jnp.bfloat16)
    d_norm, d_gain, d_shift = norm_backward(transposed_right(d_act, weight_in), unit, inverse, gain)
    return (d_out + d_norm, (hidden, d_act), (swish, d_branch), d_gain, d_shift)


def segment_ids(place, ends, group):
    inside = jnp.sum((place[:, None] >= ends[None, :]).astype(jnp.int32), axis=1)
    return jnp.where((place >= 0) & (place < group), inside, -1)


def to_heads(hidden, weight, heads):
    return matmul(hidden, weight).astype(jnp.bfloat16).reshape(hidden.shape[0], heads, -1)


def spread_band(project, start, group, left, right):
    heads, rows, width = project.shape
    band = rows + width - 1
    blank = jnp.zeros_like(project[:, :, :1])
    middle = jnp.concatenate([blank, project[:, :, 1 : width - 1], blank], axis=2)
    padded = jnp.pad(middle, ((0, 0), (0, 0), (0, band + 1 - width)))
    skewed = padded.reshape(heads, rows * (band + 1))[:, : rows * band].reshape(heads, rows, band)
    canvas = jnp.zeros((heads, rows, group + left + right), jnp.float32)
    anchor = jnp.zeros((), jnp.int32)
    canvas = lax.dynamic_update_slice(canvas, skewed, (anchor, anchor, start))
    return canvas[:, :, left : left + group]


def relative_bins(grad, difference, start, width, left, right):
    heads, rows, group = grad.shape
    band = rows + width - 1
    canvas = jnp.pad(grad, ((0, 0), (0, 0), (left, right)))
    anchor = jnp.zeros((), jnp.int32)
    strip = lax.dynamic_slice(canvas, (anchor, anchor, start), (heads, rows, band))
    flat = jnp.pad(strip.reshape(heads, rows * band), ((0, 0), (0, rows)))
    inner = flat.reshape(heads, rows, band + 1)[:, :, 1 : width - 1]
    below = jnp.sum(jnp.where(difference[None] <= -left, grad, 0.0), axis=2, keepdims=True)
    above = jnp.sum(jnp.where(difference[None] >= right, grad, 0.0), axis=2, keepdims=True)
    return jnp.concatenate([below, inner, above], axis=2)


def block_scores(rows_query, keys, table, segment, start, left, right):
    rows, heads, depth = rows_query.shape
    group = keys.shape[0]
    width = table.shape[0]
    scale = 1.0 / math.sqrt(depth)
    project = jnp.einsum("qhd,rd->hqr", rows_query, table, preferred_element_type=jnp.float32)
    content = jnp.einsum("qhd,khd->hqk", rows_query, keys, preferred_element_type=jnp.float32)
    key_place = jnp.arange(group, dtype=jnp.int32)
    row_place = start + jnp.arange(rows, dtype=jnp.int32)
    difference = key_place[None, :] - row_place[:, None]
    relative = spread_band(project, start, group, left, right)
    relative = relative + jnp.where(difference[None] <= -left, project[:, :, :1], 0.0)
    relative = relative + jnp.where(difference[None] >= right, project[:, :, width - 1 :], 0.0)
    row_segment = lax.dynamic_slice_in_dim(segment, start, rows)
    same = row_segment[:, None] == segment[None, :]
    return (jnp.where(same[None], scale * (content + relative), masked_score), difference)


def attention_forward(query, keys, values, table, segment, block_rows, left, right):
    group = query.shape[0]
    starts = jnp.arange(group // block_rows, dtype=jnp.int32) * block_rows

    def one_block(carry, start):
        rows_query = lax.dynamic_slice_in_dim(query, start, block_rows, 0)
        scores, difference = block_scores(rows_query, keys, table, segment, start, left, right)
        top = jnp.max(scores, axis=2, keepdims=True)
        weights = jnp.exp(scores - top)
        total = jnp.sum(weights, axis=2, keepdims=True)
        probs = (weights / total).astype(jnp.bfloat16)
        rows_out = jnp.einsum("hqk,khd->qhd", probs, values, preferred_element_type=jnp.float32)
        return (carry, (rows_out.astype(jnp.bfloat16), (top + jnp.log(total))[:, :, 0]))

    unused, (pieces, log_total) = lax.scan(one_block, 0, starts)
    return (pieces.reshape(query.shape), log_total)


def attention_backward(
    query, keys, values, table, segment, log_total, d_context, block_rows, left, right
):
    group, heads, depth = query.shape
    width = table.shape[0]
    scale = 1.0 / math.sqrt(depth)
    starts = jnp.arange(group // block_rows, dtype=jnp.int32) * block_rows

    def one_block(carry, operands):
        d_keys, d_values, d_table = carry
        start, block_total = operands
        rows_query = lax.dynamic_slice_in_dim(query, start, block_rows, 0)
        rows_grad = lax.dynamic_slice_in_dim(d_context, start, block_rows, 0)
        scores, difference = block_scores(rows_query, keys, table, segment, start, left, right)
        probs = jnp.exp(scores - block_total[:, :, None])
        d_values = d_values + jnp.einsum(
            "hqk,qhd->khd",
            probs.astype(jnp.bfloat16),
            rows_grad,
            preferred_element_type=jnp.float32,
        )
        d_probs = jnp.einsum("qhd,khd->hqk", rows_grad, values, preferred_element_type=jnp.float32)
        weighted = jnp.sum(probs * d_probs, axis=2, keepdims=True)
        d_scores = (probs * (d_probs - weighted)).astype(jnp.bfloat16)
        bins = relative_bins(
            scale * d_scores.astype(jnp.float32), difference, start, width, left, right
        )
        bins = bins.astype(jnp.bfloat16)
        d_rows = scale * jnp.einsum(
            "hqk,khd->qhd", d_scores, keys, preferred_element_type=jnp.float32
        )
        d_rows = d_rows + jnp.einsum("hqr,rd->qhd", bins, table, preferred_element_type=jnp.float32)
        d_keys = d_keys + scale * jnp.einsum(
            "hqk,qhd->khd", d_scores, rows_query, preferred_element_type=jnp.float32
        )
        d_table = d_table + jnp.einsum(
            "hqr,qhd->rd", bins, rows_query, preferred_element_type=jnp.float32
        )
        return ((d_keys, d_values, d_table), d_rows.astype(jnp.bfloat16))

    zeros_heads = jnp.zeros(query.shape, jnp.float32)
    zeros_table = jnp.zeros(table.shape, jnp.float32)
    (d_keys, d_values, d_table), d_rows = lax.scan(
        one_block, (zeros_heads, zeros_heads, zeros_table), (starts, log_total)
    )
    return (
        d_rows.reshape(query.shape),
        d_keys.astype(jnp.bfloat16),
        d_values.astype(jnp.bfloat16),
        d_table,
    )


def on_device(
    frames,
    lengths,
    cotangent,
    ffn1_in,
    ffn1_out,
    query_w,
    key_w,
    value_w,
    out_w,
    point_in,
    point_out,
    ffn2_in,
    ffn2_out,
    depth_w,
    rel_table,
    norm_gains,
    norm_biases,
    bn_gain,
    bn_shift,
):
    seq_count = lax.axis_size("seq")
    seq_rank = lax.axis_index("seq")
    frames_here, width = frames.shape
    group = frames_here * seq_count
    block_rows = min(512, group)
    kernel_size = depth_w.shape[0]
    reach = kernel_size // 2
    ends = jnp.cumsum(lengths[0])
    last_entry = lengths.shape[1] - 1
    first = seq_rank * frames_here
    wide_place = first - reach + jnp.arange(frames_here + 2 * reach, dtype=jnp.int32)
    wide_segment = segment_ids(wide_place, ends, group)
    own_segment = wide_segment[reach : reach + frames_here]
    mask = (own_segment < last_entry).astype(jnp.float32)[:, None]
    group_segment = segment_ids(jnp.arange(group, dtype=jnp.int32), ends, group)
    shards = (
        ffn1_in,
        ffn1_out,
        query_w,
        key_w,
        value_w,
        out_w,
        point_in,
        point_out,
        ffn2_in,
        ffn2_out,
    )
    cube = cube_of(shards, rel_table)
    gathered = gather_all(shards, cube)
    start_values = frames.astype(jnp.float32)
    after_first, kept_first = ffn_forward(
        start_values, norm_gains[0], norm_biases[0], gathered[0], gathered[1]
    )
    attn_norm, attn_unit, attn_inverse = norm_forward(after_first, norm_gains[1], norm_biases[1])
    attn_hidden = attn_norm.astype(jnp.bfloat16)
    if cube is None:
        query_heads, key_heads, value_heads = (
            lax.all_to_all(
                to_heads(attn_hidden, gathered[2], HEADS),
                "seq",
                split_axis=1,
                concat_axis=0,
                tiled=True,
            ),
            lax.all_to_all(
                to_heads(attn_hidden, gathered[3], HEADS),
                "seq",
                split_axis=1,
                concat_axis=0,
                tiled=True,
            ),
            lax.all_to_all(
                to_heads(attn_hidden, gathered[4], HEADS),
                "seq",
                split_axis=1,
                concat_axis=0,
                tiled=True,
            ),
        )
        context_heads, log_total = attention_forward(
            query_heads,
            key_heads,
            value_heads,
            rel_table,
            group_segment,
            block_rows,
            REL_LEFT,
            REL_RIGHT,
        )
        context = lax.all_to_all(context_heads, "seq", split_axis=0, concat_axis=1, tiled=True).reshape(
            frames_here, width
        )
        after_attn = after_first + matmul(context, gathered[5])
    else:
        table = jnp.pad(rel_table, ((0, 128 - rel_table.shape[0]), (0, 0)))
        same = (group_segment[:, None] == group_segment[None, :]).astype(jnp.float32)
        after_attn, context, heads_kept, probs_kept = attend_fast(
            cube, attn_hidden, after_first, same, table, gathered[2:6]
        )
    conv_norm, conv_unit, conv_inverse = norm_forward(after_attn, norm_gains[2], norm_biases[2])
    conv_hidden = conv_norm.astype(jnp.bfloat16)
    pointwise = matmul(conv_hidden, gathered[6])
    gate_half = pointwise[:, :width]
    sigma_half = jax.nn.sigmoid(pointwise[:, width:])
    gated = (gate_half * sigma_half).astype(jnp.bfloat16)
    gated_wide = padded_2(gated, (("seq", 0),), reach)
    kernel = depth_w.astype(jnp.float32)
    mixed = jnp.zeros((frames_here, width), jnp.float32)
    for offset in range(kernel_size):
        same = (wide_segment[offset : offset + frames_here] == own_segment).astype(jnp.float32)[
            :, None
        ]
        mixed = (
            mixed
            + kernel[offset] * gated_wide[offset : offset + frames_here].astype(jnp.float32) * same
        )
    total, squares, count = sum_everywhere(
        (jnp.sum(mixed * mask, axis=0), jnp.sum(mixed * mixed * mask, axis=0), jnp.sum(mask)),
        cube,
        1,
    )
    mean = total / count
    var = squares / count - mean * mean
    bn_inverse = lax.rsqrt(var + epsilon)
    centred = (mixed - mean) * bn_inverse
    bn_out = centred * bn_gain + bn_shift
    conv_swish = jax.nn.silu(bn_out).astype(jnp.bfloat16)
    after_conv = after_attn + matmul(conv_swish, gathered[7])
    after_second, kept_second = ffn_forward(
        after_conv, norm_gains[3], norm_biases[3], gathered[8], gathered[9]
    )
    final_norm, final_unit, final_inverse = norm_forward(
        after_second, norm_gains[4], norm_biases[4]
    )
    sample_variance = var * count / (count - 1.0)
    d_final = cotangent.astype(jnp.float32) * mask
    d_second, gain_four, shift_four = norm_backward(
        d_final, final_unit, final_inverse, norm_gains[4]
    )
    d_conv_res, grad_two_in, grad_two_out, gain_three, shift_three = ffn_backward(
        d_second, kept_second, norm_gains[3], gathered[8], gathered[9]
    )
    conv_branch = d_conv_res.astype(jnp.bfloat16)
    d_bn_out = transposed_right(conv_branch, gathered[7]) * swish_slope(bn_out)
    grad_bn_gain, grad_bn_shift = sum_everywhere(
        (jnp.sum(d_bn_out * centred * mask, axis=0), jnp.sum(d_bn_out * mask, axis=0)), cube, 2
    )
    d_mixed = (
        bn_gain * bn_inverse * (d_bn_out - mask * (grad_bn_shift + centred * grad_bn_gain) / count)
    )
    d_mixed = d_mixed.astype(jnp.bfloat16)
    d_mixed_wide = padded_2(d_mixed, (("seq", 0),), reach)
    d_mixed_value = d_mixed.astype(jnp.float32)
    d_gated = jnp.zeros((frames_here, width), jnp.float32)
    kernel_rows = []
    for offset in range(kernel_size):
        same = (wide_segment[offset : offset + frames_here] == own_segment).astype(jnp.float32)[
            :, None
        ]
        shifted_in = gated_wide[offset : offset + frames_here].astype(jnp.float32)
        kernel_rows.append(jnp.sum(d_mixed_value * shifted_in * same, axis=0))
        back = 2 * reach - offset
        same_back = (wide_segment[back : back + frames_here] == own_segment).astype(jnp.float32)[
            :, None
        ]
        d_gated = (
            d_gated
            + kernel[offset]
            * d_mixed_wide[back : back + frames_here].astype(jnp.float32)
            * same_back
        )
    d_pointwise = jnp.concatenate(
        [d_gated * sigma_half, d_gated * gate_half * sigma_half * (1.0 - sigma_half)], axis=1
    ).astype(jnp.bfloat16)
    d_conv_norm, gain_two, shift_two = norm_backward(
        transposed_right(d_pointwise, gathered[6]), conv_unit, conv_inverse, norm_gains[2]
    )
    d_attn_res = d_conv_res + d_conv_norm
    attn_branch = d_attn_res.astype(jnp.bfloat16)
    if cube is None:
        d_context = (
            transposed_right(attn_branch, gathered[5])
            .astype(jnp.bfloat16)
            .reshape(frames_here, HEADS, -1)
        )
        d_context_heads = lax.all_to_all(d_context, "seq", split_axis=1, concat_axis=0, tiled=True)
        d_query_heads, d_key_heads, d_value_heads, d_table = attention_backward(
            query_heads,
            key_heads,
            value_heads,
            rel_table,
            group_segment,
            log_total,
            d_context_heads,
            block_rows,
            REL_LEFT,
            REL_RIGHT,
        )
        d_query, d_keys, d_values = (
            lax.all_to_all(d_query_heads, "seq", split_axis=0, concat_axis=1, tiled=True),
            lax.all_to_all(d_key_heads, "seq", split_axis=0, concat_axis=1, tiled=True),
            lax.all_to_all(d_value_heads, "seq", split_axis=0, concat_axis=1, tiled=True),
        )
        d_query = d_query.reshape(frames_here, width)
        d_keys = d_keys.reshape(frames_here, width)
        d_values = d_values.reshape(frames_here, width)
        d_attn_hidden = (
            transposed_right(d_query, gathered[2])
            + transposed_right(d_keys, gathered[3])
            + transposed_right(d_values, gathered[4])
        )
        heads_in = jnp.concatenate([d_query, d_keys, d_values], axis=1)
    else:
        d_attn_hidden, heads_in, d_table = attend_back_fast(
            cube, attn_branch, heads_kept, probs_kept, table, gathered[2:6]
        )
        d_table = d_table[: rel_table.shape[0]]
    d_attn_norm, gain_one, shift_one = norm_backward(
        d_attn_hidden, attn_unit, attn_inverse, norm_gains[1]
    )
    d_first_res = d_attn_res + d_attn_norm
    d_input, grad_one_in, grad_one_out, gain_zero, shift_zero = ffn_backward(
        d_first_res, kept_first, norm_gains[0], gathered[0], gathered[1]
    )
    two_out, two_in, conv_out, conv_in, attn_out, attn_in, one_out, one_in = gradient_shards(
        (
            grad_two_out,
            grad_two_in,
            (conv_swish, conv_branch),
            (conv_hidden, d_pointwise),
            (context, attn_branch),
            (attn_hidden, heads_in),
            grad_one_out,
            grad_one_in,
        ),
        cube,
    )
    gains_local = jnp.stack([gain_zero, gain_one, gain_two, gain_three, gain_four])
    shifts_local = jnp.stack([shift_zero, shift_one, shift_two, shift_three, shift_four])
    kernel_local = jnp.stack(kernel_rows)
    grad_gains, grad_biases, grad_depth, grad_rel = sum_everywhere(
        (gains_local, shifts_local, kernel_local, d_table), cube, 3
    )
    return (
        final_norm.astype(jnp.bfloat16),
        d_input.astype(jnp.bfloat16),
        one_in,
        one_out,
        attn_in[:, :width],
        attn_in[:, width : 2 * width],
        attn_in[:, 2 * width :],
        attn_out,
        conv_in,
        conv_out,
        two_in,
        two_out,
        grad_depth,
        grad_rel,
        grad_gains,
        grad_biases,
        grad_bn_gain,
        grad_bn_shift,
        sample_variance,
    )


def solution(mesh):
    placed = (
        P(("batch", "seq"), None),
        P("batch", None),
        P(("batch", "seq"), None),
        P(("batch", "seq"), None),
        P(("batch", "seq"), None),
        P(("batch", "seq"), None),
        P(("batch", "seq"), None),
        P(("batch", "seq"), None),
        P(("batch", "seq"), None),
        P(("batch", "seq"), None),
        P(("batch", "seq"), None),
        P(("batch", "seq"), None),
        P(("batch", "seq"), None),
        P(),
        P(),
        P(),
        P(),
        P(),
        P(),
    )
    return jax.shard_map(
        on_device,
        mesh=mesh,
        in_specs=placed,
        out_specs=(
            P(("batch", "seq"), None),
            P(("batch", "seq"), None),
            P(("batch", "seq"), None),
            P(("batch", "seq"), None),
            P(("batch", "seq"), None),
            P(("batch", "seq"), None),
            P(("batch", "seq"), None),
            P(("batch", "seq"), None),
            P(("batch", "seq"), None),
            P(("batch", "seq"), None),
            P(("batch", "seq"), None),
            P(("batch", "seq"), None),
            P(),
            P(),
            P(),
            P(),
            P(),
            P(),
            P(),
        ),
        check_vma=False,
    )
```

```python
import functools
import math

import jax
import jax.numpy as jnp
from jax import lax
from jax.experimental import pallas as pl
from jax.experimental.pallas import tpu as pltpu
from jax.sharding import PartitionSpec as P

MESH = pl.DeviceIdType.MESH
AXES = ("batch", "seq")

HEADS = 8
REL_LEFT = 64
REL_RIGHT = 8


epsilon = 1e-05
masked_score = -1000000000.0


def padded_2(shard, sides, width):
    for axis, dim in sides:
        peers, length = (lax.axis_size(axis), shard.shape[dim])
        up = [(i, (i + 1) % peers) for i in range(peers - 1)]
        down = [(j, i) for i, j in up]
        last = lax.slice_in_dim(shard, length - width, length, axis=dim)
        first = lax.slice_in_dim(shard, 0, width, axis=dim)
        before = lax.ppermute(last, axis, up)
        after = lax.ppermute(first, axis, down)
        shard = jnp.concatenate([before, shard, after], axis=dim)
    return shard


def matmul(left, right):
    return jnp.dot(left, right, preferred_element_type=jnp.float32)


def transposed_left(left, right):
    return lax.dot_general(
        left, right, (((0,), (0,)), ((), ())), preferred_element_type=jnp.float32
    )


def transposed_right(left, right):
    return lax.dot_general(
        left, right, (((1,), (1,)), ((), ())), preferred_element_type=jnp.float32
    )


class Cube:
    def __init__(self, batch, seq):
        self.seq_bits, self.batch_bits = (seq.bit_length() - 1, batch.bit_length() - 1)
        self.count = self.seq_bits + self.batch_bits
        self.core = self.seq_bits
        wide = (self.batch_bits - 1) // 2
        self.x = list(range(self.seq_bits))[::-1]
        self.y = list(range(self.core + 1, self.core + 1 + wide))[::-1]
        self.z = list(range(self.core + 1 + wide, self.count))[::-1]

    def bit(self, k):
        if k < self.seq_bits:
            return lax.rem(lax.axis_index("seq") // (1 << k), 2)
        return lax.rem(lax.axis_index("batch") // (1 << (k - self.seq_bits)), 2)

    def partner(self, k):
        batch, seq = (lax.axis_index("batch"), lax.axis_index("seq"))
        step = 1 - 2 * self.bit(k)
        if k < self.seq_bits:
            return (batch, seq + step * (1 << k))
        return (batch + step * (1 << (k - self.seq_bits)), seq)


def greet(cube, bits):
    barrier = pltpu.get_barrier_semaphore()
    for k in bits:
        pl.semaphore_signal(barrier, inc=1, device_id=cube.partner(k), device_id_type=MESH)
    pl.semaphore_wait(barrier, len(bits))


def gather_kernel(cube, orders, count, which, cuts, *refs):
    shards, outs = (refs[:count], refs[count : 2 * count])
    send, recv, local = refs[2 * count :]
    bits = range(cube.count)
    own = [cube.bit(k) for k in bits]
    kept = []
    for m in range(count):
        kept.append(
            pltpu.make_async_copy(shards[m], outs[m].at[tuple(own[::-1])], local.at[m])
        )
        kept[m].start()
    greet(cube, bits)
    lanes = len(orders)

    def copy(chunk, lane, stage):
        m, order = (which[chunk], orders[lane])
        row, rows, column, columns = cuts[chunk][lane]
        block = (pl.ds(row, rows), pl.ds(column, columns))
        lead = tuple(slice(None) if k in order[:stage] else own[k] for k in reversed(bits))
        place = outs[m].at[lead + block]
        return pltpu.make_async_remote_copy(
            src_ref=shards[m].at[block] if stage == 0 else place,
            dst_ref=place,
            send_sem=send.at[chunk * lanes + lane, stage],
            recv_sem=recv.at[chunk * lanes + lane, stage],
            device_id=cube.partner(order[stage]),
            device_id_type=MESH,
        )

    for chunk in range(len(cuts)):
        for lane in range(lanes):
            copy(chunk, lane, 0).start()
    for one in kept:
        one.wait()
    stages = cube.count
    for turn in range(len(cuts) + stages):
        for stage in range(stages):
            chunk = turn - stage - (stage == stages - 1)
            if 0 <= chunk < len(cuts):
                for lane in range(lanes):
                    copy(chunk, lane, stage).wait_recv()
                    if stage + 1 < stages:
                        copy(chunk, lane, stage + 1).start()
    for chunk in range(len(cuts)):
        for lane in range(lanes):
            for stage in range(stages):
                copy(chunk, lane, stage).wait_send()


def column_parts(width, shares):
    units, total, at, parts = (width // 128, sum(shares), 0, [])
    for share in shares:
        size = units * share // total
        parts.append((at * 128, size * 128))
        at += size
    return parts


def gather_fast(shards, cube):
    core = [cube.core]
    orders = [
        cube.z + cube.y + cube.x + core,
        cube.z + cube.x + cube.y + core,
        cube.x + cube.y + cube.z + core,
    ]
    which, cuts = ([], [])
    for m, shard in enumerate(shards):
        rows, columns = (min(64, shard.shape[0]), min(2048, shard.shape[1]))
        for row in range(0, shard.shape[0], rows):
            for column in range(0, shard.shape[1], columns):
                which.append(m)
                cuts.append(
                    [(row, rows, column + a, w) for a, w in column_parts(columns, (3, 3, 2))]
                )
    count, items = (len(shards), len(cuts) * len(orders))
    outs = pl.pallas_call(
        functools.partial(gather_kernel, cube, orders, count, which, cuts),
        out_shape=[
            jax.ShapeDtypeStruct((2,) * cube.count + shard.shape, shard.dtype) for shard in shards
        ],
        in_specs=[pl.BlockSpec(memory_space=pl.ANY)] * count,
        out_specs=[pl.BlockSpec(memory_space=pl.ANY)] * count,
        scratch_shapes=[
            pltpu.SemaphoreType.DMA((items, cube.count)),
            pltpu.SemaphoreType.DMA((items, cube.count)),
            pltpu.SemaphoreType.DMA((count,)),
        ],
        compiler_params=pltpu.CompilerParams(collective_id=0, has_side_effects=True),
        name="gather_weights",
    )(*shards)
    return tuple(out.reshape(-1, shard.shape[1]) for out, shard in zip(outs, shards))


def sum_kernel(cube, value, out, held, sent, send, recv):
    bits = range(cube.count)
    greet(cube, bits)
    sent[0] = value[...]
    for k in bits:
        copy = pltpu.make_async_remote_copy(
            src_ref=sent.at[k],
            dst_ref=held.at[k],
            send_sem=send.at[k],
            recv_sem=recv.at[k],
            device_id=cube.partner(k),
            device_id_type=MESH,
        )
        copy.start()
        copy.wait()
        if k + 1 < cube.count:
            sent[k + 1] = sent[k] + held[k]
        else:
            out[...] = sent[k] + held[k]


def sum_fast(value, cube, number):
    return pl.pallas_call(
        functools.partial(sum_kernel, cube),
        out_shape=jax.ShapeDtypeStruct(value.shape, value.dtype),
        in_specs=[pl.BlockSpec(memory_space=pltpu.VMEM)],
        out_specs=pl.BlockSpec(memory_space=pltpu.VMEM),
        scratch_shapes=[
            pltpu.VMEM((cube.count,) + value.shape, value.dtype),
            pltpu.VMEM((cube.count,) + value.shape, value.dtype),
            pltpu.SemaphoreType.DMA((cube.count,)),
            pltpu.SemaphoreType.DMA((cube.count,)),
        ],
        compiler_params=pltpu.CompilerParams(collective_id=number, has_side_effects=True),
        name="sum_over_devices",
    )(value)


def sum_everywhere(values, cube, number):
    if cube is None:
        return lax.psum(values, AXES)
    flat = jnp.concatenate([value.reshape(-1) for value in values])
    size = -(-flat.shape[0] // 8192) * 8192
    flat = jnp.pad(flat, (0, size - flat.shape[0])).reshape(-1, 1024)
    flat = sum_fast(flat, cube, number).reshape(-1)
    out, at = ([], 0)
    for value in values:
        out.append(flat[at : at + value.size].reshape(value.shape))
        at += value.size
    return tuple(out)


def gradient_kernel(cube, count, shapes, tile, *refs):
    lefts, rights, out, refs = (
        refs[:count],
        refs[count : 2 * count],
        refs[2 * count],
        refs[2 * count + 1 :],
    )
    near, far, whole = (refs[:count], refs[count : 2 * count], refs[2 * count : 3 * count])
    refs = refs[3 * count :]
    order = cube.y + cube.z[::-1]
    stages = len(order)
    total, sent, recv_at, refs = (refs[0], refs[1 : 1 + stages], refs[1 + stages : 1 + 2 * stages], refs[1 + 2 * stages :])
    x_send, x_recv, local, c_send, c_recv, send, recv = refs
    rows, columns = tile
    number, depth = (out.shape[0], total.shape[0])
    lags = [3 + 2 * stage for stage in range(stages)]
    x, c = (cube.bit(0), cube.bit(cube.core))
    dims = sorted(order, reverse=True)
    bits = [cube.bit(k) for k in order]
    every = (slice(None),) * stages
    tokens = near[0].shape[-1] // 2
    own_lanes = pl.ds(pl.multiple_of(x * tokens, tokens), tokens)

    def spot(stage, flip):
        left = [k for k in dims if k not in order[:stage]]
        side = 1 - bits[stage] if flip else bits[stage]
        return tuple(side if k == order[stage] else slice(None) for k in left)

    def along_x(m):
        return [
            to_partner(
                cube,
                0,
                lefts[m].at[every + (slice(None), 1 - x)],
                near[m].at[every + (slice(None), slice(None), own_lanes)],
                x_send.at[m, 0],
                x_recv.at[m, 0],
            ),
            to_partner(
                cube, 0, rights[m], whole[m].at[c, own_lanes], x_send.at[m, 1], x_recv.at[m, 1]
            ),
        ]

    def at_home(m):
        return [
            pltpu.make_async_copy(
                lefts[m].at[every + (slice(None), x)],
                near[m].at[every + (slice(None), slice(None), own_lanes)],
                local.at[m, 0],
            ),
            pltpu.make_async_copy(rights[m], whole[m].at[c, own_lanes], local.at[m, 1]),
        ]

    def along_core(m):
        return [
            to_partner(
                cube,
                cube.core,
                near[m].at[every + (1 - c,)],
                far[m],
                c_send.at[m, 0],
                c_recv.at[m, 0],
            ),
            to_partner(
                cube, cube.core, whole[m].at[c], whole[m].at[c], c_send.at[m, 1], c_recv.at[m, 1]
            ),
        ]

    def remote(stage, chunk):
        return to_partner(
            cube,
            order[stage],
            sent[stage].at[chunk],
            recv_at[stage].at[chunk],
            send.at[stage, chunk],
            recv.at[stage, chunk],
        )

    def reduce(step):
        for stage in range(stages):
            chunk = step - lags[stage]

            @pl.when((chunk >= 0) & (chunk < number))
            def _(stage=stage, chunk=chunk):
                slot = lax.rem(chunk, depth)
                remote(stage, chunk).wait_recv()
                mine = tuple(
                    bits[order.index(k)] if k in order[: stage + 1] else slice(None) for k in dims
                )
                arrived = recv_at[stage]
                if stage + 1 == stages:
                    out[chunk] = total[(slot,) + mine] + arrived[chunk].astype(jnp.float32)
                else:
                    away, home = (spot(stage + 1, True), spot(stage + 1, False))
                    full = list(mine)
                    full[dims.index(order[stage + 1])] = 1 - bits[stage + 1]
                    sent[stage + 1][chunk] = (
                        total[(slot,) + tuple(full)]
                        + arrived[(chunk,) + away].astype(jnp.float32)
                    ).astype(jnp.bfloat16)
                    remote(stage + 1, chunk).start()
                    full[dims.index(order[stage + 1])] = bits[stage + 1]
                    total[(slot,) + tuple(full)] += arrived[(chunk,) + home].astype(jnp.float32)

    greet(cube, range(cube.count))
    for m in range(count):
        for copy in along_x(m) + at_home(m):
            copy.start()
    first = 0
    for m in range(count):
        for copy in at_home(m):
            copy.wait()
        for copy in along_x(m):
            copy.wait_recv()
        for copy in along_core(m):
            copy.start()
        for copy in along_core(m):
            copy.wait_recv()
        down, across = shapes[m]

        def one(j, carry, m=m, first=first, down=down, across=across):
            chunk = first + j
            slot = lax.rem(chunk, depth)
            row = pl.ds(pl.multiple_of((j // across) * rows, rows), rows)
            column = pl.ds(pl.multiple_of(lax.rem(j, across) * columns, columns), columns)

            def half(flip):
                place = spot(0, flip)
                one_left = near[m][place + (c, row, slice(None))]
                two_left = far[m][place + (row, slice(None))]
                shape = one_left.shape[:-1] + (columns,)
                one_left = one_left.reshape(-1, 2 * tokens)
                two_left = two_left.reshape(-1, 2 * tokens)
                result = matmul(one_left, whole[m][c, :, column]) + matmul(
                    two_left, whole[m][1 - c, :, column]
                )
                return result.reshape(shape)

            sent[0][chunk] = half(True).astype(jnp.bfloat16)
            remote(0, chunk).start()
            total[(slot,) + spot(0, False)] = half(False)
            reduce(chunk)
            return carry

        lax.fori_loop(0, down * across, one, 0)
        first += down * across

    def drain(step, carry):
        reduce(step)
        return carry

    lax.fori_loop(number, number + lags[-1] + 1, drain, 0)
    for m in range(count):
        for copy in along_x(m) + along_core(m):
            copy.wait_send()

    def finish(chunk, carry):
        for stage in range(stages):
            remote(stage, chunk).wait_send()
        return carry

    lax.fori_loop(0, number, finish, 0)


def gradients_fast(pairs, cube, rows, columns):
    order = cube.y + cube.z[::-1]
    stages, count, tokens = (len(order), len(pairs), pairs[0][0].shape[0])
    lefts, rights, shapes, near, far, whole = ([], [], [], [], [], [])
    for left, right in pairs:
        block = left.shape[1] >> cube.count
        lead = (2,) * stages
        lefts.append(left.T.reshape(lead + (2, 2, block, tokens)))
        rights.append(right)
        shapes.append((block // rows, right.shape[1] // columns))
        near.append(pltpu.VMEM(lead + (2, block, 2 * tokens), jnp.bfloat16))
        far.append(pltpu.VMEM(lead + (block, 2 * tokens), jnp.bfloat16))
        whole.append(pltpu.VMEM((2, 2 * tokens, right.shape[1]), jnp.bfloat16))
    number, tile = (sum(down * across for down, across in shapes), (rows, columns))
    held = [
        pltpu.VMEM((number,) + (2,) * (stages - 1 - stage) + tile, jnp.bfloat16)
        for stage in range(stages)
    ]
    depth = 3 + 2 * (stages - 1) + 1
    out = pl.pallas_call(
        functools.partial(gradient_kernel, cube, count, shapes, tile),
        out_shape=jax.ShapeDtypeStruct((number,) + tile, jnp.float32),
        in_specs=[pl.BlockSpec(memory_space=pl.ANY)] * (2 * count),
        out_specs=pl.BlockSpec(memory_space=pltpu.VMEM),
        scratch_shapes=near
        + far
        + whole
        + [pltpu.VMEM((depth,) + (2,) * stages + tile, jnp.float32)]
        + held
        + held
        + [pltpu.SemaphoreType.DMA((count, 2))] * 5
        + [pltpu.SemaphoreType.DMA((stages, number))] * 2,
        compiler_params=pltpu.CompilerParams(
            collective_id=4, has_side_effects=True, vmem_limit_bytes=60 * 1024 * 1024
        ),
        name="reduce_gradients",
    )(*lefts, *rights)
    results, at = ([], 0)
    for (down, across), right in zip(shapes, rights):
        piece = out[at : at + down * across].reshape(down, across, rows, columns)
        results.append(piece.transpose(0, 2, 1, 3).reshape(down * rows, right.shape[1]))
        at += down * across
    return results


def gradient_shards(pairs, cube):
    if cube is None:
        results = []
        for left, right in pairs:
            whole = transposed_left(left, right)
            flat = whole.reshape(-1, 128)
            shard = lax.psum_scatter(flat, AXES, scatter_dimension=0, tiled=True)
            results.append(shard.reshape(-1, whole.shape[1]))
        return results
    return gradients_fast(pairs, cube, 32, 1024)


def gather_all(shards, cube):
    if cube is None:
        return tuple(lax.all_gather(shard, AXES, axis=0, tiled=True) for shard in shards)
    return gather_fast(shards, cube)


def distance_rows(group, left, right, backwards):
    row = lax.broadcasted_iota(jnp.int32, (group, 128), 0)
    row = group - 1 - row if backwards else row
    distance = jnp.where(row >= group // 2, row - group, row)
    index = jnp.clip(distance, -left, right) + left
    hit = index == lax.broadcasted_iota(jnp.int32, (group, 128), 1)
    return jnp.where(hit, 1.0, 0.0).astype(jnp.bfloat16)


def halves(cube, rows, half):
    mine = cube.bit(0)
    return (
        pl.ds(pl.multiple_of(mine * half, half), half),
        pl.ds(pl.multiple_of((1 - mine) * half, half), half),
        pl.ds(pl.multiple_of(mine * rows, rows), rows),
        pl.ds(pl.multiple_of((1 - mine) * rows, rows), rows),
    )


def to_partner(cube, k, source, target, send, recv):
    return pltpu.make_async_remote_copy(
        src_ref=source,
        dst_ref=target,
        send_sem=send,
        recv_sem=recv,
        device_id=cube.partner(k),
        device_id_type=MESH,
    )


def attend_kernel(cube, left, right, *refs):
    hidden, before, same, table, query_w, key_w, value_w, out_w = refs[:8]
    after, context, heads_out, probs_out = refs[8:12]
    weights, heads_in, away, wide, context_away, load, send, recv, head_send, head_recv = refs[12:]
    rows, width = hidden.shape
    group, half = (2 * rows, width // 2)
    heads = half // 128
    scale = 1.0 / math.sqrt(128)
    mine = cube.bit(0)
    own_columns, away_columns, own_rows, away_rows = halves(cube, rows, half)
    loads = []
    for i, matrix in enumerate((query_w, key_w, value_w, out_w)):
        loads.append(pltpu.make_async_copy(matrix, weights.at[i], load.at[i]))
        loads[i].start()
    greet(cube, [0])

    def exchange(i):
        return to_partner(
            cube, 0, away.at[i], heads_in.at[i, own_rows], send.at[i], recv.at[i]
        )

    def context_copy(head):
        column = pl.ds(pl.multiple_of(mine * half + head * 128, 128), 128)
        return to_partner(
            cube, 0, context_away.at[head], wide.at[:, column], head_send.at[head], head_recv.at[head]
        )

    for i in range(3):
        loads[i].wait()
        away[i] = matmul(hidden[...], weights[i, :, away_columns]).astype(jnp.bfloat16)
        exchange(i).start()
    for i in range(3):
        heads_in[i, own_rows, :] = matmul(hidden[...], weights[i, :, own_columns]).astype(
            jnp.bfloat16
        )
    spread = matmul(distance_rows(group, left, right, False), table[...]).astype(jnp.bfloat16)
    loads[3].wait()
    for i in range(3):
        exchange(i).wait_recv()

    def one_head(head, carry):
        column = pl.ds(pl.multiple_of(head * 128, 128), 128)
        place = pl.ds(pl.multiple_of(mine * half + head * 128, 128), 128)
        query, keys, values = (heads_in[i, :, column] for i in range(3))
        relative = pltpu.roll(transposed_right(query, spread), 0, 1, stride=1, stride_axis=0)
        scores = scale * (transposed_right(query, keys) + relative)
        scores = jnp.where(same[...] > 0, scores, masked_score)
        weight = jnp.exp(scores - jnp.max(scores, axis=1, keepdims=True))
        probs_out[head] = weight / jnp.sum(weight, axis=1, keepdims=True)
        there = probs_out[head, away_rows, :].astype(jnp.bfloat16)
        context_away[head] = matmul(there, values).astype(jnp.bfloat16)
        context_copy(head).start()
        here = probs_out[head, own_rows, :].astype(jnp.bfloat16)
        wide[:, place] = matmul(here, values).astype(jnp.bfloat16)
        return carry

    lax.fori_loop(0, heads, one_head, 0)
    heads_out[...] = heads_in[...]
    after[...] = before[...] + matmul(wide[:, own_columns], weights[3, own_columns, :])
    for head in range(heads):
        context_copy(head).wait_recv()
    after[...] += matmul(wide[:, away_columns], weights[3, away_columns, :])
    context[...] = wide[...]
    for i in range(3):
        exchange(i).wait_send()
    for head in range(heads):
        context_copy(head).wait_send()


def attend_fast(cube, hidden, before, same, table, matrices):
    rows, width = hidden.shape
    group, half = (2 * rows, width // 2)
    heads = half // 128
    vmem = pl.BlockSpec(memory_space=pltpu.VMEM)
    return pl.pallas_call(
        functools.partial(attend_kernel, cube, REL_LEFT, REL_RIGHT),
        out_shape=[
            jax.ShapeDtypeStruct((rows, width), jnp.float32),
            jax.ShapeDtypeStruct((rows, width), jnp.bfloat16),
            jax.ShapeDtypeStruct((3, group, half), jnp.bfloat16),
            jax.ShapeDtypeStruct((heads, group, group), jnp.float32),
        ],
        in_specs=[vmem] * 4 + [pl.BlockSpec(memory_space=pl.ANY)] * 4,
        out_specs=[vmem] * 4,
        scratch_shapes=[
            pltpu.VMEM((4, width, width), jnp.bfloat16),
            pltpu.VMEM((3, group, half), jnp.bfloat16),
            pltpu.VMEM((3, rows, half), jnp.bfloat16),
            pltpu.VMEM((rows, width), jnp.bfloat16),
            pltpu.VMEM((heads, rows, 128), jnp.bfloat16),
            pltpu.SemaphoreType.DMA((4,)),
            pltpu.SemaphoreType.DMA((3,)),
            pltpu.SemaphoreType.DMA((3,)),
            pltpu.SemaphoreType.DMA((heads,)),
            pltpu.SemaphoreType.DMA((heads,)),
        ],
        compiler_params=pltpu.CompilerParams(
            collective_id=5, has_side_effects=True, vmem_limit_bytes=48 * 1024 * 1024
        ),
        name="attend",
    )(hidden, before, same, table, *matrices)


def attend_back_kernel(cube, left, right, *refs):
    branch, heads_in, probs_in, table, query_w, key_w, value_w, out_w = refs[:8]
    d_hidden, d_heads, d_table = refs[8:11]
    weights, d_context, d_context_away, wide, away, load, send, recv, head_send, head_recv = refs[
        11:
    ]
    rows, width = branch.shape
    group, half = (2 * rows, width // 2)
    heads = half // 128
    scale = 1.0 / math.sqrt(128)
    mine = cube.bit(0)
    own_columns, away_columns, own_rows, away_rows = halves(cube, rows, half)
    loads = []
    for i, matrix in enumerate((out_w, query_w, key_w, value_w)):
        loads.append(pltpu.make_async_copy(matrix, weights.at[i], load.at[i]))
        loads[i].start()
    greet(cube, [0])
    loads[0].wait()
    exchange = to_partner(
        cube, 0, d_context_away, d_context.at[own_rows], send.at[0], recv.at[0]
    )
    d_context_away[...] = transposed_right(branch[...], weights[0, away_columns, :]).astype(
        jnp.bfloat16
    )
    exchange.start()
    d_context[own_rows, :] = transposed_right(branch[...], weights[0, own_columns, :]).astype(
        jnp.bfloat16
    )
    spread = distance_rows(group, left, right, True)
    down = lax.broadcasted_iota(jnp.int32, (group, group), 0)
    across = lax.broadcasted_iota(jnp.int32, (group, group), 1)
    mirror = jnp.where(down + across == group - 1, 1.0, 0.0).astype(jnp.bfloat16)
    d_table[...] = jnp.zeros_like(d_table)
    exchange.wait_recv()

    def head_copy(head, i):
        column = pl.ds(pl.multiple_of(i * width + mine * half + head * 128, 128), 128)
        return to_partner(
            cube,
            0,
            away.at[head, i, away_rows],
            wide.at[:, column],
            head_send.at[head, i],
            head_recv.at[head, i],
        )

    def one_head(head, carry):
        column = pl.ds(pl.multiple_of(head * 128, 128), 128)
        query, keys, values = (heads_in[i, :, column] for i in range(3))
        d_rows = d_context[:, column]
        probs = probs_in[head]
        d_probs = transposed_right(d_rows, values)
        weighted = jnp.sum(probs * d_probs, axis=1, keepdims=True)
        d_scores = (probs * (d_probs - weighted)).astype(jnp.bfloat16)
        away[head, 2] = transposed_left(probs.astype(jnp.bfloat16), d_rows).astype(jnp.bfloat16)
        head_copy(head, 2).start()
        away[head, 1] = (scale * transposed_left(d_scores, query)).astype(jnp.bfloat16)
        head_copy(head, 1).start()
        turned = pltpu.roll(matmul(d_scores, mirror), 0, 1, stride=1, stride_axis=0)
        bins = (scale * matmul(turned.astype(jnp.bfloat16), spread)).astype(jnp.bfloat16)
        away[head, 0] = (scale * matmul(d_scores, keys) + matmul(bins, table[...])).astype(
            jnp.bfloat16
        )
        head_copy(head, 0).start()
        d_table[...] += transposed_left(bins, query)
        for i in range(3):
            place = pl.ds(pl.multiple_of(i * width + mine * half + head * 128, 128), 128)
            wide[:, place] = away[head, i, own_rows, :]
        return carry

    lax.fori_loop(0, heads, one_head, 0)
    for i in range(3):
        loads[1 + i].wait()

    def part(i, offset, columns):
        place = pl.ds(pl.multiple_of(i * width + offset * half, half), half)
        return transposed_right(wide[:, place], weights[1 + i, :, columns])

    total = part(0, mine, own_columns)
    for i in range(1, 3):
        total += part(i, mine, own_columns)
    d_hidden[...] = total
    for head in range(heads):
        for i in range(3):
            head_copy(head, i).wait_recv()
    total = part(0, 1 - mine, away_columns)
    for i in range(1, 3):
        total += part(i, 1 - mine, away_columns)
    d_hidden[...] += total
    d_heads[...] = wide[...]
    exchange.wait_send()
    for head in range(heads):
        for i in range(3):
            head_copy(head, i).wait_send()


def attend_back_fast(cube, branch, heads_in, probs, table, matrices):
    rows, width = branch.shape
    group, half = (2 * rows, width // 2)
    heads = half // 128
    vmem = pl.BlockSpec(memory_space=pltpu.VMEM)
    return pl.pallas_call(
        functools.partial(attend_back_kernel, cube, REL_LEFT, REL_RIGHT),
        out_shape=[
            jax.ShapeDtypeStruct((rows, width), jnp.float32),
            jax.ShapeDtypeStruct((rows, 3 * width), jnp.bfloat16),
            jax.ShapeDtypeStruct((128, 128), jnp.float32),
        ],
        in_specs=[vmem] * 4 + [pl.BlockSpec(memory_space=pl.ANY)] * 4,
        out_specs=[vmem] * 3,
        scratch_shapes=[
            pltpu.VMEM((4, width, width), jnp.bfloat16),
            pltpu.VMEM((group, half), jnp.bfloat16),
            pltpu.VMEM((rows, half), jnp.bfloat16),
            pltpu.VMEM((rows, 3 * width), jnp.bfloat16),
            pltpu.VMEM((heads, 3, group, 128), jnp.bfloat16),
            pltpu.SemaphoreType.DMA((4,)),
            pltpu.SemaphoreType.DMA((1,)),
            pltpu.SemaphoreType.DMA((1,)),
            pltpu.SemaphoreType.DMA((heads, 3)),
            pltpu.SemaphoreType.DMA((heads, 3)),
        ],
        compiler_params=pltpu.CompilerParams(
            collective_id=6, has_side_effects=True, vmem_limit_bytes=48 * 1024 * 1024
        ),
        name="attend_back",
    )(branch, heads_in, probs, table, *matrices)


def cube_of(shards, rel_table):
    batch, seq = (lax.axis_size("batch"), lax.axis_size("seq"))
    if seq != 2 or batch < 8 or batch & (batch - 1):
        return None
    if rel_table.shape[0] > 128 or rel_table.shape[1] != 128:
        return None
    if any(shard.shape[0] % 32 or shard.shape[1] % 1024 for shard in shards):
        return None
    return Cube(batch, seq)


def swish_slope(values):
    sigma = jax.nn.sigmoid(values)
    return sigma * (1.0 + values * (1.0 - sigma))


def norm_forward(values, gain, shift):
    mean = jnp.mean(values, axis=-1, keepdims=True)
    centred = values - mean
    inverse = lax.rsqrt(jnp.mean(centred * centred, axis=-1, keepdims=True) + epsilon)
    unit = centred * inverse
    return (unit * gain + shift, unit, inverse)


def norm_backward(d_out, unit, inverse, gain):
    d_unit = d_out * gain
    d_values = inverse * (
        d_unit
        - jnp.mean(d_unit, axis=-1, keepdims=True)
        - unit * jnp.mean(d_unit * unit, axis=-1, keepdims=True)
    )
    return (d_values, jnp.sum(d_out * unit, axis=0), jnp.sum(d_out, axis=0))


def ffn_forward(values, gain, shift, weight_in, weight_out):
    normed, unit, inverse = norm_forward(values, gain, shift)
    hidden = normed.astype(jnp.bfloat16)
    act = matmul(hidden, weight_in)
    swish = jax.nn.silu(act).astype(jnp.bfloat16)
    return (values + 0.5 * matmul(swish, weight_out), (hidden, act, swish, unit, inverse))


def ffn_backward(d_out, kept, gain, weight_in, weight_out):
    hidden, act, swish, unit, inverse = kept
    d_branch = (0.5 * d_out).astype(jnp.bfloat16)
    d_act = (transposed_right(d_branch, weight_out) * swish_slope(act)).astype(jnp.bfloat16)
    d_norm, d_gain, d_shift = norm_backward(transposed_right(d_act, weight_in), unit, inverse, gain)
    return (d_out + d_norm, (hidden, d_act), (swish, d_branch), d_gain, d_shift)


def segment_ids(place, ends, group):
    inside = jnp.sum((place[:, None] >= ends[None, :]).astype(jnp.int32), axis=1)
    return jnp.where((place >= 0) & (place < group), inside, -1)


def to_heads(hidden, weight, heads):
    return matmul(hidden, weight).astype(jnp.bfloat16).reshape(hidden.shape[0], heads, -1)


def spread_band(project, start, group, left, right):
    heads, rows, width = project.shape
    band = rows + width - 1
    blank = jnp.zeros_like(project[:, :, :1])
    middle = jnp.concatenate([blank, project[:, :, 1 : width - 1], blank], axis=2)
    padded = jnp.pad(middle, ((0, 0), (0, 0), (0, band + 1 - width)))
    skewed = padded.reshape(heads, rows * (band + 1))[:, : rows * band].reshape(heads, rows, band)
    canvas = jnp.zeros((heads, rows, group + left + right), jnp.float32)
    anchor = jnp.zeros((), jnp.int32)
    canvas = lax.dynamic_update_slice(canvas, skewed, (anchor, anchor, start))
    return canvas[:, :, left : left + group]


def relative_bins(grad, difference, start, width, left, right):
    heads, rows, group = grad.shape
    band = rows + width - 1
    canvas = jnp.pad(grad, ((0, 0), (0, 0), (left, right)))
    anchor = jnp.zeros((), jnp.int32)
    strip = lax.dynamic_slice(canvas, (anchor, anchor, start), (heads, rows, band))
    flat = jnp.pad(strip.reshape(heads, rows * band), ((0, 0), (0, rows)))
    inner = flat.reshape(heads, rows, band + 1)[:, :, 1 : width - 1]
    below = jnp.sum(jnp.where(difference[None] <= -left, grad, 0.0), axis=2, keepdims=True)
    above = jnp.sum(jnp.where(difference[None] >= right, grad, 0.0), axis=2, keepdims=True)
    return jnp.concatenate([below, inner, above], axis=2)


def block_scores(rows_query, keys, table, segment, start, left, right):
    rows, heads, depth = rows_query.shape
    group = keys.shape[0]
    width = table.shape[0]
    scale = 1.0 / math.sqrt(depth)
    project = jnp.einsum("qhd,rd->hqr", rows_query, table, preferred_element_type=jnp.float32)
    content = jnp.einsum("qhd,khd->hqk", rows_query, keys, preferred_element_type=jnp.float32)
    key_place = jnp.arange(group, dtype=jnp.int32)
    row_place = start + jnp.arange(rows, dtype=jnp.int32)
    difference = key_place[None, :] - row_place[:, None]
    relative = spread_band(project, start, group, left, right)
    relative = relative + jnp.where(difference[None] <= -left, project[:, :, :1], 0.0)
    relative = relative + jnp.where(difference[None] >= right, project[:, :, width - 1 :], 0.0)
    row_segment = lax.dynamic_slice_in_dim(segment, start, rows)
    same = row_segment[:, None] == segment[None, :]
    return (jnp.where(same[None], scale * (content + relative), masked_score), difference)


def attention_forward(query, keys, values, table, segment, block_rows, left, right):
    group = query.shape[0]
    starts = jnp.arange(group // block_rows, dtype=jnp.int32) * block_rows

    def one_block(carry, start):
        rows_query = lax.dynamic_slice_in_dim(query, start, block_rows, 0)
        scores, difference = block_scores(rows_query, keys, table, segment, start, left, right)
        top = jnp.max(scores, axis=2, keepdims=True)
        weights = jnp.exp(scores - top)
        total = jnp.sum(weights, axis=2, keepdims=True)
        probs = (weights / total).astype(jnp.bfloat16)
        rows_out = jnp.einsum("hqk,khd->qhd", probs, values, preferred_element_type=jnp.float32)
        return (carry, (rows_out.astype(jnp.bfloat16), (top + jnp.log(total))[:, :, 0]))

    unused, (pieces, log_total) = lax.scan(one_block, 0, starts)
    return (pieces.reshape(query.shape), log_total)


def attention_backward(
    query, keys, values, table, segment, log_total, d_context, block_rows, left, right
):
    group, heads, depth = query.shape
    width = table.shape[0]
    scale = 1.0 / math.sqrt(depth)
    starts = jnp.arange(group // block_rows, dtype=jnp.int32) * block_rows

    def one_block(carry, operands):
        d_keys, d_values, d_table = carry
        start, block_total = operands
        rows_query = lax.dynamic_slice_in_dim(query, start, block_rows, 0)
        rows_grad = lax.dynamic_slice_in_dim(d_context, start, block_rows, 0)
        scores, difference = block_scores(rows_query, keys, table, segment, start, left, right)
        probs = jnp.exp(scores - block_total[:, :, None])
        d_values = d_values + jnp.einsum(
            "hqk,qhd->khd",
            probs.astype(jnp.bfloat16),
            rows_grad,
            preferred_element_type=jnp.float32,
        )
        d_probs = jnp.einsum("qhd,khd->hqk", rows_grad, values, preferred_element_type=jnp.float32)
        weighted = jnp.sum(probs * d_probs, axis=2, keepdims=True)
        d_scores = (probs * (d_probs - weighted)).astype(jnp.bfloat16)
        bins = relative_bins(
            scale * d_scores.astype(jnp.float32), difference, start, width, left, right
        )
        bins = bins.astype(jnp.bfloat16)
        d_rows = scale * jnp.einsum(
            "hqk,khd->qhd", d_scores, keys, preferred_element_type=jnp.float32
        )
        d_rows = d_rows + jnp.einsum("hqr,rd->qhd", bins, table, preferred_element_type=jnp.float32)
        d_keys = d_keys + scale * jnp.einsum(
            "hqk,qhd->khd", d_scores, rows_query, preferred_element_type=jnp.float32
        )
        d_table = d_table + jnp.einsum(
            "hqr,qhd->rd", bins, rows_query, preferred_element_type=jnp.float32
        )
        return ((d_keys, d_values, d_table), d_rows.astype(jnp.bfloat16))

    zeros_heads = jnp.zeros(query.shape, jnp.float32)
    zeros_table = jnp.zeros(table.shape, jnp.float32)
    (d_keys, d_values, d_table), d_rows = lax.scan(
        one_block, (zeros_heads, zeros_heads, zeros_table), (starts, log_total)
    )
    return (
        d_rows.reshape(query.shape),
        d_keys.astype(jnp.bfloat16),
        d_values.astype(jnp.bfloat16),
        d_table,
    )


def on_device(
    frames,
    lengths,
    cotangent,
    ffn1_in,
    ffn1_out,
    query_w,
    key_w,
    value_w,
    out_w,
    point_in,
    point_out,
    ffn2_in,
    ffn2_out,
    depth_w,
    rel_table,
    norm_gains,
    norm_biases,
    bn_gain,
    bn_shift,
):
    seq_count = lax.axis_size("seq")
    seq_rank = lax.axis_index("seq")
    frames_here, width = frames.shape
    group = frames_here * seq_count
    block_rows = min(512, group)
    kernel_size = depth_w.shape[0]
    reach = kernel_size // 2
    ends = jnp.cumsum(lengths[0])
    last_entry = lengths.shape[1] - 1
    first = seq_rank * frames_here
    wide_place = first - reach + jnp.arange(frames_here + 2 * reach, dtype=jnp.int32)
    wide_segment = segment_ids(wide_place, ends, group)
    own_segment = wide_segment[reach : reach + frames_here]
    mask = (own_segment < last_entry).astype(jnp.float32)[:, None]
    group_segment = segment_ids(jnp.arange(group, dtype=jnp.int32), ends, group)
    shards = (
        ffn1_in,
        ffn1_out,
        query_w,
        key_w,
        value_w,
        out_w,
        point_in,
        point_out,
        ffn2_in,
        ffn2_out,
    )
    cube = cube_of(shards, rel_table)
    gathered = gather_all(shards, cube)
    start_values = frames.astype(jnp.float32)
    after_first, kept_first = ffn_forward(
        start_values, norm_gains[0], norm_biases[0], gathered[0], gathered[1]
    )
    attn_norm, attn_unit, attn_inverse = norm_forward(after_first, norm_gains[1], norm_biases[1])
    attn_hidden = attn_norm.astype(jnp.bfloat16)
    if cube is None:
        query_heads, key_heads, value_heads = (
            lax.all_to_all(
                to_heads(attn_hidden, gathered[2], HEADS),
                "seq",
                split_axis=1,
                concat_axis=0,
                tiled=True,
            ),
            lax.all_to_all(
                to_heads(attn_hidden, gathered[3], HEADS),
                "seq",
                split_axis=1,
                concat_axis=0,
                tiled=True,
            ),
            lax.all_to_all(
                to_heads(attn_hidden, gathered[4], HEADS),
                "seq",
                split_axis=1,
                concat_axis=0,
                tiled=True,
            ),
        )
        context_heads, log_total = attention_forward(
            query_heads,
            key_heads,
            value_heads,
            rel_table,
            group_segment,
            block_rows,
            REL_LEFT,
            REL_RIGHT,
        )
        context = lax.all_to_all(context_heads, "seq", split_axis=0, concat_axis=1, tiled=True).reshape(
            frames_here, width
        )
        after_attn = after_first + matmul(context, gathered[5])
    else:
        table = jnp.pad(rel_table, ((0, 128 - rel_table.shape[0]), (0, 0)))
        same = (group_segment[:, None] == group_segment[None, :]).astype(jnp.float32)
        after_attn, context, heads_kept, probs_kept = attend_fast(
            cube, attn_hidden, after_first, same, table, gathered[2:6]
        )
    conv_norm, conv_unit, conv_inverse = norm_forward(after_attn, norm_gains[2], norm_biases[2])
    conv_hidden = conv_norm.astype(jnp.bfloat16)
    pointwise = matmul(conv_hidden, gathered[6])
    gate_half = pointwise[:, :width]
    sigma_half = jax.nn.sigmoid(pointwise[:, width:])
    gated = (gate_half * sigma_half).astype(jnp.bfloat16)
    gated_wide = padded_2(gated, (("seq", 0),), reach)
    kernel = depth_w.astype(jnp.float32)
    mixed = jnp.zeros((frames_here, width), jnp.float32)
    for offset in range(kernel_size):
        same = (wide_segment[offset : offset + frames_here] == own_segment).astype(jnp.float32)[
            :, None
        ]
        mixed = (
            mixed
            + kernel[offset] * gated_wide[offset : offset + frames_here].astype(jnp.float32) * same
        )
    total, squares, count = sum_everywhere(
        (jnp.sum(mixed * mask, axis=0), jnp.sum(mixed * mixed * mask, axis=0), jnp.sum(mask)),
        cube,
        1,
    )
    mean = total / count
    var = squares / count - mean * mean
    bn_inverse = lax.rsqrt(var + epsilon)
    centred = (mixed - mean) * bn_inverse
    bn_out = centred * bn_gain + bn_shift
    conv_swish = jax.nn.silu(bn_out).astype(jnp.bfloat16)
    after_conv = after_attn + matmul(conv_swish, gathered[7])
    after_second, kept_second = ffn_forward(
        after_conv, norm_gains[3], norm_biases[3], gathered[8], gathered[9]
    )
    final_norm, final_unit, final_inverse = norm_forward(
        after_second, norm_gains[4], norm_biases[4]
    )
    sample_variance = var * count / (count - 1.0)
    d_final = cotangent.astype(jnp.float32) * mask
    d_second, gain_four, shift_four = norm_backward(
        d_final, final_unit, final_inverse, norm_gains[4]
    )
    d_conv_res, grad_two_in, grad_two_out, gain_three, shift_three = ffn_backward(
        d_second, kept_second, norm_gains[3], gathered[8], gathered[9]
    )
    conv_branch = d_conv_res.astype(jnp.bfloat16)
    d_bn_out = transposed_right(conv_branch, gathered[7]) * swish_slope(bn_out)
    grad_bn_gain, grad_bn_shift = sum_everywhere(
        (jnp.sum(d_bn_out * centred * mask, axis=0), jnp.sum(d_bn_out * mask, axis=0)), cube, 2
    )
    d_mixed = (
        bn_gain * bn_inverse * (d_bn_out - mask * (grad_bn_shift + centred * grad_bn_gain) / count)
    )
    d_mixed = d_mixed.astype(jnp.bfloat16)
    d_mixed_wide = padded_2(d_mixed, (("seq", 0),), reach)
    d_mixed_value = d_mixed.astype(jnp.float32)
    d_gated = jnp.zeros((frames_here, width), jnp.float32)
    kernel_rows = []
    for offset in range(kernel_size):
        same = (wide_segment[offset : offset + frames_here] == own_segment).astype(jnp.float32)[
            :, None
        ]
        shifted_in = gated_wide[offset : offset + frames_here].astype(jnp.float32)
        kernel_rows.append(jnp.sum(d_mixed_value * shifted_in * same, axis=0))
        back = 2 * reach - offset
        same_back = (wide_segment[back : back + frames_here] == own_segment).astype(jnp.float32)[
            :, None
        ]
        d_gated = (
            d_gated
            + kernel[offset]
            * d_mixed_wide[back : back + frames_here].astype(jnp.float32)
            * same_back
        )
    d_pointwise = jnp.concatenate(
        [d_gated * sigma_half, d_gated * gate_half * sigma_half * (1.0 - sigma_half)], axis=1
    ).astype(jnp.bfloat16)
    d_conv_norm, gain_two, shift_two = norm_backward(
        transposed_right(d_pointwise, gathered[6]), conv_unit, conv_inverse, norm_gains[2]
    )
    d_attn_res = d_conv_res + d_conv_norm
    attn_branch = d_attn_res.astype(jnp.bfloat16)
    if cube is None:
        d_context = (
            transposed_right(attn_branch, gathered[5])
            .astype(jnp.bfloat16)
            .reshape(frames_here, HEADS, -1)
        )
        d_context_heads = lax.all_to_all(d_context, "seq", split_axis=1, concat_axis=0, tiled=True)
        d_query_heads, d_key_heads, d_value_heads, d_table = attention_backward(
            query_heads,
            key_heads,
            value_heads,
            rel_table,
            group_segment,
            log_total,
            d_context_heads,
            block_rows,
            REL_LEFT,
            REL_RIGHT,
        )
        d_query, d_keys, d_values = (
            lax.all_to_all(d_query_heads, "seq", split_axis=0, concat_axis=1, tiled=True),
            lax.all_to_all(d_key_heads, "seq", split_axis=0, concat_axis=1, tiled=True),
            lax.all_to_all(d_value_heads, "seq", split_axis=0, concat_axis=1, tiled=True),
        )
        d_query = d_query.reshape(frames_here, width)
        d_keys = d_keys.reshape(frames_here, width)
        d_values = d_values.reshape(frames_here, width)
        d_attn_hidden = (
            transposed_right(d_query, gathered[2])
            + transposed_right(d_keys, gathered[3])
            + transposed_right(d_values, gathered[4])
        )
        heads_in = jnp.concatenate([d_query, d_keys, d_values], axis=1)
    else:
        d_attn_hidden, heads_in, d_table = attend_back_fast(
            cube, attn_branch, heads_kept, probs_kept, table, gathered[2:6]
        )
        d_table = d_table[: rel_table.shape[0]]
    d_attn_norm, gain_one, shift_one = norm_backward(
        d_attn_hidden, attn_unit, attn_inverse, norm_gains[1]
    )
    d_first_res = d_attn_res + d_attn_norm
    d_input, grad_one_in, grad_one_out, gain_zero, shift_zero = ffn_backward(
        d_first_res, kept_first, norm_gains[0], gathered[0], gathered[1]
    )
    attn_out, conv_out, conv_in, two_out, two_in, one_in, one_out, attn_in = gradient_shards(
        (
            (context, attn_branch),
            (conv_swish, conv_branch),
            (conv_hidden, d_pointwise),
            grad_two_out,
            grad_two_in,
            grad_one_in,
            grad_one_out,
            (attn_hidden, heads_in),
        ),
        cube,
    )
    gains_local = jnp.stack([gain_zero, gain_one, gain_two, gain_three, gain_four])
    shifts_local = jnp.stack([shift_zero, shift_one, shift_two, shift_three, shift_four])
    kernel_local = jnp.stack(kernel_rows)
    grad_gains, grad_biases, grad_depth, grad_rel = sum_everywhere(
        (gains_local, shifts_local, kernel_local, d_table), cube, 3
    )
    return (
        final_norm.astype(jnp.bfloat16),
        d_input.astype(jnp.bfloat16),
        one_in,
        one_out,
        attn_in[:, :width],
        attn_in[:, width : 2 * width],
        attn_in[:, 2 * width :],
        attn_out,
        conv_in,
        conv_out,
        two_in,
        two_out,
        grad_depth,
        grad_rel,
        grad_gains,
        grad_biases,
        grad_bn_gain,
        grad_bn_shift,
        sample_variance,
    )


def solution(mesh):
    placed = (
        P(("batch", "seq"), None),
        P("batch", None),
        P(("batch", "seq"), None),
        P(("batch", "seq"), None),
        P(("batch", "seq"), None),
        P(("batch", "seq"), None),
        P(("batch", "seq"), None),
        P(("batch", "seq"), None),
        P(("batch", "seq"), None),
        P(("batch", "seq"), None),
        P(("batch", "seq"), None),
        P(("batch", "seq"), None),
        P(("batch", "seq"), None),
        P(),
        P(),
        P(),
        P(),
        P(),
        P(),
    )
    return jax.shard_map(
        on_device,
        mesh=mesh,
        in_specs=placed,
        out_specs=(
            P(("batch", "seq"), None),
            P(("batch", "seq"), None),
            P(("batch", "seq"), None),
            P(("batch", "seq"), None),
            P(("batch", "seq"), None),
            P(("batch", "seq"), None),
            P(("batch", "seq"), None),
            P(("batch", "seq"), None),
            P(("batch", "seq"), None),
            P(("batch", "seq"), None),
            P(("batch", "seq"), None),
            P(("batch", "seq"), None),
            P(),
            P(),
            P(),
            P(),
            P(),
            P(),
            P(),
        ),
        check_vma=False,
    )
```

```python
import functools
import math

import jax
import jax.numpy as jnp
from jax import lax
from jax.experimental import pallas as pl
from jax.experimental.pallas import tpu as pltpu
from jax.sharding import PartitionSpec as P

MESH = pl.DeviceIdType.MESH
AXES = ("batch", "seq")

HEADS = 8
REL_LEFT = 64
REL_RIGHT = 8


epsilon = 1e-05
masked_score = -1000000000.0


def padded_2(shard, sides, width):
    for axis, dim in sides:
        peers, length = (lax.axis_size(axis), shard.shape[dim])
        up = [(i, (i + 1) % peers) for i in range(peers - 1)]
        down = [(j, i) for i, j in up]
        last = lax.slice_in_dim(shard, length - width, length, axis=dim)
        first = lax.slice_in_dim(shard, 0, width, axis=dim)
        before = lax.ppermute(last, axis, up)
        after = lax.ppermute(first, axis, down)
        shard = jnp.concatenate([before, shard, after], axis=dim)
    return shard


def matmul(left, right):
    return jnp.dot(left, right, preferred_element_type=jnp.float32)


def transposed_left(left, right):
    return lax.dot_general(
        left, right, (((0,), (0,)), ((), ())), preferred_element_type=jnp.float32
    )


def transposed_right(left, right):
    return lax.dot_general(
        left, right, (((1,), (1,)), ((), ())), preferred_element_type=jnp.float32
    )


class Cube:
    def __init__(self, batch, seq):
        self.seq_bits, self.batch_bits = (seq.bit_length() - 1, batch.bit_length() - 1)
        self.count = self.seq_bits + self.batch_bits
        self.core = self.seq_bits
        wide = (self.batch_bits - 1) // 2
        self.x = list(range(self.seq_bits))[::-1]
        self.y = list(range(self.core + 1, self.core + 1 + wide))[::-1]
        self.z = list(range(self.core + 1 + wide, self.count))[::-1]

    def bit(self, k):
        if k < self.seq_bits:
            return lax.rem(lax.axis_index("seq") // (1 << k), 2)
        return lax.rem(lax.axis_index("batch") // (1 << (k - self.seq_bits)), 2)

    def partner(self, k):
        batch, seq = (lax.axis_index("batch"), lax.axis_index("seq"))
        step = 1 - 2 * self.bit(k)
        if k < self.seq_bits:
            return (batch, seq + step * (1 << k))
        return (batch + step * (1 << (k - self.seq_bits)), seq)


def greet(cube, bits):
    barrier = pltpu.get_barrier_semaphore()
    for k in bits:
        pl.semaphore_signal(barrier, inc=1, device_id=cube.partner(k), device_id_type=MESH)
    pl.semaphore_wait(barrier, len(bits))


def gather_kernel(cube, plans, items, *refs):
    count = len(plans)
    shards, outs = (refs[:count], refs[count : 2 * count])
    send, recv, local = refs[2 * count :]
    own = [cube.bit(k) for k in range(cube.count)]
    kept = []
    for m, (bits, paired) in enumerate(plans):
        kept.append(
            pltpu.make_async_copy(
                shards[m].at[own[0]] if paired else shards[m],
                outs[m].at[tuple(own[k] for k in bits)],
                local.at[m],
            )
        )
        kept[m].start()
    greet(cube, range(cube.count))

    def copy(number, stage):
        m, order, block = flat[number]
        bits, paired = plans[m]
        lead = tuple(slice(None) if k in order[:stage] else own[k] for k in bits)
        place = outs[m].at[lead + block]
        source = place
        if stage == 0:
            source = shards[m].at[(1 - own[0],) + block] if paired else shards[m].at[block]
        return to_partner(
            cube, order[stage], source, place, send.at[number, stage], recv.at[number, stage]
        )

    flat = [item for chunk in items for item in chunk]
    numbers, at = ([], 0)
    for chunk in items:
        numbers.append(range(at, at + len(chunk)))
        at += len(chunk)
    for number in range(len(flat)):
        copy(number, 0).start()
    for one in kept:
        one.wait()
    most = max(len(order) for _, order, _ in flat)
    for turn in range(len(items) + most):
        for stage in range(most):
            for late in (0, 1):
                chunk = turn - stage - late
                if not 0 <= chunk < len(items):
                    continue
                for number in numbers[chunk]:
                    stages = len(flat[number][1])
                    if stage >= stages or late != (stage == stages - 1):
                        continue
                    copy(number, stage).wait_recv()
                    if stage + 1 < stages:
                        copy(number, stage + 1).start()
    for number, (_, order, _) in enumerate(flat):
        for stage in range(len(order)):
            copy(number, stage).wait_send()


def column_parts(width, shares):
    units, total, at, parts = (width // 128, sum(shares), 0, [])
    for share in shares:
        size = units * share // total
        parts.append((at * 128, size * 128))
        at += size
    return parts


def gather_fast(shards, kinds, cube):
    core, x, y, z = ([cube.core], cube.x, cube.y, cube.z)
    every = list(range(cube.count))[::-1]
    plans, items, shapes = ([], [], [])
    for m, (shard, kind) in enumerate(zip(shards, kinds)):
        if kind == "all":
            bits, shares = (every, (3, 3, 2))
            orders = [z + y + x + core, z + x + y + core, x + y + z + core]
        else:
            bits = every if kind == "pair" else every[:-1]
            first = x if kind == "pair" else []
            orders, shares = ([first + z + y + core, first + y + z + core], (7, 1))
        plans.append((bits, kind == "pair"))
        shapes.append((2,) * len(bits) + shard.shape[-2:])
        rows, columns = (min(64, shard.shape[-2]), min(2048, shard.shape[-1]))
        for row in range(0, shard.shape[-2], rows):
            for column in range(0, shard.shape[-1], columns):
                items.append(
                    [
                        (m, order, (pl.ds(row, rows), pl.ds(column + a, w)))
                        for order, (a, w) in zip(orders, column_parts(columns, shares))
                    ]
                )
    count, copies = (len(shards), sum(len(chunk) for chunk in items))
    outs = pl.pallas_call(
        functools.partial(gather_kernel, cube, plans, items),
        out_shape=[
            jax.ShapeDtypeStruct(shape, shard.dtype) for shape, shard in zip(shapes, shards)
        ],
        in_specs=[pl.BlockSpec(memory_space=pl.ANY)] * count,
        out_specs=[pl.BlockSpec(memory_space=pl.ANY)] * count,
        scratch_shapes=[
            pltpu.SemaphoreType.DMA((copies, cube.count)),
            pltpu.SemaphoreType.DMA((copies, cube.count)),
            pltpu.SemaphoreType.DMA((count,)),
        ],
        compiler_params=pltpu.CompilerParams(collective_id=0, has_side_effects=True),
        name="gather_weights",
    )(*shards)
    return tuple(out.reshape(-1, shard.shape[-1]) for out, shard in zip(outs, shards))


def sum_kernel(cube, value, out, held, sent, send, recv):
    bits = range(cube.count)
    greet(cube, bits)
    sent[0] = value[...]
    for k in bits:
        copy = pltpu.make_async_remote_copy(
            src_ref=sent.at[k],
            dst_ref=held.at[k],
            send_sem=send.at[k],
            recv_sem=recv.at[k],
            device_id=cube.partner(k),
            device_id_type=MESH,
        )
        copy.start()
        copy.wait()
        if k + 1 < cube.count:
            sent[k + 1] = sent[k] + held[k]
        else:
            out[...] = sent[k] + held[k]


def sum_fast(value, cube, number):
    return pl.pallas_call(
        functools.partial(sum_kernel, cube),
        out_shape=jax.ShapeDtypeStruct(value.shape, value.dtype),
        in_specs=[pl.BlockSpec(memory_space=pltpu.VMEM)],
        out_specs=pl.BlockSpec(memory_space=pltpu.VMEM),
        scratch_shapes=[
            pltpu.VMEM((cube.count,) + value.shape, value.dtype),
            pltpu.VMEM((cube.count,) + value.shape, value.dtype),
            pltpu.SemaphoreType.DMA((cube.count,)),
            pltpu.SemaphoreType.DMA((cube.count,)),
        ],
        compiler_params=pltpu.CompilerParams(collective_id=number, has_side_effects=True),
        name="sum_over_devices",
    )(value)


def sum_everywhere(values, cube, number):
    if cube is None:
        return lax.psum(values, AXES)
    return flat_unpack(sum_fast(flat_pack(values), cube, number), values)


def gradient_kernel(cube, shapes, kinds, tile, *refs):
    count = len(shapes)
    lefts, rights, refs = (refs[:count], refs[count : 2 * count], refs[2 * count :])
    value, out, crossed, value_out, refs = (refs[0], refs[1], refs[2], refs[3], refs[4:])
    near, far, whole = (refs[:count], refs[count : 2 * count], refs[2 * count : 3 * count])
    refs = refs[3 * count :]
    order = cube.y + cube.z[::-1]
    stages = len(order)
    total, sent, recv_at, refs = (refs[0], refs[1 : 1 + stages], refs[1 + stages : 1 + 2 * stages], refs[1 + 2 * stages :])
    cross, value_sent, value_held, refs = (refs[0], refs[1], refs[2], refs[3:])
    x_send, x_recv, local, c_send, c_recv, send, recv, cross_send, cross_recv, v_send, v_recv = refs
    rows, columns = tile
    number, depth = (out.shape[0], total.shape[0])
    lags = [3 + 2 * stage for stage in range(stages)]
    x, c = (cube.bit(0), cube.bit(cube.core))
    dims = sorted(order, reverse=True)
    bits = [cube.bit(k) for k in order]
    every = (slice(None),) * stages
    tokens = near[0].shape[-1] // 2
    pairs = [m for m in range(count) if kinds[m] == "pair"]
    own_lanes = pl.ds(pl.multiple_of(x * tokens, tokens), tokens)

    def spot(stage, flip):
        left = [k for k in dims if k not in order[:stage]]
        side = 1 - bits[stage] if flip else bits[stage]
        return tuple(side if k == order[stage] else slice(None) for k in left)

    def along_x(m):
        if kinds[m] != "all":
            return []
        return [
            to_partner(
                cube,
                0,
                lefts[m].at[every + (slice(None), 1 - x)],
                near[m].at[every + (slice(None), slice(None), own_lanes)],
                x_send.at[m, 0],
                x_recv.at[m, 0],
            ),
            to_partner(
                cube, 0, rights[m], whole[m].at[c, own_lanes], x_send.at[m, 1], x_recv.at[m, 1]
            ),
        ]

    def at_home(m):
        if kinds[m] != "all":
            return [
                pltpu.make_async_copy(lefts[m], near[m], local.at[m, 0]),
                pltpu.make_async_copy(rights[m], whole[m].at[c], local.at[m, 1]),
            ]
        return [
            pltpu.make_async_copy(
                lefts[m].at[every + (slice(None), x)],
                near[m].at[every + (slice(None), slice(None), own_lanes)],
                local.at[m, 0],
            ),
            pltpu.make_async_copy(rights[m], whole[m].at[c, own_lanes], local.at[m, 1]),
        ]

    def along_core(m):
        return [
            to_partner(
                cube,
                cube.core,
                near[m].at[every + (1 - c,)],
                far[m],
                c_send.at[m, 0],
                c_recv.at[m, 0],
            ),
            to_partner(
                cube, cube.core, whole[m].at[c], whole[m].at[c], c_send.at[m, 1], c_recv.at[m, 1]
            ),
        ]

    def remote(stage, chunk):
        return to_partner(
            cube,
            order[stage],
            sent[stage].at[chunk],
            recv_at[stage].at[chunk],
            send.at[stage, chunk],
            recv.at[stage, chunk],
        )

    def reduce(step):
        for stage in range(stages):
            chunk = step - lags[stage]

            @pl.when((chunk >= 0) & (chunk < number))
            def _(stage=stage, chunk=chunk):
                slot = lax.rem(chunk, depth)
                remote(stage, chunk).wait_recv()
                mine = tuple(
                    bits[order.index(k)] if k in order[: stage + 1] else slice(None) for k in dims
                )
                arrived = recv_at[stage]
                if stage + 1 == stages:
                    out[chunk] = total[(slot,) + mine] + arrived[chunk].astype(jnp.float32)
                else:
                    away, home = (spot(stage + 1, True), spot(stage + 1, False))
                    full = list(mine)
                    full[dims.index(order[stage + 1])] = 1 - bits[stage + 1]
                    sent[stage + 1][chunk] = (
                        total[(slot,) + tuple(full)]
                        + arrived[(chunk,) + away].astype(jnp.float32)
                    ).astype(jnp.bfloat16)
                    remote(stage + 1, chunk).start()
                    full[dims.index(order[stage + 1])] = bits[stage + 1]
                    total[(slot,) + tuple(full)] += arrived[(chunk,) + home].astype(jnp.float32)

    def value_copy(k):
        return to_partner(
            cube, k, value_sent.at[k], value_held.at[k], v_send.at[k], v_recv.at[k]
        )

    def value_turn(k):
        if k == 0:
            value_sent[0] = value[...]
        elif k <= cube.count:
            value_copy(k - 1).wait_recv()
            sum_here = value_sent[k - 1] + value_held[k - 1]
            if k < cube.count:
                value_sent[k] = sum_here
            else:
                value_out[...] = sum_here
        if k < cube.count:
            value_copy(k).start()

    def cross_copy(i, first):
        away = pl.ds(first + (1 - x) * 2, 2)
        return to_partner(cube, 0, out.at[away], cross.at[i], cross_send.at[i], cross_recv.at[i])

    greet(cube, range(cube.count))
    value_turn(0)
    for m in range(count):
        for copy in along_x(m) + at_home(m):
            copy.start()
    first, firsts = (0, {})
    for m in range(count):
        firsts[m] = first
        if m > 0:
            value_turn(m)
        for copy in at_home(m):
            copy.wait()
        for copy in along_x(m):
            copy.wait_recv()
        for copy in along_core(m):
            copy.start()
        for copy in along_core(m):
            copy.wait_recv()
        down, across = shapes[m]

        def one(j, carry, m=m, first=first, down=down, across=across):
            chunk = first + j
            slot = lax.rem(chunk, depth)
            row = pl.ds(pl.multiple_of((j // across) * rows, rows), rows)
            column = pl.ds(pl.multiple_of(lax.rem(j, across) * columns, columns), columns)

            def half(flip):
                place = spot(0, flip)
                one_left = near[m][place + (c, row, slice(None))]
                two_left = far[m][place + (row, slice(None))]
                shape = one_left.shape[:-1] + (columns,)
                one_left = one_left.reshape(-1, 2 * tokens)
                two_left = two_left.reshape(-1, 2 * tokens)
                result = matmul(one_left, whole[m][c, :, column]) + matmul(
                    two_left, whole[m][1 - c, :, column]
                )
                return result.reshape(shape)

            sent[0][chunk] = half(True).astype(jnp.bfloat16)
            remote(0, chunk).start()
            total[(slot,) + spot(0, False)] = half(False)
            reduce(chunk)
            return carry

        lax.fori_loop(0, down * across, one, 0)
        first += down * across

    def drain(step, carry):
        reduce(step)
        return carry

    for k in range(count, cube.count + 1):
        value_turn(k)
    for i, m in enumerate(pairs):
        cross_copy(i, firsts[m]).start()
    lax.fori_loop(number, number + lags[-1] + 1, drain, 0)
    for i, m in enumerate(pairs):
        cross_copy(i, firsts[m]).wait_recv()
        crossed[i, x] = out[pl.ds(firsts[m] + x * 2, 2)]
        crossed[i, 1 - x] = cross[i]
        cross_copy(i, firsts[m]).wait_send()
    for k in range(cube.count):
        value_copy(k).wait_send()
    for m in range(count):
        for copy in along_x(m) + along_core(m):
            copy.wait_send()

    def finish(chunk, carry):
        for stage in range(stages):
            remote(stage, chunk).wait_send()
        return carry

    lax.fori_loop(0, number, finish, 0)


def gradients_fast(pairs, kinds, value, cube, rows, columns):
    order = cube.y + cube.z[::-1]
    stages, count = (len(order), len(pairs))
    lefts, rights, shapes, near, far, whole = ([], [], [], [], [], [])
    for (left, right), kind in zip(pairs, kinds):
        lead = (2,) * stages
        if kind == "all":
            block, tokens = (left.shape[1] >> cube.count, left.shape[0])
            lefts.append(left.T.reshape(lead + (2, 2, block, tokens)))
        else:
            block, tokens = (left.shape[1] >> (cube.count - 1), left.shape[0] // 2)
            lefts.append(left.T.reshape(lead + (2, block, 2 * tokens)))
        rights.append(right)
        shapes.append((block // rows, right.shape[1] // columns))
        near.append(pltpu.VMEM(lead + (2, block, 2 * tokens), jnp.bfloat16))
        far.append(pltpu.VMEM(lead + (block, 2 * tokens), jnp.bfloat16))
        whole.append(pltpu.VMEM((2, 2 * tokens, right.shape[1]), jnp.bfloat16))
    number, tile = (sum(down * across for down, across in shapes), (rows, columns))
    held = [
        pltpu.VMEM((number,) + (2,) * (stages - 1 - stage) + tile, jnp.bfloat16)
        for stage in range(stages)
    ]
    depth = 3 + 2 * (stages - 1) + 1
    paired = kinds.count("pair")
    vmem = pl.BlockSpec(memory_space=pltpu.VMEM)
    values = pltpu.VMEM((cube.count,) + value.shape, value.dtype)
    out, crossed, value = pl.pallas_call(
        functools.partial(gradient_kernel, cube, shapes, kinds, tile),
        out_shape=[
            jax.ShapeDtypeStruct((number,) + tile, jnp.float32),
            jax.ShapeDtypeStruct((paired, 2, 2) + tile, jnp.float32),
            jax.ShapeDtypeStruct(value.shape, value.dtype),
        ],
        in_specs=[pl.BlockSpec(memory_space=pl.ANY)] * (2 * count) + [vmem],
        out_specs=[vmem] * 3,
        scratch_shapes=near
        + far
        + whole
        + [pltpu.VMEM((depth,) + (2,) * stages + tile, jnp.float32)]
        + held
        + held
        + [pltpu.VMEM((paired, 2) + tile, jnp.float32), values, values]
        + [pltpu.SemaphoreType.DMA((count, 2))] * 5
        + [pltpu.SemaphoreType.DMA((stages, number))] * 2
        + [pltpu.SemaphoreType.DMA((paired,))] * 2
        + [pltpu.SemaphoreType.DMA((cube.count,))] * 2,
        compiler_params=pltpu.CompilerParams(
            collective_id=4, has_side_effects=True, vmem_limit_bytes=60 * 1024 * 1024
        ),
        name="reduce_gradients",
    )(*lefts, *rights, value)
    results, at, pair = ([], 0, 0)
    for (down, across), right, kind in zip(shapes, rights, kinds):
        if kind == "pair":
            piece = crossed[pair].reshape(2, 2, rows, columns // 128, 128)
            results.append(piece.transpose(2, 1, 3, 0, 4).reshape(rows, 4 * columns))
            pair += 1
        else:
            piece = out[at : at + down * across].reshape(down, across, rows, columns)
            results.append(piece.transpose(0, 2, 1, 3).reshape(down * rows, right.shape[1]))
        at += down * across
    return results, value


def flat_pack(values):
    flat = jnp.concatenate([value.reshape(-1) for value in values])
    size = -(-flat.shape[0] // 8192) * 8192
    return jnp.pad(flat, (0, size - flat.shape[0])).reshape(-1, 1024)


def flat_unpack(flat, values):
    flat, out, at = (flat.reshape(-1), [], 0)
    for value in values:
        out.append(flat[at : at + value.size].reshape(value.shape))
        at += value.size
    return tuple(out)


def gradient_shards(pairs, values, cube):
    if cube is None:
        results = []
        for left, right in pairs:
            whole = transposed_left(left, right)
            flat = whole.reshape(-1, 128)
            shard = lax.psum_scatter(flat, AXES, scatter_dimension=0, tiled=True)
            results.append(shard.reshape(-1, whole.shape[1]))
        return results, lax.psum(values, AXES)
    kinds = ["all"] * 3 + ["half", "pair", "pair", "half", "all"]
    results, flat = gradients_fast(pairs, kinds, flat_pack(values), cube, 32, 1024)
    return results, flat_unpack(flat, values)


def parities(shard):
    rows, columns = shard.shape
    return shard.reshape(rows, columns // 256, 2, 128).transpose(2, 0, 1, 3).reshape(2, rows, -1)


def gather_all(shards, cube):
    if cube is None:
        return tuple(lax.all_gather(shard, AXES, axis=0, tiled=True) for shard in shards)
    kinds = ("pair", "half") + ("all",) * 6 + ("pair", "half")
    shards = [parities(shard) if kind == "pair" else shard for shard, kind in zip(shards, kinds)]
    return gather_fast(shards, kinds, cube)


def distance_rows(group, left, right, backwards):
    row = lax.broadcasted_iota(jnp.int32, (group, 128), 0)
    row = group - 1 - row if backwards else row
    distance = jnp.where(row >= group // 2, row - group, row)
    index = jnp.clip(distance, -left, right) + left
    hit = index == lax.broadcasted_iota(jnp.int32, (group, 128), 1)
    return jnp.where(hit, 1.0, 0.0).astype(jnp.bfloat16)


def halves(cube, rows, half):
    mine = cube.bit(0)
    return (
        pl.ds(pl.multiple_of(mine * half, half), half),
        pl.ds(pl.multiple_of((1 - mine) * half, half), half),
        pl.ds(pl.multiple_of(mine * rows, rows), rows),
        pl.ds(pl.multiple_of((1 - mine) * rows, rows), rows),
    )


def to_partner(cube, k, source, target, send, recv):
    return pltpu.make_async_remote_copy(
        src_ref=source,
        dst_ref=target,
        send_sem=send,
        recv_sem=recv,
        device_id=cube.partner(k),
        device_id_type=MESH,
    )


def attend_kernel(cube, left, right, *refs):
    hidden, before, same, table, query_w, key_w, value_w, out_w = refs[:8]
    after, context, heads_out, probs_out = refs[8:12]
    weights, heads_in, away, wide, context_away, load, send, recv, head_send, head_recv = refs[12:]
    rows, width = hidden.shape
    group, half = (2 * rows, width // 2)
    heads = half // 128
    scale = 1.0 / math.sqrt(128)
    mine = cube.bit(0)
    own_columns, away_columns, own_rows, away_rows = halves(cube, rows, half)
    loads = []
    for i, matrix in enumerate((query_w, key_w, value_w, out_w)):
        loads.append(pltpu.make_async_copy(matrix, weights.at[i], load.at[i]))
        loads[i].start()
    greet(cube, [0])

    def exchange(i):
        return to_partner(
            cube, 0, away.at[i], heads_in.at[i, own_rows], send.at[i], recv.at[i]
        )

    def context_copy(head):
        column = pl.ds(pl.multiple_of(mine * half + head * 128, 128), 128)
        return to_partner(
            cube, 0, context_away.at[head], wide.at[:, column], head_send.at[head], head_recv.at[head]
        )

    for i in range(3):
        loads[i].wait()
        away[i] = matmul(hidden[...], weights[i, :, away_columns]).astype(jnp.bfloat16)
        exchange(i).start()
    for i in range(3):
        heads_in[i, own_rows, :] = matmul(hidden[...], weights[i, :, own_columns]).astype(
            jnp.bfloat16
        )
    spread = matmul(distance_rows(group, left, right, False), table[...]).astype(jnp.bfloat16)
    loads[3].wait()
    for i in range(3):
        exchange(i).wait_recv()

    def one_head(head, carry):
        column = pl.ds(pl.multiple_of(head * 128, 128), 128)
        place = pl.ds(pl.multiple_of(mine * half + head * 128, 128), 128)
        query, keys, values = (heads_in[i, :, column] for i in range(3))
        relative = pltpu.roll(transposed_right(query, spread), 0, 1, stride=1, stride_axis=0)
        scores = scale * (transposed_right(query, keys) + relative)
        scores = jnp.where(same[...] > 0, scores, masked_score)
        weight = jnp.exp(scores - jnp.max(scores, axis=1, keepdims=True))
        probs_out[head] = weight / jnp.sum(weight, axis=1, keepdims=True)
        there = probs_out[head, away_rows, :].astype(jnp.bfloat16)
        context_away[head] = matmul(there, values).astype(jnp.bfloat16)
        context_copy(head).start()
        here = probs_out[head, own_rows, :].astype(jnp.bfloat16)
        wide[:, place] = matmul(here, values).astype(jnp.bfloat16)
        return carry

    lax.fori_loop(0, heads, one_head, 0)
    heads_out[...] = heads_in[...]
    after[...] = before[...] + matmul(wide[:, own_columns], weights[3, own_columns, :])
    for head in range(heads):
        context_copy(head).wait_recv()
    after[...] += matmul(wide[:, away_columns], weights[3, away_columns, :])
    context[...] = wide[...]
    for i in range(3):
        exchange(i).wait_send()
    for head in range(heads):
        context_copy(head).wait_send()


def attend_fast(cube, hidden, before, same, table, matrices):
    rows, width = hidden.shape
    group, half = (2 * rows, width // 2)
    heads = half // 128
    vmem = pl.BlockSpec(memory_space=pltpu.VMEM)
    return pl.pallas_call(
        functools.partial(attend_kernel, cube, REL_LEFT, REL_RIGHT),
        out_shape=[
            jax.ShapeDtypeStruct((rows, width), jnp.float32),
            jax.ShapeDtypeStruct((rows, width), jnp.bfloat16),
            jax.ShapeDtypeStruct((3, group, half), jnp.bfloat16),
            jax.ShapeDtypeStruct((heads, group, group), jnp.float32),
        ],
        in_specs=[vmem] * 4 + [pl.BlockSpec(memory_space=pl.ANY)] * 4,
        out_specs=[vmem] * 4,
        scratch_shapes=[
            pltpu.VMEM((4, width, width), jnp.bfloat16),
            pltpu.VMEM((3, group, half), jnp.bfloat16),
            pltpu.VMEM((3, rows, half), jnp.bfloat16),
            pltpu.VMEM((rows, width), jnp.bfloat16),
            pltpu.VMEM((heads, rows, 128), jnp.bfloat16),
            pltpu.SemaphoreType.DMA((4,)),
            pltpu.SemaphoreType.DMA((3,)),
            pltpu.SemaphoreType.DMA((3,)),
            pltpu.SemaphoreType.DMA((heads,)),
            pltpu.SemaphoreType.DMA((heads,)),
        ],
        compiler_params=pltpu.CompilerParams(
            collective_id=5, has_side_effects=True, vmem_limit_bytes=48 * 1024 * 1024
        ),
        name="attend",
    )(hidden, before, same, table, *matrices)


def attend_back_kernel(cube, left, right, *refs):
    branch, heads_in, probs_in, table, query_w, key_w, value_w, out_w = refs[:8]
    d_hidden, d_heads, d_table = refs[8:11]
    weights, d_context, d_context_away, wide, away, load, send, recv, head_send, head_recv = refs[
        11:
    ]
    rows, width = branch.shape
    group, half = (2 * rows, width // 2)
    heads = half // 128
    scale = 1.0 / math.sqrt(128)
    mine = cube.bit(0)
    own_columns, away_columns, own_rows, away_rows = halves(cube, rows, half)
    loads = []
    for i, matrix in enumerate((out_w, query_w, key_w, value_w)):
        loads.append(pltpu.make_async_copy(matrix, weights.at[i], load.at[i]))
        loads[i].start()
    greet(cube, [0])
    loads[0].wait()
    exchange = to_partner(
        cube, 0, d_context_away, d_context.at[own_rows], send.at[0], recv.at[0]
    )
    d_context_away[...] = transposed_right(branch[...], weights[0, away_columns, :]).astype(
        jnp.bfloat16
    )
    exchange.start()
    d_context[own_rows, :] = transposed_right(branch[...], weights[0, own_columns, :]).astype(
        jnp.bfloat16
    )
    spread = distance_rows(group, left, right, True)
    down = lax.broadcasted_iota(jnp.int32, (group, group), 0)
    across = lax.broadcasted_iota(jnp.int32, (group, group), 1)
    mirror = jnp.where(down + across == group - 1, 1.0, 0.0).astype(jnp.bfloat16)
    d_table[...] = jnp.zeros_like(d_table)
    exchange.wait_recv()

    def head_copy(head, i):
        column = pl.ds(pl.multiple_of(i * width + mine * half + head * 128, 128), 128)
        return to_partner(
            cube,
            0,
            away.at[head, i, away_rows],
            wide.at[:, column],
            head_send.at[head, i],
            head_recv.at[head, i],
        )

    def one_head(head, carry):
        column = pl.ds(pl.multiple_of(head * 128, 128), 128)
        query, keys, values = (heads_in[i, :, column] for i in range(3))
        d_rows = d_context[:, column]
        probs = probs_in[head]
        d_probs = transposed_right(d_rows, values)
        weighted = jnp.sum(probs * d_probs, axis=1, keepdims=True)
        d_scores = (probs * (d_probs - weighted)).astype(jnp.bfloat16)
        away[head, 2] = transposed_left(probs.astype(jnp.bfloat16), d_rows).astype(jnp.bfloat16)
        head_copy(head, 2).start()
        away[head, 1] = (scale * transposed_left(d_scores, query)).astype(jnp.bfloat16)
        head_copy(head, 1).start()
        turned = pltpu.roll(matmul(d_scores, mirror), 0, 1, stride=1, stride_axis=0)
        bins = (scale * matmul(turned.astype(jnp.bfloat16), spread)).astype(jnp.bfloat16)
        away[head, 0] = (scale * matmul(d_scores, keys) + matmul(bins, table[...])).astype(
            jnp.bfloat16
        )
        head_copy(head, 0).start()
        d_table[...] += transposed_left(bins, query)
        for i in range(3):
            place = pl.ds(pl.multiple_of(i * width + mine * half + head * 128, 128), 128)
            wide[:, place] = away[head, i, own_rows, :]
        return carry

    lax.fori_loop(0, heads, one_head, 0)
    for i in range(3):
        loads[1 + i].wait()

    def part(i, offset, columns):
        place = pl.ds(pl.multiple_of(i * width + offset * half, half), half)
        return transposed_right(wide[:, place], weights[1 + i, :, columns])

    total = part(0, mine, own_columns)
    for i in range(1, 3):
        total += part(i, mine, own_columns)
    d_hidden[...] = total
    for head in range(heads):
        for i in range(3):
            head_copy(head, i).wait_recv()
    total = part(0, 1 - mine, away_columns)
    for i in range(1, 3):
        total += part(i, 1 - mine, away_columns)
    d_hidden[...] += total
    d_heads[...] = wide[...]
    exchange.wait_send()
    for head in range(heads):
        for i in range(3):
            head_copy(head, i).wait_send()


def attend_back_fast(cube, branch, heads_in, probs, table, matrices):
    rows, width = branch.shape
    group, half = (2 * rows, width // 2)
    heads = half // 128
    vmem = pl.BlockSpec(memory_space=pltpu.VMEM)
    return pl.pallas_call(
        functools.partial(attend_back_kernel, cube, REL_LEFT, REL_RIGHT),
        out_shape=[
            jax.ShapeDtypeStruct((rows, width), jnp.float32),
            jax.ShapeDtypeStruct((rows, 3 * width), jnp.bfloat16),
            jax.ShapeDtypeStruct((128, 128), jnp.float32),
        ],
        in_specs=[vmem] * 4 + [pl.BlockSpec(memory_space=pl.ANY)] * 4,
        out_specs=[vmem] * 3,
        scratch_shapes=[
            pltpu.VMEM((4, width, width), jnp.bfloat16),
            pltpu.VMEM((group, half), jnp.bfloat16),
            pltpu.VMEM((rows, half), jnp.bfloat16),
            pltpu.VMEM((rows, 3 * width), jnp.bfloat16),
            pltpu.VMEM((heads, 3, group, 128), jnp.bfloat16),
            pltpu.SemaphoreType.DMA((4,)),
            pltpu.SemaphoreType.DMA((1,)),
            pltpu.SemaphoreType.DMA((1,)),
            pltpu.SemaphoreType.DMA((heads, 3)),
            pltpu.SemaphoreType.DMA((heads, 3)),
        ],
        compiler_params=pltpu.CompilerParams(
            collective_id=6, has_side_effects=True, vmem_limit_bytes=48 * 1024 * 1024
        ),
        name="attend_back",
    )(branch, heads_in, probs, table, *matrices)


def ffn_kernel(cube, *refs):
    hidden, before, weight_in, weight_out = refs[:4]
    after, act, swish, hidden_out = refs[4:8]
    into, outof, both, away, arrived, load, send, recv = refs[8:]
    rows, width = hidden.shape
    wide = into.shape[1]
    step = wide // 4
    own_columns, away_columns, own_rows, away_rows = halves(cube, rows, width // 2)
    loads = []
    for q in range(4):
        part = pl.ds(q * step, step)
        loads.append(
            pltpu.make_async_copy(weight_in.at[:, part], into.at[:, part], load.at[q])
        )
    loads.append(pltpu.make_async_copy(weight_out, outof, load.at[4]))
    for one in loads:
        one.start()
    both[own_rows, :] = hidden[...]
    greet(cube, [0])
    exchange = to_partner(
        cube, 0, both.at[own_rows], both.at[own_rows], send.at[0], recv.at[0]
    )
    exchange.start()

    def activate(q, rows_here):
        part = pl.ds(q * step, step)
        value = matmul(both[rows_here, :], into[:, part])
        act[rows_here, part] = value
        swish[rows_here, part] = jax.nn.silu(value).astype(jnp.bfloat16)

    for q in range(4):
        loads[q].wait()
        activate(q, own_rows)
    loads[4].wait()
    exchange.wait_recv()
    for q in range(4):
        activate(q, away_rows)
    half = width // 2
    back = []
    for q in range(2):
        part = pl.ds(q * half, half)
        away[:, part] = matmul(swish[away_rows, :], outof[:, part]).astype(jnp.bfloat16)
        back.append(
            to_partner(
                cube, 0, away.at[:, part], arrived.at[:, part], send.at[1 + q], recv.at[1 + q]
            )
        )
        back[q].start()
    hidden_out[...] = both[...]
    for q in range(2):
        part = pl.ds(q * half, half)
        after[:, part] = before[:, part] + 0.5 * matmul(swish[own_rows, :], outof[:, part])
    for q in range(2):
        part = pl.ds(q * half, half)
        back[q].wait_recv()
        after[:, part] += 0.5 * arrived[:, part].astype(jnp.float32)
    for one in [exchange] + back:
        one.wait_send()


def ffn_back_kernel(cube, *refs):
    branch, act, weight_in, weight_out = refs[:4]
    d_hidden, d_act, branch_out = refs[4:7]
    into, outof, both, away, arrived, load, send, recv = refs[7:]
    rows, width = branch.shape
    wide = into.shape[1]
    step = wide // 4
    own_columns, away_columns, own_rows, away_rows = halves(cube, rows, width // 2)
    loads = []
    for q in range(4):
        part = pl.ds(q * step, step)
        loads.append(
            pltpu.make_async_copy(weight_out.at[part], outof.at[part], load.at[q])
        )
    loads.append(pltpu.make_async_copy(weight_in, into, load.at[4]))
    for one in loads:
        one.start()
    both[own_rows, :] = branch[...]
    greet(cube, [0])
    exchange = to_partner(
        cube, 0, both.at[own_rows], both.at[own_rows], send.at[0], recv.at[0]
    )
    exchange.start()

    def deactivate(q, rows_here):
        part = pl.ds(q * step, step)
        value = transposed_right(both[rows_here, :], outof[part, :])
        d_act[rows_here, part] = (value * swish_slope(act[rows_here, part])).astype(jnp.bfloat16)

    for q in range(4):
        loads[q].wait()
        deactivate(q, own_rows)
    loads[4].wait()
    exchange.wait_recv()
    for q in range(4):
        deactivate(q, away_rows)
    half = width // 2
    back = []
    for q in range(2):
        part = pl.ds(q * half, half)
        away[:, part] = transposed_right(d_act[away_rows, :], into[part, :]).astype(jnp.bfloat16)
        back.append(
            to_partner(
                cube, 0, away.at[:, part], arrived.at[:, part], send.at[1 + q], recv.at[1 + q]
            )
        )
        back[q].start()
    branch_out[...] = both[...]
    for q in range(2):
        part = pl.ds(q * half, half)
        d_hidden[:, part] = transposed_right(d_act[own_rows, :], into[part, :])
    for q in range(2):
        part = pl.ds(q * half, half)
        back[q].wait_recv()
        d_hidden[:, part] += arrived[:, part].astype(jnp.float32)
    for one in [exchange] + back:
        one.wait_send()


def ffn_fast(cube, first, second, weight_in, weight_out, number, backward):
    rows, width = first.shape
    wide = weight_in.shape[1]
    vmem = pl.BlockSpec(memory_space=pltpu.VMEM)
    both = jax.ShapeDtypeStruct((2 * rows, width), jnp.bfloat16)
    result = jax.ShapeDtypeStruct((rows, width), jnp.float32)
    inner = jax.ShapeDtypeStruct((2 * rows, wide), jnp.bfloat16)
    if backward:
        shapes = [result, inner, both]
    else:
        shapes = [result, jax.ShapeDtypeStruct((2 * rows, wide), jnp.float32), inner, both]
    return pl.pallas_call(
        functools.partial(ffn_back_kernel if backward else ffn_kernel, cube),
        out_shape=shapes,
        in_specs=[vmem] * 2 + [pl.BlockSpec(memory_space=pl.ANY)] * 2,
        out_specs=[vmem] * len(shapes),
        scratch_shapes=[
            pltpu.VMEM(weight_in.shape, jnp.bfloat16),
            pltpu.VMEM(weight_out.shape, jnp.bfloat16),
            pltpu.VMEM((2 * rows, width), jnp.bfloat16),
            pltpu.VMEM((rows, width), jnp.bfloat16),
            pltpu.VMEM((rows, width), jnp.bfloat16),
            pltpu.SemaphoreType.DMA((5,)),
            pltpu.SemaphoreType.DMA((3,)),
            pltpu.SemaphoreType.DMA((3,)),
        ],
        compiler_params=pltpu.CompilerParams(
            collective_id=number, has_side_effects=True, vmem_limit_bytes=48 * 1024 * 1024
        ),
        name="ffn_back" if backward else "ffn",
    )(first, second, weight_in, weight_out)


def cube_of(shards, rel_table):
    batch, seq = (lax.axis_size("batch"), lax.axis_size("seq"))
    if seq != 2 or batch < 8 or batch & (batch - 1):
        return None
    if rel_table.shape[0] > 128 or rel_table.shape[1] != 128:
        return None
    if any(shard.shape[0] % 32 or shard.shape[1] % 1024 for shard in shards):
        return None
    return Cube(batch, seq)


def swish_slope(values):
    sigma = jax.nn.sigmoid(values)
    return sigma * (1.0 + values * (1.0 - sigma))


def norm_forward(values, gain, shift):
    mean = jnp.mean(values, axis=-1, keepdims=True)
    centred = values - mean
    inverse = lax.rsqrt(jnp.mean(centred * centred, axis=-1, keepdims=True) + epsilon)
    unit = centred * inverse
    return (unit * gain + shift, unit, inverse)


def norm_backward(d_out, unit, inverse, gain):
    d_unit = d_out * gain
    d_values = inverse * (
        d_unit
        - jnp.mean(d_unit, axis=-1, keepdims=True)
        - unit * jnp.mean(d_unit * unit, axis=-1, keepdims=True)
    )
    return (d_values, jnp.sum(d_out * unit, axis=0), jnp.sum(d_out, axis=0))


def ffn_forward(values, gain, shift, weight_in, weight_out, cube, number):
    normed, unit, inverse = norm_forward(values, gain, shift)
    hidden = normed.astype(jnp.bfloat16)
    if cube is not None:
        after, act, swish, hidden = ffn_fast(
            cube, hidden, values, weight_in, weight_out, number, False
        )
        return (after, (hidden, act, swish, unit, inverse))
    act = matmul(hidden, weight_in)
    swish = jax.nn.silu(act).astype(jnp.bfloat16)
    return (values + 0.5 * matmul(swish, weight_out), (hidden, act, swish, unit, inverse))


def ffn_backward(d_out, kept, gain, weight_in, weight_out, cube, number):
    hidden, act, swish, unit, inverse = kept
    d_branch = (0.5 * d_out).astype(jnp.bfloat16)
    if cube is not None:
        d_hidden, d_act, d_branch = ffn_fast(
            cube, d_branch, act, weight_in, weight_out, number, True
        )
    else:
        d_act = (transposed_right(d_branch, weight_out) * swish_slope(act)).astype(jnp.bfloat16)
        d_hidden = transposed_right(d_act, weight_in)
    d_norm, d_gain, d_shift = norm_backward(d_hidden, unit, inverse, gain)
    return (d_out + d_norm, (hidden, d_act), (swish, d_branch), d_gain, d_shift)


def segment_ids(place, ends, group):
    inside = jnp.sum((place[:, None] >= ends[None, :]).astype(jnp.int32), axis=1)
    return jnp.where((place >= 0) & (place < group), inside, -1)


def to_heads(hidden, weight, heads):
    return matmul(hidden, weight).astype(jnp.bfloat16).reshape(hidden.shape[0], heads, -1)


def spread_band(project, start, group, left, right):
    heads, rows, width = project.shape
    band = rows + width - 1
    blank = jnp.zeros_like(project[:, :, :1])
    middle = jnp.concatenate([blank, project[:, :, 1 : width - 1], blank], axis=2)
    padded = jnp.pad(middle, ((0, 0), (0, 0), (0, band + 1 - width)))
    skewed = padded.reshape(heads, rows * (band + 1))[:, : rows * band].reshape(heads, rows, band)
    canvas = jnp.zeros((heads, rows, group + left + right), jnp.float32)
    anchor = jnp.zeros((), jnp.int32)
    canvas = lax.dynamic_update_slice(canvas, skewed, (anchor, anchor, start))
    return canvas[:, :, left : left + group]


def relative_bins(grad, difference, start, width, left, right):
    heads, rows, group = grad.shape
    band = rows + width - 1
    canvas = jnp.pad(grad, ((0, 0), (0, 0), (left, right)))
    anchor = jnp.zeros((), jnp.int32)
    strip = lax.dynamic_slice(canvas, (anchor, anchor, start), (heads, rows, band))
    flat = jnp.pad(strip.reshape(heads, rows * band), ((0, 0), (0, rows)))
    inner = flat.reshape(heads, rows, band + 1)[:, :, 1 : width - 1]
    below = jnp.sum(jnp.where(difference[None] <= -left, grad, 0.0), axis=2, keepdims=True)
    above = jnp.sum(jnp.where(difference[None] >= right, grad, 0.0), axis=2, keepdims=True)
    return jnp.concatenate([below, inner, above], axis=2)


def block_scores(rows_query, keys, table, segment, start, left, right):
    rows, heads, depth = rows_query.shape
    group = keys.shape[0]
    width = table.shape[0]
    scale = 1.0 / math.sqrt(depth)
    project = jnp.einsum("qhd,rd->hqr", rows_query, table, preferred_element_type=jnp.float32)
    content = jnp.einsum("qhd,khd->hqk", rows_query, keys, preferred_element_type=jnp.float32)
    key_place = jnp.arange(group, dtype=jnp.int32)
    row_place = start + jnp.arange(rows, dtype=jnp.int32)
    difference = key_place[None, :] - row_place[:, None]
    relative = spread_band(project, start, group, left, right)
    relative = relative + jnp.where(difference[None] <= -left, project[:, :, :1], 0.0)
    relative = relative + jnp.where(difference[None] >= right, project[:, :, width - 1 :], 0.0)
    row_segment = lax.dynamic_slice_in_dim(segment, start, rows)
    same = row_segment[:, None] == segment[None, :]
    return (jnp.where(same[None], scale * (content + relative), masked_score), difference)


def attention_forward(query, keys, values, table, segment, block_rows, left, right):
    group = query.shape[0]
    starts = jnp.arange(group // block_rows, dtype=jnp.int32) * block_rows

    def one_block(carry, start):
        rows_query = lax.dynamic_slice_in_dim(query, start, block_rows, 0)
        scores, difference = block_scores(rows_query, keys, table, segment, start, left, right)
        top = jnp.max(scores, axis=2, keepdims=True)
        weights = jnp.exp(scores - top)
        total = jnp.sum(weights, axis=2, keepdims=True)
        probs = (weights / total).astype(jnp.bfloat16)
        rows_out = jnp.einsum("hqk,khd->qhd", probs, values, preferred_element_type=jnp.float32)
        return (carry, (rows_out.astype(jnp.bfloat16), (top + jnp.log(total))[:, :, 0]))

    unused, (pieces, log_total) = lax.scan(one_block, 0, starts)
    return (pieces.reshape(query.shape), log_total)


def attention_backward(
    query, keys, values, table, segment, log_total, d_context, block_rows, left, right
):
    group, heads, depth = query.shape
    width = table.shape[0]
    scale = 1.0 / math.sqrt(depth)
    starts = jnp.arange(group // block_rows, dtype=jnp.int32) * block_rows

    def one_block(carry, operands):
        d_keys, d_values, d_table = carry
        start, block_total = operands
        rows_query = lax.dynamic_slice_in_dim(query, start, block_rows, 0)
        rows_grad = lax.dynamic_slice_in_dim(d_context, start, block_rows, 0)
        scores, difference = block_scores(rows_query, keys, table, segment, start, left, right)
        probs = jnp.exp(scores - block_total[:, :, None])
        d_values = d_values + jnp.einsum(
            "hqk,qhd->khd",
            probs.astype(jnp.bfloat16),
            rows_grad,
            preferred_element_type=jnp.float32,
        )
        d_probs = jnp.einsum("qhd,khd->hqk", rows_grad, values, preferred_element_type=jnp.float32)
        weighted = jnp.sum(probs * d_probs, axis=2, keepdims=True)
        d_scores = (probs * (d_probs - weighted)).astype(jnp.bfloat16)
        bins = relative_bins(
            scale * d_scores.astype(jnp.float32), difference, start, width, left, right
        )
        bins = bins.astype(jnp.bfloat16)
        d_rows = scale * jnp.einsum(
            "hqk,khd->qhd", d_scores, keys, preferred_element_type=jnp.float32
        )
        d_rows = d_rows + jnp.einsum("hqr,rd->qhd", bins, table, preferred_element_type=jnp.float32)
        d_keys = d_keys + scale * jnp.einsum(
            "hqk,qhd->khd", d_scores, rows_query, preferred_element_type=jnp.float32
        )
        d_table = d_table + jnp.einsum(
            "hqr,qhd->rd", bins, rows_query, preferred_element_type=jnp.float32
        )
        return ((d_keys, d_values, d_table), d_rows.astype(jnp.bfloat16))

    zeros_heads = jnp.zeros(query.shape, jnp.float32)
    zeros_table = jnp.zeros(table.shape, jnp.float32)
    (d_keys, d_values, d_table), d_rows = lax.scan(
        one_block, (zeros_heads, zeros_heads, zeros_table), (starts, log_total)
    )
    return (
        d_rows.reshape(query.shape),
        d_keys.astype(jnp.bfloat16),
        d_values.astype(jnp.bfloat16),
        d_table,
    )


def on_device(
    frames,
    lengths,
    cotangent,
    ffn1_in,
    ffn1_out,
    query_w,
    key_w,
    value_w,
    out_w,
    point_in,
    point_out,
    ffn2_in,
    ffn2_out,
    depth_w,
    rel_table,
    norm_gains,
    norm_biases,
    bn_gain,
    bn_shift,
):
    seq_count = lax.axis_size("seq")
    seq_rank = lax.axis_index("seq")
    frames_here, width = frames.shape
    group = frames_here * seq_count
    block_rows = min(512, group)
    kernel_size = depth_w.shape[0]
    reach = kernel_size // 2
    ends = jnp.cumsum(lengths[0])
    last_entry = lengths.shape[1] - 1
    first = seq_rank * frames_here
    wide_place = first - reach + jnp.arange(frames_here + 2 * reach, dtype=jnp.int32)
    wide_segment = segment_ids(wide_place, ends, group)
    own_segment = wide_segment[reach : reach + frames_here]
    mask = (own_segment < last_entry).astype(jnp.float32)[:, None]
    group_segment = segment_ids(jnp.arange(group, dtype=jnp.int32), ends, group)
    shards = (
        ffn1_in,
        ffn1_out,
        query_w,
        key_w,
        value_w,
        out_w,
        point_in,
        point_out,
        ffn2_in,
        ffn2_out,
    )
    cube = cube_of(shards, rel_table)
    gathered = gather_all(shards, cube)
    start_values = frames.astype(jnp.float32)
    after_first, kept_first = ffn_forward(
        start_values, norm_gains[0], norm_biases[0], gathered[0], gathered[1], cube, 7
    )
    attn_norm, attn_unit, attn_inverse = norm_forward(after_first, norm_gains[1], norm_biases[1])
    attn_hidden = attn_norm.astype(jnp.bfloat16)
    if cube is None:
        query_heads, key_heads, value_heads = (
            lax.all_to_all(
                to_heads(attn_hidden, gathered[2], HEADS),
                "seq",
                split_axis=1,
                concat_axis=0,
                tiled=True,
            ),
            lax.all_to_all(
                to_heads(attn_hidden, gathered[3], HEADS),
                "seq",
                split_axis=1,
                concat_axis=0,
                tiled=True,
            ),
            lax.all_to_all(
                to_heads(attn_hidden, gathered[4], HEADS),
                "seq",
                split_axis=1,
                concat_axis=0,
                tiled=True,
            ),
        )
        context_heads, log_total = attention_forward(
            query_heads,
            key_heads,
            value_heads,
            rel_table,
            group_segment,
            block_rows,
            REL_LEFT,
            REL_RIGHT,
        )
        context = lax.all_to_all(context_heads, "seq", split_axis=0, concat_axis=1, tiled=True).reshape(
            frames_here, width
        )
        after_attn = after_first + matmul(context, gathered[5])
    else:
        table = jnp.pad(rel_table, ((0, 128 - rel_table.shape[0]), (0, 0)))
        same = (group_segment[:, None] == group_segment[None, :]).astype(jnp.float32)
        after_attn, context, heads_kept, probs_kept = attend_fast(
            cube, attn_hidden, after_first, same, table, gathered[2:6]
        )
    conv_norm, conv_unit, conv_inverse = norm_forward(after_attn, norm_gains[2], norm_biases[2])
    conv_hidden = conv_norm.astype(jnp.bfloat16)
    pointwise = matmul(conv_hidden, gathered[6])
    gate_half = pointwise[:, :width]
    sigma_half = jax.nn.sigmoid(pointwise[:, width:])
    gated = (gate_half * sigma_half).astype(jnp.bfloat16)
    gated_wide = padded_2(gated, (("seq", 0),), reach)
    kernel = depth_w.astype(jnp.float32)
    mixed = jnp.zeros((frames_here, width), jnp.float32)
    for offset in range(kernel_size):
        same = (wide_segment[offset : offset + frames_here] == own_segment).astype(jnp.float32)[
            :, None
        ]
        mixed = (
            mixed
            + kernel[offset] * gated_wide[offset : offset + frames_here].astype(jnp.float32) * same
        )
    total, squares, count = sum_everywhere(
        (jnp.sum(mixed * mask, axis=0), jnp.sum(mixed * mixed * mask, axis=0), jnp.sum(mask)),
        cube,
        1,
    )
    mean = total / count
    var = squares / count - mean * mean
    bn_inverse = lax.rsqrt(var + epsilon)
    centred = (mixed - mean) * bn_inverse
    bn_out = centred * bn_gain + bn_shift
    conv_swish = jax.nn.silu(bn_out).astype(jnp.bfloat16)
    after_conv = after_attn + matmul(conv_swish, gathered[7])
    after_second, kept_second = ffn_forward(
        after_conv, norm_gains[3], norm_biases[3], gathered[8], gathered[9], cube, 8
    )
    final_norm, final_unit, final_inverse = norm_forward(
        after_second, norm_gains[4], norm_biases[4]
    )
    sample_variance = var * count / (count - 1.0)
    d_final = cotangent.astype(jnp.float32) * mask
    d_second, gain_four, shift_four = norm_backward(
        d_final, final_unit, final_inverse, norm_gains[4]
    )
    d_conv_res, grad_two_in, grad_two_out, gain_three, shift_three = ffn_backward(
        d_second, kept_second, norm_gains[3], gathered[8], gathered[9], cube, 9
    )
    conv_branch = d_conv_res.astype(jnp.bfloat16)
    d_bn_out = transposed_right(conv_branch, gathered[7]) * swish_slope(bn_out)
    grad_bn_gain, grad_bn_shift = sum_everywhere(
        (jnp.sum(d_bn_out * centred * mask, axis=0), jnp.sum(d_bn_out * mask, axis=0)), cube, 2
    )
    d_mixed = (
        bn_gain * bn_inverse * (d_bn_out - mask * (grad_bn_shift + centred * grad_bn_gain) / count)
    )
    d_mixed = d_mixed.astype(jnp.bfloat16)
    d_mixed_wide = padded_2(d_mixed, (("seq", 0),), reach)
    d_mixed_value = d_mixed.astype(jnp.float32)
    d_gated = jnp.zeros((frames_here, width), jnp.float32)
    kernel_rows = []
    for offset in range(kernel_size):
        same = (wide_segment[offset : offset + frames_here] == own_segment).astype(jnp.float32)[
            :, None
        ]
        shifted_in = gated_wide[offset : offset + frames_here].astype(jnp.float32)
        kernel_rows.append(jnp.sum(d_mixed_value * shifted_in * same, axis=0))
        back = 2 * reach - offset
        same_back = (wide_segment[back : back + frames_here] == own_segment).astype(jnp.float32)[
            :, None
        ]
        d_gated = (
            d_gated
            + kernel[offset]
            * d_mixed_wide[back : back + frames_here].astype(jnp.float32)
            * same_back
        )
    d_pointwise = jnp.concatenate(
        [d_gated * sigma_half, d_gated * gate_half * sigma_half * (1.0 - sigma_half)], axis=1
    ).astype(jnp.bfloat16)
    d_conv_norm, gain_two, shift_two = norm_backward(
        transposed_right(d_pointwise, gathered[6]), conv_unit, conv_inverse, norm_gains[2]
    )
    d_attn_res = d_conv_res + d_conv_norm
    attn_branch = d_attn_res.astype(jnp.bfloat16)
    if cube is None:
        d_context = (
            transposed_right(attn_branch, gathered[5])
            .astype(jnp.bfloat16)
            .reshape(frames_here, HEADS, -1)
        )
        d_context_heads = lax.all_to_all(d_context, "seq", split_axis=1, concat_axis=0, tiled=True)
        d_query_heads, d_key_heads, d_value_heads, d_table = attention_backward(
            query_heads,
            key_heads,
            value_heads,
            rel_table,
            group_segment,
            log_total,
            d_context_heads,
            block_rows,
            REL_LEFT,
            REL_RIGHT,
        )
        d_query, d_keys, d_values = (
            lax.all_to_all(d_query_heads, "seq", split_axis=0, concat_axis=1, tiled=True),
            lax.all_to_all(d_key_heads, "seq", split_axis=0, concat_axis=1, tiled=True),
            lax.all_to_all(d_value_heads, "seq", split_axis=0, concat_axis=1, tiled=True),
        )
        d_query = d_query.reshape(frames_here, width)
        d_keys = d_keys.reshape(frames_here, width)
        d_values = d_values.reshape(frames_here, width)
        d_attn_hidden = (
            transposed_right(d_query, gathered[2])
            + transposed_right(d_keys, gathered[3])
            + transposed_right(d_values, gathered[4])
        )
        heads_in = jnp.concatenate([d_query, d_keys, d_values], axis=1)
    else:
        d_attn_hidden, heads_in, d_table = attend_back_fast(
            cube, attn_branch, heads_kept, probs_kept, table, gathered[2:6]
        )
        d_table = d_table[: rel_table.shape[0]]
    d_attn_norm, gain_one, shift_one = norm_backward(
        d_attn_hidden, attn_unit, attn_inverse, norm_gains[1]
    )
    d_first_res = d_attn_res + d_attn_norm
    d_input, grad_one_in, grad_one_out, gain_zero, shift_zero = ffn_backward(
        d_first_res, kept_first, norm_gains[0], gathered[0], gathered[1], cube, 10
    )
    gains_local = jnp.stack([gain_zero, gain_one, gain_two, gain_three, gain_four])
    shifts_local = jnp.stack([shift_zero, shift_one, shift_two, shift_three, shift_four])
    kernel_local = jnp.stack(kernel_rows)
    shards, (grad_gains, grad_biases, grad_depth, grad_rel) = gradient_shards(
        (
            (context, attn_branch),
            (conv_swish, conv_branch),
            (conv_hidden, d_pointwise),
            grad_two_out,
            grad_two_in,
            grad_one_in,
            grad_one_out,
            (attn_hidden, heads_in),
        ),
        (gains_local, shifts_local, kernel_local, d_table),
        cube,
    )
    attn_out, conv_out, conv_in, two_out, two_in, one_in, one_out, attn_in = shards
    return (
        final_norm.astype(jnp.bfloat16),
        d_input.astype(jnp.bfloat16),
        one_in,
        one_out,
        attn_in[:, :width],
        attn_in[:, width : 2 * width],
        attn_in[:, 2 * width :],
        attn_out,
        conv_in,
        conv_out,
        two_in,
        two_out,
        grad_depth,
        grad_rel,
        grad_gains,
        grad_biases,
        grad_bn_gain,
        grad_bn_shift,
        sample_variance,
    )


def solution(mesh):
    placed = (
        P(("batch", "seq"), None),
        P("batch", None),
        P(("batch", "seq"), None),
        P(("batch", "seq"), None),
        P(("batch", "seq"), None),
        P(("batch", "seq"), None),
        P(("batch", "seq"), None),
        P(("batch", "seq"), None),
        P(("batch", "seq"), None),
        P(("batch", "seq"), None),
        P(("batch", "seq"), None),
        P(("batch", "seq"), None),
        P(("batch", "seq"), None),
        P(),
        P(),
        P(),
        P(),
        P(),
        P(),
    )
    return jax.shard_map(
        on_device,
        mesh=mesh,
        in_specs=placed,
        out_specs=(
            P(("batch", "seq"), None),
            P(("batch", "seq"), None),
            P(("batch", "seq"), None),
            P(("batch", "seq"), None),
            P(("batch", "seq"), None),
            P(("batch", "seq"), None),
            P(("batch", "seq"), None),
            P(("batch", "seq"), None),
            P(("batch", "seq"), None),
            P(("batch", "seq"), None),
            P(("batch", "seq"), None),
            P(("batch", "seq"), None),
            P(),
            P(),
            P(),
            P(),
            P(),
            P(),
            P(),
        ),
        check_vma=False,
    )
```

```python
import functools
import math

import jax
import jax.numpy as jnp
from jax import lax
from jax.experimental import pallas as pl
from jax.experimental.pallas import tpu as pltpu
from jax.sharding import PartitionSpec as P

MESH = pl.DeviceIdType.MESH
AXES = ("batch", "seq")
ALL_SHARES = (3, 1, 0)
ROWS = 64
HALF_SHARES = (5, 3)
PAIR_SHARES = (2, 2)

HEADS = 8
REL_LEFT = 64
REL_RIGHT = 8


epsilon = 1e-05
masked_score = -1000000000.0


def padded_2(shard, sides, width):
    for axis, dim in sides:
        peers, length = (lax.axis_size(axis), shard.shape[dim])
        up = [(i, (i + 1) % peers) for i in range(peers - 1)]
        down = [(j, i) for i, j in up]
        last = lax.slice_in_dim(shard, length - width, length, axis=dim)
        first = lax.slice_in_dim(shard, 0, width, axis=dim)
        before = lax.ppermute(last, axis, up)
        after = lax.ppermute(first, axis, down)
        shard = jnp.concatenate([before, shard, after], axis=dim)
    return shard


def matmul(left, right):
    return jnp.dot(left, right, preferred_element_type=jnp.float32)


def transposed_left(left, right):
    return lax.dot_general(
        left, right, (((0,), (0,)), ((), ())), preferred_element_type=jnp.float32
    )


def transposed_right(left, right):
    return lax.dot_general(
        left, right, (((1,), (1,)), ((), ())), preferred_element_type=jnp.float32
    )


class Cube:
    def __init__(self, batch, seq):
        self.seq_bits, self.batch_bits = (seq.bit_length() - 1, batch.bit_length() - 1)
        self.count = self.seq_bits + self.batch_bits
        self.core = self.seq_bits
        wide = (self.batch_bits - 1) // 2
        self.x = list(range(self.seq_bits))[::-1]
        self.y = list(range(self.core + 1, self.core + 1 + wide))[::-1]
        self.z = list(range(self.core + 1 + wide, self.count))[::-1]

    def bit(self, k):
        if k < self.seq_bits:
            return lax.rem(lax.axis_index("seq") // (1 << k), 2)
        return lax.rem(lax.axis_index("batch") // (1 << (k - self.seq_bits)), 2)

    def partner(self, k):
        batch, seq = (lax.axis_index("batch"), lax.axis_index("seq"))
        step = 1 - 2 * self.bit(k)
        if k < self.seq_bits:
            return (batch, seq + step * (1 << k))
        return (batch + step * (1 << (k - self.seq_bits)), seq)


def greet(cube, bits):
    barrier = pltpu.get_barrier_semaphore()
    for k in bits:
        pl.semaphore_signal(barrier, inc=1, device_id=cube.partner(k), device_id_type=MESH)
    pl.semaphore_wait(barrier, len(bits))


def gather_kernel(cube, plans, items, *refs):
    count = len(plans)
    shards, outs = (refs[:count], refs[count : 2 * count])
    send, recv, local = refs[2 * count :]
    own = [cube.bit(k) for k in range(cube.count)]
    kept = []
    for m, (bits, paired) in enumerate(plans):
        kept.append(
            pltpu.make_async_copy(
                shards[m].at[own[0]] if paired else shards[m],
                outs[m].at[tuple(own[k] for k in bits)],
                local.at[m],
            )
        )
        kept[m].start()
    greet(cube, range(cube.count))

    def copy(number, stage):
        m, order, block = flat[number]
        bits, paired = plans[m]
        lead = tuple(slice(None) if k in order[:stage] else own[k] for k in bits)
        place = outs[m].at[lead + block]
        source = place
        if stage == 0:
            source = shards[m].at[(1 - own[0],) + block] if paired else shards[m].at[block]
        return to_partner(
            cube, order[stage], source, place, send.at[number, stage], recv.at[number, stage]
        )

    flat = [item for chunk in items for item in chunk]
    numbers, at = ([], 0)
    for chunk in items:
        numbers.append(range(at, at + len(chunk)))
        at += len(chunk)
    for number in range(len(flat)):
        copy(number, 0).start()
    for one in kept:
        one.wait()
    most = max(len(order) for _, order, _ in flat)
    for turn in range(len(items) + most):
        for stage in range(most):
            for late in (0, 1):
                chunk = turn - stage - late
                if not 0 <= chunk < len(items):
                    continue
                for number in numbers[chunk]:
                    stages = len(flat[number][1])
                    if stage >= stages or late != (stage == stages - 1):
                        continue
                    copy(number, stage).wait_recv()
                    if stage + 1 < stages:
                        copy(number, stage + 1).start()
    for number, (_, order, _) in enumerate(flat):
        for stage in range(len(order)):
            copy(number, stage).wait_send()


def row_parts(rows, shares):
    units, total, at, upto, parts = (rows // 8, sum(shares), 0, 0, [])
    for share in shares:
        upto += share
        end = (units * upto + total // 2) // total
        parts.append((at * 8, (end - at) * 8))
        at = end
    return parts


def gather_fast(shards, kinds, cube):
    core, x, y, z = ([cube.core], cube.x, cube.y, cube.z)
    every = list(range(cube.count))[::-1]
    plans, items, shapes = ([], [], [])
    for m, (shard, kind) in enumerate(zip(shards, kinds)):
        if kind == "all":
            bits, shares = (every, ALL_SHARES)
            orders = [z + y + x + core, z + x + y + core, x + y + z + core]
        else:
            bits = every if kind == "pair" else every[:-1]
            first = x if kind == "pair" else []
            orders = [first + z + y + core, first + y + z + core]
            shares = PAIR_SHARES if kind == "pair" else HALF_SHARES
        plans.append((bits, kind == "pair"))
        shapes.append((2,) * len(bits) + shard.shape[-2:])
        rows, columns = (min(ROWS, shard.shape[-2]), min(2048, shard.shape[-1]))
        for row in range(0, shard.shape[-2], rows):
            for column in range(0, shard.shape[-1], columns):
                items.append(
                    [
                        (m, order, (pl.ds(row + a, w), pl.ds(column, columns)))
                        for order, (a, w) in zip(orders, row_parts(rows, shares))
                        if w
                    ]
                )
    count, copies = (len(shards), sum(len(chunk) for chunk in items))
    outs = pl.pallas_call(
        functools.partial(gather_kernel, cube, plans, items),
        out_shape=[
            jax.ShapeDtypeStruct(shape, shard.dtype) for shape, shard in zip(shapes, shards)
        ],
        in_specs=[pl.BlockSpec(memory_space=pl.ANY)] * count,
        out_specs=[pl.BlockSpec(memory_space=pl.ANY)] * count,
        scratch_shapes=[
            pltpu.SemaphoreType.DMA((copies, cube.count)),
            pltpu.SemaphoreType.DMA((copies, cube.count)),
            pltpu.SemaphoreType.DMA((count,)),
        ],
        compiler_params=pltpu.CompilerParams(collective_id=0, has_side_effects=True),
        name="gather_weights",
    )(*shards)
    return tuple(out.reshape(-1, shard.shape[-1]) for out, shard in zip(outs, shards))


def sum_kernel(cube, value, out, held, sent, send, recv):
    bits = range(cube.count)
    greet(cube, bits)
    sent[0] = value[...]
    for k in bits:
        copy = pltpu.make_async_remote_copy(
            src_ref=sent.at[k],
            dst_ref=held.at[k],
            send_sem=send.at[k],
            recv_sem=recv.at[k],
            device_id=cube.partner(k),
            device_id_type=MESH,
        )
        copy.start()
        copy.wait()
        if k + 1 < cube.count:
            sent[k + 1] = sent[k] + held[k]
        else:
            out[...] = sent[k] + held[k]


def sum_fast(value, cube, number):
    return pl.pallas_call(
        functools.partial(sum_kernel, cube),
        out_shape=jax.ShapeDtypeStruct(value.shape, value.dtype),
        in_specs=[pl.BlockSpec(memory_space=pltpu.VMEM)],
        out_specs=pl.BlockSpec(memory_space=pltpu.VMEM),
        scratch_shapes=[
            pltpu.VMEM((cube.count,) + value.shape, value.dtype),
            pltpu.VMEM((cube.count,) + value.shape, value.dtype),
            pltpu.SemaphoreType.DMA((cube.count,)),
            pltpu.SemaphoreType.DMA((cube.count,)),
        ],
        compiler_params=pltpu.CompilerParams(collective_id=number, has_side_effects=True),
        name="sum_over_devices",
    )(value)


def sum_everywhere(values, cube, number):
    if cube is None:
        return lax.psum(values, AXES)
    return flat_unpack(sum_fast(flat_pack(values), cube, number), values)


def gradient_kernel(cube, shapes, kinds, tile, *refs):
    count = len(shapes)
    lefts, rights, refs = (refs[:count], refs[count : 2 * count], refs[2 * count :])
    value, out, crossed, value_out, refs = (refs[0], refs[1], refs[2], refs[3], refs[4:])
    near, far, whole = (refs[:count], refs[count : 2 * count], refs[2 * count : 3 * count])
    refs = refs[3 * count :]
    order = cube.y + cube.z[::-1]
    stages = len(order)
    total, sent, recv_at, refs = (refs[0], refs[1 : 1 + stages], refs[1 + stages : 1 + 2 * stages], refs[1 + 2 * stages :])
    cross, value_sent, value_held, refs = (refs[0], refs[1], refs[2], refs[3:])
    x_send, x_recv, local, c_send, c_recv, send, recv, cross_send, cross_recv, v_send, v_recv = refs
    rows, columns = tile
    number, depth = (out.shape[0], total.shape[0])
    lags = [3 + 2 * stage for stage in range(stages)]
    x, c = (cube.bit(0), cube.bit(cube.core))
    dims = sorted(order, reverse=True)
    bits = [cube.bit(k) for k in order]
    every = (slice(None),) * stages
    tokens = near[0].shape[-1] // 2
    pairs = [m for m in range(count) if kinds[m] == "pair"]
    own_lanes = pl.ds(pl.multiple_of(x * tokens, tokens), tokens)

    def spot(stage, flip):
        left = [k for k in dims if k not in order[:stage]]
        side = 1 - bits[stage] if flip else bits[stage]
        return tuple(side if k == order[stage] else slice(None) for k in left)

    def along_x(m):
        if kinds[m] != "all":
            return []
        return [
            to_partner(
                cube,
                0,
                lefts[m].at[every + (slice(None), 1 - x)],
                near[m].at[every + (slice(None), slice(None), own_lanes)],
                x_send.at[m, 0],
                x_recv.at[m, 0],
            ),
            to_partner(
                cube, 0, rights[m], whole[m].at[c, own_lanes], x_send.at[m, 1], x_recv.at[m, 1]
            ),
        ]

    def at_home(m):
        if kinds[m] != "all":
            return [
                pltpu.make_async_copy(lefts[m], near[m], local.at[m, 0]),
                pltpu.make_async_copy(rights[m], whole[m].at[c], local.at[m, 1]),
            ]
        return [
            pltpu.make_async_copy(
                lefts[m].at[every + (slice(None), x)],
                near[m].at[every + (slice(None), slice(None), own_lanes)],
                local.at[m, 0],
            ),
            pltpu.make_async_copy(rights[m], whole[m].at[c, own_lanes], local.at[m, 1]),
        ]

    def along_core(m):
        return [
            to_partner(
                cube,
                cube.core,
                near[m].at[every + (1 - c,)],
                far[m],
                c_send.at[m, 0],
                c_recv.at[m, 0],
            ),
            to_partner(
                cube, cube.core, whole[m].at[c], whole[m].at[c], c_send.at[m, 1], c_recv.at[m, 1]
            ),
        ]

    def remote(stage, chunk):
        return to_partner(
            cube,
            order[stage],
            sent[stage].at[chunk],
            recv_at[stage].at[chunk],
            send.at[stage, chunk],
            recv.at[stage, chunk],
        )

    def reduce(step):
        for stage in range(stages):
            chunk = step - lags[stage]

            @pl.when((chunk >= 0) & (chunk < number))
            def _(stage=stage, chunk=chunk):
                slot = lax.rem(chunk, depth)
                remote(stage, chunk).wait_recv()
                mine = tuple(
                    bits[order.index(k)] if k in order[: stage + 1] else slice(None) for k in dims
                )
                arrived = recv_at[stage]
                if stage + 1 == stages:
                    out[chunk] = total[(slot,) + mine] + arrived[chunk].astype(jnp.float32)
                else:
                    away, home = (spot(stage + 1, True), spot(stage + 1, False))
                    full = list(mine)
                    full[dims.index(order[stage + 1])] = 1 - bits[stage + 1]
                    sent[stage + 1][chunk] = (
                        total[(slot,) + tuple(full)]
                        + arrived[(chunk,) + away].astype(jnp.float32)
                    ).astype(jnp.bfloat16)
                    remote(stage + 1, chunk).start()
                    full[dims.index(order[stage + 1])] = bits[stage + 1]
                    total[(slot,) + tuple(full)] += arrived[(chunk,) + home].astype(jnp.float32)

    def value_copy(k):
        return to_partner(
            cube, k, value_sent.at[k], value_held.at[k], v_send.at[k], v_recv.at[k]
        )

    def value_turn(k):
        if k == 0:
            value_sent[0] = value[...]
        elif k <= cube.count:
            value_copy(k - 1).wait_recv()
            sum_here = value_sent[k - 1] + value_held[k - 1]
            if k < cube.count:
                value_sent[k] = sum_here
            else:
                value_out[...] = sum_here
        if k < cube.count:
            value_copy(k).start()

    def cross_copy(i, first):
        away = pl.ds(first + (1 - x) * 2, 2)
        return to_partner(cube, 0, out.at[away], cross.at[i], cross_send.at[i], cross_recv.at[i])

    greet(cube, range(cube.count))
    value_turn(0)
    for m in range(count):
        for copy in along_x(m) + at_home(m):
            copy.start()
    def to_core(m):
        for copy in at_home(m):
            copy.wait()
        for copy in along_x(m):
            copy.wait_recv()
        for copy in along_core(m):
            copy.start()

    first, firsts = (0, {})
    to_core(0)
    for m in range(count):
        firsts[m] = first
        if m > 0:
            value_turn(m)
        for copy in along_core(m):
            copy.wait_recv()
        if m + 1 < count:
            to_core(m + 1)
        down, across = shapes[m]

        def one(j, carry, m=m, first=first, down=down, across=across):
            chunk = first + j
            slot = lax.rem(chunk, depth)
            row = pl.ds(pl.multiple_of((j // across) * rows, rows), rows)
            column = pl.ds(pl.multiple_of(lax.rem(j, across) * columns, columns), columns)

            def half(flip):
                place = spot(0, flip)
                one_left = near[m][place + (c, row, slice(None))]
                two_left = far[m][place + (row, slice(None))]
                shape = one_left.shape[:-1] + (columns,)
                one_left = one_left.reshape(-1, 2 * tokens)
                two_left = two_left.reshape(-1, 2 * tokens)
                result = matmul(one_left, whole[m][c, :, column]) + matmul(
                    two_left, whole[m][1 - c, :, column]
                )
                return result.reshape(shape)

            sent[0][chunk] = half(True).astype(jnp.bfloat16)
            remote(0, chunk).start()
            total[(slot,) + spot(0, False)] = half(False)
            reduce(chunk)
            return carry

        lax.fori_loop(0, down * across, one, 0)
        first += down * across

    def drain(step, carry):
        reduce(step)
        return carry

    for k in range(count, cube.count + 1):
        value_turn(k)
    for i, m in enumerate(pairs):
        cross_copy(i, firsts[m]).start()
    lax.fori_loop(number, number + lags[-1] + 1, drain, 0)
    for i, m in enumerate(pairs):
        cross_copy(i, firsts[m]).wait_recv()
        crossed[i, x] = out[pl.ds(firsts[m] + x * 2, 2)]
        crossed[i, 1 - x] = cross[i]
        cross_copy(i, firsts[m]).wait_send()
    for k in range(cube.count):
        value_copy(k).wait_send()
    for m in range(count):
        for copy in along_x(m) + along_core(m):
            copy.wait_send()

    def finish(chunk, carry):
        for stage in range(stages):
            remote(stage, chunk).wait_send()
        return carry

    lax.fori_loop(0, number, finish, 0)


def gradients_fast(pairs, kinds, value, cube, rows, columns):
    order = cube.y + cube.z[::-1]
    stages, count = (len(order), len(pairs))
    lefts, rights, shapes, near, far, whole = ([], [], [], [], [], [])
    for (left, right), kind in zip(pairs, kinds):
        lead = (2,) * stages
        if kind == "all":
            block, tokens = (left.shape[1] >> cube.count, left.shape[0])
            lefts.append(left.T.reshape(lead + (2, 2, block, tokens)))
        else:
            block, tokens = (left.shape[1] >> (cube.count - 1), left.shape[0] // 2)
            lefts.append(left.T.reshape(lead + (2, block, 2 * tokens)))
        rights.append(right)
        shapes.append((block // rows, right.shape[1] // columns))
        near.append(pltpu.VMEM(lead + (2, block, 2 * tokens), jnp.bfloat16))
        far.append(pltpu.VMEM(lead + (block, 2 * tokens), jnp.bfloat16))
        whole.append(pltpu.VMEM((2, 2 * tokens, right.shape[1]), jnp.bfloat16))
    number, tile = (sum(down * across for down, across in shapes), (rows, columns))
    held = [
        pltpu.VMEM((number,) + (2,) * (stages - 1 - stage) + tile, jnp.bfloat16)
        for stage in range(stages)
    ]
    depth = 3 + 2 * (stages - 1) + 1
    paired = kinds.count("pair")
    vmem = pl.BlockSpec(memory_space=pltpu.VMEM)
    values = pltpu.VMEM((cube.count,) + value.shape, value.dtype)
    out, crossed, value = pl.pallas_call(
        functools.partial(gradient_kernel, cube, shapes, kinds, tile),
        out_shape=[
            jax.ShapeDtypeStruct((number,) + tile, jnp.float32),
            jax.ShapeDtypeStruct((paired, 2, 2) + tile, jnp.float32),
            jax.ShapeDtypeStruct(value.shape, value.dtype),
        ],
        in_specs=[pl.BlockSpec(memory_space=pl.ANY)] * (2 * count) + [vmem],
        out_specs=[vmem] * 3,
        scratch_shapes=near
        + far
        + whole
        + [pltpu.VMEM((depth,) + (2,) * stages + tile, jnp.float32)]
        + held
        + held
        + [pltpu.VMEM((paired, 2) + tile, jnp.float32), values, values]
        + [pltpu.SemaphoreType.DMA((count, 2))] * 5
        + [pltpu.SemaphoreType.DMA((stages, number))] * 2
        + [pltpu.SemaphoreType.DMA((paired,))] * 2
        + [pltpu.SemaphoreType.DMA((cube.count,))] * 2,
        compiler_params=pltpu.CompilerParams(
            collective_id=4, has_side_effects=True, vmem_limit_bytes=60 * 1024 * 1024
        ),
        name="reduce_gradients",
    )(*lefts, *rights, value)
    results, at, pair = ([], 0, 0)
    for (down, across), right, kind in zip(shapes, rights, kinds):
        if kind == "pair":
            piece = crossed[pair].reshape(2, 2, rows, columns // 128, 128)
            results.append(piece.transpose(2, 1, 3, 0, 4).reshape(rows, 4 * columns))
            pair += 1
        else:
            piece = out[at : at + down * across].reshape(down, across, rows, columns)
            results.append(piece.transpose(0, 2, 1, 3).reshape(down * rows, right.shape[1]))
        at += down * across
    return results, value


def flat_pack(values):
    flat = jnp.concatenate([value.reshape(-1) for value in values])
    size = -(-flat.shape[0] // 8192) * 8192
    return jnp.pad(flat, (0, size - flat.shape[0])).reshape(-1, 1024)


def flat_unpack(flat, values):
    flat, out, at = (flat.reshape(-1), [], 0)
    for value in values:
        out.append(flat[at : at + value.size].reshape(value.shape))
        at += value.size
    return tuple(out)


def gradient_shards(pairs, values, cube):
    if cube is None:
        results = []
        for left, right in pairs:
            whole = transposed_left(left, right)
            flat = whole.reshape(-1, 128)
            shard = lax.psum_scatter(flat, AXES, scatter_dimension=0, tiled=True)
            results.append(shard.reshape(-1, whole.shape[1]))
        return results, lax.psum(values, AXES)
    kinds = ["half", "pair", "pair", "half"] + ["all"] * 4
    results, flat = gradients_fast(pairs, kinds, flat_pack(values), cube, 32, 1024)
    return results, flat_unpack(flat, values)


def parities(shard):
    rows, columns = shard.shape
    return shard.reshape(rows, columns // 256, 2, 128).transpose(2, 0, 1, 3).reshape(2, rows, -1)


def gather_all(shards, cube):
    if cube is None:
        return tuple(lax.all_gather(shard, AXES, axis=0, tiled=True) for shard in shards)
    kinds = ("pair", "half") + ("all",) * 6 + ("pair", "half")
    shards = [parities(shard) if kind == "pair" else shard for shard, kind in zip(shards, kinds)]
    turns = (2, 6, 0, 3, 4, 8, 5, 7, 1, 9)
    outs = gather_fast([shards[m] for m in turns], [kinds[m] for m in turns], cube)
    return tuple(outs[turns.index(m)] for m in range(len(shards)))


def distance_rows(group, left, right, backwards):
    row = lax.broadcasted_iota(jnp.int32, (group, 128), 0)
    row = group - 1 - row if backwards else row
    distance = jnp.where(row >= group // 2, row - group, row)
    index = jnp.clip(distance, -left, right) + left
    hit = index == lax.broadcasted_iota(jnp.int32, (group, 128), 1)
    return jnp.where(hit, 1.0, 0.0).astype(jnp.bfloat16)


def halves(cube, rows, half):
    mine = cube.bit(0)
    return (
        pl.ds(pl.multiple_of(mine * half, half), half),
        pl.ds(pl.multiple_of((1 - mine) * half, half), half),
        pl.ds(pl.multiple_of(mine * rows, rows), rows),
        pl.ds(pl.multiple_of((1 - mine) * rows, rows), rows),
    )


def to_partner(cube, k, source, target, send, recv):
    return pltpu.make_async_remote_copy(
        src_ref=source,
        dst_ref=target,
        send_sem=send,
        recv_sem=recv,
        device_id=cube.partner(k),
        device_id_type=MESH,
    )


def attend_kernel(cube, left, right, *refs):
    hidden, before, same, table, query_w, key_w, value_w, out_w = refs[:8]
    after, context, heads_out, probs_out = refs[8:12]
    weights, heads_in, away, wide, context_away, load, send, recv, head_send, head_recv = refs[12:]
    rows, width = hidden.shape
    group, half = (2 * rows, width // 2)
    heads = half // 128
    scale = 1.0 / math.sqrt(128)
    mine = cube.bit(0)
    own_columns, away_columns, own_rows, away_rows = halves(cube, rows, half)
    loads = []
    for i, matrix in enumerate((query_w, key_w, value_w, out_w)):
        loads.append(pltpu.make_async_copy(matrix, weights.at[i], load.at[i]))
        loads[i].start()
    greet(cube, [0])

    def exchange(i):
        return to_partner(
            cube, 0, away.at[i], heads_in.at[i, own_rows], send.at[i], recv.at[i]
        )

    def context_copy(head):
        column = pl.ds(pl.multiple_of(mine * half + head * 128, 128), 128)
        return to_partner(
            cube, 0, context_away.at[head], wide.at[:, column], head_send.at[head], head_recv.at[head]
        )

    for i in range(3):
        loads[i].wait()
        away[i] = matmul(hidden[...], weights[i, :, away_columns]).astype(jnp.bfloat16)
        exchange(i).start()
    for i in range(3):
        heads_in[i, own_rows, :] = matmul(hidden[...], weights[i, :, own_columns]).astype(
            jnp.bfloat16
        )
    spread = matmul(distance_rows(group, left, right, False), table[...]).astype(jnp.bfloat16)
    loads[3].wait()
    for i in range(3):
        exchange(i).wait_recv()

    def one_head(head, carry):
        column = pl.ds(pl.multiple_of(head * 128, 128), 128)
        place = pl.ds(pl.multiple_of(mine * half + head * 128, 128), 128)
        query, keys, values = (heads_in[i, :, column] for i in range(3))
        relative = pltpu.roll(transposed_right(query, spread), 0, 1, stride=1, stride_axis=0)
        scores = scale * (transposed_right(query, keys) + relative)
        scores = jnp.where(same[...] > 0, scores, masked_score)
        weight = jnp.exp(scores - jnp.max(scores, axis=1, keepdims=True))
        probs_out[head] = weight / jnp.sum(weight, axis=1, keepdims=True)
        there = probs_out[head, away_rows, :].astype(jnp.bfloat16)
        context_away[head] = matmul(there, values).astype(jnp.bfloat16)
        context_copy(head).start()
        here = probs_out[head, own_rows, :].astype(jnp.bfloat16)
        wide[:, place] = matmul(here, values).astype(jnp.bfloat16)
        return carry

    lax.fori_loop(0, heads, one_head, 0)
    heads_out[...] = heads_in[...]
    after[...] = before[...] + matmul(wide[:, own_columns], weights[3, own_columns, :])
    for head in range(heads):
        context_copy(head).wait_recv()
    after[...] += matmul(wide[:, away_columns], weights[3, away_columns, :])
    context[...] = wide[...]
    for i in range(3):
        exchange(i).wait_send()
    for head in range(heads):
        context_copy(head).wait_send()


def attend_fast(cube, hidden, before, same, table, matrices):
    rows, width = hidden.shape
    group, half = (2 * rows, width // 2)
    heads = half // 128
    vmem = pl.BlockSpec(memory_space=pltpu.VMEM)
    return pl.pallas_call(
        functools.partial(attend_kernel, cube, REL_LEFT, REL_RIGHT),
        out_shape=[
            jax.ShapeDtypeStruct((rows, width), jnp.float32),
            jax.ShapeDtypeStruct((rows, width), jnp.bfloat16),
            jax.ShapeDtypeStruct((3, group, half), jnp.bfloat16),
            jax.ShapeDtypeStruct((heads, group, group), jnp.float32),
        ],
        in_specs=[vmem] * 4 + [pl.BlockSpec(memory_space=pl.ANY)] * 4,
        out_specs=[vmem] * 4,
        scratch_shapes=[
            pltpu.VMEM((4, width, width), jnp.bfloat16),
            pltpu.VMEM((3, group, half), jnp.bfloat16),
            pltpu.VMEM((3, rows, half), jnp.bfloat16),
            pltpu.VMEM((rows, width), jnp.bfloat16),
            pltpu.VMEM((heads, rows, 128), jnp.bfloat16),
            pltpu.SemaphoreType.DMA((4,)),
            pltpu.SemaphoreType.DMA((3,)),
            pltpu.SemaphoreType.DMA((3,)),
            pltpu.SemaphoreType.DMA((heads,)),
            pltpu.SemaphoreType.DMA((heads,)),
        ],
        compiler_params=pltpu.CompilerParams(
            collective_id=5, has_side_effects=True, vmem_limit_bytes=48 * 1024 * 1024
        ),
        name="attend",
    )(hidden, before, same, table, *matrices)


def attend_back_kernel(cube, left, right, *refs):
    branch, heads_in, probs_in, table, query_w, key_w, value_w, out_w = refs[:8]
    d_hidden, d_heads, d_table = refs[8:11]
    weights, d_context, d_context_away, wide, away, load, send, recv, head_send, head_recv = refs[
        11:
    ]
    rows, width = branch.shape
    group, half = (2 * rows, width // 2)
    heads = half // 128
    scale = 1.0 / math.sqrt(128)
    mine = cube.bit(0)
    own_columns, away_columns, own_rows, away_rows = halves(cube, rows, half)
    loads = []
    for i, matrix in enumerate((out_w, query_w, key_w, value_w)):
        loads.append(pltpu.make_async_copy(matrix, weights.at[i], load.at[i]))
        loads[i].start()
    greet(cube, [0])
    loads[0].wait()
    exchange = to_partner(
        cube, 0, d_context_away, d_context.at[own_rows], send.at[0], recv.at[0]
    )
    d_context_away[...] = transposed_right(branch[...], weights[0, away_columns, :]).astype(
        jnp.bfloat16
    )
    exchange.start()
    d_context[own_rows, :] = transposed_right(branch[...], weights[0, own_columns, :]).astype(
        jnp.bfloat16
    )
    spread = distance_rows(group, left, right, True)
    down = lax.broadcasted_iota(jnp.int32, (group, group), 0)
    across = lax.broadcasted_iota(jnp.int32, (group, group), 1)
    mirror = jnp.where(down + across == group - 1, 1.0, 0.0).astype(jnp.bfloat16)
    d_table[...] = jnp.zeros_like(d_table)
    exchange.wait_recv()

    def head_copy(head, i):
        column = pl.ds(pl.multiple_of(i * width + mine * half + head * 128, 128), 128)
        return to_partner(
            cube,
            0,
            away.at[head, i, away_rows],
            wide.at[:, column],
            head_send.at[head, i],
            head_recv.at[head, i],
        )

    def one_head(head, carry):
        column = pl.ds(pl.multiple_of(head * 128, 128), 128)
        query, keys, values = (heads_in[i, :, column] for i in range(3))
        d_rows = d_context[:, column]
        probs = probs_in[head]
        d_probs = transposed_right(d_rows, values)
        weighted = jnp.sum(probs * d_probs, axis=1, keepdims=True)
        d_scores = (probs * (d_probs - weighted)).astype(jnp.bfloat16)
        away[head, 2] = transposed_left(probs.astype(jnp.bfloat16), d_rows).astype(jnp.bfloat16)
        head_copy(head, 2).start()
        away[head, 1] = (scale * transposed_left(d_scores, query)).astype(jnp.bfloat16)
        head_copy(head, 1).start()
        turned = pltpu.roll(matmul(d_scores, mirror), 0, 1, stride=1, stride_axis=0)
        bins = (scale * matmul(turned.astype(jnp.bfloat16), spread)).astype(jnp.bfloat16)
        away[head, 0] = (scale * matmul(d_scores, keys) + matmul(bins, table[...])).astype(
            jnp.bfloat16
        )
        head_copy(head, 0).start()
        d_table[...] += transposed_left(bins, query)
        for i in range(3):
            place = pl.ds(pl.multiple_of(i * width + mine * half + head * 128, 128), 128)
            wide[:, place] = away[head, i, own_rows, :]
        return carry

    lax.fori_loop(0, heads, one_head, 0)
    for i in range(3):
        loads[1 + i].wait()

    def part(i, offset, columns):
        place = pl.ds(pl.multiple_of(i * width + offset * half, half), half)
        return transposed_right(wide[:, place], weights[1 + i, :, columns])

    total = part(0, mine, own_columns)
    for i in range(1, 3):
        total += part(i, mine, own_columns)
    d_hidden[...] = total
    for head in range(heads):
        for i in range(3):
            head_copy(head, i).wait_recv()
    total = part(0, 1 - mine, away_columns)
    for i in range(1, 3):
        total += part(i, 1 - mine, away_columns)
    d_hidden[...] += total
    d_heads[...] = wide[...]
    exchange.wait_send()
    for head in range(heads):
        for i in range(3):
            head_copy(head, i).wait_send()


def attend_back_fast(cube, branch, heads_in, probs, table, matrices):
    rows, width = branch.shape
    group, half = (2 * rows, width // 2)
    heads = half // 128
    vmem = pl.BlockSpec(memory_space=pltpu.VMEM)
    return pl.pallas_call(
        functools.partial(attend_back_kernel, cube, REL_LEFT, REL_RIGHT),
        out_shape=[
            jax.ShapeDtypeStruct((rows, width), jnp.float32),
            jax.ShapeDtypeStruct((rows, 3 * width), jnp.bfloat16),
            jax.ShapeDtypeStruct((128, 128), jnp.float32),
        ],
        in_specs=[vmem] * 4 + [pl.BlockSpec(memory_space=pl.ANY)] * 4,
        out_specs=[vmem] * 3,
        scratch_shapes=[
            pltpu.VMEM((4, width, width), jnp.bfloat16),
            pltpu.VMEM((group, half), jnp.bfloat16),
            pltpu.VMEM((rows, half), jnp.bfloat16),
            pltpu.VMEM((rows, 3 * width), jnp.bfloat16),
            pltpu.VMEM((heads, 3, group, 128), jnp.bfloat16),
            pltpu.SemaphoreType.DMA((4,)),
            pltpu.SemaphoreType.DMA((1,)),
            pltpu.SemaphoreType.DMA((1,)),
            pltpu.SemaphoreType.DMA((heads, 3)),
            pltpu.SemaphoreType.DMA((heads, 3)),
        ],
        compiler_params=pltpu.CompilerParams(
            collective_id=6, has_side_effects=True, vmem_limit_bytes=48 * 1024 * 1024
        ),
        name="attend_back",
    )(branch, heads_in, probs, table, *matrices)


def ffn_kernel(cube, *refs):
    hidden, before, weight_in, weight_out = refs[:4]
    after, act, swish, hidden_out = refs[4:8]
    into, outof, both, away, arrived, load, send, recv = refs[8:]
    rows, width = hidden.shape
    wide = into.shape[1]
    step = wide // 4
    own_columns, away_columns, own_rows, away_rows = halves(cube, rows, width // 2)
    loads = []
    for q in range(4):
        part = pl.ds(q * step, step)
        loads.append(
            pltpu.make_async_copy(weight_in.at[:, part], into.at[:, part], load.at[q])
        )
    loads.append(pltpu.make_async_copy(weight_out, outof, load.at[4]))
    for one in loads:
        one.start()
    both[own_rows, :] = hidden[...]
    greet(cube, [0])
    exchange = to_partner(
        cube, 0, both.at[own_rows], both.at[own_rows], send.at[0], recv.at[0]
    )
    exchange.start()

    def activate(q, rows_here):
        part = pl.ds(q * step, step)
        value = matmul(both[rows_here, :], into[:, part])
        act[rows_here, part] = value
        swish[rows_here, part] = jax.nn.silu(value).astype(jnp.bfloat16)

    for q in range(4):
        loads[q].wait()
        activate(q, own_rows)
    loads[4].wait()
    exchange.wait_recv()
    for q in range(4):
        activate(q, away_rows)
    half = width // 2
    back = []
    for q in range(2):
        part = pl.ds(q * half, half)
        away[:, part] = matmul(swish[away_rows, :], outof[:, part]).astype(jnp.bfloat16)
        back.append(
            to_partner(
                cube, 0, away.at[:, part], arrived.at[:, part], send.at[1 + q], recv.at[1 + q]
            )
        )
        back[q].start()
    hidden_out[...] = both[...]
    for q in range(2):
        part = pl.ds(q * half, half)
        after[:, part] = before[:, part] + 0.5 * matmul(swish[own_rows, :], outof[:, part])
    for q in range(2):
        part = pl.ds(q * half, half)
        back[q].wait_recv()
        after[:, part] += 0.5 * arrived[:, part].astype(jnp.float32)
    for one in [exchange] + back:
        one.wait_send()


def ffn_back_kernel(cube, *refs):
    branch, act, weight_in, weight_out = refs[:4]
    d_hidden, d_act, branch_out = refs[4:7]
    into, outof, both, away, arrived, load, send, recv = refs[7:]
    rows, width = branch.shape
    wide = into.shape[1]
    step = wide // 4
    own_columns, away_columns, own_rows, away_rows = halves(cube, rows, width // 2)
    loads = []
    for q in range(4):
        part = pl.ds(q * step, step)
        loads.append(
            pltpu.make_async_copy(weight_out.at[part], outof.at[part], load.at[q])
        )
    loads.append(pltpu.make_async_copy(weight_in, into, load.at[4]))
    for one in loads:
        one.start()
    both[own_rows, :] = branch[...]
    greet(cube, [0])
    exchange = to_partner(
        cube, 0, both.at[own_rows], both.at[own_rows], send.at[0], recv.at[0]
    )
    exchange.start()

    def deactivate(q, rows_here):
        part = pl.ds(q * step, step)
        value = transposed_right(both[rows_here, :], outof[part, :])
        d_act[rows_here, part] = (value * swish_slope(act[rows_here, part])).astype(jnp.bfloat16)

    for q in range(4):
        loads[q].wait()
        deactivate(q, own_rows)
    loads[4].wait()
    exchange.wait_recv()
    for q in range(4):
        deactivate(q, away_rows)
    half = width // 2
    back = []
    for q in range(2):
        part = pl.ds(q * half, half)
        away[:, part] = transposed_right(d_act[away_rows, :], into[part, :]).astype(jnp.bfloat16)
        back.append(
            to_partner(
                cube, 0, away.at[:, part], arrived.at[:, part], send.at[1 + q], recv.at[1 + q]
            )
        )
        back[q].start()
    branch_out[...] = both[...]
    for q in range(2):
        part = pl.ds(q * half, half)
        d_hidden[:, part] = transposed_right(d_act[own_rows, :], into[part, :])
    for q in range(2):
        part = pl.ds(q * half, half)
        back[q].wait_recv()
        d_hidden[:, part] += arrived[:, part].astype(jnp.float32)
    for one in [exchange] + back:
        one.wait_send()


def ffn_fast(cube, first, second, weight_in, weight_out, number, backward):
    rows, width = first.shape
    wide = weight_in.shape[1]
    vmem = pl.BlockSpec(memory_space=pltpu.VMEM)
    both = jax.ShapeDtypeStruct((2 * rows, width), jnp.bfloat16)
    result = jax.ShapeDtypeStruct((rows, width), jnp.float32)
    inner = jax.ShapeDtypeStruct((2 * rows, wide), jnp.bfloat16)
    if backward:
        shapes = [result, inner, both]
    else:
        shapes = [result, jax.ShapeDtypeStruct((2 * rows, wide), jnp.float32), inner, both]
    return pl.pallas_call(
        functools.partial(ffn_back_kernel if backward else ffn_kernel, cube),
        out_shape=shapes,
        in_specs=[vmem] * 2 + [pl.BlockSpec(memory_space=pl.ANY)] * 2,
        out_specs=[vmem] * len(shapes),
        scratch_shapes=[
            pltpu.VMEM(weight_in.shape, jnp.bfloat16),
            pltpu.VMEM(weight_out.shape, jnp.bfloat16),
            pltpu.VMEM((2 * rows, width), jnp.bfloat16),
            pltpu.VMEM((rows, width), jnp.bfloat16),
            pltpu.VMEM((rows, width), jnp.bfloat16),
            pltpu.SemaphoreType.DMA((5,)),
            pltpu.SemaphoreType.DMA((3,)),
            pltpu.SemaphoreType.DMA((3,)),
        ],
        compiler_params=pltpu.CompilerParams(
            collective_id=number, has_side_effects=True, vmem_limit_bytes=48 * 1024 * 1024
        ),
        name="ffn_back" if backward else "ffn",
    )(first, second, weight_in, weight_out)


def cube_of(shards, rel_table):
    batch, seq = (lax.axis_size("batch"), lax.axis_size("seq"))
    if seq != 2 or batch < 8 or batch & (batch - 1):
        return None
    if rel_table.shape[0] > 128 or rel_table.shape[1] != 128:
        return None
    if any(shard.shape[0] % 32 or shard.shape[1] % 1024 for shard in shards):
        return None
    return Cube(batch, seq)


def swish_slope(values):
    sigma = jax.nn.sigmoid(values)
    return sigma * (1.0 + values * (1.0 - sigma))


def norm_forward(values, gain, shift):
    mean = jnp.mean(values, axis=-1, keepdims=True)
    centred = values - mean
    inverse = lax.rsqrt(jnp.mean(centred * centred, axis=-1, keepdims=True) + epsilon)
    unit = centred * inverse
    return (unit * gain + shift, unit, inverse)


def norm_backward(d_out, unit, inverse, gain):
    d_unit = d_out * gain
    d_values = inverse * (
        d_unit
        - jnp.mean(d_unit, axis=-1, keepdims=True)
        - unit * jnp.mean(d_unit * unit, axis=-1, keepdims=True)
    )
    return (d_values, jnp.sum(d_out * unit, axis=0), jnp.sum(d_out, axis=0))


def ffn_forward(values, gain, shift, weight_in, weight_out, cube, number):
    normed, unit, inverse = norm_forward(values, gain, shift)
    hidden = normed.astype(jnp.bfloat16)
    if cube is not None:
        after, act, swish, hidden = ffn_fast(
            cube, hidden, values, weight_in, weight_out, number, False
        )
        return (after, (hidden, act, swish, unit, inverse))
    act = matmul(hidden, weight_in)
    swish = jax.nn.silu(act).astype(jnp.bfloat16)
    return (values + 0.5 * matmul(swish, weight_out), (hidden, act, swish, unit, inverse))


def ffn_backward(d_out, kept, gain, weight_in, weight_out, cube, number):
    hidden, act, swish, unit, inverse = kept
    d_branch = (0.5 * d_out).astype(jnp.bfloat16)
    if cube is not None:
        d_hidden, d_act, d_branch = ffn_fast(
            cube, d_branch, act, weight_in, weight_out, number, True
        )
    else:
        d_act = (transposed_right(d_branch, weight_out) * swish_slope(act)).astype(jnp.bfloat16)
        d_hidden = transposed_right(d_act, weight_in)
    d_norm, d_gain, d_shift = norm_backward(d_hidden, unit, inverse, gain)
    return (d_out + d_norm, (hidden, d_act), (swish, d_branch), d_gain, d_shift)


def segment_ids(place, ends, group):
    inside = jnp.sum((place[:, None] >= ends[None, :]).astype(jnp.int32), axis=1)
    return jnp.where((place >= 0) & (place < group), inside, -1)


def to_heads(hidden, weight, heads):
    return matmul(hidden, weight).astype(jnp.bfloat16).reshape(hidden.shape[0], heads, -1)


def spread_band(project, start, group, left, right):
    heads, rows, width = project.shape
    band = rows + width - 1
    blank = jnp.zeros_like(project[:, :, :1])
    middle = jnp.concatenate([blank, project[:, :, 1 : width - 1], blank], axis=2)
    padded = jnp.pad(middle, ((0, 0), (0, 0), (0, band + 1 - width)))
    skewed = padded.reshape(heads, rows * (band + 1))[:, : rows * band].reshape(heads, rows, band)
    canvas = jnp.zeros((heads, rows, group + left + right), jnp.float32)
    anchor = jnp.zeros((), jnp.int32)
    canvas = lax.dynamic_update_slice(canvas, skewed, (anchor, anchor, start))
    return canvas[:, :, left : left + group]


def relative_bins(grad, difference, start, width, left, right):
    heads, rows, group = grad.shape
    band = rows + width - 1
    canvas = jnp.pad(grad, ((0, 0), (0, 0), (left, right)))
    anchor = jnp.zeros((), jnp.int32)
    strip = lax.dynamic_slice(canvas, (anchor, anchor, start), (heads, rows, band))
    flat = jnp.pad(strip.reshape(heads, rows * band), ((0, 0), (0, rows)))
    inner = flat.reshape(heads, rows, band + 1)[:, :, 1 : width - 1]
    below = jnp.sum(jnp.where(difference[None] <= -left, grad, 0.0), axis=2, keepdims=True)
    above = jnp.sum(jnp.where(difference[None] >= right, grad, 0.0), axis=2, keepdims=True)
    return jnp.concatenate([below, inner, above], axis=2)


def block_scores(rows_query, keys, table, segment, start, left, right):
    rows, heads, depth = rows_query.shape
    group = keys.shape[0]
    width = table.shape[0]
    scale = 1.0 / math.sqrt(depth)
    project = jnp.einsum("qhd,rd->hqr", rows_query, table, preferred_element_type=jnp.float32)
    content = jnp.einsum("qhd,khd->hqk", rows_query, keys, preferred_element_type=jnp.float32)
    key_place = jnp.arange(group, dtype=jnp.int32)
    row_place = start + jnp.arange(rows, dtype=jnp.int32)
    difference = key_place[None, :] - row_place[:, None]
    relative = spread_band(project, start, group, left, right)
    relative = relative + jnp.where(difference[None] <= -left, project[:, :, :1], 0.0)
    relative = relative + jnp.where(difference[None] >= right, project[:, :, width - 1 :], 0.0)
    row_segment = lax.dynamic_slice_in_dim(segment, start, rows)
    same = row_segment[:, None] == segment[None, :]
    return (jnp.where(same[None], scale * (content + relative), masked_score), difference)


def attention_forward(query, keys, values, table, segment, block_rows, left, right):
    group = query.shape[0]
    starts = jnp.arange(group // block_rows, dtype=jnp.int32) * block_rows

    def one_block(carry, start):
        rows_query = lax.dynamic_slice_in_dim(query, start, block_rows, 0)
        scores, difference = block_scores(rows_query, keys, table, segment, start, left, right)
        top = jnp.max(scores, axis=2, keepdims=True)
        weights = jnp.exp(scores - top)
        total = jnp.sum(weights, axis=2, keepdims=True)
        probs = (weights / total).astype(jnp.bfloat16)
        rows_out = jnp.einsum("hqk,khd->qhd", probs, values, preferred_element_type=jnp.float32)
        return (carry, (rows_out.astype(jnp.bfloat16), (top + jnp.log(total))[:, :, 0]))

    unused, (pieces, log_total) = lax.scan(one_block, 0, starts)
    return (pieces.reshape(query.shape), log_total)


def attention_backward(
    query, keys, values, table, segment, log_total, d_context, block_rows, left, right
):
    group, heads, depth = query.shape
    width = table.shape[0]
    scale = 1.0 / math.sqrt(depth)
    starts = jnp.arange(group // block_rows, dtype=jnp.int32) * block_rows

    def one_block(carry, operands):
        d_keys, d_values, d_table = carry
        start, block_total = operands
        rows_query = lax.dynamic_slice_in_dim(query, start, block_rows, 0)
        rows_grad = lax.dynamic_slice_in_dim(d_context, start, block_rows, 0)
        scores, difference = block_scores(rows_query, keys, table, segment, start, left, right)
        probs = jnp.exp(scores - block_total[:, :, None])
        d_values = d_values + jnp.einsum(
            "hqk,qhd->khd",
            probs.astype(jnp.bfloat16),
            rows_grad,
            preferred_element_type=jnp.float32,
        )
        d_probs = jnp.einsum("qhd,khd->hqk", rows_grad, values, preferred_element_type=jnp.float32)
        weighted = jnp.sum(probs * d_probs, axis=2, keepdims=True)
        d_scores = (probs * (d_probs - weighted)).astype(jnp.bfloat16)
        bins = relative_bins(
            scale * d_scores.astype(jnp.float32), difference, start, width, left, right
        )
        bins = bins.astype(jnp.bfloat16)
        d_rows = scale * jnp.einsum(
            "hqk,khd->qhd", d_scores, keys, preferred_element_type=jnp.float32
        )
        d_rows = d_rows + jnp.einsum("hqr,rd->qhd", bins, table, preferred_element_type=jnp.float32)
        d_keys = d_keys + scale * jnp.einsum(
            "hqk,qhd->khd", d_scores, rows_query, preferred_element_type=jnp.float32
        )
        d_table = d_table + jnp.einsum(
            "hqr,qhd->rd", bins, rows_query, preferred_element_type=jnp.float32
        )
        return ((d_keys, d_values, d_table), d_rows.astype(jnp.bfloat16))

    zeros_heads = jnp.zeros(query.shape, jnp.float32)
    zeros_table = jnp.zeros(table.shape, jnp.float32)
    (d_keys, d_values, d_table), d_rows = lax.scan(
        one_block, (zeros_heads, zeros_heads, zeros_table), (starts, log_total)
    )
    return (
        d_rows.reshape(query.shape),
        d_keys.astype(jnp.bfloat16),
        d_values.astype(jnp.bfloat16),
        d_table,
    )


def on_device(
    frames,
    lengths,
    cotangent,
    ffn1_in,
    ffn1_out,
    query_w,
    key_w,
    value_w,
    out_w,
    point_in,
    point_out,
    ffn2_in,
    ffn2_out,
    depth_w,
    rel_table,
    norm_gains,
    norm_biases,
    bn_gain,
    bn_shift,
):
    seq_count = lax.axis_size("seq")
    seq_rank = lax.axis_index("seq")
    frames_here, width = frames.shape
    group = frames_here * seq_count
    block_rows = min(512, group)
    kernel_size = depth_w.shape[0]
    reach = kernel_size // 2
    ends = jnp.cumsum(lengths[0])
    last_entry = lengths.shape[1] - 1
    first = seq_rank * frames_here
    wide_place = first - reach + jnp.arange(frames_here + 2 * reach, dtype=jnp.int32)
    wide_segment = segment_ids(wide_place, ends, group)
    own_segment = wide_segment[reach : reach + frames_here]
    mask = (own_segment < last_entry).astype(jnp.float32)[:, None]
    group_segment = segment_ids(jnp.arange(group, dtype=jnp.int32), ends, group)
    shards = (
        ffn1_in,
        ffn1_out,
        query_w,
        key_w,
        value_w,
        out_w,
        point_in,
        point_out,
        ffn2_in,
        ffn2_out,
    )
    cube = cube_of(shards, rel_table)
    gathered = gather_all(shards, cube)
    start_values = frames.astype(jnp.float32)
    after_first, kept_first = ffn_forward(
        start_values, norm_gains[0], norm_biases[0], gathered[0], gathered[1], cube, 7
    )
    attn_norm, attn_unit, attn_inverse = norm_forward(after_first, norm_gains[1], norm_biases[1])
    attn_hidden = attn_norm.astype(jnp.bfloat16)
    if cube is None:
        query_heads, key_heads, value_heads = (
            lax.all_to_all(
                to_heads(attn_hidden, gathered[2], HEADS),
                "seq",
                split_axis=1,
                concat_axis=0,
                tiled=True,
            ),
            lax.all_to_all(
                to_heads(attn_hidden, gathered[3], HEADS),
                "seq",
                split_axis=1,
                concat_axis=0,
                tiled=True,
            ),
            lax.all_to_all(
                to_heads(attn_hidden, gathered[4], HEADS),
                "seq",
                split_axis=1,
                concat_axis=0,
                tiled=True,
            ),
        )
        context_heads, log_total = attention_forward(
            query_heads,
            key_heads,
            value_heads,
            rel_table,
            group_segment,
            block_rows,
            REL_LEFT,
            REL_RIGHT,
        )
        context = lax.all_to_all(context_heads, "seq", split_axis=0, concat_axis=1, tiled=True).reshape(
            frames_here, width
        )
        after_attn = after_first + matmul(context, gathered[5])
    else:
        table = jnp.pad(rel_table, ((0, 128 - rel_table.shape[0]), (0, 0)))
        same = (group_segment[:, None] == group_segment[None, :]).astype(jnp.float32)
        after_attn, context, heads_kept, probs_kept = attend_fast(
            cube, attn_hidden, after_first, same, table, gathered[2:6]
        )
    conv_norm, conv_unit, conv_inverse = norm_forward(after_attn, norm_gains[2], norm_biases[2])
    conv_hidden = conv_norm.astype(jnp.bfloat16)
    pointwise = matmul(conv_hidden, gathered[6])
    gate_half = pointwise[:, :width]
    sigma_half = jax.nn.sigmoid(pointwise[:, width:])
    gated = (gate_half * sigma_half).astype(jnp.bfloat16)
    gated_wide = padded_2(gated, (("seq", 0),), reach)
    kernel = depth_w.astype(jnp.float32)
    mixed = jnp.zeros((frames_here, width), jnp.float32)
    for offset in range(kernel_size):
        same = (wide_segment[offset : offset + frames_here] == own_segment).astype(jnp.float32)[
            :, None
        ]
        mixed = (
            mixed
            + kernel[offset] * gated_wide[offset : offset + frames_here].astype(jnp.float32) * same
        )
    total, squares, count = sum_everywhere(
        (jnp.sum(mixed * mask, axis=0), jnp.sum(mixed * mixed * mask, axis=0), jnp.sum(mask)),
        cube,
        1,
    )
    mean = total / count
    var = squares / count - mean * mean
    bn_inverse = lax.rsqrt(var + epsilon)
    centred = (mixed - mean) * bn_inverse
    bn_out = centred * bn_gain + bn_shift
    conv_swish = jax.nn.silu(bn_out).astype(jnp.bfloat16)
    after_conv = after_attn + matmul(conv_swish, gathered[7])
    after_second, kept_second = ffn_forward(
        after_conv, norm_gains[3], norm_biases[3], gathered[8], gathered[9], cube, 8
    )
    final_norm, final_unit, final_inverse = norm_forward(
        after_second, norm_gains[4], norm_biases[4]
    )
    sample_variance = var * count / (count - 1.0)
    d_final = cotangent.astype(jnp.float32) * mask
    d_second, gain_four, shift_four = norm_backward(
        d_final, final_unit, final_inverse, norm_gains[4]
    )
    d_conv_res, grad_two_in, grad_two_out, gain_three, shift_three = ffn_backward(
        d_second, kept_second, norm_gains[3], gathered[8], gathered[9], cube, 9
    )
    conv_branch = d_conv_res.astype(jnp.bfloat16)
    d_bn_out = transposed_right(conv_branch, gathered[7]) * swish_slope(bn_out)
    grad_bn_gain, grad_bn_shift = sum_everywhere(
        (jnp.sum(d_bn_out * centred * mask, axis=0), jnp.sum(d_bn_out * mask, axis=0)), cube, 2
    )
    d_mixed = (
        bn_gain * bn_inverse * (d_bn_out - mask * (grad_bn_shift + centred * grad_bn_gain) / count)
    )
    d_mixed = d_mixed.astype(jnp.bfloat16)
    d_mixed_wide = padded_2(d_mixed, (("seq", 0),), reach)
    d_mixed_value = d_mixed.astype(jnp.float32)
    d_gated = jnp.zeros((frames_here, width), jnp.float32)
    kernel_rows = []
    for offset in range(kernel_size):
        same = (wide_segment[offset : offset + frames_here] == own_segment).astype(jnp.float32)[
            :, None
        ]
        shifted_in = gated_wide[offset : offset + frames_here].astype(jnp.float32)
        kernel_rows.append(jnp.sum(d_mixed_value * shifted_in * same, axis=0))
        back = 2 * reach - offset
        same_back = (wide_segment[back : back + frames_here] == own_segment).astype(jnp.float32)[
            :, None
        ]
        d_gated = (
            d_gated
            + kernel[offset]
            * d_mixed_wide[back : back + frames_here].astype(jnp.float32)
            * same_back
        )
    d_pointwise = jnp.concatenate(
        [d_gated * sigma_half, d_gated * gate_half * sigma_half * (1.0 - sigma_half)], axis=1
    ).astype(jnp.bfloat16)
    d_conv_norm, gain_two, shift_two = norm_backward(
        transposed_right(d_pointwise, gathered[6]), conv_unit, conv_inverse, norm_gains[2]
    )
    d_attn_res = d_conv_res + d_conv_norm
    attn_branch = d_attn_res.astype(jnp.bfloat16)
    if cube is None:
        d_context = (
            transposed_right(attn_branch, gathered[5])
            .astype(jnp.bfloat16)
            .reshape(frames_here, HEADS, -1)
        )
        d_context_heads = lax.all_to_all(d_context, "seq", split_axis=1, concat_axis=0, tiled=True)
        d_query_heads, d_key_heads, d_value_heads, d_table = attention_backward(
            query_heads,
            key_heads,
            value_heads,
            rel_table,
            group_segment,
            log_total,
            d_context_heads,
            block_rows,
            REL_LEFT,
            REL_RIGHT,
        )
        d_query, d_keys, d_values = (
            lax.all_to_all(d_query_heads, "seq", split_axis=0, concat_axis=1, tiled=True),
            lax.all_to_all(d_key_heads, "seq", split_axis=0, concat_axis=1, tiled=True),
            lax.all_to_all(d_value_heads, "seq", split_axis=0, concat_axis=1, tiled=True),
        )
        d_query = d_query.reshape(frames_here, width)
        d_keys = d_keys.reshape(frames_here, width)
        d_values = d_values.reshape(frames_here, width)
        d_attn_hidden = (
            transposed_right(d_query, gathered[2])
            + transposed_right(d_keys, gathered[3])
            + transposed_right(d_values, gathered[4])
        )
        heads_in = jnp.concatenate([d_query, d_keys, d_values], axis=1)
    else:
        d_attn_hidden, heads_in, d_table = attend_back_fast(
            cube, attn_branch, heads_kept, probs_kept, table, gathered[2:6]
        )
        d_table = d_table[: rel_table.shape[0]]
    d_attn_norm, gain_one, shift_one = norm_backward(
        d_attn_hidden, attn_unit, attn_inverse, norm_gains[1]
    )
    d_first_res = d_attn_res + d_attn_norm
    d_input, grad_one_in, grad_one_out, gain_zero, shift_zero = ffn_backward(
        d_first_res, kept_first, norm_gains[0], gathered[0], gathered[1], cube, 10
    )
    gains_local = jnp.stack([gain_zero, gain_one, gain_two, gain_three, gain_four])
    shifts_local = jnp.stack([shift_zero, shift_one, shift_two, shift_three, shift_four])
    kernel_local = jnp.stack(kernel_rows)
    shards, (grad_gains, grad_biases, grad_depth, grad_rel) = gradient_shards(
        (
            grad_two_out,
            grad_two_in,
            grad_one_in,
            grad_one_out,
            (conv_hidden, d_pointwise),
            (attn_hidden, heads_in),
            (conv_swish, conv_branch),
            (context, attn_branch),
        ),
        (gains_local, shifts_local, kernel_local, d_table),
        cube,
    )
    two_out, two_in, one_in, one_out, conv_in, attn_in, conv_out, attn_out = shards
    return (
        final_norm.astype(jnp.bfloat16),
        d_input.astype(jnp.bfloat16),
        one_in,
        one_out,
        attn_in[:, :width],
        attn_in[:, width : 2 * width],
        attn_in[:, 2 * width :],
        attn_out,
        conv_in,
        conv_out,
        two_in,
        two_out,
        grad_depth,
        grad_rel,
        grad_gains,
        grad_biases,
        grad_bn_gain,
        grad_bn_shift,
        sample_variance,
    )


def solution(mesh):
    placed = (
        P(("batch", "seq"), None),
        P("batch", None),
        P(("batch", "seq"), None),
        P(("batch", "seq"), None),
        P(("batch", "seq"), None),
        P(("batch", "seq"), None),
        P(("batch", "seq"), None),
        P(("batch", "seq"), None),
        P(("batch", "seq"), None),
        P(("batch", "seq"), None),
        P(("batch", "seq"), None),
        P(("batch", "seq"), None),
        P(("batch", "seq"), None),
        P(),
        P(),
        P(),
        P(),
        P(),
        P(),
    )
    return jax.shard_map(
        on_device,
        mesh=mesh,
        in_specs=placed,
        out_specs=(
            P(("batch", "seq"), None),
            P(("batch", "seq"), None),
            P(("batch", "seq"), None),
            P(("batch", "seq"), None),
            P(("batch", "seq"), None),
            P(("batch", "seq"), None),
            P(("batch", "seq"), None),
            P(("batch", "seq"), None),
            P(("batch", "seq"), None),
            P(("batch", "seq"), None),
            P(("batch", "seq"), None),
            P(("batch", "seq"), None),
            P(),
            P(),
            P(),
            P(),
            P(),
            P(),
            P(),
        ),
        check_vma=False,
    )
```

```python
import functools
import math

import jax
import jax.numpy as jnp
from jax import lax
from jax.experimental import pallas as pl
from jax.experimental.pallas import tpu as pltpu
from jax.sharding import PartitionSpec as P

MESH = pl.DeviceIdType.MESH
AXES = ("batch", "seq")
ALL_SHARES = (3, 1, 0)
ROWS = 64
HALF_SHARES = (5, 3)
PAIR_SHARES = (2, 2)

HEADS = 8
REL_LEFT = 64
REL_RIGHT = 8


epsilon = 1e-05
masked_score = -1000000000.0


def padded_2(shard, sides, width):
    for axis, dim in sides:
        peers, length = (lax.axis_size(axis), shard.shape[dim])
        up = [(i, (i + 1) % peers) for i in range(peers - 1)]
        down = [(j, i) for i, j in up]
        last = lax.slice_in_dim(shard, length - width, length, axis=dim)
        first = lax.slice_in_dim(shard, 0, width, axis=dim)
        before = lax.ppermute(last, axis, up)
        after = lax.ppermute(first, axis, down)
        shard = jnp.concatenate([before, shard, after], axis=dim)
    return shard


def matmul(left, right):
    return jnp.dot(left, right, preferred_element_type=jnp.float32)


def transposed_left(left, right):
    return lax.dot_general(
        left, right, (((0,), (0,)), ((), ())), preferred_element_type=jnp.float32
    )


def transposed_right(left, right):
    return lax.dot_general(
        left, right, (((1,), (1,)), ((), ())), preferred_element_type=jnp.float32
    )


class Cube:
    def __init__(self, batch, seq):
        self.seq_bits, self.batch_bits = (seq.bit_length() - 1, batch.bit_length() - 1)
        self.count = self.seq_bits + self.batch_bits
        self.core = self.seq_bits
        wide = (self.batch_bits - 1) // 2
        self.x = list(range(self.seq_bits))[::-1]
        self.y = list(range(self.core + 1, self.core + 1 + wide))[::-1]
        self.z = list(range(self.core + 1 + wide, self.count))[::-1]

    def bit(self, k):
        if k < self.seq_bits:
            return lax.rem(lax.axis_index("seq") // (1 << k), 2)
        return lax.rem(lax.axis_index("batch") // (1 << (k - self.seq_bits)), 2)

    def partner(self, k):
        batch, seq = (lax.axis_index("batch"), lax.axis_index("seq"))
        step = 1 - 2 * self.bit(k)
        if k < self.seq_bits:
            return (batch, seq + step * (1 << k))
        return (batch + step * (1 << (k - self.seq_bits)), seq)


def greet(cube, bits):
    barrier = pltpu.get_barrier_semaphore()
    for k in bits:
        pl.semaphore_signal(barrier, inc=1, device_id=cube.partner(k), device_id_type=MESH)
    pl.semaphore_wait(barrier, len(bits))


def gather_kernel(cube, plans, items, *refs):
    count = len(plans)
    shards, outs = (refs[:count], refs[count : 2 * count])
    send, recv, local = refs[2 * count :]
    own = [cube.bit(k) for k in range(cube.count)]
    kept = []
    for m, (bits, paired) in enumerate(plans):
        kept.append(
            pltpu.make_async_copy(
                shards[m].at[own[0]] if paired else shards[m],
                outs[m].at[tuple(own[k] for k in bits)],
                local.at[m],
            )
        )
        kept[m].start()
    greet(cube, range(cube.count))

    def copy(number, stage):
        m, order, block = flat[number]
        bits, paired = plans[m]
        lead = tuple(slice(None) if k in order[:stage] else own[k] for k in bits)
        place = outs[m].at[lead + block]
        source = place
        if stage == 0:
            source = shards[m].at[(1 - own[0],) + block] if paired else shards[m].at[block]
        return to_partner(
            cube, order[stage], source, place, send.at[number, stage], recv.at[number, stage]
        )

    flat = [item for chunk in items for item in chunk]
    numbers, at = ([], 0)
    for chunk in items:
        numbers.append(range(at, at + len(chunk)))
        at += len(chunk)
    for number in range(len(flat)):
        copy(number, 0).start()
    for one in kept:
        one.wait()
    most = max(len(order) for _, order, _ in flat)
    for turn in range(len(items) + most):
        for stage in range(most):
            for late in (0, 1):
                chunk = turn - stage - late
                if not 0 <= chunk < len(items):
                    continue
                for number in numbers[chunk]:
                    stages = len(flat[number][1])
                    if stage >= stages or late != (stage == stages - 1):
                        continue
                    copy(number, stage).wait_recv()
                    if stage + 1 < stages:
                        copy(number, stage + 1).start()
    for number, (_, order, _) in enumerate(flat):
        for stage in range(len(order)):
            copy(number, stage).wait_send()


def row_parts(rows, shares):
    units, total, at, upto, parts = (rows // 8, sum(shares), 0, 0, [])
    for share in shares:
        upto += share
        end = (units * upto + total // 2) // total
        parts.append((at * 8, (end - at) * 8))
        at = end
    return parts


def gather_fast(shards, kinds, cube):
    core, x, y, z = ([cube.core], cube.x, cube.y, cube.z)
    every = list(range(cube.count))[::-1]
    plans, items, shapes = ([], [], [])
    for m, (shard, kind) in enumerate(zip(shards, kinds)):
        if kind == "all":
            bits, shares = (every, ALL_SHARES)
            orders = [z + y + x + core, z + x + y + core, x + y + z + core]
        else:
            bits = every if kind == "pair" else every[:-1]
            first = x if kind == "pair" else []
            orders = [first + z + y + core, first + y + z + core]
            shares = PAIR_SHARES if kind == "pair" else HALF_SHARES
        plans.append((bits, kind == "pair"))
        shapes.append((2,) * len(bits) + shard.shape[-2:])
        rows, columns = (min(ROWS, shard.shape[-2]), min(2048, shard.shape[-1]))
        for row in range(0, shard.shape[-2], rows):
            for column in range(0, shard.shape[-1], columns):
                items.append(
                    [
                        (m, order, (pl.ds(row + a, w), pl.ds(column, columns)))
                        for order, (a, w) in zip(orders, row_parts(rows, shares))
                        if w
                    ]
                )
    count, copies = (len(shards), sum(len(chunk) for chunk in items))
    outs = pl.pallas_call(
        functools.partial(gather_kernel, cube, plans, items),
        out_shape=[
            jax.ShapeDtypeStruct(shape, shard.dtype) for shape, shard in zip(shapes, shards)
        ],
        in_specs=[pl.BlockSpec(memory_space=pl.ANY)] * count,
        out_specs=[pl.BlockSpec(memory_space=pl.ANY)] * count,
        scratch_shapes=[
            pltpu.SemaphoreType.DMA((copies, cube.count)),
            pltpu.SemaphoreType.DMA((copies, cube.count)),
            pltpu.SemaphoreType.DMA((count,)),
        ],
        compiler_params=pltpu.CompilerParams(collective_id=0, has_side_effects=True),
        name="gather_weights",
    )(*shards)
    return tuple(out.reshape(-1, shard.shape[-1]) for out, shard in zip(outs, shards))


def gradient_kernel(cube, shapes, kinds, tile, *refs):
    count = len(shapes)
    lefts, rights, refs = (refs[:count], refs[count : 2 * count], refs[2 * count :])
    value, out, crossed, value_out, refs = (refs[0], refs[1], refs[2], refs[3], refs[4:])
    near, far, whole = (refs[:count], refs[count : 2 * count], refs[2 * count : 3 * count])
    refs = refs[3 * count :]
    order = cube.y + cube.z[::-1]
    stages = len(order)
    total, sent, recv_at, refs = (refs[0], refs[1 : 1 + stages], refs[1 + stages : 1 + 2 * stages], refs[1 + 2 * stages :])
    cross, value_sent, value_held, refs = (refs[0], refs[1], refs[2], refs[3:])
    x_send, x_recv, local, c_send, c_recv, send, recv, cross_send, cross_recv, v_send, v_recv = refs
    rows, columns = tile
    number, depth = (out.shape[0], total.shape[0])
    lags = [3 + 2 * stage for stage in range(stages)]
    x, c = (cube.bit(0), cube.bit(cube.core))
    dims = sorted(order, reverse=True)
    bits = [cube.bit(k) for k in order]
    every = (slice(None),) * stages
    tokens = near[0].shape[-1] // 2
    pairs = [m for m in range(count) if kinds[m] == "pair"]
    own_lanes = pl.ds(pl.multiple_of(x * tokens, tokens), tokens)

    def spot(stage, flip):
        left = [k for k in dims if k not in order[:stage]]
        side = 1 - bits[stage] if flip else bits[stage]
        return tuple(side if k == order[stage] else slice(None) for k in left)

    def along_x(m):
        if kinds[m] != "all":
            return []
        return [
            to_partner(
                cube,
                0,
                lefts[m].at[every + (slice(None), 1 - x)],
                near[m].at[every + (slice(None), slice(None), own_lanes)],
                x_send.at[m, 0],
                x_recv.at[m, 0],
            ),
            to_partner(
                cube, 0, rights[m], whole[m].at[c, own_lanes], x_send.at[m, 1], x_recv.at[m, 1]
            ),
        ]

    def at_home(m):
        if kinds[m] != "all":
            return [
                pltpu.make_async_copy(lefts[m], near[m], local.at[m, 0]),
                pltpu.make_async_copy(rights[m], whole[m].at[c], local.at[m, 1]),
            ]
        return [
            pltpu.make_async_copy(
                lefts[m].at[every + (slice(None), x)],
                near[m].at[every + (slice(None), slice(None), own_lanes)],
                local.at[m, 0],
            ),
            pltpu.make_async_copy(rights[m], whole[m].at[c, own_lanes], local.at[m, 1]),
        ]

    def along_core(m):
        return [
            to_partner(
                cube,
                cube.core,
                near[m].at[every + (1 - c,)],
                far[m],
                c_send.at[m, 0],
                c_recv.at[m, 0],
            ),
            to_partner(
                cube, cube.core, whole[m].at[c], whole[m].at[c], c_send.at[m, 1], c_recv.at[m, 1]
            ),
        ]

    def remote(stage, chunk):
        return to_partner(
            cube,
            order[stage],
            sent[stage].at[chunk],
            recv_at[stage].at[chunk],
            send.at[stage, chunk],
            recv.at[stage, chunk],
        )

    def reduce(step):
        for stage in range(stages):
            chunk = step - lags[stage]

            @pl.when((chunk >= 0) & (chunk < number))
            def _(stage=stage, chunk=chunk):
                slot = lax.rem(chunk, depth)
                remote(stage, chunk).wait_recv()
                mine = tuple(
                    bits[order.index(k)] if k in order[: stage + 1] else slice(None) for k in dims
                )
                arrived = recv_at[stage]
                if stage + 1 == stages:
                    out[chunk] = total[(slot,) + mine] + arrived[chunk].astype(jnp.float32)
                else:
                    away, home = (spot(stage + 1, True), spot(stage + 1, False))
                    full = list(mine)
                    full[dims.index(order[stage + 1])] = 1 - bits[stage + 1]
                    sent[stage + 1][chunk] = (
                        total[(slot,) + tuple(full)]
                        + arrived[(chunk,) + away].astype(jnp.float32)
                    ).astype(jnp.bfloat16)
                    remote(stage + 1, chunk).start()
                    full[dims.index(order[stage + 1])] = bits[stage + 1]
                    total[(slot,) + tuple(full)] += arrived[(chunk,) + home].astype(jnp.float32)

    def value_copy(k):
        return to_partner(
            cube, k, value_sent.at[k], value_held.at[k], v_send.at[k], v_recv.at[k]
        )

    def value_turn(k):
        if k == 0:
            value_sent[0] = value[...]
        elif k <= cube.count:
            value_copy(k - 1).wait_recv()
            sum_here = value_sent[k - 1] + value_held[k - 1]
            if k < cube.count:
                value_sent[k] = sum_here
            else:
                value_out[...] = sum_here
        if k < cube.count:
            value_copy(k).start()

    def cross_copy(i, first):
        away = pl.ds(first + (1 - x) * 2, 2)
        return to_partner(cube, 0, out.at[away], cross.at[i], cross_send.at[i], cross_recv.at[i])

    greet(cube, range(cube.count))
    value_turn(0)
    for m in range(count):
        for copy in along_x(m) + at_home(m):
            copy.start()
    def to_core(m):
        for copy in at_home(m):
            copy.wait()
        for copy in along_x(m):
            copy.wait_recv()
        for copy in along_core(m):
            copy.start()

    first, firsts = (0, {})
    to_core(0)
    for m in range(count):
        firsts[m] = first
        if m > 0:
            value_turn(m)
        for copy in along_core(m):
            copy.wait_recv()
        if m + 1 < count:
            to_core(m + 1)
        down, across = shapes[m]

        def one(j, carry, m=m, first=first, down=down, across=across):
            chunk = first + j
            slot = lax.rem(chunk, depth)
            row = pl.ds(pl.multiple_of((j // across) * rows, rows), rows)
            column = pl.ds(pl.multiple_of(lax.rem(j, across) * columns, columns), columns)

            def half(flip):
                place = spot(0, flip)
                one_left = near[m][place + (c, row, slice(None))]
                two_left = far[m][place + (row, slice(None))]
                shape = one_left.shape[:-1] + (columns,)
                one_left = one_left.reshape(-1, 2 * tokens)
                two_left = two_left.reshape(-1, 2 * tokens)
                result = matmul(one_left, whole[m][c, :, column]) + matmul(
                    two_left, whole[m][1 - c, :, column]
                )
                return result.reshape(shape)

            sent[0][chunk] = half(True).astype(jnp.bfloat16)
            remote(0, chunk).start()
            total[(slot,) + spot(0, False)] = half(False)
            reduce(chunk)
            return carry

        lax.fori_loop(0, down * across, one, 0)
        first += down * across

    def drain(step, carry):
        reduce(step)
        return carry

    for k in range(count, cube.count + 1):
        value_turn(k)
    for i, m in enumerate(pairs):
        cross_copy(i, firsts[m]).start()
    lax.fori_loop(number, number + lags[-1] + 1, drain, 0)
    for i, m in enumerate(pairs):
        cross_copy(i, firsts[m]).wait_recv()
        crossed[i, x] = out[pl.ds(firsts[m] + x * 2, 2)]
        crossed[i, 1 - x] = cross[i]
        cross_copy(i, firsts[m]).wait_send()
    for k in range(cube.count):
        value_copy(k).wait_send()
    for m in range(count):
        for copy in along_x(m) + along_core(m):
            copy.wait_send()

    def finish(chunk, carry):
        for stage in range(stages):
            remote(stage, chunk).wait_send()
        return carry

    lax.fori_loop(0, number, finish, 0)


def gradients_fast(pairs, kinds, value, cube, rows, columns):
    order = cube.y + cube.z[::-1]
    stages, count = (len(order), len(pairs))
    lefts, rights, shapes, near, far, whole = ([], [], [], [], [], [])
    for (left, right), kind in zip(pairs, kinds):
        lead = (2,) * stages
        if kind == "all":
            block, tokens = (left.shape[1] >> cube.count, left.shape[0])
            lefts.append(left.T.reshape(lead + (2, 2, block, tokens)))
        else:
            block, tokens = (left.shape[1] >> (cube.count - 1), left.shape[0] // 2)
            lefts.append(left.T.reshape(lead + (2, block, 2 * tokens)))
        rights.append(right)
        shapes.append((block // rows, right.shape[1] // columns))
        near.append(pltpu.VMEM(lead + (2, block, 2 * tokens), jnp.bfloat16))
        far.append(pltpu.VMEM(lead + (block, 2 * tokens), jnp.bfloat16))
        whole.append(pltpu.VMEM((2, 2 * tokens, right.shape[1]), jnp.bfloat16))
    number, tile = (sum(down * across for down, across in shapes), (rows, columns))
    held = [
        pltpu.VMEM((number,) + (2,) * (stages - 1 - stage) + tile, jnp.bfloat16)
        for stage in range(stages)
    ]
    depth = 3 + 2 * (stages - 1) + 1
    paired = kinds.count("pair")
    vmem = pl.BlockSpec(memory_space=pltpu.VMEM)
    values = pltpu.VMEM((cube.count,) + value.shape, value.dtype)
    out, crossed, value = pl.pallas_call(
        functools.partial(gradient_kernel, cube, shapes, kinds, tile),
        out_shape=[
            jax.ShapeDtypeStruct((number,) + tile, jnp.float32),
            jax.ShapeDtypeStruct((paired, 2, 2) + tile, jnp.float32),
            jax.ShapeDtypeStruct(value.shape, value.dtype),
        ],
        in_specs=[pl.BlockSpec(memory_space=pl.ANY)] * (2 * count) + [vmem],
        out_specs=[vmem] * 3,
        scratch_shapes=near
        + far
        + whole
        + [pltpu.VMEM((depth,) + (2,) * stages + tile, jnp.float32)]
        + held
        + held
        + [pltpu.VMEM((paired, 2) + tile, jnp.float32), values, values]
        + [pltpu.SemaphoreType.DMA((count, 2))] * 5
        + [pltpu.SemaphoreType.DMA((stages, number))] * 2
        + [pltpu.SemaphoreType.DMA((paired,))] * 2
        + [pltpu.SemaphoreType.DMA((cube.count,))] * 2,
        compiler_params=pltpu.CompilerParams(
            collective_id=4, has_side_effects=True, vmem_limit_bytes=60 * 1024 * 1024
        ),
        name="reduce_gradients",
    )(*lefts, *rights, value)
    results, at, pair = ([], 0, 0)
    for (down, across), right, kind in zip(shapes, rights, kinds):
        if kind == "pair":
            piece = crossed[pair].reshape(2, 2, rows, columns // 128, 128)
            results.append(piece.transpose(2, 1, 3, 0, 4).reshape(rows, 4 * columns))
            pair += 1
        else:
            piece = out[at : at + down * across].reshape(down, across, rows, columns)
            results.append(piece.transpose(0, 2, 1, 3).reshape(down * rows, right.shape[1]))
        at += down * across
    return results, value


def flat_pack(values):
    flat = jnp.concatenate([value.reshape(-1) for value in values])
    size = -(-flat.shape[0] // 8192) * 8192
    return jnp.pad(flat, (0, size - flat.shape[0])).reshape(-1, 1024)


def flat_unpack(flat, values):
    flat, out, at = (flat.reshape(-1), [], 0)
    for value in values:
        out.append(flat[at : at + value.size].reshape(value.shape))
        at += value.size
    return tuple(out)


def gradient_shards(pairs, values, cube):
    if cube is None:
        results = []
        for left, right in pairs:
            whole = transposed_left(left, right)
            flat = whole.reshape(-1, 128)
            shard = lax.psum_scatter(flat, AXES, scatter_dimension=0, tiled=True)
            results.append(shard.reshape(-1, whole.shape[1]))
        return results, lax.psum(values, AXES)
    kinds = ["half", "pair", "pair", "half"] + ["all"] * 4
    results, flat = gradients_fast(pairs, kinds, flat_pack(values), cube, 32, 1024)
    return results, flat_unpack(flat, values)


def parities(shard):
    rows, columns = shard.shape
    return shard.reshape(rows, columns // 256, 2, 128).transpose(2, 0, 1, 3).reshape(2, rows, -1)


def gather_all(shards, cube):
    if cube is None:
        return tuple(lax.all_gather(shard, AXES, axis=0, tiled=True) for shard in shards)
    kinds = ("pair", "half") + ("all",) * 6 + ("pair", "half")
    shards = [parities(shard) if kind == "pair" else shard for shard, kind in zip(shards, kinds)]
    turns = (2, 6, 0, 3, 4, 8, 5, 7, 1, 9)
    outs = gather_fast([shards[m] for m in turns], [kinds[m] for m in turns], cube)
    return tuple(outs[turns.index(m)] for m in range(len(shards)))


def distance_rows(group, left, right, backwards):
    row = lax.broadcasted_iota(jnp.int32, (group, 128), 0)
    row = group - 1 - row if backwards else row
    distance = jnp.where(row >= group // 2, row - group, row)
    index = jnp.clip(distance, -left, right) + left
    hit = index == lax.broadcasted_iota(jnp.int32, (group, 128), 1)
    return jnp.where(hit, 1.0, 0.0).astype(jnp.bfloat16)


def halves(cube, rows, half):
    mine = cube.bit(0)
    return (
        pl.ds(pl.multiple_of(mine * half, half), half),
        pl.ds(pl.multiple_of((1 - mine) * half, half), half),
        pl.ds(pl.multiple_of(mine * rows, rows), rows),
        pl.ds(pl.multiple_of((1 - mine) * rows, rows), rows),
    )


def to_partner(cube, k, source, target, send, recv):
    return pltpu.make_async_remote_copy(
        src_ref=source,
        dst_ref=target,
        send_sem=send,
        recv_sem=recv,
        device_id=cube.partner(k),
        device_id_type=MESH,
    )


def attend_kernel(cube, left, right, *refs):
    hidden, before, same, table, query_w, key_w, value_w, out_w = refs[:8]
    after, context, heads_out, probs_out = refs[8:12]
    weights, heads_in, away, wide, context_away, load, send, recv, head_send, head_recv = refs[12:]
    rows, width = hidden.shape
    group, half = (2 * rows, width // 2)
    heads = half // 128
    scale = 1.0 / math.sqrt(128)
    mine = cube.bit(0)
    own_columns, away_columns, own_rows, away_rows = halves(cube, rows, half)
    loads = []
    for i, matrix in enumerate((query_w, key_w, value_w, out_w)):
        loads.append(pltpu.make_async_copy(matrix, weights.at[i], load.at[i]))
        loads[i].start()
    greet(cube, [0])

    def exchange(i):
        return to_partner(
            cube, 0, away.at[i], heads_in.at[i, own_rows], send.at[i], recv.at[i]
        )

    def context_copy(head):
        column = pl.ds(pl.multiple_of(mine * half + head * 128, 128), 128)
        return to_partner(
            cube, 0, context_away.at[head], wide.at[:, column], head_send.at[head], head_recv.at[head]
        )

    for i in range(3):
        loads[i].wait()
        away[i] = matmul(hidden[...], weights[i, :, away_columns]).astype(jnp.bfloat16)
        exchange(i).start()
    for i in range(3):
        heads_in[i, own_rows, :] = matmul(hidden[...], weights[i, :, own_columns]).astype(
            jnp.bfloat16
        )
    spread = matmul(distance_rows(group, left, right, False), table[...]).astype(jnp.bfloat16)
    loads[3].wait()
    for i in range(3):
        exchange(i).wait_recv()

    def one_head(head, carry):
        column = pl.ds(pl.multiple_of(head * 128, 128), 128)
        place = pl.ds(pl.multiple_of(mine * half + head * 128, 128), 128)
        query, keys, values = (heads_in[i, :, column] for i in range(3))
        relative = pltpu.roll(transposed_right(query, spread), 0, 1, stride=1, stride_axis=0)
        scores = scale * (transposed_right(query, keys) + relative)
        scores = jnp.where(same[...] > 0, scores, masked_score)
        weight = jnp.exp(scores - jnp.max(scores, axis=1, keepdims=True))
        probs_out[head] = weight / jnp.sum(weight, axis=1, keepdims=True)
        there = probs_out[head, away_rows, :].astype(jnp.bfloat16)
        context_away[head] = matmul(there, values).astype(jnp.bfloat16)
        context_copy(head).start()
        here = probs_out[head, own_rows, :].astype(jnp.bfloat16)
        wide[:, place] = matmul(here, values).astype(jnp.bfloat16)
        return carry

    lax.fori_loop(0, heads, one_head, 0)
    heads_out[...] = heads_in[...]
    after[...] = before[...] + matmul(wide[:, own_columns], weights[3, own_columns, :])
    for head in range(heads):
        context_copy(head).wait_recv()
    after[...] += matmul(wide[:, away_columns], weights[3, away_columns, :])
    context[...] = wide[...]
    for i in range(3):
        exchange(i).wait_send()
    for head in range(heads):
        context_copy(head).wait_send()


def attend_fast(cube, hidden, before, same, table, matrices):
    rows, width = hidden.shape
    group, half = (2 * rows, width // 2)
    heads = half // 128
    vmem = pl.BlockSpec(memory_space=pltpu.VMEM)
    return pl.pallas_call(
        functools.partial(attend_kernel, cube, REL_LEFT, REL_RIGHT),
        out_shape=[
            jax.ShapeDtypeStruct((rows, width), jnp.float32),
            jax.ShapeDtypeStruct((rows, width), jnp.bfloat16),
            jax.ShapeDtypeStruct((3, group, half), jnp.bfloat16),
            jax.ShapeDtypeStruct((heads, group, group), jnp.float32),
        ],
        in_specs=[vmem] * 4 + [pl.BlockSpec(memory_space=pl.ANY)] * 4,
        out_specs=[vmem] * 4,
        scratch_shapes=[
            pltpu.VMEM((4, width, width), jnp.bfloat16),
            pltpu.VMEM((3, group, half), jnp.bfloat16),
            pltpu.VMEM((3, rows, half), jnp.bfloat16),
            pltpu.VMEM((rows, width), jnp.bfloat16),
            pltpu.VMEM((heads, rows, 128), jnp.bfloat16),
            pltpu.SemaphoreType.DMA((4,)),
            pltpu.SemaphoreType.DMA((3,)),
            pltpu.SemaphoreType.DMA((3,)),
            pltpu.SemaphoreType.DMA((heads,)),
            pltpu.SemaphoreType.DMA((heads,)),
        ],
        compiler_params=pltpu.CompilerParams(
            collective_id=5, has_side_effects=True, vmem_limit_bytes=48 * 1024 * 1024
        ),
        name="attend",
    )(hidden, before, same, table, *matrices)


def attend_back_kernel(cube, left, right, *refs):
    branch, heads_in, probs_in, table, query_w, key_w, value_w, out_w = refs[:8]
    d_hidden, d_heads, d_table = refs[8:11]
    weights, d_context, d_context_away, wide, away, load, send, recv, head_send, head_recv = refs[
        11:
    ]
    rows, width = branch.shape
    group, half = (2 * rows, width // 2)
    heads = half // 128
    scale = 1.0 / math.sqrt(128)
    mine = cube.bit(0)
    own_columns, away_columns, own_rows, away_rows = halves(cube, rows, half)
    loads = []
    for i, matrix in enumerate((out_w, query_w, key_w, value_w)):
        loads.append(pltpu.make_async_copy(matrix, weights.at[i], load.at[i]))
        loads[i].start()
    greet(cube, [0])
    loads[0].wait()
    exchange = to_partner(
        cube, 0, d_context_away, d_context.at[own_rows], send.at[0], recv.at[0]
    )
    d_context_away[...] = transposed_right(branch[...], weights[0, away_columns, :]).astype(
        jnp.bfloat16
    )
    exchange.start()
    d_context[own_rows, :] = transposed_right(branch[...], weights[0, own_columns, :]).astype(
        jnp.bfloat16
    )
    spread = distance_rows(group, left, right, True)
    down = lax.broadcasted_iota(jnp.int32, (group, group), 0)
    across = lax.broadcasted_iota(jnp.int32, (group, group), 1)
    mirror = jnp.where(down + across == group - 1, 1.0, 0.0).astype(jnp.bfloat16)
    d_table[...] = jnp.zeros_like(d_table)
    exchange.wait_recv()

    def head_copy(head, i):
        column = pl.ds(pl.multiple_of(i * width + mine * half + head * 128, 128), 128)
        return to_partner(
            cube,
            0,
            away.at[head, i, away_rows],
            wide.at[:, column],
            head_send.at[head, i],
            head_recv.at[head, i],
        )

    def one_head(head, carry):
        column = pl.ds(pl.multiple_of(head * 128, 128), 128)
        query, keys, values = (heads_in[i, :, column] for i in range(3))
        d_rows = d_context[:, column]
        probs = probs_in[head]
        d_probs = transposed_right(d_rows, values)
        weighted = jnp.sum(probs * d_probs, axis=1, keepdims=True)
        d_scores = (probs * (d_probs - weighted)).astype(jnp.bfloat16)
        away[head, 2] = transposed_left(probs.astype(jnp.bfloat16), d_rows).astype(jnp.bfloat16)
        head_copy(head, 2).start()
        away[head, 1] = (scale * transposed_left(d_scores, query)).astype(jnp.bfloat16)
        head_copy(head, 1).start()
        turned = pltpu.roll(matmul(d_scores, mirror), 0, 1, stride=1, stride_axis=0)
        bins = (scale * matmul(turned.astype(jnp.bfloat16), spread)).astype(jnp.bfloat16)
        away[head, 0] = (scale * matmul(d_scores, keys) + matmul(bins, table[...])).astype(
            jnp.bfloat16
        )
        head_copy(head, 0).start()
        d_table[...] += transposed_left(bins, query)
        for i in range(3):
            place = pl.ds(pl.multiple_of(i * width + mine * half + head * 128, 128), 128)
            wide[:, place] = away[head, i, own_rows, :]
        return carry

    lax.fori_loop(0, heads, one_head, 0)
    for i in range(3):
        loads[1 + i].wait()

    def part(i, offset, columns):
        place = pl.ds(pl.multiple_of(i * width + offset * half, half), half)
        return transposed_right(wide[:, place], weights[1 + i, :, columns])

    total = part(0, mine, own_columns)
    for i in range(1, 3):
        total += part(i, mine, own_columns)
    d_hidden[...] = total
    for head in range(heads):
        for i in range(3):
            head_copy(head, i).wait_recv()
    total = part(0, 1 - mine, away_columns)
    for i in range(1, 3):
        total += part(i, 1 - mine, away_columns)
    d_hidden[...] += total
    d_heads[...] = wide[...]
    exchange.wait_send()
    for head in range(heads):
        for i in range(3):
            head_copy(head, i).wait_send()


def attend_back_fast(cube, branch, heads_in, probs, table, matrices):
    rows, width = branch.shape
    group, half = (2 * rows, width // 2)
    heads = half // 128
    vmem = pl.BlockSpec(memory_space=pltpu.VMEM)
    return pl.pallas_call(
        functools.partial(attend_back_kernel, cube, REL_LEFT, REL_RIGHT),
        out_shape=[
            jax.ShapeDtypeStruct((rows, width), jnp.float32),
            jax.ShapeDtypeStruct((rows, 3 * width), jnp.bfloat16),
            jax.ShapeDtypeStruct((128, 128), jnp.float32),
        ],
        in_specs=[vmem] * 4 + [pl.BlockSpec(memory_space=pl.ANY)] * 4,
        out_specs=[vmem] * 3,
        scratch_shapes=[
            pltpu.VMEM((4, width, width), jnp.bfloat16),
            pltpu.VMEM((group, half), jnp.bfloat16),
            pltpu.VMEM((rows, half), jnp.bfloat16),
            pltpu.VMEM((rows, 3 * width), jnp.bfloat16),
            pltpu.VMEM((heads, 3, group, 128), jnp.bfloat16),
            pltpu.SemaphoreType.DMA((4,)),
            pltpu.SemaphoreType.DMA((1,)),
            pltpu.SemaphoreType.DMA((1,)),
            pltpu.SemaphoreType.DMA((heads, 3)),
            pltpu.SemaphoreType.DMA((heads, 3)),
        ],
        compiler_params=pltpu.CompilerParams(
            collective_id=6, has_side_effects=True, vmem_limit_bytes=48 * 1024 * 1024
        ),
        name="attend_back",
    )(branch, heads_in, probs, table, *matrices)


def ffn_kernel(cube, *refs):
    hidden, before, weight_in, weight_out = refs[:4]
    after, act, swish, hidden_out = refs[4:8]
    into, outof, both, away, arrived, load, send, recv = refs[8:]
    rows, width = hidden.shape
    wide = into.shape[1]
    step = wide // 4
    own_columns, away_columns, own_rows, away_rows = halves(cube, rows, width // 2)
    loads = []
    for q in range(4):
        part = pl.ds(q * step, step)
        loads.append(
            pltpu.make_async_copy(weight_in.at[:, part], into.at[:, part], load.at[q])
        )
    loads.append(pltpu.make_async_copy(weight_out, outof, load.at[4]))
    for one in loads:
        one.start()
    both[own_rows, :] = hidden[...]
    greet(cube, [0])
    exchange = to_partner(
        cube, 0, both.at[own_rows], both.at[own_rows], send.at[0], recv.at[0]
    )
    exchange.start()

    def activate(q, rows_here):
        part = pl.ds(q * step, step)
        value = matmul(both[rows_here, :], into[:, part])
        act[rows_here, part] = value
        swish[rows_here, part] = jax.nn.silu(value).astype(jnp.bfloat16)

    for q in range(4):
        loads[q].wait()
        activate(q, own_rows)
    loads[4].wait()
    exchange.wait_recv()
    for q in range(4):
        activate(q, away_rows)
    half = width // 2
    back = []
    for q in range(2):
        part = pl.ds(q * half, half)
        away[:, part] = matmul(swish[away_rows, :], outof[:, part]).astype(jnp.bfloat16)
        back.append(
            to_partner(
                cube, 0, away.at[:, part], arrived.at[:, part], send.at[1 + q], recv.at[1 + q]
            )
        )
        back[q].start()
    hidden_out[...] = both[...]
    for q in range(2):
        part = pl.ds(q * half, half)
        after[:, part] = before[:, part] + 0.5 * matmul(swish[own_rows, :], outof[:, part])
    for q in range(2):
        part = pl.ds(q * half, half)
        back[q].wait_recv()
        after[:, part] += 0.5 * arrived[:, part].astype(jnp.float32)
    for one in [exchange] + back:
        one.wait_send()


def ffn_back_kernel(cube, *refs):
    branch, act, weight_in, weight_out = refs[:4]
    d_hidden, d_act, branch_out = refs[4:7]
    into, outof, both, away, arrived, load, send, recv = refs[7:]
    rows, width = branch.shape
    wide = into.shape[1]
    step = wide // 4
    own_columns, away_columns, own_rows, away_rows = halves(cube, rows, width // 2)
    loads = []
    for q in range(4):
        part = pl.ds(q * step, step)
        loads.append(
            pltpu.make_async_copy(weight_out.at[part], outof.at[part], load.at[q])
        )
    loads.append(pltpu.make_async_copy(weight_in, into, load.at[4]))
    for one in loads:
        one.start()
    both[own_rows, :] = branch[...]
    greet(cube, [0])
    exchange = to_partner(
        cube, 0, both.at[own_rows], both.at[own_rows], send.at[0], recv.at[0]
    )
    exchange.start()

    def deactivate(q, rows_here):
        part = pl.ds(q * step, step)
        value = transposed_right(both[rows_here, :], outof[part, :])
        d_act[rows_here, part] = (value * swish_slope(act[rows_here, part])).astype(jnp.bfloat16)

    for q in range(4):
        loads[q].wait()
        deactivate(q, own_rows)
    loads[4].wait()
    exchange.wait_recv()
    for q in range(4):
        deactivate(q, away_rows)
    half = width // 2
    back = []
    for q in range(2):
        part = pl.ds(q * half, half)
        away[:, part] = transposed_right(d_act[away_rows, :], into[part, :]).astype(jnp.bfloat16)
        back.append(
            to_partner(
                cube, 0, away.at[:, part], arrived.at[:, part], send.at[1 + q], recv.at[1 + q]
            )
        )
        back[q].start()
    branch_out[...] = both[...]
    for q in range(2):
        part = pl.ds(q * half, half)
        d_hidden[:, part] = transposed_right(d_act[own_rows, :], into[part, :])
    for q in range(2):
        part = pl.ds(q * half, half)
        back[q].wait_recv()
        d_hidden[:, part] += arrived[:, part].astype(jnp.float32)
    for one in [exchange] + back:
        one.wait_send()


def ffn_fast(cube, first, second, weight_in, weight_out, number, backward):
    rows, width = first.shape
    wide = weight_in.shape[1]
    vmem = pl.BlockSpec(memory_space=pltpu.VMEM)
    both = jax.ShapeDtypeStruct((2 * rows, width), jnp.bfloat16)
    result = jax.ShapeDtypeStruct((rows, width), jnp.float32)
    inner = jax.ShapeDtypeStruct((2 * rows, wide), jnp.bfloat16)
    if backward:
        shapes = [result, inner, both]
    else:
        shapes = [result, jax.ShapeDtypeStruct((2 * rows, wide), jnp.float32), inner, both]
    return pl.pallas_call(
        functools.partial(ffn_back_kernel if backward else ffn_kernel, cube),
        out_shape=shapes,
        in_specs=[vmem] * 2 + [pl.BlockSpec(memory_space=pl.ANY)] * 2,
        out_specs=[vmem] * len(shapes),
        scratch_shapes=[
            pltpu.VMEM(weight_in.shape, jnp.bfloat16),
            pltpu.VMEM(weight_out.shape, jnp.bfloat16),
            pltpu.VMEM((2 * rows, width), jnp.bfloat16),
            pltpu.VMEM((rows, width), jnp.bfloat16),
            pltpu.VMEM((rows, width), jnp.bfloat16),
            pltpu.SemaphoreType.DMA((5,)),
            pltpu.SemaphoreType.DMA((3,)),
            pltpu.SemaphoreType.DMA((3,)),
        ],
        compiler_params=pltpu.CompilerParams(
            collective_id=number, has_side_effects=True, vmem_limit_bytes=48 * 1024 * 1024
        ),
        name="ffn_back" if backward else "ffn",
    )(first, second, weight_in, weight_out)


def rounds_of(cube):
    bits = list(range(cube.count))
    return [bits[i : i + 2] for i in range(0, cube.count, 2)]


def flipped(cube, bits):
    batch, seq = (lax.axis_index("batch"), lax.axis_index("seq"))
    for k in bits:
        step = 1 - 2 * cube.bit(k)
        if k < cube.seq_bits:
            seq = seq + step * (1 << k)
        else:
            batch = batch + step * (1 << (k - cube.seq_bits))
    return (batch, seq)


def masks_of(bits):
    return [[bits[0]], [bits[1]], bits] if len(bits) == 2 else [bits]


def greet_rounds(cube):
    barrier, count = (pltpu.get_barrier_semaphore(), 0)
    for bits in rounds_of(cube):
        for mask in masks_of(bits):
            pl.semaphore_signal(
                barrier, inc=1, device_id=flipped(cube, mask), device_id_type=MESH
            )
            count += 1
    pl.semaphore_wait(barrier, count)


def sum_rounds(cube, value, slots, send, recv):
    for r, bits in enumerate(rounds_of(cube)):
        mine = sum(cube.bit(k) * (1 << i) for i, k in enumerate(bits))
        slots[r, mine] = value
        copies = []
        for i, mask in enumerate(masks_of(bits)):
            copies.append(
                pltpu.make_async_remote_copy(
                    src_ref=slots.at[r, mine],
                    dst_ref=slots.at[r, mine],
                    send_sem=send.at[r, i],
                    recv_sem=recv.at[r, i],
                    device_id=flipped(cube, mask),
                    device_id_type=MESH,
                )
            )
            copies[i].start()
        for copy in copies:
            copy.wait()
        value = slots[r, 0] + slots[r, 1]
        if len(bits) == 2:
            value = value + (slots[r, 2] + slots[r, 3])
    return value


def conv_halo(cube, wide, halo_send, halo_recv, send, recv):
    rows = wide.shape[0] - 16
    mine = cube.bit(0)
    halo_send[...] = wide[pl.ds(pl.multiple_of(8 + (1 - mine) * (rows - 8), 8), 8), :]
    copy = to_partner(cube, 0, halo_send, halo_recv, send.at[0], recv.at[0])
    copy.start()
    edge = pl.ds(pl.multiple_of(mine * (rows + 8), 8), 8)
    wide[edge, :] = jnp.zeros((8, wide.shape[1]), jnp.float32)
    copy.wait()
    wide[pl.ds(pl.multiple_of((1 - mine) * (rows + 8), 8), 8), :] = halo_recv[...]


def row_sum(values):
    return jnp.sum(values, axis=0, keepdims=True)


def conv_kernel(cube, taps, *refs):
    values, norms, marks, weight_in, weight_out = refs[:5]
    after, unit_out, inverse_out, hidden, gate, sigma, wide, centred, swish, stats = refs[5:15]
    into, outof, mixed, slots, halo_send, halo_recv, load, send, recv, h_send, h_recv = refs[15:]
    rows, width = values.shape
    block = width // 4
    loads = [
        pltpu.make_async_copy(weight_in, into, load.at[0]),
        pltpu.make_async_copy(weight_out, outof, load.at[1]),
    ]
    for one in loads:
        one.start()

    def normalise(i, carry):
        part = pl.ds(pl.multiple_of(i * 32, 32), 32)
        here = values[part, :]
        away = here - jnp.mean(here, axis=1, keepdims=True)
        inverse = lax.rsqrt(jnp.mean(away * away, axis=1, keepdims=True) + epsilon)
        unit = away * inverse
        unit_out[part, :] = unit
        inverse_out[part, :] = jnp.broadcast_to(inverse, (32, 128))
        hidden[part, :] = (unit * norms[0:1, :] + norms[1:2, :]).astype(jnp.bfloat16)
        return carry

    lax.fori_loop(0, rows // 32, normalise, 0)
    greet_rounds(cube)
    loads[0].wait()

    def point(i, carry):
        part = pl.ds(pl.multiple_of(i * block, block), block)
        other = pl.ds(pl.multiple_of(width + i * block, block), block)
        level = matmul(hidden[...], into[:, part])
        open_ = jax.nn.sigmoid(matmul(hidden[...], into[:, other]))
        gate[:, part] = level
        sigma[:, part] = open_
        wide[pl.ds(8, rows), part] = (level * open_).astype(jnp.bfloat16).astype(jnp.float32)
        return carry

    lax.fori_loop(0, 4, point, 0)
    conv_halo(cube, wide, halo_send, halo_recv, h_send, h_recv)
    reach = taps // 2
    mask = marks[:, taps : taps + 1]

    def mix(i, carry):
        part = pl.ds(pl.multiple_of(i * block, block), block)
        total = jnp.zeros((rows, block), jnp.float32)
        for o in range(taps):
            total = total + norms[8 + o : 9 + o, part] * (
                wide[8 + o - reach : 8 + o - reach + rows, part] * marks[:, o : o + 1]
            )
        mixed[:, part] = total
        masked = total * mask
        stats[0:1, part] = row_sum(masked)
        stats[1:2, part] = row_sum(masked * total)
        return carry

    lax.fori_loop(0, 4, mix, 0)
    stats[2:3, :] = jnp.broadcast_to(row_sum(mask), (1, width))
    stats[3:8, :] = jnp.zeros((5, width), jnp.float32)
    total = sum_rounds(cube, stats[...], slots, send, recv)
    count = total[2:3, :]
    mean = total[0:1, :] / count
    var = total[1:2, :] / count - mean * mean
    stats[0:1, :] = mean
    stats[1:2, :] = var
    stats[2:3, :] = count
    stats[3:4, :] = lax.rsqrt(var + epsilon)

    def finish(i, carry):
        part = pl.ds(pl.multiple_of(i * block, block), block)
        middle = (mixed[:, part] - stats[0:1, part]) * stats[3:4, part]
        centred[:, part] = middle
        swish[:, part] = jax.nn.silu(middle * norms[2:3, part] + norms[3:4, part]).astype(
            jnp.bfloat16
        )
        return carry

    lax.fori_loop(0, 4, finish, 0)
    loads[1].wait()

    def project(i, carry):
        part = pl.ds(pl.multiple_of(i * block, block), block)
        after[:, part] = values[:, part] + matmul(swish[...], outof[:, part])
        return carry

    lax.fori_loop(0, 4, project, 0)


def conv_back_kernel(cube, taps, *refs):
    d_values, norms, marks, stats, centred, wide, gate, sigma, unit, inverse = refs[:10]
    weight_in, weight_out = refs[10:12]
    d_after, attn_branch, branch, d_point, sums = refs[12:17]
    into, outof, d_bn, d_wide, d_norm, pack, slots, halo_send, halo_recv, load, send, recv, h_send, h_recv = refs[17:]
    rows, width = d_values.shape
    block = width // 4
    loads = [
        pltpu.make_async_copy(weight_out, outof, load.at[0]),
        pltpu.make_async_copy(weight_in, into, load.at[1]),
    ]
    for one in loads:
        one.start()
    branch[...] = d_values[...].astype(jnp.bfloat16)
    greet_rounds(cube)
    reach = taps // 2
    mask = marks[:, taps : taps + 1]
    loads[0].wait()

    def enter(i, carry):
        part = pl.ds(pl.multiple_of(i * block, block), block)
        middle = centred[:, part]
        slope = swish_slope(middle * norms[2:3, part] + norms[3:4, part])
        value = transposed_right(branch[...], outof[part, :]) * slope
        d_bn[:, part] = value
        masked = value * mask
        pack[0:1, part] = row_sum(masked * middle)
        pack[1:2, part] = row_sum(masked)
        return carry

    lax.fori_loop(0, 4, enter, 0)
    pack[2:8, :] = jnp.zeros((6, width), jnp.float32)
    pack[...] = sum_rounds(cube, pack[...], slots, send, recv)

    def spread(i, carry):
        part = pl.ds(pl.multiple_of(i * block, block), block)
        share = mask * (pack[1:2, part] + centred[:, part] * pack[0:1, part])
        value = (
            norms[2:3, part] * stats[3:4, part] * (d_bn[:, part] - share / stats[2:3, part])
        )
        d_wide[pl.ds(8, rows), part] = value.astype(jnp.bfloat16).astype(jnp.float32)
        return carry

    lax.fori_loop(0, 4, spread, 0)
    conv_halo(cube, d_wide, halo_send, halo_recv, h_send, h_recv)
    sums[...] = jnp.zeros_like(sums)

    def unmix(i, carry):
        part = pl.ds(pl.multiple_of(i * block, block), block)
        own = d_wide[8 : 8 + rows, part]
        total = jnp.zeros((rows, block), jnp.float32)
        for o in range(taps):
            back = taps - 1 - o
            sums[o : o + 1, part] = row_sum(
                own * (wide[8 + o - reach : 8 + o - reach + rows, part] * marks[:, o : o + 1])
            )
            total = total + norms[8 + o : 9 + o, part] * (
                d_wide[8 + back - reach : 8 + back - reach + rows, part]
                * marks[:, back : back + 1]
            )
        open_ = sigma[:, part]
        other = pl.ds(pl.multiple_of(width + i * block, block), block)
        d_point[:, part] = (total * open_).astype(jnp.bfloat16)
        d_point[:, other] = (total * gate[:, part] * open_ * (1.0 - open_)).astype(jnp.bfloat16)
        return carry

    lax.fori_loop(0, 4, unmix, 0)
    loads[1].wait()

    def project(i, carry):
        part = pl.ds(pl.multiple_of(i * block, block), block)
        value = transposed_right(d_point[...], into[part, :])
        d_norm[:, part] = value
        sums[8:9, part] = row_sum(value * unit[:, part])
        sums[9:10, part] = row_sum(value)
        return carry

    lax.fori_loop(0, 4, project, 0)
    sums[10:12, :] = pack[0:2, :]

    def leave(i, carry):
        part = pl.ds(pl.multiple_of(i * 32, 32), 32)
        here = unit[part, :]
        d_unit = d_norm[part, :] * norms[0:1, :]
        value = d_values[part, :] + inverse[part, 0:1] * (
            d_unit
            - jnp.mean(d_unit, axis=1, keepdims=True)
            - here * jnp.mean(d_unit * here, axis=1, keepdims=True)
        )
        d_after[part, :] = value
        attn_branch[part, :] = value.astype(jnp.bfloat16)
        return carry

    lax.fori_loop(0, rows // 32, leave, 0)


def conv_fast(cube, taps, small, weights, forward):
    rows, width = small[0].shape
    vmem = pl.BlockSpec(memory_space=pltpu.VMEM)
    wide, full, half = ((rows + 16, width), (rows, width), (rows, 2 * width))
    single, double = (jnp.float32, jnp.bfloat16)
    if forward:
        shapes = [
            (full, single),
            (full, single),
            ((rows, 128), single),
            (full, double),
            (full, single),
            (full, single),
            (wide, single),
            (full, single),
            (full, double),
            ((8, width), single),
        ]
        own = [pltpu.VMEM(full, single)]
    else:
        shapes = [(full, single), (full, double), (full, double), (half, double), ((16, width), single)]
        own = [
            pltpu.VMEM(full, single),
            pltpu.VMEM(wide, single),
            pltpu.VMEM(full, single),
            pltpu.VMEM((8, width), single),
        ]
    rounds = len(rounds_of(cube))
    return pl.pallas_call(
        functools.partial(conv_kernel if forward else conv_back_kernel, cube, taps),
        out_shape=[jax.ShapeDtypeStruct(shape, dtype) for shape, dtype in shapes],
        in_specs=[vmem] * len(small) + [pl.BlockSpec(memory_space=pl.ANY)] * 2,
        out_specs=[vmem] * len(shapes),
        scratch_shapes=[
            pltpu.VMEM(weights[0].shape, double),
            pltpu.VMEM(weights[1].shape, double),
        ]
        + own
        + [
            pltpu.VMEM((rounds, 4, 8, width), single),
            pltpu.VMEM((8, width), single),
            pltpu.VMEM((8, width), single),
            pltpu.SemaphoreType.DMA((2,)),
            pltpu.SemaphoreType.DMA((rounds, 3)),
            pltpu.SemaphoreType.DMA((rounds, 3)),
            pltpu.SemaphoreType.DMA((1,)),
            pltpu.SemaphoreType.DMA((1,)),
        ],
        compiler_params=pltpu.CompilerParams(
            collective_id=1 if forward else 2,
            has_side_effects=True,
            vmem_limit_bytes=48 * 1024 * 1024,
        ),
        name="conv" if forward else "conv_back",
    )(*small, *weights)


def cube_of(shards, rel_table, depth_w):
    batch, seq = (lax.axis_size("batch"), lax.axis_size("seq"))
    if seq != 2 or batch < 8 or batch & (batch - 1):
        return None
    if depth_w.shape[0] > 5 or rel_table.shape[0] > 128 or rel_table.shape[1] != 128:
        return None
    if any(shard.shape[0] % 32 or shard.shape[1] % 1024 for shard in shards):
        return None
    return Cube(batch, seq)


def swish_slope(values):
    sigma = jax.nn.sigmoid(values)
    return sigma * (1.0 + values * (1.0 - sigma))


def norm_forward(values, gain, shift):
    mean = jnp.mean(values, axis=-1, keepdims=True)
    centred = values - mean
    inverse = lax.rsqrt(jnp.mean(centred * centred, axis=-1, keepdims=True) + epsilon)
    unit = centred * inverse
    return (unit * gain + shift, unit, inverse)


def norm_backward(d_out, unit, inverse, gain):
    d_unit = d_out * gain
    d_values = inverse * (
        d_unit
        - jnp.mean(d_unit, axis=-1, keepdims=True)
        - unit * jnp.mean(d_unit * unit, axis=-1, keepdims=True)
    )
    return (d_values, jnp.sum(d_out * unit, axis=0), jnp.sum(d_out, axis=0))


def ffn_forward(values, gain, shift, weight_in, weight_out, cube, number):
    normed, unit, inverse = norm_forward(values, gain, shift)
    hidden = normed.astype(jnp.bfloat16)
    if cube is not None:
        after, act, swish, hidden = ffn_fast(
            cube, hidden, values, weight_in, weight_out, number, False
        )
        return (after, (hidden, act, swish, unit, inverse))
    act = matmul(hidden, weight_in)
    swish = jax.nn.silu(act).astype(jnp.bfloat16)
    return (values + 0.5 * matmul(swish, weight_out), (hidden, act, swish, unit, inverse))


def ffn_backward(d_out, kept, gain, weight_in, weight_out, cube, number):
    hidden, act, swish, unit, inverse = kept
    d_branch = (0.5 * d_out).astype(jnp.bfloat16)
    if cube is not None:
        d_hidden, d_act, d_branch = ffn_fast(
            cube, d_branch, act, weight_in, weight_out, number, True
        )
    else:
        d_act = (transposed_right(d_branch, weight_out) * swish_slope(act)).astype(jnp.bfloat16)
        d_hidden = transposed_right(d_act, weight_in)
    d_norm, d_gain, d_shift = norm_backward(d_hidden, unit, inverse, gain)
    return (d_out + d_norm, (hidden, d_act), (swish, d_branch), d_gain, d_shift)


def segment_ids(place, ends, group):
    inside = jnp.sum((place[:, None] >= ends[None, :]).astype(jnp.int32), axis=1)
    return jnp.where((place >= 0) & (place < group), inside, -1)


def to_heads(hidden, weight, heads):
    return matmul(hidden, weight).astype(jnp.bfloat16).reshape(hidden.shape[0], heads, -1)


def spread_band(project, start, group, left, right):
    heads, rows, width = project.shape
    band = rows + width - 1
    blank = jnp.zeros_like(project[:, :, :1])
    middle = jnp.concatenate([blank, project[:, :, 1 : width - 1], blank], axis=2)
    padded = jnp.pad(middle, ((0, 0), (0, 0), (0, band + 1 - width)))
    skewed = padded.reshape(heads, rows * (band + 1))[:, : rows * band].reshape(heads, rows, band)
    canvas = jnp.zeros((heads, rows, group + left + right), jnp.float32)
    anchor = jnp.zeros((), jnp.int32)
    canvas = lax.dynamic_update_slice(canvas, skewed, (anchor, anchor, start))
    return canvas[:, :, left : left + group]


def relative_bins(grad, difference, start, width, left, right):
    heads, rows, group = grad.shape
    band = rows + width - 1
    canvas = jnp.pad(grad, ((0, 0), (0, 0), (left, right)))
    anchor = jnp.zeros((), jnp.int32)
    strip = lax.dynamic_slice(canvas, (anchor, anchor, start), (heads, rows, band))
    flat = jnp.pad(strip.reshape(heads, rows * band), ((0, 0), (0, rows)))
    inner = flat.reshape(heads, rows, band + 1)[:, :, 1 : width - 1]
    below = jnp.sum(jnp.where(difference[None] <= -left, grad, 0.0), axis=2, keepdims=True)
    above = jnp.sum(jnp.where(difference[None] >= right, grad, 0.0), axis=2, keepdims=True)
    return jnp.concatenate([below, inner, above], axis=2)


def block_scores(rows_query, keys, table, segment, start, left, right):
    rows, heads, depth = rows_query.shape
    group = keys.shape[0]
    width = table.shape[0]
    scale = 1.0 / math.sqrt(depth)
    project = jnp.einsum("qhd,rd->hqr", rows_query, table, preferred_element_type=jnp.float32)
    content = jnp.einsum("qhd,khd->hqk", rows_query, keys, preferred_element_type=jnp.float32)
    key_place = jnp.arange(group, dtype=jnp.int32)
    row_place = start + jnp.arange(rows, dtype=jnp.int32)
    difference = key_place[None, :] - row_place[:, None]
    relative = spread_band(project, start, group, left, right)
    relative = relative + jnp.where(difference[None] <= -left, project[:, :, :1], 0.0)
    relative = relative + jnp.where(difference[None] >= right, project[:, :, width - 1 :], 0.0)
    row_segment = lax.dynamic_slice_in_dim(segment, start, rows)
    same = row_segment[:, None] == segment[None, :]
    return (jnp.where(same[None], scale * (content + relative), masked_score), difference)


def attention_forward(query, keys, values, table, segment, block_rows, left, right):
    group = query.shape[0]
    starts = jnp.arange(group // block_rows, dtype=jnp.int32) * block_rows

    def one_block(carry, start):
        rows_query = lax.dynamic_slice_in_dim(query, start, block_rows, 0)
        scores, difference = block_scores(rows_query, keys, table, segment, start, left, right)
        top = jnp.max(scores, axis=2, keepdims=True)
        weights = jnp.exp(scores - top)
        total = jnp.sum(weights, axis=2, keepdims=True)
        probs = (weights / total).astype(jnp.bfloat16)
        rows_out = jnp.einsum("hqk,khd->qhd", probs, values, preferred_element_type=jnp.float32)
        return (carry, (rows_out.astype(jnp.bfloat16), (top + jnp.log(total))[:, :, 0]))

    unused, (pieces, log_total) = lax.scan(one_block, 0, starts)
    return (pieces.reshape(query.shape), log_total)


def attention_backward(
    query, keys, values, table, segment, log_total, d_context, block_rows, left, right
):
    group, heads, depth = query.shape
    width = table.shape[0]
    scale = 1.0 / math.sqrt(depth)
    starts = jnp.arange(group // block_rows, dtype=jnp.int32) * block_rows

    def one_block(carry, operands):
        d_keys, d_values, d_table = carry
        start, block_total = operands
        rows_query = lax.dynamic_slice_in_dim(query, start, block_rows, 0)
        rows_grad = lax.dynamic_slice_in_dim(d_context, start, block_rows, 0)
        scores, difference = block_scores(rows_query, keys, table, segment, start, left, right)
        probs = jnp.exp(scores - block_total[:, :, None])
        d_values = d_values + jnp.einsum(
            "hqk,qhd->khd",
            probs.astype(jnp.bfloat16),
            rows_grad,
            preferred_element_type=jnp.float32,
        )
        d_probs = jnp.einsum("qhd,khd->hqk", rows_grad, values, preferred_element_type=jnp.float32)
        weighted = jnp.sum(probs * d_probs, axis=2, keepdims=True)
        d_scores = (probs * (d_probs - weighted)).astype(jnp.bfloat16)
        bins = relative_bins(
            scale * d_scores.astype(jnp.float32), difference, start, width, left, right
        )
        bins = bins.astype(jnp.bfloat16)
        d_rows = scale * jnp.einsum(
            "hqk,khd->qhd", d_scores, keys, preferred_element_type=jnp.float32
        )
        d_rows = d_rows + jnp.einsum("hqr,rd->qhd", bins, table, preferred_element_type=jnp.float32)
        d_keys = d_keys + scale * jnp.einsum(
            "hqk,qhd->khd", d_scores, rows_query, preferred_element_type=jnp.float32
        )
        d_table = d_table + jnp.einsum(
            "hqr,qhd->rd", bins, rows_query, preferred_element_type=jnp.float32
        )
        return ((d_keys, d_values, d_table), d_rows.astype(jnp.bfloat16))

    zeros_heads = jnp.zeros(query.shape, jnp.float32)
    zeros_table = jnp.zeros(table.shape, jnp.float32)
    (d_keys, d_values, d_table), d_rows = lax.scan(
        one_block, (zeros_heads, zeros_heads, zeros_table), (starts, log_total)
    )
    return (
        d_rows.reshape(query.shape),
        d_keys.astype(jnp.bfloat16),
        d_values.astype(jnp.bfloat16),
        d_table,
    )


def on_device(
    frames,
    lengths,
    cotangent,
    ffn1_in,
    ffn1_out,
    query_w,
    key_w,
    value_w,
    out_w,
    point_in,
    point_out,
    ffn2_in,
    ffn2_out,
    depth_w,
    rel_table,
    norm_gains,
    norm_biases,
    bn_gain,
    bn_shift,
):
    seq_count = lax.axis_size("seq")
    seq_rank = lax.axis_index("seq")
    frames_here, width = frames.shape
    group = frames_here * seq_count
    block_rows = min(512, group)
    kernel_size = depth_w.shape[0]
    reach = kernel_size // 2
    ends = jnp.cumsum(lengths[0])
    last_entry = lengths.shape[1] - 1
    first = seq_rank * frames_here
    wide_place = first - reach + jnp.arange(frames_here + 2 * reach, dtype=jnp.int32)
    wide_segment = segment_ids(wide_place, ends, group)
    own_segment = wide_segment[reach : reach + frames_here]
    mask = (own_segment < last_entry).astype(jnp.float32)[:, None]
    group_segment = segment_ids(jnp.arange(group, dtype=jnp.int32), ends, group)
    shards = (
        ffn1_in,
        ffn1_out,
        query_w,
        key_w,
        value_w,
        out_w,
        point_in,
        point_out,
        ffn2_in,
        ffn2_out,
    )
    cube = cube_of(shards, rel_table, depth_w)
    gathered = gather_all(shards, cube)
    start_values = frames.astype(jnp.float32)
    after_first, kept_first = ffn_forward(
        start_values, norm_gains[0], norm_biases[0], gathered[0], gathered[1], cube, 7
    )
    attn_norm, attn_unit, attn_inverse = norm_forward(after_first, norm_gains[1], norm_biases[1])
    attn_hidden = attn_norm.astype(jnp.bfloat16)
    if cube is None:
        query_heads, key_heads, value_heads = (
            lax.all_to_all(
                to_heads(attn_hidden, gathered[2], HEADS),
                "seq",
                split_axis=1,
                concat_axis=0,
                tiled=True,
            ),
            lax.all_to_all(
                to_heads(attn_hidden, gathered[3], HEADS),
                "seq",
                split_axis=1,
                concat_axis=0,
                tiled=True,
            ),
            lax.all_to_all(
                to_heads(attn_hidden, gathered[4], HEADS),
                "seq",
                split_axis=1,
                concat_axis=0,
                tiled=True,
            ),
        )
        context_heads, log_total = attention_forward(
            query_heads,
            key_heads,
            value_heads,
            rel_table,
            group_segment,
            block_rows,
            REL_LEFT,
            REL_RIGHT,
        )
        context = lax.all_to_all(context_heads, "seq", split_axis=0, concat_axis=1, tiled=True).reshape(
            frames_here, width
        )
        after_attn = after_first + matmul(context, gathered[5])
    else:
        table = jnp.pad(rel_table, ((0, 128 - rel_table.shape[0]), (0, 0)))
        same = (group_segment[:, None] == group_segment[None, :]).astype(jnp.float32)
        after_attn, context, heads_kept, probs_kept = attend_fast(
            cube, attn_hidden, after_first, same, table, gathered[2:6]
        )
    kernel = depth_w.astype(jnp.float32)
    if cube is None:
        conv_norm, conv_unit, conv_inverse = norm_forward(after_attn, norm_gains[2], norm_biases[2])
        conv_hidden = conv_norm.astype(jnp.bfloat16)
        pointwise = matmul(conv_hidden, gathered[6])
        gate_half = pointwise[:, :width]
        sigma_half = jax.nn.sigmoid(pointwise[:, width:])
        gated = (gate_half * sigma_half).astype(jnp.bfloat16)
        gated_wide = padded_2(gated, (("seq", 0),), reach)
        mixed = jnp.zeros((frames_here, width), jnp.float32)
        for offset in range(kernel_size):
            same = (wide_segment[offset : offset + frames_here] == own_segment).astype(jnp.float32)[
                :, None
            ]
            mixed = (
                mixed
                + kernel[offset] * gated_wide[offset : offset + frames_here].astype(jnp.float32) * same
            )
        total, squares, count = lax.psum(
            (jnp.sum(mixed * mask, axis=0), jnp.sum(mixed * mixed * mask, axis=0), jnp.sum(mask)),
            AXES,
        )
        mean = total / count
        var = squares / count - mean * mean
        bn_inverse = lax.rsqrt(var + epsilon)
        centred = (mixed - mean) * bn_inverse
        bn_out = centred * bn_gain + bn_shift
        conv_swish = jax.nn.silu(bn_out).astype(jnp.bfloat16)
        after_conv = after_attn + matmul(conv_swish, gathered[7])
    else:
        marks = [
            wide_segment[offset : offset + frames_here] == own_segment
            for offset in range(kernel_size)
        ]
        marks = jnp.stack(marks, axis=1).astype(jnp.float32)
        marks = jnp.concatenate([marks, mask], axis=1)
        marks = jnp.pad(marks, ((0, 0), (0, 8 - marks.shape[1])))
        blank = jnp.zeros((4, width), jnp.float32)
        norms = [norm_gains[2], norm_biases[2], bn_gain, bn_shift]
        norms = jnp.concatenate([jnp.stack(norms), blank, kernel, blank[:3]])
        after_conv, *conv_kept, conv_swish, stats = conv_fast(
            cube, kernel_size, (after_attn, norms, marks), (gathered[6], gathered[7]), True
        )
        conv_unit, conv_inverse, conv_hidden, gate_half, sigma_half, gated_wide, centred = conv_kept
        var, count = (stats[1], stats[2])
    after_second, kept_second = ffn_forward(
        after_conv, norm_gains[3], norm_biases[3], gathered[8], gathered[9], cube, 8
    )
    final_norm, final_unit, final_inverse = norm_forward(
        after_second, norm_gains[4], norm_biases[4]
    )
    sample_variance = var * count / (count - 1.0)
    d_final = cotangent.astype(jnp.float32) * mask
    d_second, gain_four, shift_four = norm_backward(
        d_final, final_unit, final_inverse, norm_gains[4]
    )
    d_conv_res, grad_two_in, grad_two_out, gain_three, shift_three = ffn_backward(
        d_second, kept_second, norm_gains[3], gathered[8], gathered[9], cube, 9
    )
    if cube is None:
        conv_branch = d_conv_res.astype(jnp.bfloat16)
        d_bn_out = transposed_right(conv_branch, gathered[7]) * swish_slope(bn_out)
        grad_bn_gain, grad_bn_shift = lax.psum(
            (jnp.sum(d_bn_out * centred * mask, axis=0), jnp.sum(d_bn_out * mask, axis=0)), AXES
        )
        d_mixed = (
            bn_gain * bn_inverse * (d_bn_out - mask * (grad_bn_shift + centred * grad_bn_gain) / count)
        )
        d_mixed = d_mixed.astype(jnp.bfloat16)
        d_mixed_wide = padded_2(d_mixed, (("seq", 0),), reach)
        d_mixed_value = d_mixed.astype(jnp.float32)
        d_gated = jnp.zeros((frames_here, width), jnp.float32)
        kernel_rows = []
        for offset in range(kernel_size):
            same = (wide_segment[offset : offset + frames_here] == own_segment).astype(jnp.float32)[
                :, None
            ]
            shifted_in = gated_wide[offset : offset + frames_here].astype(jnp.float32)
            kernel_rows.append(jnp.sum(d_mixed_value * shifted_in * same, axis=0))
            back = 2 * reach - offset
            same_back = (wide_segment[back : back + frames_here] == own_segment).astype(jnp.float32)[
                :, None
            ]
            d_gated = (
                d_gated
                + kernel[offset]
                * d_mixed_wide[back : back + frames_here].astype(jnp.float32)
                * same_back
            )
        d_pointwise = jnp.concatenate(
            [d_gated * sigma_half, d_gated * gate_half * sigma_half * (1.0 - sigma_half)], axis=1
        ).astype(jnp.bfloat16)
        d_conv_norm, gain_two, shift_two = norm_backward(
            transposed_right(d_pointwise, gathered[6]), conv_unit, conv_inverse, norm_gains[2]
        )
        d_attn_res = d_conv_res + d_conv_norm
        attn_branch = d_attn_res.astype(jnp.bfloat16)
    else:
        d_attn_res, attn_branch, conv_branch, d_pointwise, sums = conv_fast(
            cube,
            kernel_size,
            (
                d_conv_res,
                norms,
                marks,
                stats,
                centred,
                gated_wide,
                gate_half,
                sigma_half,
                conv_unit,
                conv_inverse,
            ),
            (gathered[6], gathered[7]),
            False,
        )
        kernel_rows = [sums[offset] for offset in range(kernel_size)]
        gain_two, shift_two, grad_bn_gain, grad_bn_shift = sums[8], sums[9], sums[10], sums[11]
    if cube is None:
        d_context = (
            transposed_right(attn_branch, gathered[5])
            .astype(jnp.bfloat16)
            .reshape(frames_here, HEADS, -1)
        )
        d_context_heads = lax.all_to_all(d_context, "seq", split_axis=1, concat_axis=0, tiled=True)
        d_query_heads, d_key_heads, d_value_heads, d_table = attention_backward(
            query_heads,
            key_heads,
            value_heads,
            rel_table,
            group_segment,
            log_total,
            d_context_heads,
            block_rows,
            REL_LEFT,
            REL_RIGHT,
        )
        d_query, d_keys, d_values = (
            lax.all_to_all(d_query_heads, "seq", split_axis=0, concat_axis=1, tiled=True),
            lax.all_to_all(d_key_heads, "seq", split_axis=0, concat_axis=1, tiled=True),
            lax.all_to_all(d_value_heads, "seq", split_axis=0, concat_axis=1, tiled=True),
        )
        d_query = d_query.reshape(frames_here, width)
        d_keys = d_keys.reshape(frames_here, width)
        d_values = d_values.reshape(frames_here, width)
        d_attn_hidden = (
            transposed_right(d_query, gathered[2])
            + transposed_right(d_keys, gathered[3])
            + transposed_right(d_values, gathered[4])
        )
        heads_in = jnp.concatenate([d_query, d_keys, d_values], axis=1)
    else:
        d_attn_hidden, heads_in, d_table = attend_back_fast(
            cube, attn_branch, heads_kept, probs_kept, table, gathered[2:6]
        )
        d_table = d_table[: rel_table.shape[0]]
    d_attn_norm, gain_one, shift_one = norm_backward(
        d_attn_hidden, attn_unit, attn_inverse, norm_gains[1]
    )
    d_first_res = d_attn_res + d_attn_norm
    d_input, grad_one_in, grad_one_out, gain_zero, shift_zero = ffn_backward(
        d_first_res, kept_first, norm_gains[0], gathered[0], gathered[1], cube, 10
    )
    gains_local = jnp.stack([gain_zero, gain_one, gain_two, gain_three, gain_four])
    shifts_local = jnp.stack([shift_zero, shift_one, shift_two, shift_three, shift_four])
    kernel_local = jnp.stack(kernel_rows)
    shards, (grad_gains, grad_biases, grad_depth, grad_rel) = gradient_shards(
        (
            grad_two_out,
            grad_two_in,
            grad_one_in,
            grad_one_out,
            (conv_hidden, d_pointwise),
            (attn_hidden, heads_in),
            (conv_swish, conv_branch),
            (context, attn_branch),
        ),
        (gains_local, shifts_local, kernel_local, d_table),
        cube,
    )
    two_out, two_in, one_in, one_out, conv_in, attn_in, conv_out, attn_out = shards
    return (
        final_norm.astype(jnp.bfloat16),
        d_input.astype(jnp.bfloat16),
        one_in,
        one_out,
        attn_in[:, :width],
        attn_in[:, width : 2 * width],
        attn_in[:, 2 * width :],
        attn_out,
        conv_in,
        conv_out,
        two_in,
        two_out,
        grad_depth,
        grad_rel,
        grad_gains,
        grad_biases,
        grad_bn_gain,
        grad_bn_shift,
        sample_variance,
    )


def solution(mesh):
    placed = (
        P(("batch", "seq"), None),
        P("batch", None),
        P(("batch", "seq"), None),
        P(("batch", "seq"), None),
        P(("batch", "seq"), None),
        P(("batch", "seq"), None),
        P(("batch", "seq"), None),
        P(("batch", "seq"), None),
        P(("batch", "seq"), None),
        P(("batch", "seq"), None),
        P(("batch", "seq"), None),
        P(("batch", "seq"), None),
        P(("batch", "seq"), None),
        P(),
        P(),
        P(),
        P(),
        P(),
        P(),
    )
    return jax.shard_map(
        on_device,
        mesh=mesh,
        in_specs=placed,
        out_specs=(
            P(("batch", "seq"), None),
            P(("batch", "seq"), None),
            P(("batch", "seq"), None),
            P(("batch", "seq"), None),
            P(("batch", "seq"), None),
            P(("batch", "seq"), None),
            P(("batch", "seq"), None),
            P(("batch", "seq"), None),
            P(("batch", "seq"), None),
            P(("batch", "seq"), None),
            P(("batch", "seq"), None),
            P(("batch", "seq"), None),
            P(),
            P(),
            P(),
            P(),
            P(),
            P(),
            P(),
        ),
        check_vma=False,
    )
```

```python
import functools
import math

import jax
import jax.numpy as jnp
from jax import lax
from jax.experimental import pallas as pl
from jax.experimental.pallas import tpu as pltpu
from jax.sharding import PartitionSpec as P

MESH = pl.DeviceIdType.MESH
AXES = ("batch", "seq")
ALL_SHARES = (3, 1, 0)
ROWS = 64
PACE = 1
TURNS = (1, 0, 3, 4, 5, 8, 6, 2, 7, 9)
HALF_SHARES = (5, 3)
PAIR_SHARES = (2, 2)

HEADS = 8
REL_LEFT = 64
REL_RIGHT = 8


epsilon = 1e-05
masked_score = -1000000000.0


def padded_2(shard, sides, width):
    for axis, dim in sides:
        peers, length = (lax.axis_size(axis), shard.shape[dim])
        up = [(i, (i + 1) % peers) for i in range(peers - 1)]
        down = [(j, i) for i, j in up]
        last = lax.slice_in_dim(shard, length - width, length, axis=dim)
        first = lax.slice_in_dim(shard, 0, width, axis=dim)
        before = lax.ppermute(last, axis, up)
        after = lax.ppermute(first, axis, down)
        shard = jnp.concatenate([before, shard, after], axis=dim)
    return shard


def matmul(left, right):
    return jnp.dot(left, right, preferred_element_type=jnp.float32)


def transposed_left(left, right):
    return lax.dot_general(
        left, right, (((0,), (0,)), ((), ())), preferred_element_type=jnp.float32
    )


def transposed_right(left, right):
    return lax.dot_general(
        left, right, (((1,), (1,)), ((), ())), preferred_element_type=jnp.float32
    )


class Cube:
    def __init__(self, batch, seq):
        self.seq_bits, self.batch_bits = (seq.bit_length() - 1, batch.bit_length() - 1)
        self.count = self.seq_bits + self.batch_bits
        self.core = self.seq_bits
        wide = (self.batch_bits - 1) // 2
        self.x = list(range(self.seq_bits))[::-1]
        self.y = list(range(self.core + 1, self.core + 1 + wide))[::-1]
        self.z = list(range(self.core + 1 + wide, self.count))[::-1]

    def bit(self, k):
        if k < self.seq_bits:
            return lax.rem(lax.axis_index("seq") // (1 << k), 2)
        return lax.rem(lax.axis_index("batch") // (1 << (k - self.seq_bits)), 2)

    def partner(self, k):
        batch, seq = (lax.axis_index("batch"), lax.axis_index("seq"))
        step = 1 - 2 * self.bit(k)
        if k < self.seq_bits:
            return (batch, seq + step * (1 << k))
        return (batch + step * (1 << (k - self.seq_bits)), seq)


def greet(cube, bits):
    barrier = pltpu.get_barrier_semaphore()
    for k in bits:
        pl.semaphore_signal(barrier, inc=1, device_id=cube.partner(k), device_id_type=MESH)
    pl.semaphore_wait(barrier, len(bits))


def gather_kernel(cube, plans, items, first_in, first_out, *refs):
    count = len(plans)
    shards, (hidden, before), refs = (refs[:count], refs[count : count + 2], refs[count + 2 :])
    outs, results, refs = (refs[:count], refs[count : count + 4], refs[count + 4 :])
    (send, recv, local), scratch = (refs[:3], refs[3:])
    own = [cube.bit(k) for k in range(cube.count)]
    kept = []
    for m, (bits, paired) in enumerate(plans):
        kept.append(
            pltpu.make_async_copy(
                shards[m].at[own[0]] if paired else shards[m],
                outs[m].at[tuple(own[k] for k in bits)],
                local.at[m],
            )
        )
        kept[m].start()
    greet(cube, range(cube.count))

    def copy(number, stage):
        m, order, block = flat[number]
        bits, paired = plans[m]
        lead = tuple(slice(None) if k in order[:stage] else own[k] for k in bits)
        place = outs[m].at[lead + block]
        source = place
        if stage == 0:
            source = shards[m].at[(1 - own[0],) + block] if paired else shards[m].at[block]
        return to_partner(
            cube, order[stage], source, place, send.at[number, stage], recv.at[number, stage]
        )

    flat = [item for chunk in items for item in chunk]
    numbers, at = ([], 0)
    for chunk in items:
        numbers.append(range(at, at + len(chunk)))
        at += len(chunk)
    arrive, steps = ffn_steps(
        cube, hidden, before, outs[first_in].at, outs[first_out].at, *results, *scratch
    )
    arrive[0]()
    for number in range(len(flat)):
        copy(number, 0).start()
    for one in kept:
        one.wait()
    most = max(len(order) for _, order, _ in flat)
    waiting = {m: sum(item[0] == m for item in flat) for m in (first_in, first_out)}
    pending = []
    for turn in range(len(items) + most):
        for stage in range(most):
            for late in (0, 1):
                chunk = turn - stage - late
                if not 0 <= chunk < len(items):
                    continue
                for number in numbers[chunk]:
                    stages = len(flat[number][1])
                    if stage >= stages or late != (stage == stages - 1):
                        continue
                    copy(number, stage).wait_recv()
                    if stage + 1 < stages:
                        copy(number, stage + 1).start()
                    elif flat[number][0] in waiting:
                        waiting[flat[number][0]] -= 1
        if waiting[first_in] == 0:
            waiting[first_in] = -1
            arrive[1]()
            pending += steps[0]
        if waiting[first_out] == 0 and waiting[first_in] < 0:
            waiting[first_out] = -1
            arrive[2]()
            pending += steps[1]
        for _ in range(PACE):
            if pending:
                pending.pop(0)()
    for step in pending:
        step()
    for number, (_, order, _) in enumerate(flat):
        for stage in range(len(order)):
            copy(number, stage).wait_send()


def row_parts(rows, shares):
    units, total, at, upto, parts = (rows // 8, sum(shares), 0, 0, [])
    for share in shares:
        upto += share
        end = (units * upto + total // 2) // total
        parts.append((at * 8, (end - at) * 8))
        at = end
    return parts


def gather_fast(shards, kinds, cube, hidden, values, first_in, first_out):
    core, x, y, z = ([cube.core], cube.x, cube.y, cube.z)
    every = list(range(cube.count))[::-1]
    plans, items, shapes = ([], [], [])
    for m, (shard, kind) in enumerate(zip(shards, kinds)):
        if kind == "all":
            bits, shares = (every, ALL_SHARES)
            orders = [z + y + x + core, z + x + y + core, x + y + z + core]
        else:
            bits = every if kind == "pair" else every[:-1]
            first = x if kind == "pair" else []
            orders = [first + z + y + core, first + y + z + core]
            shares = PAIR_SHARES if kind == "pair" else HALF_SHARES
        plans.append((bits, kind == "pair"))
        shapes.append((2,) * len(bits) + shard.shape[-2:])
        rows, columns = (min(ROWS, shard.shape[-2]), min(2048, shard.shape[-1]))
        for row in range(0, shard.shape[-2], rows):
            for column in range(0, shard.shape[-1], columns):
                items.append(
                    [
                        (m, order, (pl.ds(row + a, w), pl.ds(column, columns)))
                        for order, (a, w) in zip(orders, row_parts(rows, shares))
                        if w
                    ]
                )
    count, copies = (len(shards), sum(len(chunk) for chunk in items))
    local, width = values.shape
    wide = shards[first_in].shape[-1]
    vmem = pl.BlockSpec(memory_space=pltpu.VMEM)
    outs = pl.pallas_call(
        functools.partial(gather_kernel, cube, plans, items, first_in, first_out),
        out_shape=[
            jax.ShapeDtypeStruct(shape, shard.dtype) for shape, shard in zip(shapes, shards)
        ]
        + [
            jax.ShapeDtypeStruct((local, width), jnp.float32),
            jax.ShapeDtypeStruct((2 * local, wide), jnp.float32),
            jax.ShapeDtypeStruct((2 * local, wide), jnp.bfloat16),
            jax.ShapeDtypeStruct((2 * local, width), jnp.bfloat16),
        ],
        in_specs=[pl.BlockSpec(memory_space=pl.ANY)] * count + [vmem] * 2,
        out_specs=[pl.BlockSpec(memory_space=pl.ANY)] * count + [vmem] * 4,
        scratch_shapes=[
            pltpu.SemaphoreType.DMA((copies, cube.count)),
            pltpu.SemaphoreType.DMA((copies, cube.count)),
            pltpu.SemaphoreType.DMA((count,)),
            pltpu.VMEM(shapes[first_in], jnp.bfloat16),
            pltpu.VMEM(shapes[first_out], jnp.bfloat16),
            pltpu.VMEM((2 * local, width), jnp.bfloat16),
            pltpu.VMEM((local, width), jnp.bfloat16),
            pltpu.VMEM((local, width), jnp.bfloat16),
            pltpu.SemaphoreType.DMA((5,)),
            pltpu.SemaphoreType.DMA((3,)),
            pltpu.SemaphoreType.DMA((3,)),
        ],
        compiler_params=pltpu.CompilerParams(
            collective_id=0, has_side_effects=True, vmem_limit_bytes=48 * 1024 * 1024
        ),
        name="gather_weights",
    )(*shards, hidden, values)
    whole = tuple(out.reshape(-1, shard.shape[-1]) for out, shard in zip(outs, shards))
    return whole, outs[count:]


def gradient_kernel(cube, shapes, kinds, tile, *refs):
    count = len(shapes)
    lefts, rights, refs = (refs[:count], refs[count : 2 * count], refs[2 * count :])
    value, out, crossed, value_out, refs = (refs[0], refs[1], refs[2], refs[3], refs[4:])
    near, far, whole = (refs[:count], refs[count : 2 * count], refs[2 * count : 3 * count])
    refs = refs[3 * count :]
    order = cube.y + cube.z[::-1]
    stages = len(order)
    total, sent, recv_at, refs = (refs[0], refs[1 : 1 + stages], refs[1 + stages : 1 + 2 * stages], refs[1 + 2 * stages :])
    cross, value_sent, value_held, refs = (refs[0], refs[1], refs[2], refs[3:])
    x_send, x_recv, local, c_send, c_recv, send, recv, cross_send, cross_recv, v_send, v_recv = refs
    rows, columns = tile
    number, depth = (out.shape[0], total.shape[0])
    lags = [3 + 2 * stage for stage in range(stages)]
    x, c = (cube.bit(0), cube.bit(cube.core))
    dims = sorted(order, reverse=True)
    bits = [cube.bit(k) for k in order]
    every = (slice(None),) * stages
    tokens = near[0].shape[-1] // 2
    pairs = [m for m in range(count) if kinds[m] == "pair"]
    own_lanes = pl.ds(pl.multiple_of(x * tokens, tokens), tokens)

    def spot(stage, flip):
        left = [k for k in dims if k not in order[:stage]]
        side = 1 - bits[stage] if flip else bits[stage]
        return tuple(side if k == order[stage] else slice(None) for k in left)

    def along_x(m):
        if kinds[m] != "all":
            return []
        return [
            to_partner(
                cube,
                0,
                lefts[m].at[every + (slice(None), 1 - x)],
                near[m].at[every + (slice(None), slice(None), own_lanes)],
                x_send.at[m, 0],
                x_recv.at[m, 0],
            ),
            to_partner(
                cube, 0, rights[m], whole[m].at[c, own_lanes], x_send.at[m, 1], x_recv.at[m, 1]
            ),
        ]

    def at_home(m):
        if kinds[m] != "all":
            return [
                pltpu.make_async_copy(lefts[m], near[m], local.at[m, 0]),
                pltpu.make_async_copy(rights[m], whole[m].at[c], local.at[m, 1]),
            ]
        return [
            pltpu.make_async_copy(
                lefts[m].at[every + (slice(None), x)],
                near[m].at[every + (slice(None), slice(None), own_lanes)],
                local.at[m, 0],
            ),
            pltpu.make_async_copy(rights[m], whole[m].at[c, own_lanes], local.at[m, 1]),
        ]

    def along_core(m):
        return [
            to_partner(
                cube,
                cube.core,
                near[m].at[every + (1 - c,)],
                far[m],
                c_send.at[m, 0],
                c_recv.at[m, 0],
            ),
            to_partner(
                cube, cube.core, whole[m].at[c], whole[m].at[c], c_send.at[m, 1], c_recv.at[m, 1]
            ),
        ]

    def remote(stage, chunk):
        return to_partner(
            cube,
            order[stage],
            sent[stage].at[chunk],
            recv_at[stage].at[chunk],
            send.at[stage, chunk],
            recv.at[stage, chunk],
        )

    def reduce(step):
        for stage in range(stages):
            chunk = step - lags[stage]

            @pl.when((chunk >= 0) & (chunk < number))
            def _(stage=stage, chunk=chunk):
                slot = lax.rem(chunk, depth)
                remote(stage, chunk).wait_recv()
                mine = tuple(
                    bits[order.index(k)] if k in order[: stage + 1] else slice(None) for k in dims
                )
                arrived = recv_at[stage]
                if stage + 1 == stages:
                    out[chunk] = total[(slot,) + mine] + arrived[chunk].astype(jnp.float32)
                else:
                    away, home = (spot(stage + 1, True), spot(stage + 1, False))
                    full = list(mine)
                    full[dims.index(order[stage + 1])] = 1 - bits[stage + 1]
                    sent[stage + 1][chunk] = (
                        total[(slot,) + tuple(full)]
                        + arrived[(chunk,) + away].astype(jnp.float32)
                    ).astype(jnp.bfloat16)
                    remote(stage + 1, chunk).start()
                    full[dims.index(order[stage + 1])] = bits[stage + 1]
                    total[(slot,) + tuple(full)] += arrived[(chunk,) + home].astype(jnp.float32)

    def value_copy(k):
        return to_partner(
            cube, k, value_sent.at[k], value_held.at[k], v_send.at[k], v_recv.at[k]
        )

    def value_turn(k):
        if k == 0:
            value_sent[0] = value[...]
        elif k <= cube.count:
            value_copy(k - 1).wait_recv()
            sum_here = value_sent[k - 1] + value_held[k - 1]
            if k < cube.count:
                value_sent[k] = sum_here
            else:
                value_out[...] = sum_here
        if k < cube.count:
            value_copy(k).start()

    def cross_copy(i, first):
        away = pl.ds(first + (1 - x) * 2, 2)
        return to_partner(cube, 0, out.at[away], cross.at[i], cross_send.at[i], cross_recv.at[i])

    greet(cube, range(cube.count))
    value_turn(0)
    for m in range(count):
        for copy in along_x(m) + at_home(m):
            copy.start()
    def to_core(m):
        for copy in at_home(m):
            copy.wait()
        for copy in along_x(m):
            copy.wait_recv()
        for copy in along_core(m):
            copy.start()

    first, firsts = (0, {})
    to_core(0)
    for m in range(count):
        firsts[m] = first
        if m > 0:
            value_turn(m)
        for copy in along_core(m):
            copy.wait_recv()
        if m + 1 < count:
            to_core(m + 1)
        down, across = shapes[m]

        def one(j, carry, m=m, first=first, down=down, across=across):
            chunk = first + j
            slot = lax.rem(chunk, depth)
            row = pl.ds(pl.multiple_of((j // across) * rows, rows), rows)
            column = pl.ds(pl.multiple_of(lax.rem(j, across) * columns, columns), columns)

            def half(flip):
                place = spot(0, flip)
                one_left = near[m][place + (c, row, slice(None))]
                two_left = far[m][place + (row, slice(None))]
                shape = one_left.shape[:-1] + (columns,)
                one_left = one_left.reshape(-1, 2 * tokens)
                two_left = two_left.reshape(-1, 2 * tokens)
                result = matmul(one_left, whole[m][c, :, column]) + matmul(
                    two_left, whole[m][1 - c, :, column]
                )
                return result.reshape(shape)

            sent[0][chunk] = half(True).astype(jnp.bfloat16)
            remote(0, chunk).start()
            total[(slot,) + spot(0, False)] = half(False)
            reduce(chunk)
            return carry

        lax.fori_loop(0, down * across, one, 0)
        first += down * across

    def drain(step, carry):
        reduce(step)
        return carry

    for k in range(count, cube.count + 1):
        value_turn(k)
    for i, m in enumerate(pairs):
        cross_copy(i, firsts[m]).start()
    lax.fori_loop(number, number + lags[-1] + 1, drain, 0)
    for i, m in enumerate(pairs):
        cross_copy(i, firsts[m]).wait_recv()
        crossed[i, x] = out[pl.ds(firsts[m] + x * 2, 2)]
        crossed[i, 1 - x] = cross[i]
        cross_copy(i, firsts[m]).wait_send()
    for k in range(cube.count):
        value_copy(k).wait_send()
    for m in range(count):
        for copy in along_x(m) + along_core(m):
            copy.wait_send()

    def finish(chunk, carry):
        for stage in range(stages):
            remote(stage, chunk).wait_send()
        return carry

    lax.fori_loop(0, number, finish, 0)


def gradients_fast(pairs, kinds, value, cube, rows, columns):
    order = cube.y + cube.z[::-1]
    stages, count = (len(order), len(pairs))
    lefts, rights, shapes, near, far, whole = ([], [], [], [], [], [])
    for (left, right), kind in zip(pairs, kinds):
        lead = (2,) * stages
        if kind == "all":
            block, tokens = (left.shape[1] >> cube.count, left.shape[0])
            lefts.append(left.T.reshape(lead + (2, 2, block, tokens)))
        else:
            block, tokens = (left.shape[1] >> (cube.count - 1), left.shape[0] // 2)
            lefts.append(left.T.reshape(lead + (2, block, 2 * tokens)))
        rights.append(right)
        shapes.append((block // rows, right.shape[1] // columns))
        near.append(pltpu.VMEM(lead + (2, block, 2 * tokens), jnp.bfloat16))
        far.append(pltpu.VMEM(lead + (block, 2 * tokens), jnp.bfloat16))
        whole.append(pltpu.VMEM((2, 2 * tokens, right.shape[1]), jnp.bfloat16))
    number, tile = (sum(down * across for down, across in shapes), (rows, columns))
    held = [
        pltpu.VMEM((number,) + (2,) * (stages - 1 - stage) + tile, jnp.bfloat16)
        for stage in range(stages)
    ]
    depth = 3 + 2 * (stages - 1) + 1
    paired = kinds.count("pair")
    vmem = pl.BlockSpec(memory_space=pltpu.VMEM)
    values = pltpu.VMEM((cube.count,) + value.shape, value.dtype)
    out, crossed, value = pl.pallas_call(
        functools.partial(gradient_kernel, cube, shapes, kinds, tile),
        out_shape=[
            jax.ShapeDtypeStruct((number,) + tile, jnp.float32),
            jax.ShapeDtypeStruct((paired, 2, 2) + tile, jnp.float32),
            jax.ShapeDtypeStruct(value.shape, value.dtype),
        ],
        in_specs=[pl.BlockSpec(memory_space=pl.ANY)] * (2 * count) + [vmem],
        out_specs=[vmem] * 3,
        scratch_shapes=near
        + far
        + whole
        + [pltpu.VMEM((depth,) + (2,) * stages + tile, jnp.float32)]
        + held
        + held
        + [pltpu.VMEM((paired, 2) + tile, jnp.float32), values, values]
        + [pltpu.SemaphoreType.DMA((count, 2))] * 5
        + [pltpu.SemaphoreType.DMA((stages, number))] * 2
        + [pltpu.SemaphoreType.DMA((paired,))] * 2
        + [pltpu.SemaphoreType.DMA((cube.count,))] * 2,
        compiler_params=pltpu.CompilerParams(
            collective_id=4, has_side_effects=True, vmem_limit_bytes=60 * 1024 * 1024
        ),
        name="reduce_gradients",
    )(*lefts, *rights, value)
    results, at, pair = ([], 0, 0)
    for (down, across), right, kind in zip(shapes, rights, kinds):
        if kind == "pair":
            piece = crossed[pair].reshape(2, 2, rows, columns // 128, 128)
            results.append(piece.transpose(2, 1, 3, 0, 4).reshape(rows, 4 * columns))
            pair += 1
        else:
            piece = out[at : at + down * across].reshape(down, across, rows, columns)
            results.append(piece.transpose(0, 2, 1, 3).reshape(down * rows, right.shape[1]))
        at += down * across
    return results, value


def flat_pack(values):
    flat = jnp.concatenate([value.reshape(-1) for value in values])
    size = -(-flat.shape[0] // 8192) * 8192
    return jnp.pad(flat, (0, size - flat.shape[0])).reshape(-1, 1024)


def flat_unpack(flat, values):
    flat, out, at = (flat.reshape(-1), [], 0)
    for value in values:
        out.append(flat[at : at + value.size].reshape(value.shape))
        at += value.size
    return tuple(out)


def gradient_shards(pairs, values, cube):
    if cube is None:
        results = []
        for left, right in pairs:
            whole = transposed_left(left, right)
            flat = whole.reshape(-1, 128)
            shard = lax.psum_scatter(flat, AXES, scatter_dimension=0, tiled=True)
            results.append(shard.reshape(-1, whole.shape[1]))
        return results, lax.psum(values, AXES)
    kinds = ["half", "pair", "pair", "half"] + ["all"] * 4
    results, flat = gradients_fast(pairs, kinds, flat_pack(values), cube, 32, 1024)
    return results, flat_unpack(flat, values)


def parities(shard):
    rows, columns = shard.shape
    return shard.reshape(rows, columns // 256, 2, 128).transpose(2, 0, 1, 3).reshape(2, rows, -1)


def gather_all(shards, cube, hidden, values):
    if cube is None:
        return tuple(lax.all_gather(shard, AXES, axis=0, tiled=True) for shard in shards), None
    kinds = ("pair", "half") + ("all",) * 6 + ("pair", "half")
    shards = [parities(shard) if kind == "pair" else shard for shard, kind in zip(shards, kinds)]
    turns = TURNS
    outs, first = gather_fast(
        [shards[m] for m in turns],
        [kinds[m] for m in turns],
        cube,
        hidden,
        values,
        turns.index(0),
        turns.index(1),
    )
    return tuple(outs[turns.index(m)] for m in range(len(shards))), first


def distance_rows(group, left, right, backwards):
    row = lax.broadcasted_iota(jnp.int32, (group, 128), 0)
    row = group - 1 - row if backwards else row
    distance = jnp.where(row >= group // 2, row - group, row)
    index = jnp.clip(distance, -left, right) + left
    hit = index == lax.broadcasted_iota(jnp.int32, (group, 128), 1)
    return jnp.where(hit, 1.0, 0.0).astype(jnp.bfloat16)


def halves(cube, rows, half):
    mine = cube.bit(0)
    return (
        pl.ds(pl.multiple_of(mine * half, half), half),
        pl.ds(pl.multiple_of((1 - mine) * half, half), half),
        pl.ds(pl.multiple_of(mine * rows, rows), rows),
        pl.ds(pl.multiple_of((1 - mine) * rows, rows), rows),
    )


def to_partner(cube, k, source, target, send, recv):
    return pltpu.make_async_remote_copy(
        src_ref=source,
        dst_ref=target,
        send_sem=send,
        recv_sem=recv,
        device_id=cube.partner(k),
        device_id_type=MESH,
    )


def attend_kernel(cube, left, right, *refs):
    hidden, before, same, table, query_w, key_w, value_w, out_w = refs[:8]
    after, context, heads_out, probs_out = refs[8:12]
    weights, heads_in, away, wide, context_away, load, send, recv, head_send, head_recv = refs[12:]
    rows, width = hidden.shape
    group, half = (2 * rows, width // 2)
    heads = half // 128
    scale = 1.0 / math.sqrt(128)
    mine = cube.bit(0)
    own_columns, away_columns, own_rows, away_rows = halves(cube, rows, half)
    loads = []
    for i, matrix in enumerate((query_w, key_w, value_w, out_w)):
        loads.append(pltpu.make_async_copy(matrix, weights.at[i], load.at[i]))
        loads[i].start()
    greet(cube, [0])

    def exchange(i):
        return to_partner(
            cube, 0, away.at[i], heads_in.at[i, own_rows], send.at[i], recv.at[i]
        )

    def context_copy(head):
        column = pl.ds(pl.multiple_of(mine * half + head * 128, 128), 128)
        return to_partner(
            cube, 0, context_away.at[head], wide.at[:, column], head_send.at[head], head_recv.at[head]
        )

    for i in range(3):
        loads[i].wait()
        away[i] = matmul(hidden[...], weights[i, :, away_columns]).astype(jnp.bfloat16)
        exchange(i).start()
    for i in range(3):
        heads_in[i, own_rows, :] = matmul(hidden[...], weights[i, :, own_columns]).astype(
            jnp.bfloat16
        )
    spread = matmul(distance_rows(group, left, right, False), table[...]).astype(jnp.bfloat16)
    loads[3].wait()
    for i in range(3):
        exchange(i).wait_recv()

    def one_head(head, carry):
        column = pl.ds(pl.multiple_of(head * 128, 128), 128)
        place = pl.ds(pl.multiple_of(mine * half + head * 128, 128), 128)
        query, keys, values = (heads_in[i, :, column] for i in range(3))
        relative = pltpu.roll(transposed_right(query, spread), 0, 1, stride=1, stride_axis=0)
        scores = scale * (transposed_right(query, keys) + relative)
        scores = jnp.where(same[...] > 0, scores, masked_score)
        weight = jnp.exp(scores - jnp.max(scores, axis=1, keepdims=True))
        probs_out[head] = weight / jnp.sum(weight, axis=1, keepdims=True)
        there = probs_out[head, away_rows, :].astype(jnp.bfloat16)
        context_away[head] = matmul(there, values).astype(jnp.bfloat16)
        context_copy(head).start()
        here = probs_out[head, own_rows, :].astype(jnp.bfloat16)
        wide[:, place] = matmul(here, values).astype(jnp.bfloat16)
        return carry

    lax.fori_loop(0, heads, one_head, 0)
    heads_out[...] = heads_in[...]
    after[...] = before[...] + matmul(wide[:, own_columns], weights[3, own_columns, :])
    for head in range(heads):
        context_copy(head).wait_recv()
    after[...] += matmul(wide[:, away_columns], weights[3, away_columns, :])
    context[...] = wide[...]
    for i in range(3):
        exchange(i).wait_send()
    for head in range(heads):
        context_copy(head).wait_send()


def attend_fast(cube, hidden, before, same, table, matrices):
    rows, width = hidden.shape
    group, half = (2 * rows, width // 2)
    heads = half // 128
    vmem = pl.BlockSpec(memory_space=pltpu.VMEM)
    return pl.pallas_call(
        functools.partial(attend_kernel, cube, REL_LEFT, REL_RIGHT),
        out_shape=[
            jax.ShapeDtypeStruct((rows, width), jnp.float32),
            jax.ShapeDtypeStruct((rows, width), jnp.bfloat16),
            jax.ShapeDtypeStruct((3, group, half), jnp.bfloat16),
            jax.ShapeDtypeStruct((heads, group, group), jnp.float32),
        ],
        in_specs=[vmem] * 4 + [pl.BlockSpec(memory_space=pl.ANY)] * 4,
        out_specs=[vmem] * 4,
        scratch_shapes=[
            pltpu.VMEM((4, width, width), jnp.bfloat16),
            pltpu.VMEM((3, group, half), jnp.bfloat16),
            pltpu.VMEM((3, rows, half), jnp.bfloat16),
            pltpu.VMEM((rows, width), jnp.bfloat16),
            pltpu.VMEM((heads, rows, 128), jnp.bfloat16),
            pltpu.SemaphoreType.DMA((4,)),
            pltpu.SemaphoreType.DMA((3,)),
            pltpu.SemaphoreType.DMA((3,)),
            pltpu.SemaphoreType.DMA((heads,)),
            pltpu.SemaphoreType.DMA((heads,)),
        ],
        compiler_params=pltpu.CompilerParams(
            collective_id=5, has_side_effects=True, vmem_limit_bytes=48 * 1024 * 1024
        ),
        name="attend",
    )(hidden, before, same, table, *matrices)


def attend_back_kernel(cube, left, right, *refs):
    branch, heads_in, probs_in, table, query_w, key_w, value_w, out_w = refs[:8]
    d_hidden, d_heads, d_table = refs[8:11]
    weights, d_context, d_context_away, wide, away, load, send, recv, head_send, head_recv = refs[
        11:
    ]
    rows, width = branch.shape
    group, half = (2 * rows, width // 2)
    heads = half // 128
    scale = 1.0 / math.sqrt(128)
    mine = cube.bit(0)
    own_columns, away_columns, own_rows, away_rows = halves(cube, rows, half)
    loads = []
    for i, matrix in enumerate((out_w, query_w, key_w, value_w)):
        loads.append(pltpu.make_async_copy(matrix, weights.at[i], load.at[i]))
        loads[i].start()
    greet(cube, [0])
    loads[0].wait()
    exchange = to_partner(
        cube, 0, d_context_away, d_context.at[own_rows], send.at[0], recv.at[0]
    )
    d_context_away[...] = transposed_right(branch[...], weights[0, away_columns, :]).astype(
        jnp.bfloat16
    )
    exchange.start()
    d_context[own_rows, :] = transposed_right(branch[...], weights[0, own_columns, :]).astype(
        jnp.bfloat16
    )
    spread = distance_rows(group, left, right, True)
    down = lax.broadcasted_iota(jnp.int32, (group, group), 0)
    across = lax.broadcasted_iota(jnp.int32, (group, group), 1)
    mirror = jnp.where(down + across == group - 1, 1.0, 0.0).astype(jnp.bfloat16)
    d_table[...] = jnp.zeros_like(d_table)
    exchange.wait_recv()

    def head_copy(head, i):
        column = pl.ds(pl.multiple_of(i * width + mine * half + head * 128, 128), 128)
        return to_partner(
            cube,
            0,
            away.at[head, i, away_rows],
            wide.at[:, column],
            head_send.at[head, i],
            head_recv.at[head, i],
        )

    def one_head(head, carry):
        column = pl.ds(pl.multiple_of(head * 128, 128), 128)
        query, keys, values = (heads_in[i, :, column] for i in range(3))
        d_rows = d_context[:, column]
        probs = probs_in[head]
        d_probs = transposed_right(d_rows, values)
        weighted = jnp.sum(probs * d_probs, axis=1, keepdims=True)
        d_scores = (probs * (d_probs - weighted)).astype(jnp.bfloat16)
        away[head, 2] = transposed_left(probs.astype(jnp.bfloat16), d_rows).astype(jnp.bfloat16)
        head_copy(head, 2).start()
        away[head, 1] = (scale * transposed_left(d_scores, query)).astype(jnp.bfloat16)
        head_copy(head, 1).start()
        turned = pltpu.roll(matmul(d_scores, mirror), 0, 1, stride=1, stride_axis=0)
        bins = (scale * matmul(turned.astype(jnp.bfloat16), spread)).astype(jnp.bfloat16)
        away[head, 0] = (scale * matmul(d_scores, keys) + matmul(bins, table[...])).astype(
            jnp.bfloat16
        )
        head_copy(head, 0).start()
        d_table[...] += transposed_left(bins, query)
        for i in range(3):
            place = pl.ds(pl.multiple_of(i * width + mine * half + head * 128, 128), 128)
            wide[:, place] = away[head, i, own_rows, :]
        return carry

    lax.fori_loop(0, heads, one_head, 0)
    for i in range(3):
        loads[1 + i].wait()

    def part(i, offset, columns):
        place = pl.ds(pl.multiple_of(i * width + offset * half, half), half)
        return transposed_right(wide[:, place], weights[1 + i, :, columns])

    total = part(0, mine, own_columns)
    for i in range(1, 3):
        total += part(i, mine, own_columns)
    d_hidden[...] = total
    for head in range(heads):
        for i in range(3):
            head_copy(head, i).wait_recv()
    total = part(0, 1 - mine, away_columns)
    for i in range(1, 3):
        total += part(i, 1 - mine, away_columns)
    d_hidden[...] += total
    d_heads[...] = wide[...]
    exchange.wait_send()
    for head in range(heads):
        for i in range(3):
            head_copy(head, i).wait_send()


def attend_back_fast(cube, branch, heads_in, probs, table, matrices):
    rows, width = branch.shape
    group, half = (2 * rows, width // 2)
    heads = half // 128
    vmem = pl.BlockSpec(memory_space=pltpu.VMEM)
    return pl.pallas_call(
        functools.partial(attend_back_kernel, cube, REL_LEFT, REL_RIGHT),
        out_shape=[
            jax.ShapeDtypeStruct((rows, width), jnp.float32),
            jax.ShapeDtypeStruct((rows, 3 * width), jnp.bfloat16),
            jax.ShapeDtypeStruct((128, 128), jnp.float32),
        ],
        in_specs=[vmem] * 4 + [pl.BlockSpec(memory_space=pl.ANY)] * 4,
        out_specs=[vmem] * 3,
        scratch_shapes=[
            pltpu.VMEM((4, width, width), jnp.bfloat16),
            pltpu.VMEM((group, half), jnp.bfloat16),
            pltpu.VMEM((rows, half), jnp.bfloat16),
            pltpu.VMEM((rows, 3 * width), jnp.bfloat16),
            pltpu.VMEM((heads, 3, group, 128), jnp.bfloat16),
            pltpu.SemaphoreType.DMA((4,)),
            pltpu.SemaphoreType.DMA((1,)),
            pltpu.SemaphoreType.DMA((1,)),
            pltpu.SemaphoreType.DMA((heads, 3)),
            pltpu.SemaphoreType.DMA((heads, 3)),
        ],
        compiler_params=pltpu.CompilerParams(
            collective_id=6, has_side_effects=True, vmem_limit_bytes=48 * 1024 * 1024
        ),
        name="attend_back",
    )(branch, heads_in, probs, table, *matrices)


def ffn_steps(
    cube,
    hidden,
    before,
    weight_in,
    weight_out,
    after,
    act,
    swish,
    hidden_out,
    into,
    outof,
    both,
    away,
    arrived,
    load,
    send,
    recv,
):
    rows, width = hidden.shape
    depth, wide = into.shape[-2:]
    step, half = (wide // 4, width // 2)
    _, _, own_rows, away_rows = halves(cube, rows, half)
    exchange = to_partner(cube, 0, both.at[own_rows], both.at[own_rows], send.at[0], recv.at[0])
    lead = (slice(None),) * (len(into.shape) - 2)

    def load_in(q):
        part = lead + (slice(None), pl.ds(q * step, step))
        return pltpu.make_async_copy(weight_in[part], into.at[part], load.at[q])

    def load_out():
        whole = (slice(None),) * len(outof.shape)
        return pltpu.make_async_copy(weight_out[whole], outof.at[whole], load.at[4])

    def back(q):
        part = pl.ds(q * half, half)
        return to_partner(
            cube, 0, away.at[:, part], arrived.at[:, part], send.at[1 + q], recv.at[1 + q]
        )

    def begin():
        both[own_rows, :] = hidden[...]
        exchange.start()

    def first_there():
        for q in range(4):
            load_in(q).start()

    def second_there():
        load_out().start()

    def activate(q, rows_here, wait):
        wait()
        part = pl.ds(q * step, step)
        weights = into[lead + (slice(None), part)].reshape(width, step)
        value = matmul(both[rows_here, :], weights)
        act[rows_here, part] = value
        swish[rows_here, part] = jax.nn.silu(value).astype(jnp.bfloat16)

    def there(q):
        if q == 0:
            load_out().wait()
        part = pl.ds(q * half, half)
        weights = outof[(slice(None),) * (len(outof.shape) - 1) + (part,)].reshape(wide, half)
        away[:, part] = matmul(swish[away_rows, :], weights).astype(jnp.bfloat16)
        back(q).start()

    def here(q):
        part = pl.ds(q * half, half)
        weights = outof[(slice(None),) * (len(outof.shape) - 1) + (part,)].reshape(wide, half)
        after[:, part] = before[:, part] + 0.5 * matmul(swish[own_rows, :], weights)

    def end():
        hidden_out[...] = both[...]
        for q in range(2):
            part = pl.ds(q * half, half)
            back(q).wait_recv()
            after[:, part] += 0.5 * arrived[:, part].astype(jnp.float32)
        exchange.wait_send()
        for q in range(2):
            back(q).wait_send()

    def nothing():
        pass

    one = [functools.partial(activate, q, own_rows, load_in(q).wait) for q in range(4)]
    one += [
        functools.partial(activate, q, away_rows, nothing if q else exchange.wait_recv)
        for q in range(4)
    ]
    two = [functools.partial(there, q) for q in range(2)]
    two += [functools.partial(here, q) for q in range(2)] + [end]
    return (begin, first_there, second_there), (one, two)


def ffn_kernel(cube, *refs):
    hidden, before, weight_in, weight_out = refs[:4]
    arrive, steps = ffn_steps(cube, hidden, before, weight_in.at, weight_out.at, *refs[4:])
    arrive[1]()
    arrive[2]()
    greet(cube, [0])
    arrive[0]()
    for step in steps[0] + steps[1]:
        step()


def ffn_back_kernel(cube, *refs):
    branch, act, weight_in, weight_out = refs[:4]
    d_hidden, d_act, branch_out = refs[4:7]
    into, outof, both, away, arrived, load, send, recv = refs[7:]
    rows, width = branch.shape
    wide = into.shape[1]
    step = wide // 4
    own_columns, away_columns, own_rows, away_rows = halves(cube, rows, width // 2)
    loads = []
    for q in range(4):
        part = pl.ds(q * step, step)
        loads.append(
            pltpu.make_async_copy(weight_out.at[part], outof.at[part], load.at[q])
        )
    loads.append(pltpu.make_async_copy(weight_in, into, load.at[4]))
    for one in loads:
        one.start()
    both[own_rows, :] = branch[...]
    greet(cube, [0])
    exchange = to_partner(
        cube, 0, both.at[own_rows], both.at[own_rows], send.at[0], recv.at[0]
    )
    exchange.start()

    def deactivate(q, rows_here):
        part = pl.ds(q * step, step)
        value = transposed_right(both[rows_here, :], outof[part, :])
        d_act[rows_here, part] = (value * swish_slope(act[rows_here, part])).astype(jnp.bfloat16)

    for q in range(4):
        loads[q].wait()
        deactivate(q, own_rows)
    loads[4].wait()
    exchange.wait_recv()
    for q in range(4):
        deactivate(q, away_rows)
    half = width // 2
    back = []
    for q in range(2):
        part = pl.ds(q * half, half)
        away[:, part] = transposed_right(d_act[away_rows, :], into[part, :]).astype(jnp.bfloat16)
        back.append(
            to_partner(
                cube, 0, away.at[:, part], arrived.at[:, part], send.at[1 + q], recv.at[1 + q]
            )
        )
        back[q].start()
    branch_out[...] = both[...]
    for q in range(2):
        part = pl.ds(q * half, half)
        d_hidden[:, part] = transposed_right(d_act[own_rows, :], into[part, :])
    for q in range(2):
        part = pl.ds(q * half, half)
        back[q].wait_recv()
        d_hidden[:, part] += arrived[:, part].astype(jnp.float32)
    for one in [exchange] + back:
        one.wait_send()


def ffn_fast(cube, first, second, weight_in, weight_out, number, backward):
    rows, width = first.shape
    wide = weight_in.shape[1]
    vmem = pl.BlockSpec(memory_space=pltpu.VMEM)
    both = jax.ShapeDtypeStruct((2 * rows, width), jnp.bfloat16)
    result = jax.ShapeDtypeStruct((rows, width), jnp.float32)
    inner = jax.ShapeDtypeStruct((2 * rows, wide), jnp.bfloat16)
    if backward:
        shapes = [result, inner, both]
    else:
        shapes = [result, jax.ShapeDtypeStruct((2 * rows, wide), jnp.float32), inner, both]
    return pl.pallas_call(
        functools.partial(ffn_back_kernel if backward else ffn_kernel, cube),
        out_shape=shapes,
        in_specs=[vmem] * 2 + [pl.BlockSpec(memory_space=pl.ANY)] * 2,
        out_specs=[vmem] * len(shapes),
        scratch_shapes=[
            pltpu.VMEM(weight_in.shape, jnp.bfloat16),
            pltpu.VMEM(weight_out.shape, jnp.bfloat16),
            pltpu.VMEM((2 * rows, width), jnp.bfloat16),
            pltpu.VMEM((rows, width), jnp.bfloat16),
            pltpu.VMEM((rows, width), jnp.bfloat16),
            pltpu.SemaphoreType.DMA((5,)),
            pltpu.SemaphoreType.DMA((3,)),
            pltpu.SemaphoreType.DMA((3,)),
        ],
        compiler_params=pltpu.CompilerParams(
            collective_id=number, has_side_effects=True, vmem_limit_bytes=48 * 1024 * 1024
        ),
        name="ffn_back" if backward else "ffn",
    )(first, second, weight_in, weight_out)


def rounds_of(cube):
    bits = list(range(cube.count))
    return [bits[i : i + 2] for i in range(0, cube.count, 2)]


def flipped(cube, bits):
    batch, seq = (lax.axis_index("batch"), lax.axis_index("seq"))
    for k in bits:
        step = 1 - 2 * cube.bit(k)
        if k < cube.seq_bits:
            seq = seq + step * (1 << k)
        else:
            batch = batch + step * (1 << (k - cube.seq_bits))
    return (batch, seq)


def masks_of(bits):
    return [[bits[0]], [bits[1]], bits] if len(bits) == 2 else [bits]


def greet_rounds(cube):
    barrier, count = (pltpu.get_barrier_semaphore(), 0)
    for bits in rounds_of(cube):
        for mask in masks_of(bits):
            pl.semaphore_signal(
                barrier, inc=1, device_id=flipped(cube, mask), device_id_type=MESH
            )
            count += 1
    pl.semaphore_wait(barrier, count)


def sum_rounds(cube, value, slots, send, recv):
    for r, bits in enumerate(rounds_of(cube)):
        mine = sum(cube.bit(k) * (1 << i) for i, k in enumerate(bits))
        slots[r, mine] = value
        copies = []
        for i, mask in enumerate(masks_of(bits)):
            copies.append(
                pltpu.make_async_remote_copy(
                    src_ref=slots.at[r, mine],
                    dst_ref=slots.at[r, mine],
                    send_sem=send.at[r, i],
                    recv_sem=recv.at[r, i],
                    device_id=flipped(cube, mask),
                    device_id_type=MESH,
                )
            )
            copies[i].start()
        for copy in copies:
            copy.wait()
        value = slots[r, 0] + slots[r, 1]
        if len(bits) == 2:
            value = value + (slots[r, 2] + slots[r, 3])
    return value


def conv_halo(cube, wide, halo_send, halo_recv, send, recv):
    rows = wide.shape[0] - 16
    mine = cube.bit(0)
    halo_send[...] = wide[pl.ds(pl.multiple_of(8 + (1 - mine) * (rows - 8), 8), 8), :]
    copy = to_partner(cube, 0, halo_send, halo_recv, send.at[0], recv.at[0])
    copy.start()
    edge = pl.ds(pl.multiple_of(mine * (rows + 8), 8), 8)
    wide[edge, :] = jnp.zeros((8, wide.shape[1]), jnp.float32)
    copy.wait()
    wide[pl.ds(pl.multiple_of((1 - mine) * (rows + 8), 8), 8), :] = halo_recv[...]


def row_sum(values):
    return jnp.sum(values, axis=0, keepdims=True)


def conv_kernel(cube, taps, *refs):
    values, norms, marks, weight_in, weight_out = refs[:5]
    after, unit_out, inverse_out, hidden, gate, sigma, wide, centred, swish, stats = refs[5:15]
    into, outof, mixed, slots, halo_send, halo_recv, load, send, recv, h_send, h_recv = refs[15:]
    rows, width = values.shape
    block = width // 4
    loads = [
        pltpu.make_async_copy(weight_in, into, load.at[0]),
        pltpu.make_async_copy(weight_out, outof, load.at[1]),
    ]
    for one in loads:
        one.start()

    def normalise(i, carry):
        part = pl.ds(pl.multiple_of(i * 32, 32), 32)
        here = values[part, :]
        away = here - jnp.mean(here, axis=1, keepdims=True)
        inverse = lax.rsqrt(jnp.mean(away * away, axis=1, keepdims=True) + epsilon)
        unit = away * inverse
        unit_out[part, :] = unit
        inverse_out[part, :] = jnp.broadcast_to(inverse, (32, 128))
        hidden[part, :] = (unit * norms[0:1, :] + norms[1:2, :]).astype(jnp.bfloat16)
        return carry

    lax.fori_loop(0, rows // 32, normalise, 0)
    greet_rounds(cube)
    loads[0].wait()

    def point(i, carry):
        part = pl.ds(pl.multiple_of(i * block, block), block)
        other = pl.ds(pl.multiple_of(width + i * block, block), block)
        level = matmul(hidden[...], into[:, part])
        open_ = jax.nn.sigmoid(matmul(hidden[...], into[:, other]))
        gate[:, part] = level
        sigma[:, part] = open_
        wide[pl.ds(8, rows), part] = (level * open_).astype(jnp.bfloat16).astype(jnp.float32)
        return carry

    lax.fori_loop(0, 4, point, 0)
    conv_halo(cube, wide, halo_send, halo_recv, h_send, h_recv)
    reach = taps // 2
    mask = marks[:, taps : taps + 1]

    def mix(i, carry):
        part = pl.ds(pl.multiple_of(i * block, block), block)
        total = jnp.zeros((rows, block), jnp.float32)
        for o in range(taps):
            total = total + norms[8 + o : 9 + o, part] * (
                wide[8 + o - reach : 8 + o - reach + rows, part] * marks[:, o : o + 1]
            )
        mixed[:, part] = total
        masked = total * mask
        stats[0:1, part] = row_sum(masked)
        stats[1:2, part] = row_sum(masked * total)
        return carry

    lax.fori_loop(0, 4, mix, 0)
    stats[2:3, :] = jnp.broadcast_to(row_sum(mask), (1, width))
    stats[3:8, :] = jnp.zeros((5, width), jnp.float32)
    total = sum_rounds(cube, stats[...], slots, send, recv)
    count = total[2:3, :]
    mean = total[0:1, :] / count
    var = total[1:2, :] / count - mean * mean
    stats[0:1, :] = mean
    stats[1:2, :] = var
    stats[2:3, :] = count
    stats[3:4, :] = lax.rsqrt(var + epsilon)

    def finish(i, carry):
        part = pl.ds(pl.multiple_of(i * block, block), block)
        middle = (mixed[:, part] - stats[0:1, part]) * stats[3:4, part]
        centred[:, part] = middle
        swish[:, part] = jax.nn.silu(middle * norms[2:3, part] + norms[3:4, part]).astype(
            jnp.bfloat16
        )
        return carry

    lax.fori_loop(0, 4, finish, 0)
    loads[1].wait()

    def project(i, carry):
        part = pl.ds(pl.multiple_of(i * block, block), block)
        after[:, part] = values[:, part] + matmul(swish[...], outof[:, part])
        return carry

    lax.fori_loop(0, 4, project, 0)


def conv_back_kernel(cube, taps, *refs):
    d_values, norms, marks, stats, centred, wide, gate, sigma, unit, inverse = refs[:10]
    weight_in, weight_out = refs[10:12]
    d_after, attn_branch, branch, d_point, sums = refs[12:17]
    into, outof, d_bn, d_wide, d_norm, pack, slots, halo_send, halo_recv, load, send, recv, h_send, h_recv = refs[17:]
    rows, width = d_values.shape
    block = width // 4
    loads = [
        pltpu.make_async_copy(weight_out, outof, load.at[0]),
        pltpu.make_async_copy(weight_in, into, load.at[1]),
    ]
    for one in loads:
        one.start()
    branch[...] = d_values[...].astype(jnp.bfloat16)
    greet_rounds(cube)
    reach = taps // 2
    mask = marks[:, taps : taps + 1]
    loads[0].wait()

    def enter(i, carry):
        part = pl.ds(pl.multiple_of(i * block, block), block)
        middle = centred[:, part]
        slope = swish_slope(middle * norms[2:3, part] + norms[3:4, part])
        value = transposed_right(branch[...], outof[part, :]) * slope
        d_bn[:, part] = value
        masked = value * mask
        pack[0:1, part] = row_sum(masked * middle)
        pack[1:2, part] = row_sum(masked)
        return carry

    lax.fori_loop(0, 4, enter, 0)
    pack[2:8, :] = jnp.zeros((6, width), jnp.float32)
    pack[...] = sum_rounds(cube, pack[...], slots, send, recv)

    def spread(i, carry):
        part = pl.ds(pl.multiple_of(i * block, block), block)
        share = mask * (pack[1:2, part] + centred[:, part] * pack[0:1, part])
        value = (
            norms[2:3, part] * stats[3:4, part] * (d_bn[:, part] - share / stats[2:3, part])
        )
        d_wide[pl.ds(8, rows), part] = value.astype(jnp.bfloat16).astype(jnp.float32)
        return carry

    lax.fori_loop(0, 4, spread, 0)
    conv_halo(cube, d_wide, halo_send, halo_recv, h_send, h_recv)
    sums[...] = jnp.zeros_like(sums)

    def unmix(i, carry):
        part = pl.ds(pl.multiple_of(i * block, block), block)
        own = d_wide[8 : 8 + rows, part]
        total = jnp.zeros((rows, block), jnp.float32)
        for o in range(taps):
            back = taps - 1 - o
            sums[o : o + 1, part] = row_sum(
                own * (wide[8 + o - reach : 8 + o - reach + rows, part] * marks[:, o : o + 1])
            )
            total = total + norms[8 + o : 9 + o, part] * (
                d_wide[8 + back - reach : 8 + back - reach + rows, part]
                * marks[:, back : back + 1]
            )
        open_ = sigma[:, part]
        other = pl.ds(pl.multiple_of(width + i * block, block), block)
        d_point[:, part] = (total * open_).astype(jnp.bfloat16)
        d_point[:, other] = (total * gate[:, part] * open_ * (1.0 - open_)).astype(jnp.bfloat16)
        return carry

    lax.fori_loop(0, 4, unmix, 0)
    loads[1].wait()

    def project(i, carry):
        part = pl.ds(pl.multiple_of(i * block, block), block)
        value = transposed_right(d_point[...], into[part, :])
        d_norm[:, part] = value
        sums[8:9, part] = row_sum(value * unit[:, part])
        sums[9:10, part] = row_sum(value)
        return carry

    lax.fori_loop(0, 4, project, 0)
    sums[10:12, :] = pack[0:2, :]

    def leave(i, carry):
        part = pl.ds(pl.multiple_of(i * 32, 32), 32)
        here = unit[part, :]
        d_unit = d_norm[part, :] * norms[0:1, :]
        value = d_values[part, :] + inverse[part, 0:1] * (
            d_unit
            - jnp.mean(d_unit, axis=1, keepdims=True)
            - here * jnp.mean(d_unit * here, axis=1, keepdims=True)
        )
        d_after[part, :] = value
        attn_branch[part, :] = value.astype(jnp.bfloat16)
        return carry

    lax.fori_loop(0, rows // 32, leave, 0)


def conv_fast(cube, taps, small, weights, forward):
    rows, width = small[0].shape
    vmem = pl.BlockSpec(memory_space=pltpu.VMEM)
    wide, full, half = ((rows + 16, width), (rows, width), (rows, 2 * width))
    single, double = (jnp.float32, jnp.bfloat16)
    if forward:
        shapes = [
            (full, single),
            (full, single),
            ((rows, 128), single),
            (full, double),
            (full, single),
            (full, single),
            (wide, single),
            (full, single),
            (full, double),
            ((8, width), single),
        ]
        own = [pltpu.VMEM(full, single)]
    else:
        shapes = [(full, single), (full, double), (full, double), (half, double), ((16, width), single)]
        own = [
            pltpu.VMEM(full, single),
            pltpu.VMEM(wide, single),
            pltpu.VMEM(full, single),
            pltpu.VMEM((8, width), single),
        ]
    rounds = len(rounds_of(cube))
    return pl.pallas_call(
        functools.partial(conv_kernel if forward else conv_back_kernel, cube, taps),
        out_shape=[jax.ShapeDtypeStruct(shape, dtype) for shape, dtype in shapes],
        in_specs=[vmem] * len(small) + [pl.BlockSpec(memory_space=pl.ANY)] * 2,
        out_specs=[vmem] * len(shapes),
        scratch_shapes=[
            pltpu.VMEM(weights[0].shape, double),
            pltpu.VMEM(weights[1].shape, double),
        ]
        + own
        + [
            pltpu.VMEM((rounds, 4, 8, width), single),
            pltpu.VMEM((8, width), single),
            pltpu.VMEM((8, width), single),
            pltpu.SemaphoreType.DMA((2,)),
            pltpu.SemaphoreType.DMA((rounds, 3)),
            pltpu.SemaphoreType.DMA((rounds, 3)),
            pltpu.SemaphoreType.DMA((1,)),
            pltpu.SemaphoreType.DMA((1,)),
        ],
        compiler_params=pltpu.CompilerParams(
            collective_id=1 if forward else 2,
            has_side_effects=True,
            vmem_limit_bytes=48 * 1024 * 1024,
        ),
        name="conv" if forward else "conv_back",
    )(*small, *weights)


def cube_of(shards, rel_table, depth_w):
    batch, seq = (lax.axis_size("batch"), lax.axis_size("seq"))
    if seq != 2 or batch < 8 or batch & (batch - 1):
        return None
    if depth_w.shape[0] > 5 or rel_table.shape[0] > 128 or rel_table.shape[1] != 128:
        return None
    if any(shard.shape[0] % 32 or shard.shape[1] % 1024 for shard in shards):
        return None
    return Cube(batch, seq)


def swish_slope(values):
    sigma = jax.nn.sigmoid(values)
    return sigma * (1.0 + values * (1.0 - sigma))


def norm_forward(values, gain, shift):
    mean = jnp.mean(values, axis=-1, keepdims=True)
    centred = values - mean
    inverse = lax.rsqrt(jnp.mean(centred * centred, axis=-1, keepdims=True) + epsilon)
    unit = centred * inverse
    return (unit * gain + shift, unit, inverse)


def norm_backward(d_out, unit, inverse, gain):
    d_unit = d_out * gain
    d_values = inverse * (
        d_unit
        - jnp.mean(d_unit, axis=-1, keepdims=True)
        - unit * jnp.mean(d_unit * unit, axis=-1, keepdims=True)
    )
    return (d_values, jnp.sum(d_out * unit, axis=0), jnp.sum(d_out, axis=0))


def ffn_forward(values, gain, shift, weight_in, weight_out, cube, number):
    normed, unit, inverse = norm_forward(values, gain, shift)
    hidden = normed.astype(jnp.bfloat16)
    if cube is not None:
        after, act, swish, hidden = ffn_fast(
            cube, hidden, values, weight_in, weight_out, number, False
        )
        return (after, (hidden, act, swish, unit, inverse))
    act = matmul(hidden, weight_in)
    swish = jax.nn.silu(act).astype(jnp.bfloat16)
    return (values + 0.5 * matmul(swish, weight_out), (hidden, act, swish, unit, inverse))


def ffn_backward(d_out, kept, gain, weight_in, weight_out, cube, number):
    hidden, act, swish, unit, inverse = kept
    d_branch = (0.5 * d_out).astype(jnp.bfloat16)
    if cube is not None:
        d_hidden, d_act, d_branch = ffn_fast(
            cube, d_branch, act, weight_in, weight_out, number, True
        )
    else:
        d_act = (transposed_right(d_branch, weight_out) * swish_slope(act)).astype(jnp.bfloat16)
        d_hidden = transposed_right(d_act, weight_in)
    d_norm, d_gain, d_shift = norm_backward(d_hidden, unit, inverse, gain)
    return (d_out + d_norm, (hidden, d_act), (swish, d_branch), d_gain, d_shift)


def segment_ids(place, ends, group):
    inside = jnp.sum((place[:, None] >= ends[None, :]).astype(jnp.int32), axis=1)
    return jnp.where((place >= 0) & (place < group), inside, -1)


def to_heads(hidden, weight, heads):
    return matmul(hidden, weight).astype(jnp.bfloat16).reshape(hidden.shape[0], heads, -1)


def spread_band(project, start, group, left, right):
    heads, rows, width = project.shape
    band = rows + width - 1
    blank = jnp.zeros_like(project[:, :, :1])
    middle = jnp.concatenate([blank, project[:, :, 1 : width - 1], blank], axis=2)
    padded = jnp.pad(middle, ((0, 0), (0, 0), (0, band + 1 - width)))
    skewed = padded.reshape(heads, rows * (band + 1))[:, : rows * band].reshape(heads, rows, band)
    canvas = jnp.zeros((heads, rows, group + left + right), jnp.float32)
    anchor = jnp.zeros((), jnp.int32)
    canvas = lax.dynamic_update_slice(canvas, skewed, (anchor, anchor, start))
    return canvas[:, :, left : left + group]


def relative_bins(grad, difference, start, width, left, right):
    heads, rows, group = grad.shape
    band = rows + width - 1
    canvas = jnp.pad(grad, ((0, 0), (0, 0), (left, right)))
    anchor = jnp.zeros((), jnp.int32)
    strip = lax.dynamic_slice(canvas, (anchor, anchor, start), (heads, rows, band))
    flat = jnp.pad(strip.reshape(heads, rows * band), ((0, 0), (0, rows)))
    inner = flat.reshape(heads, rows, band + 1)[:, :, 1 : width - 1]
    below = jnp.sum(jnp.where(difference[None] <= -left, grad, 0.0), axis=2, keepdims=True)
    above = jnp.sum(jnp.where(difference[None] >= right, grad, 0.0), axis=2, keepdims=True)
    return jnp.concatenate([below, inner, above], axis=2)


def block_scores(rows_query, keys, table, segment, start, left, right):
    rows, heads, depth = rows_query.shape
    group = keys.shape[0]
    width = table.shape[0]
    scale = 1.0 / math.sqrt(depth)
    project = jnp.einsum("qhd,rd->hqr", rows_query, table, preferred_element_type=jnp.float32)
    content = jnp.einsum("qhd,khd->hqk", rows_query, keys, preferred_element_type=jnp.float32)
    key_place = jnp.arange(group, dtype=jnp.int32)
    row_place = start + jnp.arange(rows, dtype=jnp.int32)
    difference = key_place[None, :] - row_place[:, None]
    relative = spread_band(project, start, group, left, right)
    relative = relative + jnp.where(difference[None] <= -left, project[:, :, :1], 0.0)
    relative = relative + jnp.where(difference[None] >= right, project[:, :, width - 1 :], 0.0)
    row_segment = lax.dynamic_slice_in_dim(segment, start, rows)
    same = row_segment[:, None] == segment[None, :]
    return (jnp.where(same[None], scale * (content + relative), masked_score), difference)


def attention_forward(query, keys, values, table, segment, block_rows, left, right):
    group = query.shape[0]
    starts = jnp.arange(group // block_rows, dtype=jnp.int32) * block_rows

    def one_block(carry, start):
        rows_query = lax.dynamic_slice_in_dim(query, start, block_rows, 0)
        scores, difference = block_scores(rows_query, keys, table, segment, start, left, right)
        top = jnp.max(scores, axis=2, keepdims=True)
        weights = jnp.exp(scores - top)
        total = jnp.sum(weights, axis=2, keepdims=True)
        probs = (weights / total).astype(jnp.bfloat16)
        rows_out = jnp.einsum("hqk,khd->qhd", probs, values, preferred_element_type=jnp.float32)
        return (carry, (rows_out.astype(jnp.bfloat16), (top + jnp.log(total))[:, :, 0]))

    unused, (pieces, log_total) = lax.scan(one_block, 0, starts)
    return (pieces.reshape(query.shape), log_total)


def attention_backward(
    query, keys, values, table, segment, log_total, d_context, block_rows, left, right
):
    group, heads, depth = query.shape
    width = table.shape[0]
    scale = 1.0 / math.sqrt(depth)
    starts = jnp.arange(group // block_rows, dtype=jnp.int32) * block_rows

    def one_block(carry, operands):
        d_keys, d_values, d_table = carry
        start, block_total = operands
        rows_query = lax.dynamic_slice_in_dim(query, start, block_rows, 0)
        rows_grad = lax.dynamic_slice_in_dim(d_context, start, block_rows, 0)
        scores, difference = block_scores(rows_query, keys, table, segment, start, left, right)
        probs = jnp.exp(scores - block_total[:, :, None])
        d_values = d_values + jnp.einsum(
            "hqk,qhd->khd",
            probs.astype(jnp.bfloat16),
            rows_grad,
            preferred_element_type=jnp.float32,
        )
        d_probs = jnp.einsum("qhd,khd->hqk", rows_grad, values, preferred_element_type=jnp.float32)
        weighted = jnp.sum(probs * d_probs, axis=2, keepdims=True)
        d_scores = (probs * (d_probs - weighted)).astype(jnp.bfloat16)
        bins = relative_bins(
            scale * d_scores.astype(jnp.float32), difference, start, width, left, right
        )
        bins = bins.astype(jnp.bfloat16)
        d_rows = scale * jnp.einsum(
            "hqk,khd->qhd", d_scores, keys, preferred_element_type=jnp.float32
        )
        d_rows = d_rows + jnp.einsum("hqr,rd->qhd", bins, table, preferred_element_type=jnp.float32)
        d_keys = d_keys + scale * jnp.einsum(
            "hqk,qhd->khd", d_scores, rows_query, preferred_element_type=jnp.float32
        )
        d_table = d_table + jnp.einsum(
            "hqr,qhd->rd", bins, rows_query, preferred_element_type=jnp.float32
        )
        return ((d_keys, d_values, d_table), d_rows.astype(jnp.bfloat16))

    zeros_heads = jnp.zeros(query.shape, jnp.float32)
    zeros_table = jnp.zeros(table.shape, jnp.float32)
    (d_keys, d_values, d_table), d_rows = lax.scan(
        one_block, (zeros_heads, zeros_heads, zeros_table), (starts, log_total)
    )
    return (
        d_rows.reshape(query.shape),
        d_keys.astype(jnp.bfloat16),
        d_values.astype(jnp.bfloat16),
        d_table,
    )


def on_device(
    frames,
    lengths,
    cotangent,
    ffn1_in,
    ffn1_out,
    query_w,
    key_w,
    value_w,
    out_w,
    point_in,
    point_out,
    ffn2_in,
    ffn2_out,
    depth_w,
    rel_table,
    norm_gains,
    norm_biases,
    bn_gain,
    bn_shift,
):
    seq_count = lax.axis_size("seq")
    seq_rank = lax.axis_index("seq")
    frames_here, width = frames.shape
    group = frames_here * seq_count
    block_rows = min(512, group)
    kernel_size = depth_w.shape[0]
    reach = kernel_size // 2
    ends = jnp.cumsum(lengths[0])
    last_entry = lengths.shape[1] - 1
    first = seq_rank * frames_here
    wide_place = first - reach + jnp.arange(frames_here + 2 * reach, dtype=jnp.int32)
    wide_segment = segment_ids(wide_place, ends, group)
    own_segment = wide_segment[reach : reach + frames_here]
    mask = (own_segment < last_entry).astype(jnp.float32)[:, None]
    group_segment = segment_ids(jnp.arange(group, dtype=jnp.int32), ends, group)
    shards = (
        ffn1_in,
        ffn1_out,
        query_w,
        key_w,
        value_w,
        out_w,
        point_in,
        point_out,
        ffn2_in,
        ffn2_out,
    )
    cube = cube_of(shards, rel_table, depth_w)
    start_values = frames.astype(jnp.float32)
    first_norm, first_unit, first_inverse = norm_forward(
        start_values, norm_gains[0], norm_biases[0]
    )
    gathered, kept_first = gather_all(
        shards, cube, first_norm.astype(jnp.bfloat16), start_values
    )
    if cube is None:
        after_first, kept_first = ffn_forward(
            start_values, norm_gains[0], norm_biases[0], gathered[0], gathered[1], cube, 7
        )
    else:
        after_first, act, swish, hidden = kept_first
        kept_first = (hidden, act, swish, first_unit, first_inverse)
    attn_norm, attn_unit, attn_inverse = norm_forward(after_first, norm_gains[1], norm_biases[1])
    attn_hidden = attn_norm.astype(jnp.bfloat16)
    if cube is None:
        query_heads, key_heads, value_heads = (
            lax.all_to_all(
                to_heads(attn_hidden, gathered[2], HEADS),
                "seq",
                split_axis=1,
                concat_axis=0,
                tiled=True,
            ),
            lax.all_to_all(
                to_heads(attn_hidden, gathered[3], HEADS),
                "seq",
                split_axis=1,
                concat_axis=0,
                tiled=True,
            ),
            lax.all_to_all(
                to_heads(attn_hidden, gathered[4], HEADS),
                "seq",
                split_axis=1,
                concat_axis=0,
                tiled=True,
            ),
        )
        context_heads, log_total = attention_forward(
            query_heads,
            key_heads,
            value_heads,
            rel_table,
            group_segment,
            block_rows,
            REL_LEFT,
            REL_RIGHT,
        )
        context = lax.all_to_all(context_heads, "seq", split_axis=0, concat_axis=1, tiled=True).reshape(
            frames_here, width
        )
        after_attn = after_first + matmul(context, gathered[5])
    else:
        table = jnp.pad(rel_table, ((0, 128 - rel_table.shape[0]), (0, 0)))
        same = (group_segment[:, None] == group_segment[None, :]).astype(jnp.float32)
        after_attn, context, heads_kept, probs_kept = attend_fast(
            cube, attn_hidden, after_first, same, table, gathered[2:6]
        )
    kernel = depth_w.astype(jnp.float32)
    if cube is None:
        conv_norm, conv_unit, conv_inverse = norm_forward(after_attn, norm_gains[2], norm_biases[2])
        conv_hidden = conv_norm.astype(jnp.bfloat16)
        pointwise = matmul(conv_hidden, gathered[6])
        gate_half = pointwise[:, :width]
        sigma_half = jax.nn.sigmoid(pointwise[:, width:])
        gated = (gate_half * sigma_half).astype(jnp.bfloat16)
        gated_wide = padded_2(gated, (("seq", 0),), reach)
        mixed = jnp.zeros((frames_here, width), jnp.float32)
        for offset in range(kernel_size):
            same = (wide_segment[offset : offset + frames_here] == own_segment).astype(jnp.float32)[
                :, None
            ]
            mixed = (
                mixed
                + kernel[offset] * gated_wide[offset : offset + frames_here].astype(jnp.float32) * same
            )
        total, squares, count = lax.psum(
            (jnp.sum(mixed * mask, axis=0), jnp.sum(mixed * mixed * mask, axis=0), jnp.sum(mask)),
            AXES,
        )
        mean = total / count
        var = squares / count - mean * mean
        bn_inverse = lax.rsqrt(var + epsilon)
        centred = (mixed - mean) * bn_inverse
        bn_out = centred * bn_gain + bn_shift
        conv_swish = jax.nn.silu(bn_out).astype(jnp.bfloat16)
        after_conv = after_attn + matmul(conv_swish, gathered[7])
    else:
        marks = [
            wide_segment[offset : offset + frames_here] == own_segment
            for offset in range(kernel_size)
        ]
        marks = jnp.stack(marks, axis=1).astype(jnp.float32)
        marks = jnp.concatenate([marks, mask], axis=1)
        marks = jnp.pad(marks, ((0, 0), (0, 8 - marks.shape[1])))
        blank = jnp.zeros((4, width), jnp.float32)
        norms = [norm_gains[2], norm_biases[2], bn_gain, bn_shift]
        norms = jnp.concatenate([jnp.stack(norms), blank, kernel, blank[:3]])
        after_conv, *conv_kept, conv_swish, stats = conv_fast(
            cube, kernel_size, (after_attn, norms, marks), (gathered[6], gathered[7]), True
        )
        conv_unit, conv_inverse, conv_hidden, gate_half, sigma_half, gated_wide, centred = conv_kept
        var, count = (stats[1], stats[2])
    after_second, kept_second = ffn_forward(
        after_conv, norm_gains[3], norm_biases[3], gathered[8], gathered[9], cube, 8
    )
    final_norm, final_unit, final_inverse = norm_forward(
        after_second, norm_gains[4], norm_biases[4]
    )
    sample_variance = var * count / (count - 1.0)
    d_final = cotangent.astype(jnp.float32) * mask
    d_second, gain_four, shift_four = norm_backward(
        d_final, final_unit, final_inverse, norm_gains[4]
    )
    d_conv_res, grad_two_in, grad_two_out, gain_three, shift_three = ffn_backward(
        d_second, kept_second, norm_gains[3], gathered[8], gathered[9], cube, 9
    )
    if cube is None:
        conv_branch = d_conv_res.astype(jnp.bfloat16)
        d_bn_out = transposed_right(conv_branch, gathered[7]) * swish_slope(bn_out)
        grad_bn_gain, grad_bn_shift = lax.psum(
            (jnp.sum(d_bn_out * centred * mask, axis=0), jnp.sum(d_bn_out * mask, axis=0)), AXES
        )
        d_mixed = (
            bn_gain * bn_inverse * (d_bn_out - mask * (grad_bn_shift + centred * grad_bn_gain) / count)
        )
        d_mixed = d_mixed.astype(jnp.bfloat16)
        d_mixed_wide = padded_2(d_mixed, (("seq", 0),), reach)
        d_mixed_value = d_mixed.astype(jnp.float32)
        d_gated = jnp.zeros((frames_here, width), jnp.float32)
        kernel_rows = []
        for offset in range(kernel_size):
            same = (wide_segment[offset : offset + frames_here] == own_segment).astype(jnp.float32)[
                :, None
            ]
            shifted_in = gated_wide[offset : offset + frames_here].astype(jnp.float32)
            kernel_rows.append(jnp.sum(d_mixed_value * shifted_in * same, axis=0))
            back = 2 * reach - offset
            same_back = (wide_segment[back : back + frames_here] == own_segment).astype(jnp.float32)[
                :, None
            ]
            d_gated = (
                d_gated
                + kernel[offset]
                * d_mixed_wide[back : back + frames_here].astype(jnp.float32)
                * same_back
            )
        d_pointwise = jnp.concatenate(
            [d_gated * sigma_half, d_gated * gate_half * sigma_half * (1.0 - sigma_half)], axis=1
        ).astype(jnp.bfloat16)
        d_conv_norm, gain_two, shift_two = norm_backward(
            transposed_right(d_pointwise, gathered[6]), conv_unit, conv_inverse, norm_gains[2]
        )
        d_attn_res = d_conv_res + d_conv_norm
        attn_branch = d_attn_res.astype(jnp.bfloat16)
    else:
        d_attn_res, attn_branch, conv_branch, d_pointwise, sums = conv_fast(
            cube,
            kernel_size,
            (
                d_conv_res,
                norms,
                marks,
                stats,
                centred,
                gated_wide,
                gate_half,
                sigma_half,
                conv_unit,
                conv_inverse,
            ),
            (gathered[6], gathered[7]),
            False,
        )
        kernel_rows = [sums[offset] for offset in range(kernel_size)]
        gain_two, shift_two, grad_bn_gain, grad_bn_shift = sums[8], sums[9], sums[10], sums[11]
    if cube is None:
        d_context = (
            transposed_right(attn_branch, gathered[5])
            .astype(jnp.bfloat16)
            .reshape(frames_here, HEADS, -1)
        )
        d_context_heads = lax.all_to_all(d_context, "seq", split_axis=1, concat_axis=0, tiled=True)
        d_query_heads, d_key_heads, d_value_heads, d_table = attention_backward(
            query_heads,
            key_heads,
            value_heads,
            rel_table,
            group_segment,
            log_total,
            d_context_heads,
            block_rows,
            REL_LEFT,
            REL_RIGHT,
        )
        d_query, d_keys, d_values = (
            lax.all_to_all(d_query_heads, "seq", split_axis=0, concat_axis=1, tiled=True),
            lax.all_to_all(d_key_heads, "seq", split_axis=0, concat_axis=1, tiled=True),
            lax.all_to_all(d_value_heads, "seq", split_axis=0, concat_axis=1, tiled=True),
        )
        d_query = d_query.reshape(frames_here, width)
        d_keys = d_keys.reshape(frames_here, width)
        d_values = d_values.reshape(frames_here, width)
        d_attn_hidden = (
            transposed_right(d_query, gathered[2])
            + transposed_right(d_keys, gathered[3])
            + transposed_right(d_values, gathered[4])
        )
        heads_in = jnp.concatenate([d_query, d_keys, d_values], axis=1)
    else:
        d_attn_hidden, heads_in, d_table = attend_back_fast(
            cube, attn_branch, heads_kept, probs_kept, table, gathered[2:6]
        )
        d_table = d_table[: rel_table.shape[0]]
    d_attn_norm, gain_one, shift_one = norm_backward(
        d_attn_hidden, attn_unit, attn_inverse, norm_gains[1]
    )
    d_first_res = d_attn_res + d_attn_norm
    d_input, grad_one_in, grad_one_out, gain_zero, shift_zero = ffn_backward(
        d_first_res, kept_first, norm_gains[0], gathered[0], gathered[1], cube, 10
    )
    gains_local = jnp.stack([gain_zero, gain_one, gain_two, gain_three, gain_four])
    shifts_local = jnp.stack([shift_zero, shift_one, shift_two, shift_three, shift_four])
    kernel_local = jnp.stack(kernel_rows)
    shards, (grad_gains, grad_biases, grad_depth, grad_rel) = gradient_shards(
        (
            grad_two_out,
            grad_two_in,
            grad_one_in,
            grad_one_out,
            (conv_hidden, d_pointwise),
            (attn_hidden, heads_in),
            (conv_swish, conv_branch),
            (context, attn_branch),
        ),
        (gains_local, shifts_local, kernel_local, d_table),
        cube,
    )
    two_out, two_in, one_in, one_out, conv_in, attn_in, conv_out, attn_out = shards
    return (
        final_norm.astype(jnp.bfloat16),
        d_input.astype(jnp.bfloat16),
        one_in,
        one_out,
        attn_in[:, :width],
        attn_in[:, width : 2 * width],
        attn_in[:, 2 * width :],
        attn_out,
        conv_in,
        conv_out,
        two_in,
        two_out,
        grad_depth,
        grad_rel,
        grad_gains,
        grad_biases,
        grad_bn_gain,
        grad_bn_shift,
        sample_variance,
    )


def solution(mesh):
    placed = (
        P(("batch", "seq"), None),
        P("batch", None),
        P(("batch", "seq"), None),
        P(("batch", "seq"), None),
        P(("batch", "seq"), None),
        P(("batch", "seq"), None),
        P(("batch", "seq"), None),
        P(("batch", "seq"), None),
        P(("batch", "seq"), None),
        P(("batch", "seq"), None),
        P(("batch", "seq"), None),
        P(("batch", "seq"), None),
        P(("batch", "seq"), None),
        P(),
        P(),
        P(),
        P(),
        P(),
        P(),
    )
    return jax.shard_map(
        on_device,
        mesh=mesh,
        in_specs=placed,
        out_specs=(
            P(("batch", "seq"), None),
            P(("batch", "seq"), None),
            P(("batch", "seq"), None),
            P(("batch", "seq"), None),
            P(("batch", "seq"), None),
            P(("batch", "seq"), None),
            P(("batch", "seq"), None),
            P(("batch", "seq"), None),
            P(("batch", "seq"), None),
            P(("batch", "seq"), None),
            P(("batch", "seq"), None),
            P(("batch", "seq"), None),
            P(),
            P(),
            P(),
            P(),
            P(),
            P(),
            P(),
        ),
        check_vma=False,
    )
```

```python
import functools
import math

import jax
import jax.numpy as jnp
from jax import lax
from jax.experimental import pallas as pl
from jax.experimental.pallas import tpu as pltpu
from jax.sharding import PartitionSpec as P

MESH = pl.DeviceIdType.MESH
AXES = ("batch", "seq")
ALL_SHARES = (3, 1, 0)
ROWS = 64
PACE = 2
TURNS = (1, 0, 3, 4, 5, 8, 6, 2, 7, 9)
HALF_SHARES = (5, 3)
PAIR_SHARES = (2, 2)

HEADS = 8
REL_LEFT = 64
REL_RIGHT = 8


epsilon = 1e-05
masked_score = -1000000000.0


def padded_2(shard, sides, width):
    for axis, dim in sides:
        peers, length = (lax.axis_size(axis), shard.shape[dim])
        up = [(i, (i + 1) % peers) for i in range(peers - 1)]
        down = [(j, i) for i, j in up]
        last = lax.slice_in_dim(shard, length - width, length, axis=dim)
        first = lax.slice_in_dim(shard, 0, width, axis=dim)
        before = lax.ppermute(last, axis, up)
        after = lax.ppermute(first, axis, down)
        shard = jnp.concatenate([before, shard, after], axis=dim)
    return shard


def matmul(left, right):
    return jnp.dot(left, right, preferred_element_type=jnp.float32)


def transposed_left(left, right):
    return lax.dot_general(
        left, right, (((0,), (0,)), ((), ())), preferred_element_type=jnp.float32
    )


def transposed_right(left, right):
    return lax.dot_general(
        left, right, (((1,), (1,)), ((), ())), preferred_element_type=jnp.float32
    )


class Cube:
    def __init__(self, batch, seq):
        self.seq_bits, self.batch_bits = (seq.bit_length() - 1, batch.bit_length() - 1)
        self.count = self.seq_bits + self.batch_bits
        self.core = self.seq_bits
        wide = (self.batch_bits - 1) // 2
        self.x = list(range(self.seq_bits))[::-1]
        self.y = list(range(self.core + 1, self.core + 1 + wide))[::-1]
        self.z = list(range(self.core + 1 + wide, self.count))[::-1]

    def bit(self, k):
        if k < self.seq_bits:
            return lax.rem(lax.axis_index("seq") // (1 << k), 2)
        return lax.rem(lax.axis_index("batch") // (1 << (k - self.seq_bits)), 2)

    def partner(self, k):
        batch, seq = (lax.axis_index("batch"), lax.axis_index("seq"))
        step = 1 - 2 * self.bit(k)
        if k < self.seq_bits:
            return (batch, seq + step * (1 << k))
        return (batch + step * (1 << (k - self.seq_bits)), seq)


def greet(cube, bits):
    barrier = pltpu.get_barrier_semaphore()
    for k in bits:
        pl.semaphore_signal(barrier, inc=1, device_id=cube.partner(k), device_id_type=MESH)
    pl.semaphore_wait(barrier, len(bits))


def gather_kernel(cube, plans, items, first_in, first_out, *refs):
    count = len(plans)
    shards, (hidden, before), refs = (refs[:count], refs[count : count + 2], refs[count + 2 :])
    outs, results, refs = (refs[:count], refs[count : count + 4], refs[count + 4 :])
    (send, recv, local), scratch = (refs[:3], refs[3:])
    own = [cube.bit(k) for k in range(cube.count)]
    kept = []
    for m, (bits, paired) in enumerate(plans):
        kept.append(
            pltpu.make_async_copy(
                shards[m].at[own[0]] if paired else shards[m],
                outs[m].at[tuple(own[k] for k in bits)],
                local.at[m],
            )
        )
        kept[m].start()
    greet(cube, range(cube.count))

    def copy(number, stage):
        m, order, block = flat[number]
        bits, paired = plans[m]
        lead = tuple(slice(None) if k in order[:stage] else own[k] for k in bits)
        place = outs[m].at[lead + block]
        source = place
        if stage == 0:
            source = shards[m].at[(1 - own[0],) + block] if paired else shards[m].at[block]
        return to_partner(
            cube, order[stage], source, place, send.at[number, stage], recv.at[number, stage]
        )

    flat = [item for chunk in items for item in chunk]
    numbers, at = ([], 0)
    for chunk in items:
        numbers.append(range(at, at + len(chunk)))
        at += len(chunk)
    arrive, steps = ffn_steps(
        cube, hidden, before, outs[first_in].at, outs[first_out].at, *results, *scratch
    )
    arrive[0]()
    for number in range(len(flat)):
        copy(number, 0).start()
    for one in kept:
        one.wait()
    most = max(len(order) for _, order, _ in flat)
    waiting = {m: sum(item[0] == m for item in flat) for m in (first_in, first_out)}
    pending = []
    for turn in range(len(items) + most):
        for stage in range(most):
            for late in (0, 1):
                chunk = turn - stage - late
                if not 0 <= chunk < len(items):
                    continue
                for number in numbers[chunk]:
                    stages = len(flat[number][1])
                    if stage >= stages or late != (stage == stages - 1):
                        continue
                    copy(number, stage).wait_recv()
                    if stage + 1 < stages:
                        copy(number, stage + 1).start()
                    elif flat[number][0] in waiting:
                        waiting[flat[number][0]] -= 1
        if waiting[first_in] == 0:
            waiting[first_in] = -1
            arrive[1]()
            pending += steps[0]
        if waiting[first_out] == 0 and waiting[first_in] < 0:
            waiting[first_out] = -1
            arrive[2]()
            pending += steps[1]
        for _ in range(PACE):
            if pending:
                pending.pop(0)()
    for step in pending:
        step()
    for number, (_, order, _) in enumerate(flat):
        for stage in range(len(order)):
            copy(number, stage).wait_send()


def row_parts(rows, shares):
    units, total, at, upto, parts = (rows // 8, sum(shares), 0, 0, [])
    for share in shares:
        upto += share
        end = (units * upto + total // 2) // total
        parts.append((at * 8, (end - at) * 8))
        at = end
    return parts


def gather_fast(shards, kinds, cube, hidden, values, first_in, first_out):
    core, x, y, z = ([cube.core], cube.x, cube.y, cube.z)
    every = list(range(cube.count))[::-1]
    plans, items, shapes = ([], [], [])
    for m, (shard, kind) in enumerate(zip(shards, kinds)):
        if kind == "all":
            bits, shares = (every, ALL_SHARES)
            orders = [z + y + x + core, z + x + y + core, x + y + z + core]
        else:
            bits = every if kind == "pair" else every[:-1]
            first = x if kind == "pair" else []
            orders = [first + z + y + core, first + y + z + core]
            shares = PAIR_SHARES if kind == "pair" else HALF_SHARES
        plans.append((bits, kind == "pair"))
        shapes.append((2,) * len(bits) + shard.shape[-2:])
        rows, columns = (min(ROWS, shard.shape[-2]), min(2048, shard.shape[-1]))
        for row in range(0, shard.shape[-2], rows):
            for column in range(0, shard.shape[-1], columns):
                items.append(
                    [
                        (m, order, (pl.ds(row + a, w), pl.ds(column, columns)))
                        for order, (a, w) in zip(orders, row_parts(rows, shares))
                        if w
                    ]
                )
    count, copies = (len(shards), sum(len(chunk) for chunk in items))
    local, width = values.shape
    wide = shards[first_in].shape[-1]
    vmem = pl.BlockSpec(memory_space=pltpu.VMEM)
    outs = pl.pallas_call(
        functools.partial(gather_kernel, cube, plans, items, first_in, first_out),
        out_shape=[
            jax.ShapeDtypeStruct(shape, shard.dtype) for shape, shard in zip(shapes, shards)
        ]
        + [
            jax.ShapeDtypeStruct((local, width), jnp.float32),
            jax.ShapeDtypeStruct((2 * local, wide), jnp.float32),
            jax.ShapeDtypeStruct((2 * local, wide), jnp.bfloat16),
            jax.ShapeDtypeStruct((2 * local, width), jnp.bfloat16),
        ],
        in_specs=[pl.BlockSpec(memory_space=pl.ANY)] * count + [vmem] * 2,
        out_specs=[pl.BlockSpec(memory_space=pl.ANY)] * count + [vmem] * 4,
        scratch_shapes=[
            pltpu.SemaphoreType.DMA((copies, cube.count)),
            pltpu.SemaphoreType.DMA((copies, cube.count)),
            pltpu.SemaphoreType.DMA((count,)),
            pltpu.VMEM(shapes[first_in], jnp.bfloat16),
            pltpu.VMEM(shapes[first_out], jnp.bfloat16),
            pltpu.VMEM((2 * local, width), jnp.bfloat16),
            pltpu.VMEM((local, width), jnp.bfloat16),
            pltpu.VMEM((local, width), jnp.bfloat16),
            pltpu.SemaphoreType.DMA((5,)),
            pltpu.SemaphoreType.DMA((3,)),
            pltpu.SemaphoreType.DMA((3,)),
        ],
        compiler_params=pltpu.CompilerParams(
            collective_id=0, has_side_effects=True, vmem_limit_bytes=48 * 1024 * 1024
        ),
        name="gather_weights",
    )(*shards, hidden, values)
    whole = tuple(out.reshape(-1, shard.shape[-1]) for out, shard in zip(outs, shards))
    return whole, outs[count:]


def gradient_kernel(cube, shapes, kinds, tile, *refs):
    count = len(shapes)
    lefts, rights, refs = (refs[:count], refs[count : 2 * count], refs[2 * count :])
    value, out, crossed, value_out, refs = (refs[0], refs[1], refs[2], refs[3], refs[4:])
    near, far, whole = (refs[:count], refs[count : 2 * count], refs[2 * count : 3 * count])
    refs = refs[3 * count :]
    order = cube.y + cube.z[::-1]
    stages = len(order)
    total, sent, recv_at, refs = (refs[0], refs[1 : 1 + stages], refs[1 + stages : 1 + 2 * stages], refs[1 + 2 * stages :])
    cross, value_sent, value_held, refs = (refs[0], refs[1], refs[2], refs[3:])
    x_send, x_recv, local, c_send, c_recv, send, recv, cross_send, cross_recv, v_send, v_recv = refs
    rows, columns = tile
    number, depth = (out.shape[0], total.shape[0])
    lags = [3 + stage + stage // 2 for stage in range(stages)]
    x, c = (cube.bit(0), cube.bit(cube.core))
    dims = sorted(order, reverse=True)
    bits = [cube.bit(k) for k in order]
    every = (slice(None),) * stages
    tokens = near[0].shape[-1] // 2
    pairs = [m for m in range(count) if kinds[m] == "pair"]
    own_lanes = pl.ds(pl.multiple_of(x * tokens, tokens), tokens)

    def spot(stage, flip):
        left = [k for k in dims if k not in order[:stage]]
        side = 1 - bits[stage] if flip else bits[stage]
        return tuple(side if k == order[stage] else slice(None) for k in left)

    def along_x(m):
        if kinds[m] != "all":
            return []
        return [
            to_partner(
                cube,
                0,
                lefts[m].at[every + (slice(None), 1 - x)],
                near[m].at[every + (slice(None), slice(None), own_lanes)],
                x_send.at[m, 0],
                x_recv.at[m, 0],
            ),
            to_partner(
                cube, 0, rights[m], whole[m].at[c, own_lanes], x_send.at[m, 1], x_recv.at[m, 1]
            ),
        ]

    def at_home(m):
        if kinds[m] != "all":
            return [
                pltpu.make_async_copy(lefts[m], near[m], local.at[m, 0]),
                pltpu.make_async_copy(rights[m], whole[m].at[c], local.at[m, 1]),
            ]
        return [
            pltpu.make_async_copy(
                lefts[m].at[every + (slice(None), x)],
                near[m].at[every + (slice(None), slice(None), own_lanes)],
                local.at[m, 0],
            ),
            pltpu.make_async_copy(rights[m], whole[m].at[c, own_lanes], local.at[m, 1]),
        ]

    def along_core(m):
        return [
            to_partner(
                cube,
                cube.core,
                near[m].at[every + (1 - c,)],
                far[m],
                c_send.at[m, 0],
                c_recv.at[m, 0],
            ),
            to_partner(
                cube, cube.core, whole[m].at[c], whole[m].at[c], c_send.at[m, 1], c_recv.at[m, 1]
            ),
        ]

    def remote(stage, chunk):
        return to_partner(
            cube,
            order[stage],
            sent[stage].at[chunk],
            recv_at[stage].at[chunk],
            send.at[stage, chunk],
            recv.at[stage, chunk],
        )

    def reduce(step):
        for stage in range(stages):
            chunk = step - lags[stage]

            @pl.when((chunk >= 0) & (chunk < number))
            def _(stage=stage, chunk=chunk):
                slot = lax.rem(chunk, depth)
                remote(stage, chunk).wait_recv()
                mine = tuple(
                    bits[order.index(k)] if k in order[: stage + 1] else slice(None) for k in dims
                )
                arrived = recv_at[stage]
                if stage + 1 == stages:
                    out[chunk] = total[(slot,) + mine] + arrived[chunk].astype(jnp.float32)
                else:
                    away, home = (spot(stage + 1, True), spot(stage + 1, False))
                    full = list(mine)
                    full[dims.index(order[stage + 1])] = 1 - bits[stage + 1]
                    sent[stage + 1][chunk] = (
                        total[(slot,) + tuple(full)]
                        + arrived[(chunk,) + away].astype(jnp.float32)
                    ).astype(jnp.bfloat16)
                    remote(stage + 1, chunk).start()
                    full[dims.index(order[stage + 1])] = bits[stage + 1]
                    total[(slot,) + tuple(full)] += arrived[(chunk,) + home].astype(jnp.float32)

    def value_copy(k):
        return to_partner(
            cube, k, value_sent.at[k], value_held.at[k], v_send.at[k], v_recv.at[k]
        )

    def value_turn(k):
        if k == 0:
            value_sent[0] = value[...]
        elif k <= cube.count:
            value_copy(k - 1).wait_recv()
            sum_here = value_sent[k - 1] + value_held[k - 1]
            if k < cube.count:
                value_sent[k] = sum_here
            else:
                value_out[...] = sum_here
        if k < cube.count:
            value_copy(k).start()

    def cross_copy(i, first):
        away = pl.ds(first + (1 - x) * 2, 2)
        return to_partner(cube, 0, out.at[away], cross.at[i], cross_send.at[i], cross_recv.at[i])

    greet(cube, range(cube.count))
    value_turn(0)
    for m in range(count):
        for copy in along_x(m) + at_home(m):
            copy.start()
    def to_core(m):
        for copy in at_home(m):
            copy.wait()
        for copy in along_x(m):
            copy.wait_recv()
        for copy in along_core(m):
            copy.start()

    first, firsts = (0, {})
    to_core(0)
    for m in range(count):
        firsts[m] = first
        if m > 0:
            value_turn(m)
        for copy in along_core(m):
            copy.wait_recv()
        if m + 1 < count:
            to_core(m + 1)
        down, across = shapes[m]

        def one(j, carry, m=m, first=first, down=down, across=across):
            chunk = first + j
            slot = lax.rem(chunk, depth)
            row = pl.ds(pl.multiple_of((j // across) * rows, rows), rows)
            column = pl.ds(pl.multiple_of(lax.rem(j, across) * columns, columns), columns)

            def half(flip):
                place = spot(0, flip)
                one_left = near[m][place + (c, row, slice(None))]
                two_left = far[m][place + (row, slice(None))]
                shape = one_left.shape[:-1] + (columns,)
                one_left = one_left.reshape(-1, 2 * tokens)
                two_left = two_left.reshape(-1, 2 * tokens)
                result = matmul(one_left, whole[m][c, :, column]) + matmul(
                    two_left, whole[m][1 - c, :, column]
                )
                return result.reshape(shape)

            sent[0][chunk] = half(True).astype(jnp.bfloat16)
            remote(0, chunk).start()
            total[(slot,) + spot(0, False)] = half(False)
            reduce(chunk)
            return carry

        lax.fori_loop(0, down * across, one, 0)
        first += down * across

    def drain(step, carry):
        reduce(step)
        return carry

    for k in range(count, cube.count + 1):
        value_turn(k)
    for i, m in enumerate(pairs):
        cross_copy(i, firsts[m]).start()
    lax.fori_loop(number, number + lags[-1] + 1, drain, 0)
    for i, m in enumerate(pairs):
        cross_copy(i, firsts[m]).wait_recv()
        crossed[i, x] = out[pl.ds(firsts[m] + x * 2, 2)]
        crossed[i, 1 - x] = cross[i]
        cross_copy(i, firsts[m]).wait_send()
    for k in range(cube.count):
        value_copy(k).wait_send()
    for m in range(count):
        for copy in along_x(m) + along_core(m):
            copy.wait_send()

    def finish(chunk, carry):
        for stage in range(stages):
            remote(stage, chunk).wait_send()
        return carry

    lax.fori_loop(0, number, finish, 0)


def gradients_fast(pairs, kinds, value, cube, rows, columns):
    order = cube.y + cube.z[::-1]
    stages, count = (len(order), len(pairs))
    lefts, rights, shapes, near, far, whole = ([], [], [], [], [], [])
    for (left, right), kind in zip(pairs, kinds):
        lead = (2,) * stages
        if kind == "all":
            block, tokens = (left.shape[1] >> cube.count, left.shape[0])
            lefts.append(left.T.reshape(lead + (2, 2, block, tokens)))
        else:
            block, tokens = (left.shape[1] >> (cube.count - 1), left.shape[0] // 2)
            lefts.append(left.T.reshape(lead + (2, block, 2 * tokens)))
        rights.append(right)
        shapes.append((block // rows, right.shape[1] // columns))
        near.append(pltpu.VMEM(lead + (2, block, 2 * tokens), jnp.bfloat16))
        far.append(pltpu.VMEM(lead + (block, 2 * tokens), jnp.bfloat16))
        whole.append(pltpu.VMEM((2, 2 * tokens, right.shape[1]), jnp.bfloat16))
    number, tile = (sum(down * across for down, across in shapes), (rows, columns))
    held = [
        pltpu.VMEM((number,) + (2,) * (stages - 1 - stage) + tile, jnp.bfloat16)
        for stage in range(stages)
    ]
    depth = 3 + (stages - 1) + (stages - 1) // 2 + 1
    paired = kinds.count("pair")
    vmem = pl.BlockSpec(memory_space=pltpu.VMEM)
    values = pltpu.VMEM((cube.count,) + value.shape, value.dtype)
    out, crossed, value = pl.pallas_call(
        functools.partial(gradient_kernel, cube, shapes, kinds, tile),
        out_shape=[
            jax.ShapeDtypeStruct((number,) + tile, jnp.float32),
            jax.ShapeDtypeStruct((paired, 2, 2) + tile, jnp.float32),
            jax.ShapeDtypeStruct(value.shape, value.dtype),
        ],
        in_specs=[pl.BlockSpec(memory_space=pl.ANY)] * (2 * count) + [vmem],
        out_specs=[vmem] * 3,
        scratch_shapes=near
        + far
        + whole
        + [pltpu.VMEM((depth,) + (2,) * stages + tile, jnp.float32)]
        + held
        + held
        + [pltpu.VMEM((paired, 2) + tile, jnp.float32), values, values]
        + [pltpu.SemaphoreType.DMA((count, 2))] * 5
        + [pltpu.SemaphoreType.DMA((stages, number))] * 2
        + [pltpu.SemaphoreType.DMA((paired,))] * 2
        + [pltpu.SemaphoreType.DMA((cube.count,))] * 2,
        compiler_params=pltpu.CompilerParams(
            collective_id=4, has_side_effects=True, vmem_limit_bytes=60 * 1024 * 1024
        ),
        name="reduce_gradients",
    )(*lefts, *rights, value)
    results, at, pair = ([], 0, 0)
    for (down, across), right, kind in zip(shapes, rights, kinds):
        if kind == "pair":
            piece = crossed[pair].reshape(2, 2, rows, columns // 128, 128)
            results.append(piece.transpose(2, 1, 3, 0, 4).reshape(rows, 4 * columns))
            pair += 1
        else:
            piece = out[at : at + down * across].reshape(down, across, rows, columns)
            results.append(piece.transpose(0, 2, 1, 3).reshape(down * rows, right.shape[1]))
        at += down * across
    return results, value


def flat_pack(values):
    flat = jnp.concatenate([value.reshape(-1) for value in values])
    size = -(-flat.shape[0] // 8192) * 8192
    return jnp.pad(flat, (0, size - flat.shape[0])).reshape(-1, 1024)


def flat_unpack(flat, values):
    flat, out, at = (flat.reshape(-1), [], 0)
    for value in values:
        out.append(flat[at : at + value.size].reshape(value.shape))
        at += value.size
    return tuple(out)


def gradient_shards(pairs, values, cube):
    if cube is None:
        results = []
        for left, right in pairs:
            whole = transposed_left(left, right)
            flat = whole.reshape(-1, 128)
            shard = lax.psum_scatter(flat, AXES, scatter_dimension=0, tiled=True)
            results.append(shard.reshape(-1, whole.shape[1]))
        return results, lax.psum(values, AXES)
    kinds = ["half", "pair", "pair", "half"] + ["all"] * 4
    results, flat = gradients_fast(pairs, kinds, flat_pack(values), cube, 32, 1024)
    return results, flat_unpack(flat, values)


def parities(shard):
    rows, columns = shard.shape
    return shard.reshape(rows, columns // 256, 2, 128).transpose(2, 0, 1, 3).reshape(2, rows, -1)


def gather_all(shards, cube, hidden, values):
    if cube is None:
        return tuple(lax.all_gather(shard, AXES, axis=0, tiled=True) for shard in shards), None
    kinds = ("pair", "half") + ("all",) * 6 + ("pair", "half")
    shards = [parities(shard) if kind == "pair" else shard for shard, kind in zip(shards, kinds)]
    turns = TURNS
    outs, first = gather_fast(
        [shards[m] for m in turns],
        [kinds[m] for m in turns],
        cube,
        hidden,
        values,
        turns.index(0),
        turns.index(1),
    )
    return tuple(outs[turns.index(m)] for m in range(len(shards))), first


def distance_rows(group, left, right, backwards):
    row = lax.broadcasted_iota(jnp.int32, (group, 128), 0)
    row = group - 1 - row if backwards else row
    distance = jnp.where(row >= group // 2, row - group, row)
    index = jnp.clip(distance, -left, right) + left
    hit = index == lax.broadcasted_iota(jnp.int32, (group, 128), 1)
    return jnp.where(hit, 1.0, 0.0).astype(jnp.bfloat16)


def halves(cube, rows, half):
    mine = cube.bit(0)
    return (
        pl.ds(pl.multiple_of(mine * half, half), half),
        pl.ds(pl.multiple_of((1 - mine) * half, half), half),
        pl.ds(pl.multiple_of(mine * rows, rows), rows),
        pl.ds(pl.multiple_of((1 - mine) * rows, rows), rows),
    )


def to_partner(cube, k, source, target, send, recv):
    return pltpu.make_async_remote_copy(
        src_ref=source,
        dst_ref=target,
        send_sem=send,
        recv_sem=recv,
        device_id=cube.partner(k),
        device_id_type=MESH,
    )


def attend_kernel(cube, left, right, *refs):
    hidden, before, same, table, query_w, key_w, value_w, out_w = refs[:8]
    after, context, heads_out, probs_out = refs[8:12]
    weights, heads_in, away, wide, context_away, load, send, recv, head_send, head_recv = refs[12:]
    rows, width = hidden.shape
    group, half = (2 * rows, width // 2)
    heads = half // 128
    scale = 1.0 / math.sqrt(128)
    mine = cube.bit(0)
    own_columns, away_columns, own_rows, away_rows = halves(cube, rows, half)
    loads = []
    for i, matrix in enumerate((query_w, key_w, value_w, out_w)):
        loads.append(pltpu.make_async_copy(matrix, weights.at[i], load.at[i]))
        loads[i].start()
    greet(cube, [0])

    def exchange(i):
        return to_partner(
            cube, 0, away.at[i], heads_in.at[i, own_rows], send.at[i], recv.at[i]
        )

    def context_copy(head):
        column = pl.ds(pl.multiple_of(mine * half + head * 128, 128), 128)
        return to_partner(
            cube, 0, context_away.at[head], wide.at[:, column], head_send.at[head], head_recv.at[head]
        )

    for i in range(3):
        loads[i].wait()
        away[i] = matmul(hidden[...], weights[i, :, away_columns]).astype(jnp.bfloat16)
        exchange(i).start()
    for i in range(3):
        heads_in[i, own_rows, :] = matmul(hidden[...], weights[i, :, own_columns]).astype(
            jnp.bfloat16
        )
    spread = matmul(distance_rows(group, left, right, False), table[...]).astype(jnp.bfloat16)
    loads[3].wait()
    for i in range(3):
        exchange(i).wait_recv()

    def one_head(head, carry):
        column = pl.ds(pl.multiple_of(head * 128, 128), 128)
        place = pl.ds(pl.multiple_of(mine * half + head * 128, 128), 128)
        query, keys, values = (heads_in[i, :, column] for i in range(3))
        relative = pltpu.roll(transposed_right(query, spread), 0, 1, stride=1, stride_axis=0)
        scores = scale * (transposed_right(query, keys) + relative)
        scores = jnp.where(same[...] > 0, scores, masked_score)
        weight = jnp.exp(scores - jnp.max(scores, axis=1, keepdims=True))
        probs_out[head] = weight / jnp.sum(weight, axis=1, keepdims=True)
        there = probs_out[head, away_rows, :].astype(jnp.bfloat16)
        context_away[head] = matmul(there, values).astype(jnp.bfloat16)
        context_copy(head).start()
        here = probs_out[head, own_rows, :].astype(jnp.bfloat16)
        wide[:, place] = matmul(here, values).astype(jnp.bfloat16)
        return carry

    lax.fori_loop(0, heads, one_head, 0)
    heads_out[...] = heads_in[...]
    after[...] = before[...] + matmul(wide[:, own_columns], weights[3, own_columns, :])
    for head in range(heads):
        context_copy(head).wait_recv()
    after[...] += matmul(wide[:, away_columns], weights[3, away_columns, :])
    context[...] = wide[...]
    for i in range(3):
        exchange(i).wait_send()
    for head in range(heads):
        context_copy(head).wait_send()


def attend_fast(cube, hidden, before, same, table, matrices):
    rows, width = hidden.shape
    group, half = (2 * rows, width // 2)
    heads = half // 128
    vmem = pl.BlockSpec(memory_space=pltpu.VMEM)
    return pl.pallas_call(
        functools.partial(attend_kernel, cube, REL_LEFT, REL_RIGHT),
        out_shape=[
            jax.ShapeDtypeStruct((rows, width), jnp.float32),
            jax.ShapeDtypeStruct((rows, width), jnp.bfloat16),
            jax.ShapeDtypeStruct((3, group, half), jnp.bfloat16),
            jax.ShapeDtypeStruct((heads, group, group), jnp.float32),
        ],
        in_specs=[vmem] * 4 + [pl.BlockSpec(memory_space=pl.ANY)] * 4,
        out_specs=[vmem] * 4,
        scratch_shapes=[
            pltpu.VMEM((4, width, width), jnp.bfloat16),
            pltpu.VMEM((3, group, half), jnp.bfloat16),
            pltpu.VMEM((3, rows, half), jnp.bfloat16),
            pltpu.VMEM((rows, width), jnp.bfloat16),
            pltpu.VMEM((heads, rows, 128), jnp.bfloat16),
            pltpu.SemaphoreType.DMA((4,)),
            pltpu.SemaphoreType.DMA((3,)),
            pltpu.SemaphoreType.DMA((3,)),
            pltpu.SemaphoreType.DMA((heads,)),
            pltpu.SemaphoreType.DMA((heads,)),
        ],
        compiler_params=pltpu.CompilerParams(
            collective_id=5, has_side_effects=True, vmem_limit_bytes=48 * 1024 * 1024
        ),
        name="attend",
    )(hidden, before, same, table, *matrices)


def attend_back_kernel(cube, left, right, *refs):
    branch, heads_in, probs_in, table, query_w, key_w, value_w, out_w = refs[:8]
    d_hidden, d_heads, d_table = refs[8:11]
    weights, d_context, d_context_away, wide, away, load, send, recv, head_send, head_recv = refs[
        11:
    ]
    rows, width = branch.shape
    group, half = (2 * rows, width // 2)
    heads = half // 128
    scale = 1.0 / math.sqrt(128)
    mine = cube.bit(0)
    own_columns, away_columns, own_rows, away_rows = halves(cube, rows, half)
    loads = []
    for i, matrix in enumerate((out_w, query_w, key_w, value_w)):
        loads.append(pltpu.make_async_copy(matrix, weights.at[i], load.at[i]))
        loads[i].start()
    greet(cube, [0])
    loads[0].wait()
    exchange = to_partner(
        cube, 0, d_context_away, d_context.at[own_rows], send.at[0], recv.at[0]
    )
    d_context_away[...] = transposed_right(branch[...], weights[0, away_columns, :]).astype(
        jnp.bfloat16
    )
    exchange.start()
    d_context[own_rows, :] = transposed_right(branch[...], weights[0, own_columns, :]).astype(
        jnp.bfloat16
    )
    spread = distance_rows(group, left, right, True)
    down = lax.broadcasted_iota(jnp.int32, (group, group), 0)
    across = lax.broadcasted_iota(jnp.int32, (group, group), 1)
    mirror = jnp.where(down + across == group - 1, 1.0, 0.0).astype(jnp.bfloat16)
    d_table[...] = jnp.zeros_like(d_table)
    exchange.wait_recv()

    def head_copy(head, i):
        column = pl.ds(pl.multiple_of(i * width + mine * half + head * 128, 128), 128)
        return to_partner(
            cube,
            0,
            away.at[head, i, away_rows],
            wide.at[:, column],
            head_send.at[head, i],
            head_recv.at[head, i],
        )

    def one_head(head, carry):
        column = pl.ds(pl.multiple_of(head * 128, 128), 128)
        query, keys, values = (heads_in[i, :, column] for i in range(3))
        d_rows = d_context[:, column]
        probs = probs_in[head]
        d_probs = transposed_right(d_rows, values)
        weighted = jnp.sum(probs * d_probs, axis=1, keepdims=True)
        d_scores = (probs * (d_probs - weighted)).astype(jnp.bfloat16)
        away[head, 2] = transposed_left(probs.astype(jnp.bfloat16), d_rows).astype(jnp.bfloat16)
        head_copy(head, 2).start()
        away[head, 1] = (scale * transposed_left(d_scores, query)).astype(jnp.bfloat16)
        head_copy(head, 1).start()
        turned = pltpu.roll(matmul(d_scores, mirror), 0, 1, stride=1, stride_axis=0)
        bins = (scale * matmul(turned.astype(jnp.bfloat16), spread)).astype(jnp.bfloat16)
        away[head, 0] = (scale * matmul(d_scores, keys) + matmul(bins, table[...])).astype(
            jnp.bfloat16
        )
        head_copy(head, 0).start()
        d_table[...] += transposed_left(bins, query)
        for i in range(3):
            place = pl.ds(pl.multiple_of(i * width + mine * half + head * 128, 128), 128)
            wide[:, place] = away[head, i, own_rows, :]
        return carry

    lax.fori_loop(0, heads, one_head, 0)
    for i in range(3):
        loads[1 + i].wait()

    def part(i, offset, columns):
        place = pl.ds(pl.multiple_of(i * width + offset * half, half), half)
        return transposed_right(wide[:, place], weights[1 + i, :, columns])

    total = part(0, mine, own_columns)
    for i in range(1, 3):
        total += part(i, mine, own_columns)
    d_hidden[...] = total
    for head in range(heads):
        for i in range(3):
            head_copy(head, i).wait_recv()
    total = part(0, 1 - mine, away_columns)
    for i in range(1, 3):
        total += part(i, 1 - mine, away_columns)
    d_hidden[...] += total
    d_heads[...] = wide[...]
    exchange.wait_send()
    for head in range(heads):
        for i in range(3):
            head_copy(head, i).wait_send()


def attend_back_fast(cube, branch, heads_in, probs, table, matrices):
    rows, width = branch.shape
    group, half = (2 * rows, width // 2)
    heads = half // 128
    vmem = pl.BlockSpec(memory_space=pltpu.VMEM)
    return pl.pallas_call(
        functools.partial(attend_back_kernel, cube, REL_LEFT, REL_RIGHT),
        out_shape=[
            jax.ShapeDtypeStruct((rows, width), jnp.float32),
            jax.ShapeDtypeStruct((rows, 3 * width), jnp.bfloat16),
            jax.ShapeDtypeStruct((128, 128), jnp.float32),
        ],
        in_specs=[vmem] * 4 + [pl.BlockSpec(memory_space=pl.ANY)] * 4,
        out_specs=[vmem] * 3,
        scratch_shapes=[
            pltpu.VMEM((4, width, width), jnp.bfloat16),
            pltpu.VMEM((group, half), jnp.bfloat16),
            pltpu.VMEM((rows, half), jnp.bfloat16),
            pltpu.VMEM((rows, 3 * width), jnp.bfloat16),
            pltpu.VMEM((heads, 3, group, 128), jnp.bfloat16),
            pltpu.SemaphoreType.DMA((4,)),
            pltpu.SemaphoreType.DMA((1,)),
            pltpu.SemaphoreType.DMA((1,)),
            pltpu.SemaphoreType.DMA((heads, 3)),
            pltpu.SemaphoreType.DMA((heads, 3)),
        ],
        compiler_params=pltpu.CompilerParams(
            collective_id=6, has_side_effects=True, vmem_limit_bytes=48 * 1024 * 1024
        ),
        name="attend_back",
    )(branch, heads_in, probs, table, *matrices)


def ffn_steps(
    cube,
    hidden,
    before,
    weight_in,
    weight_out,
    after,
    act,
    swish,
    hidden_out,
    into,
    outof,
    both,
    away,
    arrived,
    load,
    send,
    recv,
):
    rows, width = hidden.shape
    depth, wide = into.shape[-2:]
    step, half = (wide // 4, width // 2)
    _, _, own_rows, away_rows = halves(cube, rows, half)
    exchange = to_partner(cube, 0, both.at[own_rows], both.at[own_rows], send.at[0], recv.at[0])
    lead = (slice(None),) * (len(into.shape) - 2)

    def load_in(q):
        part = lead + (slice(None), pl.ds(q * step, step))
        return pltpu.make_async_copy(weight_in[part], into.at[part], load.at[q])

    def load_out():
        whole = (slice(None),) * len(outof.shape)
        return pltpu.make_async_copy(weight_out[whole], outof.at[whole], load.at[4])

    def back(q):
        part = pl.ds(q * half, half)
        return to_partner(
            cube, 0, away.at[:, part], arrived.at[:, part], send.at[1 + q], recv.at[1 + q]
        )

    def begin():
        both[own_rows, :] = hidden[...]
        exchange.start()

    def first_there():
        for q in range(4):
            load_in(q).start()

    def second_there():
        load_out().start()

    def activate(q, rows_here, wait):
        wait()
        part = pl.ds(q * step, step)
        weights = into[lead + (slice(None), part)].reshape(width, step)
        value = matmul(both[rows_here, :], weights)
        act[rows_here, part] = value
        swish[rows_here, part] = jax.nn.silu(value).astype(jnp.bfloat16)

    def there(q):
        if q == 0:
            load_out().wait()
        part = pl.ds(q * half, half)
        weights = outof[(slice(None),) * (len(outof.shape) - 1) + (part,)].reshape(wide, half)
        away[:, part] = matmul(swish[away_rows, :], weights).astype(jnp.bfloat16)
        back(q).start()

    def here(q):
        part = pl.ds(q * half, half)
        weights = outof[(slice(None),) * (len(outof.shape) - 1) + (part,)].reshape(wide, half)
        after[:, part] = before[:, part] + 0.5 * matmul(swish[own_rows, :], weights)

    def end():
        hidden_out[...] = both[...]
        for q in range(2):
            part = pl.ds(q * half, half)
            back(q).wait_recv()
            after[:, part] += 0.5 * arrived[:, part].astype(jnp.float32)
        exchange.wait_send()
        for q in range(2):
            back(q).wait_send()

    def nothing():
        pass

    one = [functools.partial(activate, q, own_rows, load_in(q).wait) for q in range(4)]
    one += [
        functools.partial(activate, q, away_rows, nothing if q else exchange.wait_recv)
        for q in range(4)
    ]
    two = [functools.partial(there, q) for q in range(2)]
    two += [functools.partial(here, q) for q in range(2)] + [end]
    return (begin, first_there, second_there), (one, two)


def ffn_kernel(cube, *refs):
    hidden, before, weight_in, weight_out = refs[:4]
    arrive, steps = ffn_steps(cube, hidden, before, weight_in.at, weight_out.at, *refs[4:])
    arrive[1]()
    arrive[2]()
    greet(cube, [0])
    arrive[0]()
    for step in steps[0] + steps[1]:
        step()


def ffn_back_kernel(cube, *refs):
    branch, act, weight_in, weight_out = refs[:4]
    d_hidden, d_act, branch_out = refs[4:7]
    into, outof, both, away, arrived, load, send, recv = refs[7:]
    rows, width = branch.shape
    wide = into.shape[1]
    step = wide // 4
    own_columns, away_columns, own_rows, away_rows = halves(cube, rows, width // 2)
    loads = []
    for q in range(4):
        part = pl.ds(q * step, step)
        loads.append(
            pltpu.make_async_copy(weight_out.at[part], outof.at[part], load.at[q])
        )
    loads.append(pltpu.make_async_copy(weight_in, into, load.at[4]))
    for one in loads:
        one.start()
    both[own_rows, :] = branch[...]
    greet(cube, [0])
    exchange = to_partner(
        cube, 0, both.at[own_rows], both.at[own_rows], send.at[0], recv.at[0]
    )
    exchange.start()

    def deactivate(q, rows_here):
        part = pl.ds(q * step, step)
        value = transposed_right(both[rows_here, :], outof[part, :])
        d_act[rows_here, part] = (value * swish_slope(act[rows_here, part])).astype(jnp.bfloat16)

    for q in range(4):
        loads[q].wait()
        deactivate(q, own_rows)
    loads[4].wait()
    exchange.wait_recv()
    for q in range(4):
        deactivate(q, away_rows)
    half = width // 2
    back = []
    for q in range(2):
        part = pl.ds(q * half, half)
        away[:, part] = transposed_right(d_act[away_rows, :], into[part, :]).astype(jnp.bfloat16)
        back.append(
            to_partner(
                cube, 0, away.at[:, part], arrived.at[:, part], send.at[1 + q], recv.at[1 + q]
            )
        )
        back[q].start()
    branch_out[...] = both[...]
    for q in range(2):
        part = pl.ds(q * half, half)
        d_hidden[:, part] = transposed_right(d_act[own_rows, :], into[part, :])
    for q in range(2):
        part = pl.ds(q * half, half)
        back[q].wait_recv()
        d_hidden[:, part] += arrived[:, part].astype(jnp.float32)
    for one in [exchange] + back:
        one.wait_send()


def ffn_fast(cube, first, second, weight_in, weight_out, number, backward):
    rows, width = first.shape
    wide = weight_in.shape[1]
    vmem = pl.BlockSpec(memory_space=pltpu.VMEM)
    both = jax.ShapeDtypeStruct((2 * rows, width), jnp.bfloat16)
    result = jax.ShapeDtypeStruct((rows, width), jnp.float32)
    inner = jax.ShapeDtypeStruct((2 * rows, wide), jnp.bfloat16)
    if backward:
        shapes = [result, inner, both]
    else:
        shapes = [result, jax.ShapeDtypeStruct((2 * rows, wide), jnp.float32), inner, both]
    return pl.pallas_call(
        functools.partial(ffn_back_kernel if backward else ffn_kernel, cube),
        out_shape=shapes,
        in_specs=[vmem] * 2 + [pl.BlockSpec(memory_space=pl.ANY)] * 2,
        out_specs=[vmem] * len(shapes),
        scratch_shapes=[
            pltpu.VMEM(weight_in.shape, jnp.bfloat16),
            pltpu.VMEM(weight_out.shape, jnp.bfloat16),
            pltpu.VMEM((2 * rows, width), jnp.bfloat16),
            pltpu.VMEM((rows, width), jnp.bfloat16),
            pltpu.VMEM((rows, width), jnp.bfloat16),
            pltpu.SemaphoreType.DMA((5,)),
            pltpu.SemaphoreType.DMA((3,)),
            pltpu.SemaphoreType.DMA((3,)),
        ],
        compiler_params=pltpu.CompilerParams(
            collective_id=number, has_side_effects=True, vmem_limit_bytes=48 * 1024 * 1024
        ),
        name="ffn_back" if backward else "ffn",
    )(first, second, weight_in, weight_out)


def rounds_of(cube):
    bits = list(range(cube.count))
    return [bits[i : i + 2] for i in range(0, cube.count, 2)]


def flipped(cube, bits):
    batch, seq = (lax.axis_index("batch"), lax.axis_index("seq"))
    for k in bits:
        step = 1 - 2 * cube.bit(k)
        if k < cube.seq_bits:
            seq = seq + step * (1 << k)
        else:
            batch = batch + step * (1 << (k - cube.seq_bits))
    return (batch, seq)


def masks_of(bits):
    return [[bits[0]], [bits[1]], bits] if len(bits) == 2 else [bits]


def greet_rounds(cube):
    barrier, count = (pltpu.get_barrier_semaphore(), 0)
    for bits in rounds_of(cube):
        for mask in masks_of(bits):
            pl.semaphore_signal(
                barrier, inc=1, device_id=flipped(cube, mask), device_id_type=MESH
            )
            count += 1
    pl.semaphore_wait(barrier, count)


def sum_rounds(cube, value, slots, send, recv):
    for r, bits in enumerate(rounds_of(cube)):
        mine = sum(cube.bit(k) * (1 << i) for i, k in enumerate(bits))
        slots[r, mine] = value
        copies = []
        for i, mask in enumerate(masks_of(bits)):
            copies.append(
                pltpu.make_async_remote_copy(
                    src_ref=slots.at[r, mine],
                    dst_ref=slots.at[r, mine],
                    send_sem=send.at[r, i],
                    recv_sem=recv.at[r, i],
                    device_id=flipped(cube, mask),
                    device_id_type=MESH,
                )
            )
            copies[i].start()
        for copy in copies:
            copy.wait()
        value = slots[r, 0] + slots[r, 1]
        if len(bits) == 2:
            value = value + (slots[r, 2] + slots[r, 3])
    return value


def conv_halo(cube, wide, halo_send, halo_recv, send, recv):
    rows = wide.shape[0] - 16
    mine = cube.bit(0)
    halo_send[...] = wide[pl.ds(pl.multiple_of(8 + (1 - mine) * (rows - 8), 8), 8), :]
    copy = to_partner(cube, 0, halo_send, halo_recv, send.at[0], recv.at[0])
    copy.start()
    edge = pl.ds(pl.multiple_of(mine * (rows + 8), 8), 8)
    wide[edge, :] = jnp.zeros((8, wide.shape[1]), jnp.float32)
    copy.wait()
    wide[pl.ds(pl.multiple_of((1 - mine) * (rows + 8), 8), 8), :] = halo_recv[...]


def row_sum(values):
    return jnp.sum(values, axis=0, keepdims=True)


def conv_kernel(cube, taps, *refs):
    values, norms, marks, weight_in, weight_out = refs[:5]
    after, unit_out, inverse_out, hidden, gate, sigma, wide, centred, swish, stats = refs[5:15]
    into, outof, mixed, slots, halo_send, halo_recv, load, send, recv, h_send, h_recv = refs[15:]
    rows, width = values.shape
    block = width // 4
    loads = [
        pltpu.make_async_copy(weight_in, into, load.at[0]),
        pltpu.make_async_copy(weight_out, outof, load.at[1]),
    ]
    for one in loads:
        one.start()

    def normalise(i, carry):
        part = pl.ds(pl.multiple_of(i * 32, 32), 32)
        here = values[part, :]
        away = here - jnp.mean(here, axis=1, keepdims=True)
        inverse = lax.rsqrt(jnp.mean(away * away, axis=1, keepdims=True) + epsilon)
        unit = away * inverse
        unit_out[part, :] = unit
        inverse_out[part, :] = jnp.broadcast_to(inverse, (32, 128))
        hidden[part, :] = (unit * norms[0:1, :] + norms[1:2, :]).astype(jnp.bfloat16)
        return carry

    lax.fori_loop(0, rows // 32, normalise, 0)
    greet_rounds(cube)
    loads[0].wait()

    def point(i, carry):
        part = pl.ds(pl.multiple_of(i * block, block), block)
        other = pl.ds(pl.multiple_of(width + i * block, block), block)
        level = matmul(hidden[...], into[:, part])
        open_ = jax.nn.sigmoid(matmul(hidden[...], into[:, other]))
        gate[:, part] = level
        sigma[:, part] = open_
        wide[pl.ds(8, rows), part] = (level * open_).astype(jnp.bfloat16).astype(jnp.float32)
        return carry

    lax.fori_loop(0, 4, point, 0)
    conv_halo(cube, wide, halo_send, halo_recv, h_send, h_recv)
    reach = taps // 2
    mask = marks[:, taps : taps + 1]

    def mix(i, carry):
        part = pl.ds(pl.multiple_of(i * block, block), block)
        total = jnp.zeros((rows, block), jnp.float32)
        for o in range(taps):
            total = total + norms[8 + o : 9 + o, part] * (
                wide[8 + o - reach : 8 + o - reach + rows, part] * marks[:, o : o + 1]
            )
        mixed[:, part] = total
        masked = total * mask
        stats[0:1, part] = row_sum(masked)
        stats[1:2, part] = row_sum(masked * total)
        return carry

    lax.fori_loop(0, 4, mix, 0)
    stats[2:3, :] = jnp.broadcast_to(row_sum(mask), (1, width))
    stats[3:8, :] = jnp.zeros((5, width), jnp.float32)
    total = sum_rounds(cube, stats[...], slots, send, recv)
    count = total[2:3, :]
    mean = total[0:1, :] / count
    var = total[1:2, :] / count - mean * mean
    stats[0:1, :] = mean
    stats[1:2, :] = var
    stats[2:3, :] = count
    stats[3:4, :] = lax.rsqrt(var + epsilon)

    def finish(i, carry):
        part = pl.ds(pl.multiple_of(i * block, block), block)
        middle = (mixed[:, part] - stats[0:1, part]) * stats[3:4, part]
        centred[:, part] = middle
        swish[:, part] = jax.nn.silu(middle * norms[2:3, part] + norms[3:4, part]).astype(
            jnp.bfloat16
        )
        return carry

    lax.fori_loop(0, 4, finish, 0)
    loads[1].wait()

    def project(i, carry):
        part = pl.ds(pl.multiple_of(i * block, block), block)
        after[:, part] = values[:, part] + matmul(swish[...], outof[:, part])
        return carry

    lax.fori_loop(0, 4, project, 0)


def conv_back_kernel(cube, taps, *refs):
    d_values, norms, marks, stats, centred, wide, gate, sigma, unit, inverse = refs[:10]
    weight_in, weight_out = refs[10:12]
    d_after, attn_branch, branch, d_point, sums = refs[12:17]
    into, outof, d_bn, d_wide, d_norm, pack, slots, halo_send, halo_recv, load, send, recv, h_send, h_recv = refs[17:]
    rows, width = d_values.shape
    block = width // 4
    loads = [
        pltpu.make_async_copy(weight_out, outof, load.at[0]),
        pltpu.make_async_copy(weight_in, into, load.at[1]),
    ]
    for one in loads:
        one.start()
    branch[...] = d_values[...].astype(jnp.bfloat16)
    greet_rounds(cube)
    reach = taps // 2
    mask = marks[:, taps : taps + 1]
    loads[0].wait()

    def enter(i, carry):
        part = pl.ds(pl.multiple_of(i * block, block), block)
        middle = centred[:, part]
        slope = swish_slope(middle * norms[2:3, part] + norms[3:4, part])
        value = transposed_right(branch[...], outof[part, :]) * slope
        d_bn[:, part] = value
        masked = value * mask
        pack[0:1, part] = row_sum(masked * middle)
        pack[1:2, part] = row_sum(masked)
        return carry

    lax.fori_loop(0, 4, enter, 0)
    pack[2:8, :] = jnp.zeros((6, width), jnp.float32)
    pack[...] = sum_rounds(cube, pack[...], slots, send, recv)

    def spread(i, carry):
        part = pl.ds(pl.multiple_of(i * block, block), block)
        share = mask * (pack[1:2, part] + centred[:, part] * pack[0:1, part])
        value = (
            norms[2:3, part] * stats[3:4, part] * (d_bn[:, part] - share / stats[2:3, part])
        )
        d_wide[pl.ds(8, rows), part] = value.astype(jnp.bfloat16).astype(jnp.float32)
        return carry

    lax.fori_loop(0, 4, spread, 0)
    conv_halo(cube, d_wide, halo_send, halo_recv, h_send, h_recv)
    sums[...] = jnp.zeros_like(sums)

    def unmix(i, carry):
        part = pl.ds(pl.multiple_of(i * block, block), block)
        own = d_wide[8 : 8 + rows, part]
        total = jnp.zeros((rows, block), jnp.float32)
        for o in range(taps):
            back = taps - 1 - o
            sums[o : o + 1, part] = row_sum(
                own * (wide[8 + o - reach : 8 + o - reach + rows, part] * marks[:, o : o + 1])
            )
            total = total + norms[8 + o : 9 + o, part] * (
                d_wide[8 + back - reach : 8 + back - reach + rows, part]
                * marks[:, back : back + 1]
            )
        open_ = sigma[:, part]
        other = pl.ds(pl.multiple_of(width + i * block, block), block)
        d_point[:, part] = (total * open_).astype(jnp.bfloat16)
        d_point[:, other] = (total * gate[:, part] * open_ * (1.0 - open_)).astype(jnp.bfloat16)
        return carry

    lax.fori_loop(0, 4, unmix, 0)
    loads[1].wait()

    def project(i, carry):
        part = pl.ds(pl.multiple_of(i * block, block), block)
        value = transposed_right(d_point[...], into[part, :])
        d_norm[:, part] = value
        sums[8:9, part] = row_sum(value * unit[:, part])
        sums[9:10, part] = row_sum(value)
        return carry

    lax.fori_loop(0, 4, project, 0)
    sums[10:12, :] = pack[0:2, :]

    def leave(i, carry):
        part = pl.ds(pl.multiple_of(i * 32, 32), 32)
        here = unit[part, :]
        d_unit = d_norm[part, :] * norms[0:1, :]
        value = d_values[part, :] + inverse[part, 0:1] * (
            d_unit
            - jnp.mean(d_unit, axis=1, keepdims=True)
            - here * jnp.mean(d_unit * here, axis=1, keepdims=True)
        )
        d_after[part, :] = value
        attn_branch[part, :] = value.astype(jnp.bfloat16)
        return carry

    lax.fori_loop(0, rows // 32, leave, 0)


def conv_fast(cube, taps, small, weights, forward):
    rows, width = small[0].shape
    vmem = pl.BlockSpec(memory_space=pltpu.VMEM)
    wide, full, half = ((rows + 16, width), (rows, width), (rows, 2 * width))
    single, double = (jnp.float32, jnp.bfloat16)
    if forward:
        shapes = [
            (full, single),
            (full, single),
            ((rows, 128), single),
            (full, double),
            (full, single),
            (full, single),
            (wide, single),
            (full, single),
            (full, double),
            ((8, width), single),
        ]
        own = [pltpu.VMEM(full, single)]
    else:
        shapes = [(full, single), (full, double), (full, double), (half, double), ((16, width), single)]
        own = [
            pltpu.VMEM(full, single),
            pltpu.VMEM(wide, single),
            pltpu.VMEM(full, single),
            pltpu.VMEM((8, width), single),
        ]
    rounds = len(rounds_of(cube))
    return pl.pallas_call(
        functools.partial(conv_kernel if forward else conv_back_kernel, cube, taps),
        out_shape=[jax.ShapeDtypeStruct(shape, dtype) for shape, dtype in shapes],
        in_specs=[vmem] * len(small) + [pl.BlockSpec(memory_space=pl.ANY)] * 2,
        out_specs=[vmem] * len(shapes),
        scratch_shapes=[
            pltpu.VMEM(weights[0].shape, double),
            pltpu.VMEM(weights[1].shape, double),
        ]
        + own
        + [
            pltpu.VMEM((rounds, 4, 8, width), single),
            pltpu.VMEM((8, width), single),
            pltpu.VMEM((8, width), single),
            pltpu.SemaphoreType.DMA((2,)),
            pltpu.SemaphoreType.DMA((rounds, 3)),
            pltpu.SemaphoreType.DMA((rounds, 3)),
            pltpu.SemaphoreType.DMA((1,)),
            pltpu.SemaphoreType.DMA((1,)),
        ],
        compiler_params=pltpu.CompilerParams(
            collective_id=1 if forward else 2,
            has_side_effects=True,
            vmem_limit_bytes=48 * 1024 * 1024,
        ),
        name="conv" if forward else "conv_back",
    )(*small, *weights)


def cube_of(shards, rel_table, depth_w):
    batch, seq = (lax.axis_size("batch"), lax.axis_size("seq"))
    if seq != 2 or batch < 8 or batch & (batch - 1):
        return None
    if depth_w.shape[0] > 5 or rel_table.shape[0] > 128 or rel_table.shape[1] != 128:
        return None
    if any(shard.shape[0] % 32 or shard.shape[1] % 1024 for shard in shards):
        return None
    return Cube(batch, seq)


def swish_slope(values):
    sigma = jax.nn.sigmoid(values)
    return sigma * (1.0 + values * (1.0 - sigma))


def norm_forward(values, gain, shift):
    mean = jnp.mean(values, axis=-1, keepdims=True)
    centred = values - mean
    inverse = lax.rsqrt(jnp.mean(centred * centred, axis=-1, keepdims=True) + epsilon)
    unit = centred * inverse
    return (unit * gain + shift, unit, inverse)


def norm_backward(d_out, unit, inverse, gain):
    d_unit = d_out * gain
    d_values = inverse * (
        d_unit
        - jnp.mean(d_unit, axis=-1, keepdims=True)
        - unit * jnp.mean(d_unit * unit, axis=-1, keepdims=True)
    )
    return (d_values, jnp.sum(d_out * unit, axis=0), jnp.sum(d_out, axis=0))


def ffn_forward(values, gain, shift, weight_in, weight_out, cube, number):
    normed, unit, inverse = norm_forward(values, gain, shift)
    hidden = normed.astype(jnp.bfloat16)
    if cube is not None:
        after, act, swish, hidden = ffn_fast(
            cube, hidden, values, weight_in, weight_out, number, False
        )
        return (after, (hidden, act, swish, unit, inverse))
    act = matmul(hidden, weight_in)
    swish = jax.nn.silu(act).astype(jnp.bfloat16)
    return (values + 0.5 * matmul(swish, weight_out), (hidden, act, swish, unit, inverse))


def ffn_backward(d_out, kept, gain, weight_in, weight_out, cube, number):
    hidden, act, swish, unit, inverse = kept
    d_branch = (0.5 * d_out).astype(jnp.bfloat16)
    if cube is not None:
        d_hidden, d_act, d_branch = ffn_fast(
            cube, d_branch, act, weight_in, weight_out, number, True
        )
    else:
        d_act = (transposed_right(d_branch, weight_out) * swish_slope(act)).astype(jnp.bfloat16)
        d_hidden = transposed_right(d_act, weight_in)
    d_norm, d_gain, d_shift = norm_backward(d_hidden, unit, inverse, gain)
    return (d_out + d_norm, (hidden, d_act), (swish, d_branch), d_gain, d_shift)


def segment_ids(place, ends, group):
    inside = jnp.sum((place[:, None] >= ends[None, :]).astype(jnp.int32), axis=1)
    return jnp.where((place >= 0) & (place < group), inside, -1)


def to_heads(hidden, weight, heads):
    return matmul(hidden, weight).astype(jnp.bfloat16).reshape(hidden.shape[0], heads, -1)


def spread_band(project, start, group, left, right):
    heads, rows, width = project.shape
    band = rows + width - 1
    blank = jnp.zeros_like(project[:, :, :1])
    middle = jnp.concatenate([blank, project[:, :, 1 : width - 1], blank], axis=2)
    padded = jnp.pad(middle, ((0, 0), (0, 0), (0, band + 1 - width)))
    skewed = padded.reshape(heads, rows * (band + 1))[:, : rows * band].reshape(heads, rows, band)
    canvas = jnp.zeros((heads, rows, group + left + right), jnp.float32)
    anchor = jnp.zeros((), jnp.int32)
    canvas = lax.dynamic_update_slice(canvas, skewed, (anchor, anchor, start))
    return canvas[:, :, left : left + group]


def relative_bins(grad, difference, start, width, left, right):
    heads, rows, group = grad.shape
    band = rows + width - 1
    canvas = jnp.pad(grad, ((0, 0), (0, 0), (left, right)))
    anchor = jnp.zeros((), jnp.int32)
    strip = lax.dynamic_slice(canvas, (anchor, anchor, start), (heads, rows, band))
    flat = jnp.pad(strip.reshape(heads, rows * band), ((0, 0), (0, rows)))
    inner = flat.reshape(heads, rows, band + 1)[:, :, 1 : width - 1]
    below = jnp.sum(jnp.where(difference[None] <= -left, grad, 0.0), axis=2, keepdims=True)
    above = jnp.sum(jnp.where(difference[None] >= right, grad, 0.0), axis=2, keepdims=True)
    return jnp.concatenate([below, inner, above], axis=2)


def block_scores(rows_query, keys, table, segment, start, left, right):
    rows, heads, depth = rows_query.shape
    group = keys.shape[0]
    width = table.shape[0]
    scale = 1.0 / math.sqrt(depth)
    project = jnp.einsum("qhd,rd->hqr", rows_query, table, preferred_element_type=jnp.float32)
    content = jnp.einsum("qhd,khd->hqk", rows_query, keys, preferred_element_type=jnp.float32)
    key_place = jnp.arange(group, dtype=jnp.int32)
    row_place = start + jnp.arange(rows, dtype=jnp.int32)
    difference = key_place[None, :] - row_place[:, None]
    relative = spread_band(project, start, group, left, right)
    relative = relative + jnp.where(difference[None] <= -left, project[:, :, :1], 0.0)
    relative = relative + jnp.where(difference[None] >= right, project[:, :, width - 1 :], 0.0)
    row_segment = lax.dynamic_slice_in_dim(segment, start, rows)
    same = row_segment[:, None] == segment[None, :]
    return (jnp.where(same[None], scale * (content + relative), masked_score), difference)


def attention_forward(query, keys, values, table, segment, block_rows, left, right):
    group = query.shape[0]
    starts = jnp.arange(group // block_rows, dtype=jnp.int32) * block_rows

    def one_block(carry, start):
        rows_query = lax.dynamic_slice_in_dim(query, start, block_rows, 0)
        scores, difference = block_scores(rows_query, keys, table, segment, start, left, right)
        top = jnp.max(scores, axis=2, keepdims=True)
        weights = jnp.exp(scores - top)
        total = jnp.sum(weights, axis=2, keepdims=True)
        probs = (weights / total).astype(jnp.bfloat16)
        rows_out = jnp.einsum("hqk,khd->qhd", probs, values, preferred_element_type=jnp.float32)
        return (carry, (rows_out.astype(jnp.bfloat16), (top + jnp.log(total))[:, :, 0]))

    unused, (pieces, log_total) = lax.scan(one_block, 0, starts)
    return (pieces.reshape(query.shape), log_total)


def attention_backward(
    query, keys, values, table, segment, log_total, d_context, block_rows, left, right
):
    group, heads, depth = query.shape
    width = table.shape[0]
    scale = 1.0 / math.sqrt(depth)
    starts = jnp.arange(group // block_rows, dtype=jnp.int32) * block_rows

    def one_block(carry, operands):
        d_keys, d_values, d_table = carry
        start, block_total = operands
        rows_query = lax.dynamic_slice_in_dim(query, start, block_rows, 0)
        rows_grad = lax.dynamic_slice_in_dim(d_context, start, block_rows, 0)
        scores, difference = block_scores(rows_query, keys, table, segment, start, left, right)
        probs = jnp.exp(scores - block_total[:, :, None])
        d_values = d_values + jnp.einsum(
            "hqk,qhd->khd",
            probs.astype(jnp.bfloat16),
            rows_grad,
            preferred_element_type=jnp.float32,
        )
        d_probs = jnp.einsum("qhd,khd->hqk", rows_grad, values, preferred_element_type=jnp.float32)
        weighted = jnp.sum(probs * d_probs, axis=2, keepdims=True)
        d_scores = (probs * (d_probs - weighted)).astype(jnp.bfloat16)
        bins = relative_bins(
            scale * d_scores.astype(jnp.float32), difference, start, width, left, right
        )
        bins = bins.astype(jnp.bfloat16)
        d_rows = scale * jnp.einsum(
            "hqk,khd->qhd", d_scores, keys, preferred_element_type=jnp.float32
        )
        d_rows = d_rows + jnp.einsum("hqr,rd->qhd", bins, table, preferred_element_type=jnp.float32)
        d_keys = d_keys + scale * jnp.einsum(
            "hqk,qhd->khd", d_scores, rows_query, preferred_element_type=jnp.float32
        )
        d_table = d_table + jnp.einsum(
            "hqr,qhd->rd", bins, rows_query, preferred_element_type=jnp.float32
        )
        return ((d_keys, d_values, d_table), d_rows.astype(jnp.bfloat16))

    zeros_heads = jnp.zeros(query.shape, jnp.float32)
    zeros_table = jnp.zeros(table.shape, jnp.float32)
    (d_keys, d_values, d_table), d_rows = lax.scan(
        one_block, (zeros_heads, zeros_heads, zeros_table), (starts, log_total)
    )
    return (
        d_rows.reshape(query.shape),
        d_keys.astype(jnp.bfloat16),
        d_values.astype(jnp.bfloat16),
        d_table,
    )


def on_device(
    frames,
    lengths,
    cotangent,
    ffn1_in,
    ffn1_out,
    query_w,
    key_w,
    value_w,
    out_w,
    point_in,
    point_out,
    ffn2_in,
    ffn2_out,
    depth_w,
    rel_table,
    norm_gains,
    norm_biases,
    bn_gain,
    bn_shift,
):
    seq_count = lax.axis_size("seq")
    seq_rank = lax.axis_index("seq")
    frames_here, width = frames.shape
    group = frames_here * seq_count
    block_rows = min(512, group)
    kernel_size = depth_w.shape[0]
    reach = kernel_size // 2
    ends = jnp.cumsum(lengths[0])
    last_entry = lengths.shape[1] - 1
    first = seq_rank * frames_here
    wide_place = first - reach + jnp.arange(frames_here + 2 * reach, dtype=jnp.int32)
    wide_segment = segment_ids(wide_place, ends, group)
    own_segment = wide_segment[reach : reach + frames_here]
    mask = (own_segment < last_entry).astype(jnp.float32)[:, None]
    group_segment = segment_ids(jnp.arange(group, dtype=jnp.int32), ends, group)
    shards = (
        ffn1_in,
        ffn1_out,
        query_w,
        key_w,
        value_w,
        out_w,
        point_in,
        point_out,
        ffn2_in,
        ffn2_out,
    )
    cube = cube_of(shards, rel_table, depth_w)
    start_values = frames.astype(jnp.float32)
    first_norm, first_unit, first_inverse = norm_forward(
        start_values, norm_gains[0], norm_biases[0]
    )
    gathered, kept_first = gather_all(
        shards, cube, first_norm.astype(jnp.bfloat16), start_values
    )
    if cube is None:
        after_first, kept_first = ffn_forward(
            start_values, norm_gains[0], norm_biases[0], gathered[0], gathered[1], cube, 7
        )
    else:
        after_first, act, swish, hidden = kept_first
        kept_first = (hidden, act, swish, first_unit, first_inverse)
    attn_norm, attn_unit, attn_inverse = norm_forward(after_first, norm_gains[1], norm_biases[1])
    attn_hidden = attn_norm.astype(jnp.bfloat16)
    if cube is None:
        query_heads, key_heads, value_heads = (
            lax.all_to_all(
                to_heads(attn_hidden, gathered[2], HEADS),
                "seq",
                split_axis=1,
                concat_axis=0,
                tiled=True,
            ),
            lax.all_to_all(
                to_heads(attn_hidden, gathered[3], HEADS),
                "seq",
                split_axis=1,
                concat_axis=0,
                tiled=True,
            ),
            lax.all_to_all(
                to_heads(attn_hidden, gathered[4], HEADS),
                "seq",
                split_axis=1,
                concat_axis=0,
                tiled=True,
            ),
        )
        context_heads, log_total = attention_forward(
            query_heads,
            key_heads,
            value_heads,
            rel_table,
            group_segment,
            block_rows,
            REL_LEFT,
            REL_RIGHT,
        )
        context = lax.all_to_all(context_heads, "seq", split_axis=0, concat_axis=1, tiled=True).reshape(
            frames_here, width
        )
        after_attn = after_first + matmul(context, gathered[5])
    else:
        table = jnp.pad(rel_table, ((0, 128 - rel_table.shape[0]), (0, 0)))
        same = (group_segment[:, None] == group_segment[None, :]).astype(jnp.float32)
        after_attn, context, heads_kept, probs_kept = attend_fast(
            cube, attn_hidden, after_first, same, table, gathered[2:6]
        )
    kernel = depth_w.astype(jnp.float32)
    if cube is None:
        conv_norm, conv_unit, conv_inverse = norm_forward(after_attn, norm_gains[2], norm_biases[2])
        conv_hidden = conv_norm.astype(jnp.bfloat16)
        pointwise = matmul(conv_hidden, gathered[6])
        gate_half = pointwise[:, :width]
        sigma_half = jax.nn.sigmoid(pointwise[:, width:])
        gated = (gate_half * sigma_half).astype(jnp.bfloat16)
        gated_wide = padded_2(gated, (("seq", 0),), reach)
        mixed = jnp.zeros((frames_here, width), jnp.float32)
        for offset in range(kernel_size):
            same = (wide_segment[offset : offset + frames_here] == own_segment).astype(jnp.float32)[
                :, None
            ]
            mixed = (
                mixed
                + kernel[offset] * gated_wide[offset : offset + frames_here].astype(jnp.float32) * same
            )
        total, squares, count = lax.psum(
            (jnp.sum(mixed * mask, axis=0), jnp.sum(mixed * mixed * mask, axis=0), jnp.sum(mask)),
            AXES,
        )
        mean = total / count
        var = squares / count - mean * mean
        bn_inverse = lax.rsqrt(var + epsilon)
        centred = (mixed - mean) * bn_inverse
        bn_out = centred * bn_gain + bn_shift
        conv_swish = jax.nn.silu(bn_out).astype(jnp.bfloat16)
        after_conv = after_attn + matmul(conv_swish, gathered[7])
    else:
        marks = [
            wide_segment[offset : offset + frames_here] == own_segment
            for offset in range(kernel_size)
        ]
        marks = jnp.stack(marks, axis=1).astype(jnp.float32)
        marks = jnp.concatenate([marks, mask], axis=1)
        marks = jnp.pad(marks, ((0, 0), (0, 8 - marks.shape[1])))
        blank = jnp.zeros((4, width), jnp.float32)
        norms = [norm_gains[2], norm_biases[2], bn_gain, bn_shift]
        norms = jnp.concatenate([jnp.stack(norms), blank, kernel, blank[:3]])
        after_conv, *conv_kept, conv_swish, stats = conv_fast(
            cube, kernel_size, (after_attn, norms, marks), (gathered[6], gathered[7]), True
        )
        conv_unit, conv_inverse, conv_hidden, gate_half, sigma_half, gated_wide, centred = conv_kept
        var, count = (stats[1], stats[2])
    after_second, kept_second = ffn_forward(
        after_conv, norm_gains[3], norm_biases[3], gathered[8], gathered[9], cube, 8
    )
    final_norm, final_unit, final_inverse = norm_forward(
        after_second, norm_gains[4], norm_biases[4]
    )
    sample_variance = var * count / (count - 1.0)
    d_final = cotangent.astype(jnp.float32) * mask
    d_second, gain_four, shift_four = norm_backward(
        d_final, final_unit, final_inverse, norm_gains[4]
    )
    d_conv_res, grad_two_in, grad_two_out, gain_three, shift_three = ffn_backward(
        d_second, kept_second, norm_gains[3], gathered[8], gathered[9], cube, 9
    )
    if cube is None:
        conv_branch = d_conv_res.astype(jnp.bfloat16)
        d_bn_out = transposed_right(conv_branch, gathered[7]) * swish_slope(bn_out)
        grad_bn_gain, grad_bn_shift = lax.psum(
            (jnp.sum(d_bn_out * centred * mask, axis=0), jnp.sum(d_bn_out * mask, axis=0)), AXES
        )
        d_mixed = (
            bn_gain * bn_inverse * (d_bn_out - mask * (grad_bn_shift + centred * grad_bn_gain) / count)
        )
        d_mixed = d_mixed.astype(jnp.bfloat16)
        d_mixed_wide = padded_2(d_mixed, (("seq", 0),), reach)
        d_mixed_value = d_mixed.astype(jnp.float32)
        d_gated = jnp.zeros((frames_here, width), jnp.float32)
        kernel_rows = []
        for offset in range(kernel_size):
            same = (wide_segment[offset : offset + frames_here] == own_segment).astype(jnp.float32)[
                :, None
            ]
            shifted_in = gated_wide[offset : offset + frames_here].astype(jnp.float32)
            kernel_rows.append(jnp.sum(d_mixed_value * shifted_in * same, axis=0))
            back = 2 * reach - offset
            same_back = (wide_segment[back : back + frames_here] == own_segment).astype(jnp.float32)[
                :, None
            ]
            d_gated = (
                d_gated
                + kernel[offset]
                * d_mixed_wide[back : back + frames_here].astype(jnp.float32)
                * same_back
            )
        d_pointwise = jnp.concatenate(
            [d_gated * sigma_half, d_gated * gate_half * sigma_half * (1.0 - sigma_half)], axis=1
        ).astype(jnp.bfloat16)
        d_conv_norm, gain_two, shift_two = norm_backward(
            transposed_right(d_pointwise, gathered[6]), conv_unit, conv_inverse, norm_gains[2]
        )
        d_attn_res = d_conv_res + d_conv_norm
        attn_branch = d_attn_res.astype(jnp.bfloat16)
    else:
        d_attn_res, attn_branch, conv_branch, d_pointwise, sums = conv_fast(
            cube,
            kernel_size,
            (
                d_conv_res,
                norms,
                marks,
                stats,
                centred,
                gated_wide,
                gate_half,
                sigma_half,
                conv_unit,
                conv_inverse,
            ),
            (gathered[6], gathered[7]),
            False,
        )
        kernel_rows = [sums[offset] for offset in range(kernel_size)]
        gain_two, shift_two, grad_bn_gain, grad_bn_shift = sums[8], sums[9], sums[10], sums[11]
    if cube is None:
        d_context = (
            transposed_right(attn_branch, gathered[5])
            .astype(jnp.bfloat16)
            .reshape(frames_here, HEADS, -1)
        )
        d_context_heads = lax.all_to_all(d_context, "seq", split_axis=1, concat_axis=0, tiled=True)
        d_query_heads, d_key_heads, d_value_heads, d_table = attention_backward(
            query_heads,
            key_heads,
            value_heads,
            rel_table,
            group_segment,
            log_total,
            d_context_heads,
            block_rows,
            REL_LEFT,
            REL_RIGHT,
        )
        d_query, d_keys, d_values = (
            lax.all_to_all(d_query_heads, "seq", split_axis=0, concat_axis=1, tiled=True),
            lax.all_to_all(d_key_heads, "seq", split_axis=0, concat_axis=1, tiled=True),
            lax.all_to_all(d_value_heads, "seq", split_axis=0, concat_axis=1, tiled=True),
        )
        d_query = d_query.reshape(frames_here, width)
        d_keys = d_keys.reshape(frames_here, width)
        d_values = d_values.reshape(frames_here, width)
        d_attn_hidden = (
            transposed_right(d_query, gathered[2])
            + transposed_right(d_keys, gathered[3])
            + transposed_right(d_values, gathered[4])
        )
        heads_in = jnp.concatenate([d_query, d_keys, d_values], axis=1)
    else:
        d_attn_hidden, heads_in, d_table = attend_back_fast(
            cube, attn_branch, heads_kept, probs_kept, table, gathered[2:6]
        )
        d_table = d_table[: rel_table.shape[0]]
    d_attn_norm, gain_one, shift_one = norm_backward(
        d_attn_hidden, attn_unit, attn_inverse, norm_gains[1]
    )
    d_first_res = d_attn_res + d_attn_norm
    d_input, grad_one_in, grad_one_out, gain_zero, shift_zero = ffn_backward(
        d_first_res, kept_first, norm_gains[0], gathered[0], gathered[1], cube, 10
    )
    gains_local = jnp.stack([gain_zero, gain_one, gain_two, gain_three, gain_four])
    shifts_local = jnp.stack([shift_zero, shift_one, shift_two, shift_three, shift_four])
    kernel_local = jnp.stack(kernel_rows)
    shards, (grad_gains, grad_biases, grad_depth, grad_rel) = gradient_shards(
        (
            grad_two_out,
            grad_two_in,
            grad_one_in,
            grad_one_out,
            (conv_hidden, d_pointwise),
            (attn_hidden, heads_in),
            (conv_swish, conv_branch),
            (context, attn_branch),
        ),
        (gains_local, shifts_local, kernel_local, d_table),
        cube,
    )
    two_out, two_in, one_in, one_out, conv_in, attn_in, conv_out, attn_out = shards
    return (
        final_norm.astype(jnp.bfloat16),
        d_input.astype(jnp.bfloat16),
        one_in,
        one_out,
        attn_in[:, :width],
        attn_in[:, width : 2 * width],
        attn_in[:, 2 * width :],
        attn_out,
        conv_in,
        conv_out,
        two_in,
        two_out,
        grad_depth,
        grad_rel,
        grad_gains,
        grad_biases,
        grad_bn_gain,
        grad_bn_shift,
        sample_variance,
    )


def solution(mesh):
    placed = (
        P(("batch", "seq"), None),
        P("batch", None),
        P(("batch", "seq"), None),
        P(("batch", "seq"), None),
        P(("batch", "seq"), None),
        P(("batch", "seq"), None),
        P(("batch", "seq"), None),
        P(("batch", "seq"), None),
        P(("batch", "seq"), None),
        P(("batch", "seq"), None),
        P(("batch", "seq"), None),
        P(("batch", "seq"), None),
        P(("batch", "seq"), None),
        P(),
        P(),
        P(),
        P(),
        P(),
        P(),
    )
    return jax.shard_map(
        on_device,
        mesh=mesh,
        in_specs=placed,
        out_specs=(
            P(("batch", "seq"), None),
            P(("batch", "seq"), None),
            P(("batch", "seq"), None),
            P(("batch", "seq"), None),
            P(("batch", "seq"), None),
            P(("batch", "seq"), None),
            P(("batch", "seq"), None),
            P(("batch", "seq"), None),
            P(("batch", "seq"), None),
            P(("batch", "seq"), None),
            P(("batch", "seq"), None),
            P(("batch", "seq"), None),
            P(),
            P(),
            P(),
            P(),
            P(),
            P(),
            P(),
        ),
        check_vma=False,
    )
```
